128 devices in a mesh: tile: 32 (over y, x, core), vis: 4 (over z).
Axes of the slice: x: 4, y: 4, z: 4, core: 2. Of those that a mesh axis runs over, the one named last changes fastest.
Arguments:
- pieces: float32 [4096, 16, 1024], P(('tile', 'vis')), may hold values from -6 to 6
- coeffs: float32 [4096, 5, 4], P(('tile', 'vis')), may hold values from -1.8 to 1.8
- weights: float32 [4096], P(('tile', 'vis')), may hold values from 0.1 to 1
- routes: int32 [4096, 1], P(('tile', 'vis')), may hold values from 0 to 31; in each aligned block of 32 rows (0 to 31, 32 to 63, ...) at most 2 rows name the same one
- offsets: int32 [4096], P(('tile', 'vis')), may hold values from 0 to 63
Outputs:
- coadd: float32 [32768, 1024], P(('tile', 'vis'))
- detection: float32 [32768, 1024], P(('tile', 'vis'))
The draws below stay inside these ranges and needn't reach their ends.
Inputs may be any that keep to these rules, and one draw needn't show every extreme that they name: `routes`: among the 32 pieces of one device no strip index appears more than 2 times, and some index appears exactly 2 times; every strip index appears somewhere.
All inputs are finite; a program needn't handle non-finite values.
Results may differ from the reference program's by a relative error of at most 0.0003.
Values sent between devices are 32-bit elements; how exact they have to be, the bound alone decides.
No kernel may reach another device: no remote copies, remote signals or barrier semaphores. Data moves between devices by JAX's collectives and lax.ppermute only.
A program may use at most 128 MiB of HBM per device.

```python
import math
import jax
import jax.numpy as jnp
import numpy as np
from jax import lax

SC = 1024
PR = 16
PIECES_DEV = 32
NROW = 5
NCOL = 4
TAPS = 10
REACH = 15
CAP = 2
NBLK = 64
PIECES = 4096
TRACT_ROWS = 32768
N_TILE = 32


def place_ends(values, rng, least, largest):
    extent = values.shape
    place = [jax.random.randint(jax.random.fold_in(rng, axis), (), 0, extent[axis]) for axis in range(len(extent))]
    values = values.at[tuple(place)].set(least)
    longest = extent.index(max(extent))
    place[longest] = (place[longest] + 1) % extent[longest]
    return values.at[tuple(place)].set(largest)


def block_levels(rng, shape, cuts, least, top_value):
    def one(dim, parts):
        heights = jax.random.uniform(jax.random.fold_in(jax.random.fold_in(rng, 6), dim), (parts,), jnp.float32, least / len(cuts), top_value / len(cuts))
        return jnp.repeat(jnp.exp(heights), shape[dim] // parts).reshape((-1,) + (1,) * (len(shape) - dim - 1))

    factor_of = one(*cuts[0])
    for cut in cuts[1:]:
        factor_of = factor_of * one(*cut)
    return factor_of


def shared_out(rng, own, number, rows, count, top, limit, lean):
    order = jax.random.permutation(rng, count)
    crowded, ordinary = load_shares(count, rows * top, limit, lean, True), load_shares(count, rows * top, limit, lean, False)
    places = jnp.arange(count)

    def named(sizes, offset_by):
        used = int((sizes > 0).sum())
        fixed = max(1, used // 4)
        passed = fixed + (places - fixed + offset_by * (used - fixed)) % max(1, count - fixed)
        return jnp.zeros((count,), jnp.int32).at[order[jnp.where(places < fixed, places, passed)]].set(jnp.asarray(sizes, jnp.int32))

    sizes = jnp.where(number % 4 == 0, named(crowded, number // 4), named(ordinary, number - number // 4 - 1))
    mixed = jax.random.permutation(jax.random.fold_in(own, 3), count)
    donor, taker = mixed[0:count // 2 * 2:2], mixed[1:count // 2 * 2:2]
    margin = jnp.minimum(sizes[donor] - 1, limit - sizes[taker]) // 2
    margin = jnp.where((donor == order[0]) | (taker == order[0]) | (sizes[taker] == 0), 0, jnp.maximum(margin, 0))
    passed = jax.random.randint(jax.random.fold_in(own, 4), (count // 2,), 0, 1 << 20) % (margin + 1)
    sizes = sizes.at[donor].add(-passed).at[taker].add(passed)
    labels = jnp.searchsorted(jnp.cumsum(sizes), jnp.arange(rows * top), side="right").astype(jnp.int32)
    listing = labels.reshape(top, rows).T
    listing = listing[jax.random.permutation(jax.random.fold_in(own, 1), rows)]
    offset_by = jax.random.randint(jax.random.fold_in(own, 2), (rows, 1), 0, top)
    return jnp.take_along_axis(listing, (jnp.arange(top)[None, :] + offset_by) % top, axis=1)


def load_shares(count, total, most, lean, full):
    weights = [(1 << 20) // math.isqrt(rank ** lean) + 1 for rank in range(1, count + 1)]
    largest = most if full else min(most, max(-(-total // count), total * weights[0] // sum(weights)))
    least = 1 if total - largest >= count - 1 else 0
    counts, spare = [largest] + [least] * (count - 1), total - largest - least * (count - 1)
    while spare > 0:
        free = [i for i in range(1, count) if counts[i] < largest] or [i for i in range(1, count) if counts[i] < most]
        mass, remaining = sum([weights[i] for i in free]), spare
        for i in free:
            addition = min(most - counts[i], max(1, remaining * weights[i] // mass), spare)
            counts[i] = counts[i] + addition
            spare = spare - addition
    return np.array(counts)


def normal_values(own_key, dims, deviation, reach, cuts=(), dtype=jnp.bfloat16):
    loudness = block_levels(own_key, dims, cuts, -0.22, 0.18) if cuts else 1.0
    values = jax.random.normal(own_key, dims, jnp.float32) * deviation * loudness
    return jnp.minimum(jnp.maximum(values, -reach), reach).astype(dtype)


def setup_inputs(seed: int = 0) -> dict:
    seeds = jax.random.split(jax.random.key(seed), 6)
    pieces = normal_values(seeds[0], (PIECES, PR, SC), 1.0, 6.0, ((0, 128),), jnp.float32)
    coeffs = normal_values(seeds[1], (PIECES, NROW, NCOL), 0.3, 1.8, ((0, 128),), jnp.float32)
    weights = jnp.clip(jnp.exp(math.log(1.0) - 2.3025851 * jax.random.uniform(seeds[2], (PIECES,), jnp.float32) ** block_levels(seeds[2], (PIECES,), ((0, 128),), -0.2, 0.2)), 0.1, 1.0)
    routes_keys = jax.random.split(jax.random.fold_in(seeds[3], 1), PIECES // PIECES_DEV)
    routes_turns = jax.random.permutation(jax.random.fold_in(seeds[3], 3), PIECES // PIECES_DEV)
    routes = jax.vmap(lambda own, number: shared_out(jax.random.fold_in(seeds[3], 2), own, number, PIECES_DEV, N_TILE, 1, CAP, 2))(routes_keys, routes_turns).reshape((PIECES, 1))
    offsets = place_ends(jax.random.randint(seeds[4], (PIECES,), 0, NBLK), jax.random.fold_in(seeds[4], 1), 0, NBLK - 1).astype(jnp.int32)
    return {"pieces": pieces, "coeffs": coeffs, "weights": weights, "routes": routes, "offsets": offsets}


row_shapes = ((1.0, 0), (1.0, 1), (2.0, 0), (2.0, 2), (3.5, 0))
column_shapes = ((1.0, 0), (2.0, 0), (2.0, 1), (3.5, 0))
highest = lax.Precision.HIGHEST

def shaped_taps(lag_table, shape_list, tap_reach):
    tap_spots = jnp.arange(-tap_reach, tap_reach + 1).astype(jnp.float32)
    lagged = lag_table.astype(jnp.float32)
    stacked = []
    for spread, degree in shape_list:
        full_taps = jnp.exp(-tap_spots * tap_spots / (2.0 * spread * spread)) * (tap_spots / spread) ** degree
        unit_scale = 1.0 / jnp.sqrt(jnp.sum(full_taps * full_taps))
        values = jnp.exp(-lagged * lagged / (2.0 * spread * spread)) * (lagged / spread) ** degree * unit_scale
        stacked.append(jnp.where(jnp.abs(lag_table) <= tap_reach, values, 0.0))
    return jnp.stack(stacked)

def detect_taps(lag_table, tap_reach):
    tap_spots = jnp.arange(-tap_reach, tap_reach + 1).astype(jnp.float32)
    gauss_total = jnp.sum(jnp.exp(-tap_spots * tap_spots / 18.0))
    lagged = lag_table.astype(jnp.float32)
    values = jnp.exp(-lagged * lagged / 18.0) / gauss_total - 1.0 / (2 * tap_reach + 1)
    return jnp.where(jnp.abs(lag_table) <= tap_reach, values, 0.0)

def basis_tables(piece_rows):
    row_lag = jnp.arange(piece_rows)[None, :] - jnp.arange(piece_rows)[:, None]
    row_bank = shaped_taps(row_lag, row_shapes, TAPS)
    column_lag = jnp.arange(384)[:, None] - 128 - jnp.arange(128)[None, :]
    column_windows = shaped_taps(column_lag, column_shapes, TAPS)
    detect_windows = detect_taps(column_lag, REACH)[None]
    return (row_bank, column_windows, detect_windows)

def column_pass(images, windows):
    lead_count, kernel_count, rows_count, strip_width = images.shape
    blocks = strip_width // 128
    padded = jnp.pad(images, ((0, 0), (0, 0), (0, 0), (128, 128)))
    viewed = padded.reshape(lead_count, kernel_count, rows_count, blocks + 2, 128)
    framed = jnp.concatenate([viewed[:, :, :, 0:blocks], viewed[:, :, :, 1:blocks + 1], viewed[:, :, :, 2:blocks + 2]], axis=4)
    result = jnp.einsum('mnrjk,nko->mrjo', framed, windows, precision=highest)
    return result.reshape(lead_count, rows_count, strip_width)

def match_pieces(images, factors, row_bank, column_windows):
    rowed = jnp.einsum('aqp,mpc->maqc', row_bank, images, precision=highest)
    mixed = jnp.einsum('mab,maqc->mbqc', factors, rowed, precision=highest)
    return column_pass(mixed, column_windows)

def reference(pieces, coeffs, weights, routes, offsets):
    piece_rows = pieces.shape[1]
    strip_width = pieces.shape[2]
    row_bank, column_windows, detect_windows = basis_tables(piece_rows)
    batch_size = PIECES_DEV
    groups = pieces.shape[0] // batch_size
    segments_all = N_TILE * NBLK

    def one_group(running, group_data):
        numerator, weight_total = running
        images, factors, masses, targets, places = group_data
        matched = match_pieces(images, factors, row_bank, column_windows)
        segment = (targets[:, 0] * NBLK + places).astype(jnp.int32)
        numerator = numerator + jax.ops.segment_sum(matched * masses[:, None, None], segment, num_segments=segments_all)
        weight_total = weight_total + jax.ops.segment_sum(masses, segment, num_segments=segments_all)
        return ((numerator, weight_total), None)
    start_state = (jnp.zeros((segments_all, piece_rows, strip_width), jnp.float32), jnp.zeros((segments_all,), jnp.float32))
    grouped = (pieces.reshape(groups, batch_size, piece_rows, strip_width), coeffs.reshape(groups, batch_size, NROW, NCOL), weights.reshape(groups, batch_size), routes.reshape(groups, batch_size, 1), offsets.reshape(groups, batch_size))
    (numerator, weight_total), unused = lax.scan(one_group, start_state, grouped)
    has_weight = weight_total > 0.0
    divisor = jnp.where(has_weight, weight_total, 1.0)
    coadd = jnp.where(has_weight[:, None, None], numerator / divisor[:, None, None], 0.0).reshape(TRACT_ROWS, strip_width)
    filtered = column_pass(coadd[None, None], detect_windows)[0]
    padded = jnp.pad(filtered, ((REACH, REACH), (0, 0)))
    row_taps = detect_taps(jnp.arange(-REACH, REACH + 1), REACH)
    detection = jnp.zeros_like(filtered)
    for shift_index in range(2 * REACH + 1):
        detection = detection + row_taps[shift_index] * padded[shift_index:shift_index + TRACT_ROWS]
    return (coadd, detection)
```

```python
import functools
import math

import jax
import jax.numpy as jnp
import numpy as np
from jax import lax
from jax.experimental import pallas as pl
from jax.experimental.pallas import tpu as pltpu
from jax.sharding import PartitionSpec as P

TAPS = 10
REACH = 15
ROW_SHAPES = ((1.0, 0), (1.0, 1), (2.0, 0), (2.0, 2), (3.5, 0))
COLUMN_SHAPES = ((1.0, 0), (2.0, 0), (2.0, 1), (3.5, 0))
LANES = 128
CHUNKS = (4, 4)
BF = jnp.bfloat16
F32 = jnp.float32


def basis_taps(lags, shapes):
    spots = np.arange(-TAPS, TAPS + 1, dtype=np.float64)
    out = []
    for s, d in shapes:
        full = np.exp(-spots * spots / (2 * s * s)) * (spots / s) ** d
        scale = 1.0 / math.sqrt(np.sum(full * full))
        vals = np.exp(-lags * lags / (2 * s * s)) * (lags / s) ** d * scale
        out.append(np.where(np.abs(lags) <= TAPS, vals, 0.0))
    return np.stack(out)


def detect_taps(lags):
    spots = np.arange(-REACH, REACH + 1, dtype=np.float64)
    total = np.sum(np.exp(-spots * spots / 18.0))
    vals = np.exp(-lags * lags / 18.0) / total - 1.0 / (2 * REACH + 1)
    return np.where(np.abs(lags) <= REACH, vals, 0.0)


def halves(a):
    a = np.asarray(a, np.float32)
    hi = a.astype(jnp.bfloat16)
    lo = (a - hi.astype(np.float32)).astype(jnp.bfloat16)
    return hi, lo


def window_lags(n):
    k = np.arange(256, dtype=np.float64)[:, None] - 64
    return k - np.arange(n, dtype=np.float64)[None, :]


def column_weights():
    bank = basis_taps(window_lags(128), COLUMN_SHAPES)
    pairs = np.stack(
        [np.concatenate([bank[0], bank[1]], 1), np.concatenate([bank[2], bank[3]], 1)]
    )
    return halves(pairs)


def row_tables():
    lags = (np.arange(16)[None, :] - np.arange(16)[:, None]).astype(np.float64)
    bank = basis_taps(lags, ROW_SHAPES)
    return np.tile(bank, (1, 1, 16)).astype(np.float32)


def split(x):
    hi = x.astype(BF)
    lo = (x - hi.astype(F32)).astype(BF)
    return hi, lo


def mm(a, b):
    return jnp.dot(a, b, preferred_element_type=F32)


def mm3(ah, al, bh, bl):
    return mm(ah, bh) + (mm(al, bh) + mm(ah, bl))


def shift64(prev, cur, lane):
    return jnp.where(lane < 64, pltpu.roll(prev, 64, 1), pltpu.roll(cur, 64, 1))


def match_kernel(
    nt, at_start, at_end, has_meta,
    routes, offsets, weights, coeffs,
    gt, whi, wlo, left, main, right,
    out,
    xs_hi, xs_lo, yhi, ylo, lhi, llo, cnt, dst, rnk,
):
    def clear(i, _):
        cnt[i] = 0
        return 0

    lax.fori_loop(0, 32, clear, 0, unroll=8)

    def place(p, _):
        s = routes[p]
        r = cnt[s]
        cnt[s] = r + 1
        dst[p] = s
        rnk[p] = r
        return 0

    lax.fori_loop(0, 32, place, 0, unroll=4)
    tiles = out.shape[1]
    zero = jnp.zeros((8, LANES), F32)

    def wipe(d, _):
        for t in range(tiles):
            out[d, t] = zero
        return 0

    lax.fori_loop(0, 32, wipe, 0)
    def shift_rows(rb, _):
        rows = pl.ds(pl.multiple_of(rb * 64, 64), 64)
        lane = lax.broadcasted_iota(jnp.int32, (64, LANES), 1)
        blank = jnp.zeros((64, LANES), F32)
        parts = [blank if at_start else left[rows, :]]
        for t in range(nt):
            parts.append(main[rows, t * LANES : (t + 1) * LANES])
        parts.append(blank if at_end else right[rows, :])
        turned = [pltpu.roll(x, 64, 1) for x in parts]
        for t in range(nt + 1):
            v = jnp.where(lane < 64, turned[t], turned[t + 1])
            hi, lo = split(v)
            xs_hi[rows, t * LANES : (t + 1) * LANES] = hi
            xs_lo[rows, t * LANES : (t + 1) * LANES] = lo
        return 0

    lax.fori_loop(0, 8, shift_rows, 0)

    def row_matrix(g, _):
        lane = lax.broadcasted_iota(jnp.int32, (16, LANES), 1)
        for i in range(4):
            p = g * 4 + i
            w = weights[p]
            for h in range(2):
                acc = None
                for a in range(5):
                    c0 = coeffs[a, 2 * h, p] * w
                    c1 = coeffs[a, 2 * h + 1, p] * w
                    term = jnp.where(lane < 64, c0, c1) * gt[a, :, h * LANES : (h + 1) * LANES]
                    acc = term if acc is None else acc + term
                acc = jnp.where((lane // 16) % 4 == i, acc, 0.0)
                hi, lo = split(acc)
                lhi[g, 16 * i : 16 * i + 16, h * LANES : (h + 1) * LANES] = hi
                llo[g, 16 * i : 16 * i + 16, h * LANES : (h + 1) * LANES] = lo
        return 0

    lax.fori_loop(0, 8, row_matrix, 0)

    for jp in range(nt // 2):
        for w in range(2):
            j = 2 * jp + w
            win_hi = xs_hi[:, j * LANES : j * LANES + 256]
            win_lo = xs_lo[:, j * LANES : j * LANES + 256]
            for bp in range(2):
                y = mm3(win_hi, win_lo, whi[bp], wlo[bp])
                hi, lo = split(y)
                for e in range(2):
                    b = 2 * bp + e
                    for g in range(8):
                        part = (slice(64 * g, 64 * g + 64), slice(e * LANES, (e + 1) * LANES))
                        spot = (g, slice(64 * b, 64 * b + 64), slice(w * LANES, (w + 1) * LANES))
                        yhi[spot] = hi[part]
                        ylo[spot] = lo[part]

        def row_pass(g, _):
            z = mm3(lhi[g], llo[g], yhi[g], ylo[g])
            for i in range(4):
                p = g * 4 + i
                d = dst[p]
                base = rnk[p] * (2 * nt)
                for h in range(2):
                    for w in range(2):
                        out[d, base + (h * nt + 2 * jp + w)] = z[
                            16 * i + 8 * h : 16 * i + 8 * h + 8, w * LANES : (w + 1) * LANES
                        ]
            return 0

        lax.fori_loop(0, 8, row_pass, 0)

    if has_meta:
        lane = lax.broadcasted_iota(jnp.int32, (8, LANES), 1)

        def note(p, _):
            d = dst[p]
            at = 2 * rnk[p]
            k = offsets[p].astype(F32)
            old = out[d, tiles - 1]
            out[d, tiles - 1] = jnp.where(
                lane == at, k, jnp.where(lane == at + 1, weights[p], old)
            )
            return 0

        lax.fori_loop(0, 32, note, 0)


def match_chunk(pieces2d, routes, offsets, weights, coeffs, tables, first, nt, total, has_meta):
    gt, whi, wlo = tables
    tiles = 4 * nt + (1 if has_meta else 0)
    width = nt * LANES
    smem = pl.BlockSpec(memory_space=pltpu.SMEM)
    full = lambda shape: pl.BlockSpec(shape, lambda i: (0,) * len(shape))
    kernel = functools.partial(match_kernel, nt, first == 0, first + nt == total, has_meta)
    return pl.pallas_call(
        kernel,
        grid=(1,),
        out_shape=jax.ShapeDtypeStruct((32, tiles, 8, LANES), F32),
        in_specs=[
            smem, smem, smem, smem,
            full(gt.shape), full(whi.shape), full(wlo.shape),
            pl.BlockSpec((512, LANES), lambda i: (0, max(first - 1, 0))),
            pl.BlockSpec((512, width), lambda i: (0, first // nt)),
            pl.BlockSpec((512, LANES), lambda i: (0, min(first + nt, total - 1))),
        ],
        out_specs=full((32, tiles, 8, LANES)),
        scratch_shapes=[
            pltpu.VMEM((512, width + LANES), BF),
            pltpu.VMEM((512, width + LANES), BF),
            pltpu.VMEM((8, 256, 256), BF),
            pltpu.VMEM((8, 256, 256), BF),
            pltpu.VMEM((8, 64, 256), BF),
            pltpu.VMEM((8, 64, 256), BF),
            pltpu.SMEM((32,), jnp.int32),
            pltpu.SMEM((32,), jnp.int32),
            pltpu.SMEM((32,), jnp.int32),
        ],
        compiler_params=pltpu.CompilerParams(vmem_limit_bytes=32 << 20),
        cost_estimate=pl.CostEstimate(
            flops=4 * 10**9 * nt // 8, bytes_accessed=(4 << 20) * nt // 8, transcendentals=0
        ),
        name="match",
    )(routes, offsets, weights, coeffs, gt, whi, wlo, pieces2d, pieces2d, pieces2d)


def land_kernel(nt, has_meta, vis_ref, meta, recv, own, p1, m1, p2, m2, acc, wsum):
    me = vis_ref[0]
    per = 2 * nt

    zero = jnp.zeros((8, LANES), F32)

    def wipe(i, _):
        for t in range(per):
            acc[i, t] = zero
        return 0

    lax.fori_loop(0, 64, wipe, 0)
    lane = lax.broadcasted_iota(jnp.int32, (8, LANES), 1)
    if has_meta:
        wsum[...] = zero

    def land(s, _):
        for r in range(2):
            k = meta[s, 2 * r].astype(jnp.int32)
            at = (((k >> 4) - me) & 3) * 16 + (k & 15)
            got = [recv[s, r * per + t] for t in range(per)]
            for t in range(per):
                acc[at, t] += got[t]
            if has_meta:
                wsum[...] += jnp.where(lane == at, meta[s, 2 * r + 1], 0.0)
        return 0

    lax.fori_loop(0, 32, land, 0)

    def move(ref, start, block, count):
        def one(i, _):
            for t in range(per):
                ref[start + i * per + t] = acc[block + i, t]
            return 0

        lax.fori_loop(0, count, one, 0)

    half = 8 * per
    extra = 1 if has_meta else 0
    move(own, 0, 0, 16)
    move(p1, 0, 32, 8)
    move(p1, half + extra, 24, 8)
    move(m1, 0, 40, 8)
    move(m1, half + extra, 48, 8)
    move(p2, 0, 16, 8)
    move(m2, 0, 56, 8)
    if has_meta:
        w = wsum[...]
        own[2 * half] = w
        p2[half] = pltpu.roll(w, LANES - 16, 1)
        p1[half] = pltpu.roll(w, LANES - 32, 1)
        m1[half] = zero
        m2[half] = pltpu.roll(w, LANES - 48, 1)


def land_chunk(vis, meta, recv, nt, has_meta):
    tiles = recv.shape[1]
    per = 2 * nt
    half = 8 * per
    extra = 1 if has_meta else 0
    full = lambda shape: pl.BlockSpec(shape, lambda i: (0,) * len(shape))
    shapes = [
        (2 * half + extra, 8, LANES),
        (2 * half + extra, 8, LANES),
        (2 * half + extra, 8, LANES),
        (half + extra, 8, LANES),
        (half + extra, 8, LANES),
    ]
    return pl.pallas_call(
        functools.partial(land_kernel, nt, has_meta),
        grid=(1,),
        out_shape=[jax.ShapeDtypeStruct(s, F32) for s in shapes],
        in_specs=[
            pl.BlockSpec(memory_space=pltpu.SMEM),
            pl.BlockSpec(memory_space=pltpu.SMEM),
            full((32, tiles, 8, LANES)),
        ],
        out_specs=[full(s) for s in shapes],
        scratch_shapes=[
            pltpu.VMEM((64, per, 8, LANES), F32),
            pltpu.VMEM((8, LANES), F32),
        ],
        compiler_params=pltpu.CompilerParams(vmem_limit_bytes=32 << 20),
        cost_estimate=pl.CostEstimate(
            flops=10**6, bytes_accessed=(8 << 20) * nt // 8, transcendentals=0
        ),
        name="land",
    )(vis, meta, recv)


def coadd_kernel(chunks, *refs):
    n = len(chunks)
    groups = [refs[5 * c : 5 * c + 5] for c in range(n)]
    coadd, top, bottom = refs[5 * n :]
    lane = lax.broadcasted_iota(jnp.int32, (8, LANES), 1)
    own, p1r, m1r, p2r, m2r = groups[0]
    half = 16 * chunks[0]
    weight = own[2 * half] + p2r[half] + m2r[half]

    def block(kk, high):
        total = jnp.sum(jnp.where(lane == kk, weight, 0.0), axis=1, keepdims=True)
        good = total > 0.0
        div = jnp.where(good, total, 1.0)
        first = 0
        for c in range(n):
            nt = chunks[c]
            per = 2 * nt
            own, p1r, m1r, p2r, m2r = groups[c]
            extra = 1 if c == 0 else 0
            half = 8 * per
            for h in range(2):
                for ct in range(nt):
                    t = h * nt + ct
                    near = (kk - 8) * per + t if high else kk * per + t
                    v = own[kk * per + t]
                    if high:
                        v = v + p1r[half + extra + near] + m2r[near]
                    else:
                        v = v + m1r[half + extra + near] + p2r[near]
                    v = jnp.where(good, v / div, 0.0)
                    rows = pl.ds(pl.multiple_of(kk * 16 + 8 * h, 8), 8)
                    coadd[rows, (first + ct) * LANES : (first + ct + 1) * LANES] = v
            first += nt

    lax.fori_loop(0, 8, lambda kk, _: (block(kk, False), 0)[1], 0)
    lax.fori_loop(8, 16, lambda kk, _: (block(kk, True), 0)[1], 0)
    top[...] = coadd[0:16, :]
    bottom[...] = coadd[240:256, :]


def coadd_all(parts, chunks):
    full = lambda shape: pl.BlockSpec(shape, lambda i: (0,) * len(shape))
    flat = [a for group in parts for a in group]
    total = sum(chunks) * LANES
    outs = [(256, total), (16, total), (16, total)]
    return pl.pallas_call(
        functools.partial(coadd_kernel, chunks),
        grid=(1,),
        out_shape=[jax.ShapeDtypeStruct(s, F32) for s in outs],
        in_specs=[full(a.shape) for a in flat],
        out_specs=[full(s) for s in outs],
        compiler_params=pltpu.CompilerParams(vmem_limit_bytes=32 << 20),
        cost_estimate=pl.CostEstimate(flops=10**6, bytes_accessed=5 << 20, transcendentals=0),
        name="coadd",
    )(*flat)


def column_filter(x_ref, rows, nt, dhi, dlo, xs_hi, xs_lo):
    lane = lax.broadcasted_iota(jnp.int32, (rows, LANES), 1)
    blank = jnp.zeros((rows, LANES), F32)
    parts = [blank] + [x_ref[:, t * LANES : (t + 1) * LANES] for t in range(nt)] + [blank]
    turned = [pltpu.roll(x, 64, 1) for x in parts]
    for t in range(nt + 1):
        v = jnp.where(lane < 64, turned[t], turned[t + 1])
        hi, lo = split(v)
        xs_hi[:, t * LANES : (t + 1) * LANES] = hi
        xs_lo[:, t * LANES : (t + 1) * LANES] = lo
    out = []
    for j in range(nt):
        out.append(
            mm3(
                xs_hi[:, j * LANES : j * LANES + 256],
                xs_lo[:, j * LANES : j * LANES + 256],
                dhi[...],
                dlo[...],
            )
        )
    return out


def inner_kernel(nt, dhi, dlo, bhi, blo, x_ref, out, xs_hi, xs_lo):
    cols = column_filter(x_ref, 256, nt, dhi, dlo, xs_hi, xs_lo)
    for j in range(nt // 2):
        y = jnp.concatenate([cols[2 * j], cols[2 * j + 1]], axis=1)
        yhi, ylo = split(y)
        out[:, j * 256 : (j + 1) * 256] = mm3(bhi[...], blo[...], yhi, ylo)


def inner_detect(coadd, tables):
    dhi, dlo, bhi, blo = tables
    total = coadd.shape[1]
    full = lambda shape: pl.BlockSpec(shape, lambda i: (0,) * len(shape))
    return pl.pallas_call(
        functools.partial(inner_kernel, total // LANES),
        grid=(1,),
        out_shape=jax.ShapeDtypeStruct(coadd.shape, F32),
        in_specs=[full(a.shape) for a in (dhi, dlo, bhi, blo, coadd)],
        out_specs=full(coadd.shape),
        scratch_shapes=[
            pltpu.VMEM((256, total + LANES), BF),
            pltpu.VMEM((256, total + LANES), BF),
        ],
        compiler_params=pltpu.CompilerParams(vmem_limit_bytes=32 << 20),
        cost_estimate=pl.CostEstimate(
            flops=2 * 10**9, bytes_accessed=2 << 20, transcendentals=0
        ),
        name="inner",
    )(dhi, dlo, bhi, blo, coadd)


def edge_kernel(nt, dhi, dlo, ehi, elo, part, above, below, out, both, xs_hi, xs_lo):
    both[0:16, :] = above[...]
    both[16:32, :] = below[...]
    cols = column_filter(both, 32, nt, dhi, dlo, xs_hi, xs_lo)
    for j in range(nt):
        yhi, ylo = split(cols[j])
        out[:, j * LANES : (j + 1) * LANES] = part[:, j * LANES : (j + 1) * LANES] + mm3(
            ehi[...], elo[...], yhi, ylo
        )


def edge_detect(part, above, below, tables, etables):
    dhi, dlo = tables[:2]
    ehi, elo = etables
    total = part.shape[1]
    whole = lambda a: pl.BlockSpec(a.shape, lambda i: (0,) * a.ndim)
    return pl.pallas_call(
        functools.partial(edge_kernel, total // LANES),
        grid=(2,),
        out_shape=jax.ShapeDtypeStruct(part.shape, F32),
        in_specs=[
            whole(dhi), whole(dlo),
            pl.BlockSpec((16, 32), lambda i: (i, 0)),
            pl.BlockSpec((16, 32), lambda i: (i, 0)),
            pl.BlockSpec((16, total), lambda i: (15 * i, 0)),
            whole(above), whole(below),
        ],
        out_specs=pl.BlockSpec((16, total), lambda i: (15 * i, 0)),
        scratch_shapes=[
            pltpu.VMEM((32, total), F32),
            pltpu.VMEM((32, total + LANES), BF),
            pltpu.VMEM((32, total + LANES), BF),
        ],
        input_output_aliases={4: 0},
        compiler_params=pltpu.CompilerParams(vmem_limit_bytes=16 << 20),
        cost_estimate=pl.CostEstimate(
            flops=10**8, bytes_accessed=1 << 18, transcendentals=0
        ),
        name="edge",
    )(dhi, dlo, ehi, elo, part, above, below)


def detect_tables():
    dhi, dlo = halves(detect_taps(window_lags(128)))
    idx = np.arange(256, dtype=np.float64)
    bhi, blo = halves(detect_taps(idx[None, :] - idx[:, None]))
    q = np.arange(16, dtype=np.float64)
    edge = np.zeros((32, 32))
    edge[0:16, 0:16] = detect_taps((q[None, :] - 16) - q[:, None])
    edge[16:32, 16:32] = detect_taps((q[None, :] + 16) - q[:, None])
    ehi, elo = halves(edge)
    return (dhi, dlo, bhi, blo), (ehi, elo)


def shards(pieces, coeffs, weights, routes, offsets):
    count, rows, width = pieces.shape
    total = width // LANES
    pieces2d = pieces.reshape(count * rows, width)
    route1 = routes.reshape(count)
    coeffs_t = jnp.transpose(coeffs, (1, 2, 0))
    whi, wlo = column_weights()
    tables = (jnp.asarray(row_tables()), jnp.asarray(whi), jnp.asarray(wlo))
    dtables, etables = detect_tables()
    dtables = tuple(jnp.asarray(a) for a in dtables)
    etables = tuple(jnp.asarray(a) for a in etables)
    vis = lax.axis_index("vis").reshape(1)
    nv = lax.axis_size("vis")
    up = [(i, (i + 1) % nv) for i in range(nv)]
    down = [((i + 1) % nv, i) for i in range(nv)]

    first = 0
    parts = []
    meta = None
    for c, nt in enumerate(CHUNKS):
        slots = match_chunk(
            pieces2d, route1, offsets, weights, coeffs_t, tables, first, nt, total, c == 0
        )
        recv = lax.all_to_all(slots, "tile", split_axis=0, concat_axis=0, tiled=True)
        if c == 0:
            meta = recv[:, 4 * nt, 0, 0:4]
        own, p1, m1, p2, m2 = land_chunk(vis, meta, recv, nt, c == 0)
        head = p2.shape[0]
        p1r = lax.ppermute(p1, "vis", up)
        m1r = lax.ppermute(m1, "vis", down)
        p2r = lax.ppermute(p2 + p1r[:head], "vis", up)
        m2r = lax.ppermute(m2 + m1r[:head], "vis", down)
        parts.append((own, p1r, m1r, p2r, m2r))
        first += nt

    coadd, top, bottom = coadd_all(parts, CHUNKS)
    n = lax.axis_size("tile") * nv
    axes = ("tile", "vis")
    above = lax.ppermute(bottom, axes, [(i, i + 1) for i in range(n - 1)])
    below = lax.ppermute(top, axes, [(i + 1, i) for i in range(n - 1)])
    part = inner_detect(coadd, dtables)
    detection = edge_detect(part, above, below, dtables, etables)
    return (coadd, detection)


def solution(mesh):
    placed = (
        P(("tile", "vis"), None, None),
        P(("tile", "vis"), None, None),
        P(("tile", "vis")),
        P(("tile", "vis"), None),
        P(("tile", "vis")),
    )
    return jax.shard_map(
        shards,
        mesh=mesh,
        in_specs=placed,
        out_specs=(P(("tile", "vis"), None), P(("tile", "vis"), None)),
        check_vma=False,
    )
```

```python
import functools
import math

import jax
import jax.numpy as jnp
import numpy as np
from jax import lax
from jax.experimental import pallas as pl
from jax.experimental.pallas import tpu as pltpu
from jax.sharding import PartitionSpec as P


TAPS = 10
REACH = 15
ROW_SHAPES = ((1.0, 0), (1.0, 1), (2.0, 0), (2.0, 2), (3.5, 0))
COLUMN_SHAPES = ((1.0, 0), (2.0, 0), (2.0, 1), (3.5, 0))
LANES = 128
CHUNKS = (4, 4)
BF = jnp.bfloat16
F32 = jnp.float32


def basis_taps(lags, shapes):
    spots = np.arange(-TAPS, TAPS + 1, dtype=np.float64)
    out = []
    for s, d in shapes:
        full = np.exp(-spots * spots / (2 * s * s)) * (spots / s) ** d
        scale = 1.0 / math.sqrt(np.sum(full * full))
        vals = np.exp(-lags * lags / (2 * s * s)) * (lags / s) ** d * scale
        out.append(np.where(np.abs(lags) <= TAPS, vals, 0.0))
    return np.stack(out)


def detect_taps(lags):
    spots = np.arange(-REACH, REACH + 1, dtype=np.float64)
    total = np.sum(np.exp(-spots * spots / 18.0))
    vals = np.exp(-lags * lags / 18.0) / total - 1.0 / (2 * REACH + 1)
    return np.where(np.abs(lags) <= REACH, vals, 0.0)


def halves(a):
    a = np.asarray(a, np.float32)
    hi = a.astype(jnp.bfloat16)
    lo = (a - hi.astype(np.float32)).astype(jnp.bfloat16)
    return hi, lo


def window_lags(n):
    k = np.arange(256, dtype=np.float64)[:, None] - 64
    return k - np.arange(n, dtype=np.float64)[None, :]


def column_weights():
    bank = basis_taps(window_lags(128), COLUMN_SHAPES)
    nt = np.stack(
        [np.concatenate([bank[0], bank[1]], 1), np.concatenate([bank[2], bank[3]], 1)]
    )
    return halves(nt)


def row_tables():
    lags = (np.arange(16)[None, :] - np.arange(16)[:, None]).astype(np.float64)
    bank = basis_taps(lags, ROW_SHAPES)
    return np.tile(bank, (1, 1, 16)).astype(np.float32)


def split(x):
    hi = x.astype(BF)
    lo = (x - hi.astype(F32)).astype(BF)
    return hi, lo


def mm(a, b):
    return jnp.dot(a, b, preferred_element_type=F32)


def mm3(ah, al, bh, bl):
    return mm(ah, bh) + (mm(al, bh) + mm(ah, bl))


def match_kernel(
    at_start, at_end, nt, has_meta,
    routes, offsets, weights, coeffs,
    gt, whi, wlo, left, main, right,
    out,
    xs_hi, xs_lo, cnt, dst, rnk,
):
    tiles = out.shape[1]

    def clear(i, _):
        cnt[i] = 0
        return 0

    lax.fori_loop(0, 32, clear, 0, unroll=8)

    def place(p, _):
        s = routes[p]
        r = cnt[s]
        cnt[s] = r + 1
        dst[p] = s
        rnk[p] = r
        return 0

    lax.fori_loop(0, 32, place, 0, unroll=4)
    zero = jnp.zeros((8, LANES), F32)

    def wipe(d, _):
        for t in range(tiles):
            out[d, t] = zero
        return 0

    lax.fori_loop(0, 32, wipe, 0)

    def group(g, _):
        rows = pl.ds(pl.multiple_of(g * 64, 64), 64)
        lane = lax.broadcasted_iota(jnp.int32, (64, LANES), 1)
        blank = jnp.zeros((64, LANES), F32)
        parts = [blank if at_start else left[rows, :]]
        parts += [main[rows, t * LANES : (t + 1) * LANES] for t in range(nt)]
        parts += [blank if at_end else right[rows, :]]
        turned = [pltpu.roll(x, 64, 1) for x in parts]
        for t in range(nt + 1):
            v = jnp.where(lane < 64, turned[t], turned[t + 1])
            hi, lo = split(v)
            xs_hi[:, t * LANES : (t + 1) * LANES] = hi
            xs_lo[:, t * LANES : (t + 1) * LANES] = lo
        stack = lambda ref: jnp.concatenate(
            [ref[:, w * LANES : w * LANES + 256] for w in range(nt)], axis=0
        )
        x_hi, x_lo = stack(xs_hi), stack(xs_lo)

        lane = lax.broadcasted_iota(jnp.int32, (16, LANES), 1)
        left_hi, left_lo = [], []
        for i in range(4):
            p = g * 4 + i
            w = weights[p]
            pair = []
            for h in range(2):
                acc = None
                for a in range(5):
                    both = jnp.where(lane < 64, coeffs[a, 2 * h, p], coeffs[a, 2 * h + 1, p])
                    term = both * gt[a, :, h * LANES : (h + 1) * LANES]
                    acc = term if acc is None else acc + term
                acc = jnp.where((lane // 16) % 4 == i, acc * w, 0.0)
                pair.append(split(acc))
            left_hi.append(jnp.concatenate([pair[0][0], pair[1][0]], axis=1))
            left_lo.append(jnp.concatenate([pair[0][1], pair[1][1]], axis=1))
        l_hi = jnp.concatenate(left_hi, axis=0)
        l_both = jnp.concatenate(left_hi + left_lo, axis=0)

        cols = []
        for bp in range(2):
            y = mm3(x_hi, x_lo, whi[bp], wlo[bp])
            cols.append(split(y))

        for jp in range(nt // 2):
            def operand(k):
                blocks = []
                for b in range(4):
                    src = cols[b // 2][k]
                    lanes = slice((b % 2) * LANES, (b % 2 + 1) * LANES)
                    w0 = src[64 * (2 * jp) : 64 * (2 * jp) + 64, lanes]
                    w1 = src[64 * (2 * jp + 1) : 64 * (2 * jp + 1) + 64, lanes]
                    blocks.append(jnp.concatenate([w0, w1], axis=1))
                return jnp.concatenate(blocks, axis=0)

            zz = mm(l_both, operand(0))
            z = zz[0:64] + (zz[64:128] + mm(l_hi, operand(1)))
            for i in range(4):
                p = g * 4 + i
                d = dst[p]
                base = 8 * jp + rnk[p] * 2
                for h in range(2):
                    for w in range(2):
                        out[d, base + (4 * w + h)] = z[
                            16 * i + 8 * h : 16 * i + 8 * h + 8, w * LANES : (w + 1) * LANES
                        ]
        return 0

    lax.fori_loop(0, 8, group, 0)

    if has_meta:
        lane = lax.broadcasted_iota(jnp.int32, (8, LANES), 1)

        def note(p, _):
            d = dst[p]
            at = 2 * rnk[p]
            k = offsets[p].astype(F32)
            old = out[d, tiles - 1]
            out[d, tiles - 1] = jnp.where(
                lane == at, k, jnp.where(lane == at + 1, weights[p], old)
            )
            return 0

        lax.fori_loop(0, 32, note, 0)


def full(shape):
    return pl.BlockSpec(shape, lambda i: (0,) * len(shape))


def match_chunk(pieces2d, routes, offsets, weights, coeffs, tables, first, nt, has_meta):
    gt, whi, wlo = tables
    tiles = 4 * nt + (1 if has_meta else 0)
    width = nt * LANES
    smem = pl.BlockSpec(memory_space=pltpu.SMEM)
    kernel = functools.partial(match_kernel, first == 0, first + nt == 8, nt, has_meta)
    return pl.pallas_call(
        kernel,
        grid=(1,),
        out_shape=jax.ShapeDtypeStruct((32, tiles, 8, LANES), F32),
        in_specs=[
            smem, smem, smem, smem,
            full(gt.shape), full(whi.shape), full(wlo.shape),
            pl.BlockSpec((512, LANES), lambda i: (0, max(first - 1, 0))),
            pl.BlockSpec((512, width), lambda i: (0, first // nt)),
            pl.BlockSpec((512, LANES), lambda i: (0, min(first + nt, 7))),
        ],
        out_specs=full((32, tiles, 8, LANES)),
        scratch_shapes=[
            pltpu.VMEM((64, width + LANES), BF),
            pltpu.VMEM((64, width + LANES), BF),
            pltpu.SMEM((32,), jnp.int32),
            pltpu.SMEM((32,), jnp.int32),
            pltpu.SMEM((32,), jnp.int32),
        ],
        compiler_params=pltpu.CompilerParams(
            vmem_limit_bytes=(60 << 20) if first == 0 else (24 << 20)
        ),
        cost_estimate=pl.CostEstimate(
            flops=10**9 * nt, bytes_accessed=(1 << 19) * nt, transcendentals=0
        ),
        name="match",
    )(routes, offsets, weights, coeffs, gt, whi, wlo, pieces2d, pieces2d, pieces2d)


def land_kernel(nt, has_meta, vis_ref, meta, recv, own, up, opp, down, acc, wsum, spot):
    me = vis_ref[0]
    per = 2 * nt
    zero = jnp.zeros((8, LANES), F32)

    def wipe(i, _):
        for t in range(per):
            acc[i, t] = zero
        return 0

    lax.fori_loop(0, 64, wipe, 0, unroll=4)
    lane = lax.broadcasted_iota(jnp.int32, (8, LANES), 1)
    if has_meta:
        wsum[...] = zero

    def address(s, _):
        for r in range(2):
            k = meta[s, 2 * r].astype(jnp.int32)
            spot[2 * s + r] = (((k >> 4) - me) & 3) * 16 + (k & 15)
        return 0

    lax.fori_loop(0, 32, address, 0, unroll=4)

    def land(s, _):
        for r in range(2):
            at = spot[2 * s + r]
            got = [recv[s, (t // 2) * 4 + 2 * r + t % 2] for t in range(per)]
            for t in range(per):
                acc[at, t] += got[t]
            if has_meta:
                wsum[...] += jnp.where(lane == at, meta[s, 2 * r + 1], 0.0)
        return 0

    lax.fori_loop(0, 32, land, 0, unroll=4)

    for rel, ref in enumerate((own, up, opp, down)):
        def one(i, _, rel=rel, ref=ref):
            for t in range(per):
                ref[(t // 2) * 32 + i * 2 + t % 2] = acc[16 * rel + i, t]
            return 0

        lax.fori_loop(0, 16, one, 0, unroll=4)
        if has_meta:
            w = wsum[...]
            ref[16 * per] = w if rel == 0 else pltpu.roll(w, LANES - 16 * rel, 1)


def land_chunk(vis, meta, recv, nt, has_meta):
    per = 2 * nt
    shape = (16 * per + (1 if has_meta else 0), 8, LANES)
    smem = pl.BlockSpec(memory_space=pltpu.SMEM)
    return pl.pallas_call(
        functools.partial(land_kernel, nt, has_meta),
        grid=(1,),
        out_shape=[jax.ShapeDtypeStruct(shape, F32)] * 4,
        in_specs=[smem, smem, full(recv.shape)],
        out_specs=[full(shape)] * 4,
        scratch_shapes=[
            pltpu.VMEM((64, per, 8, LANES), F32),
            pltpu.VMEM((8, LANES), F32),
            pltpu.SMEM((64,), jnp.int32),
        ],
        compiler_params=pltpu.CompilerParams(vmem_limit_bytes=24 << 20),
        cost_estimate=pl.CostEstimate(
            flops=10**6, bytes_accessed=(2 << 20) * nt, transcendentals=0
        ),
        name="land",
    )(vis, meta, recv)


def coadd_kernel(first, nt, own, a, b, c, w0, w1, w2, w3, *refs):
    coadd, top, bottom = refs[-3:]
    lane = lax.broadcasted_iota(jnp.int32, (8, LANES), 1)
    weight = w0[0] + w1[0] + w2[0] + w3[0]

    def block(kk, _):
        total = jnp.sum(jnp.where(lane == kk, weight, 0.0), axis=1, keepdims=True)
        good = total > 0.0
        inverse = jnp.where(good, 1.0 / jnp.where(good, total, 1.0), 0.0)
        for ct in range(nt):
            for h in range(2):
                t = ct * 32 + kk * 2 + h
                v = ((own[t] + b[t]) + (a[t] + c[t])) * inverse
                rows = pl.ds(pl.multiple_of(kk * 16 + 8 * h, 8), 8)
                coadd[rows, ct * LANES : (ct + 1) * LANES] = v
        return 0

    lax.fori_loop(0, 16, block, 0, unroll=2)
    here = slice(first * LANES, (first + nt) * LANES)
    if len(refs) > 3:
        for edge, old in ((top, refs[1]), (bottom, refs[2])):
            edge[:, : first * LANES] = old[...]
    top[:, here] = coadd[0:16, :]
    bottom[:, here] = coadd[240:256, :]


def coadd_chunk(group, wgroup, wat, first, nt, before):
    wspec = pl.BlockSpec((1, 8, LANES), lambda i: (wat, 0, 0))
    in_specs = [pl.BlockSpec((32 * nt, 8, LANES), lambda i: (0, 0, 0))] * 4 + [wspec] * 4
    args = list(group) + list(wgroup)
    aliases = {}
    if before is not None:
        in_specs.append(pl.BlockSpec(memory_space=pl.ANY))
        in_specs += [full(x.shape) for x in before[1:]]
        args += list(before)
        aliases = {8: 0}
    edge = (16, LANES * (first + nt))
    return pl.pallas_call(
        functools.partial(coadd_kernel, first, nt),
        grid=(1,),
        out_shape=[
            jax.ShapeDtypeStruct((256, 1024), F32),
            jax.ShapeDtypeStruct(edge, F32),
            jax.ShapeDtypeStruct(edge, F32),
        ],
        in_specs=in_specs,
        out_specs=[
            pl.BlockSpec((256, LANES * nt), lambda i: (0, first // nt)),
            full(edge),
            full(edge),
        ],
        input_output_aliases=aliases,
        compiler_params=pltpu.CompilerParams(vmem_limit_bytes=16 << 20),
        cost_estimate=pl.CostEstimate(
            flops=10**6, bytes_accessed=(5 << 17) * nt, transcendentals=0
        ),
        name="coadd",
    )(*args)


def shifted(rows, parts, store):
    lane = lax.broadcasted_iota(jnp.int32, (rows, LANES), 1)
    blank = jnp.zeros((rows, LANES), F32)
    turned = [pltpu.roll(x, 64, 1) for x in [blank] + parts + [blank]]
    for t in range(len(parts) + 1):
        v = jnp.where(lane < 64, turned[t], turned[t + 1])
        store(slice(t * LANES, (t + 1) * LANES), *split(v))


def inner_kernel(dhi, dlo, bhi, blo, x_ref, out, xs_hi, xs_lo):
    def own_rows(rb, _):
        rows = pl.ds(pl.multiple_of(rb * 32, 32), 32)

        def store(lanes, hi, lo):
            xs_hi[rows, lanes] = hi
            xs_lo[rows, lanes] = lo

        shifted(32, [x_ref[rows, t * LANES : (t + 1) * LANES] for t in range(8)], store)
        return 0

    lax.fori_loop(0, 8, own_rows, 0)
    for j in range(4):
        parts = []
        for w in range(2):
            win = slice((2 * j + w) * LANES, (2 * j + w) * LANES + 256)
            parts.append(mm3(xs_hi[:, win], xs_lo[:, win], dhi[...], dlo[...]))
        hi, lo = split(jnp.concatenate(parts, axis=1))
        out[:, j * 256 : (j + 1) * 256] = mm3(bhi[...], blo[...], hi, lo)


def inner_detect(coadd, tables):
    args = [*tables, coadd]
    return pl.pallas_call(
        inner_kernel,
        grid=(1,),
        out_shape=jax.ShapeDtypeStruct(coadd.shape, F32),
        in_specs=[full(a.shape) for a in args],
        out_specs=full(coadd.shape),
        scratch_shapes=[pltpu.VMEM((256, 1152), BF), pltpu.VMEM((256, 1152), BF)],
        compiler_params=pltpu.CompilerParams(vmem_limit_bytes=16 << 20),
        cost_estimate=pl.CostEstimate(
            flops=2 * 10**9, bytes_accessed=2 << 20, transcendentals=0
        ),
        name="inner",
    )(*args)


def edge_kernel(dhi, dlo, ehi, elo, part, above, below, out, xs_hi, xs_lo, delta):
    step = pl.program_id(0)

    @pl.when(step == 0)
    def _():
        for base, ref in ((0, above), (16, below)):
            rows = slice(base, base + 16)

            def store(lanes, hi, lo, rows=rows):
                xs_hi[rows, lanes] = hi
                xs_lo[rows, lanes] = lo

            shifted(16, [ref[:, t * LANES : (t + 1) * LANES] for t in range(8)], store)
        stack = lambda ref: jnp.concatenate(
            [ref[:, j * LANES : j * LANES + 256] for j in range(8)], axis=0
        )
        y = mm3(stack(xs_hi), stack(xs_lo), dhi[...], dlo[...])
        hi, lo = split(y)
        lay = lambda v: jnp.concatenate([v[32 * j : 32 * j + 32] for j in range(8)], axis=1)
        delta[...] = mm3(ehi[...], elo[...], lay(hi), lay(lo))

    out[...] = part[...] + delta[pl.ds(pl.multiple_of(step * 16, 16), 16), :]


def edge_detect(part, above, below, tables, etables):
    dhi, dlo = tables[:2]
    ehi, elo = etables
    band = pl.BlockSpec((16, 1024), lambda i: (15 * i, 0))
    return pl.pallas_call(
        edge_kernel,
        grid=(2,),
        out_shape=jax.ShapeDtypeStruct(part.shape, F32),
        in_specs=[
            full(dhi.shape), full(dlo.shape), full(ehi.shape), full(elo.shape),
            band, full(above.shape), full(below.shape),
        ],
        out_specs=band,
        scratch_shapes=[
            pltpu.VMEM((32, 1152), BF),
            pltpu.VMEM((32, 1152), BF),
            pltpu.VMEM((32, 1024), F32),
        ],
        input_output_aliases={4: 0},
        compiler_params=pltpu.CompilerParams(vmem_limit_bytes=16 << 20),
        cost_estimate=pl.CostEstimate(
            flops=10**8, bytes_accessed=1 << 18, transcendentals=0
        ),
        name="edge",
    )(dhi, dlo, ehi, elo, part, above, below)


def detect_tables():
    dhi, dlo = halves(detect_taps(window_lags(128)))
    idx = np.arange(256, dtype=np.float64)
    bhi, blo = halves(detect_taps(idx[None, :] - idx[:, None]))
    q = np.arange(16, dtype=np.float64)
    edge = np.zeros((32, 32))
    edge[0:16, 0:16] = detect_taps((q[None, :] - 16) - q[:, None])
    edge[16:32, 16:32] = detect_taps((q[None, :] + 16) - q[:, None])
    ehi, elo = halves(edge)
    return (dhi, dlo, bhi, blo), (ehi, elo)


def shards(pieces, coeffs, weights, routes, offsets):
    count, rows, width = pieces.shape
    pieces2d = pieces.reshape(count * rows, width)
    route1 = routes.reshape(count)
    coeffs_t = jnp.transpose(coeffs, (1, 2, 0))
    whi, wlo = column_weights()
    tables = (jnp.asarray(row_tables()), jnp.asarray(whi), jnp.asarray(wlo))
    dtables, etables = (tuple(map(jnp.asarray, s)) for s in detect_tables())
    vis = lax.axis_index("vis").reshape(1)
    nv = lax.axis_size("vis")
    n = lax.axis_size("tile") * nv
    shifts = [[(i, (i + d) % nv) for i in range(nv)] for d in (1, 2, 3)]
    axes = ("tile", "vis")

    first = 0
    meta = None
    before = None
    wgroup = None
    wat = 16 * 2 * CHUNKS[0]
    for c, nt in enumerate(CHUNKS):
        slots = match_chunk(
            pieces2d, route1, offsets, weights, coeffs_t, tables, first, nt, c == 0
        )
        recv = lax.all_to_all(slots, "tile", split_axis=0, concat_axis=0, tiled=True)
        if c == 0:
            meta = recv[:, 4 * nt, 0, 0:4]
        group = land_chunk(vis, meta, recv, nt, c == 0)
        moved = [group[0]]
        for d in range(3):
            moved.append(lax.ppermute(group[d + 1], "vis", shifts[d]))
        if c == 0:
            wgroup = moved
        before = coadd_chunk(moved, wgroup, wat, first, nt, before)
        first += nt
    coadd, top, bottom = before
    above = lax.ppermute(bottom, axes, [(i, i + 1) for i in range(n - 1)])
    below = lax.ppermute(top, axes, [(i + 1, i) for i in range(n - 1)])
    part = inner_detect(coadd, dtables)
    detection = edge_detect(part, above, below, dtables, etables)
    return (coadd, detection)


def solution(mesh):
    placed = (
        P(("tile", "vis"), None, None),
        P(("tile", "vis"), None, None),
        P(("tile", "vis")),
        P(("tile", "vis"), None),
        P(("tile", "vis")),
    )
    return jax.shard_map(
        shards,
        mesh=mesh,
        in_specs=placed,
        out_specs=(P(("tile", "vis"), None), P(("tile", "vis"), None)),
        check_vma=False,
    )
```

```python
import functools
import math

import jax
import jax.numpy as jnp
import numpy as np
from jax import lax
from jax.experimental import pallas as pl
from jax.experimental.pallas import tpu as pltpu
from jax.sharding import PartitionSpec as P


TAPS = 10
REACH = 15
ROW_SHAPES = ((1.0, 0), (1.0, 1), (2.0, 0), (2.0, 2), (3.5, 0))
COLUMN_SHAPES = ((1.0, 0), (2.0, 0), (2.0, 1), (3.5, 0))
LANES = 128
CHUNKS = (3, 3, 2)
BF = jnp.bfloat16
F32 = jnp.float32


def basis_taps(lags, shapes):
    spots = np.arange(-TAPS, TAPS + 1, dtype=np.float64)
    out = []
    for s, d in shapes:
        full = np.exp(-spots * spots / (2 * s * s)) * (spots / s) ** d
        scale = 1.0 / math.sqrt(np.sum(full * full))
        vals = np.exp(-lags * lags / (2 * s * s)) * (lags / s) ** d * scale
        out.append(np.where(np.abs(lags) <= TAPS, vals, 0.0))
    return np.stack(out)


def detect_taps(lags):
    spots = np.arange(-REACH, REACH + 1, dtype=np.float64)
    total = np.sum(np.exp(-spots * spots / 18.0))
    vals = np.exp(-lags * lags / 18.0) / total - 1.0 / (2 * REACH + 1)
    return np.where(np.abs(lags) <= REACH, vals, 0.0)


def halves(a):
    a = np.asarray(a, np.float32)
    hi = a.astype(jnp.bfloat16)
    lo = (a - hi.astype(np.float32)).astype(jnp.bfloat16)
    return hi, lo


def window_lags(n):
    k = np.arange(256, dtype=np.float64)[:, None] - 64
    return k - np.arange(n, dtype=np.float64)[None, :]


def column_weights():
    bank = basis_taps(window_lags(128), COLUMN_SHAPES)
    nt = np.stack(
        [np.concatenate([bank[0], bank[1]], 1), np.concatenate([bank[2], bank[3]], 1)]
    )
    return halves(nt)


def row_tables():
    lags = (np.arange(16)[None, :] - np.arange(16)[:, None]).astype(np.float64)
    bank = basis_taps(lags, ROW_SHAPES)
    return np.tile(bank, (1, 1, 16)).astype(np.float32)


def split(x):
    hi = x.astype(BF)
    lo = (x - hi.astype(F32)).astype(BF)
    return hi, lo


def mm(a, b):
    return jnp.dot(a, b, preferred_element_type=F32)


def mm3(ah, al, bh, bl):
    return mm(ah, bh) + (mm(al, bh) + mm(ah, bl))


def match_kernel(
    at_start, at_end, nt, has_meta,
    routes, offsets, weights, coeffs,
    gt, whi, wlo, left, main, right,
    out,
    xs_hi, xs_lo, cnt, dst, rnk,
):
    tiles = out.shape[1]

    def clear(i, _):
        cnt[i] = 0
        return 0

    lax.fori_loop(0, 32, clear, 0, unroll=8)

    def place(p, _):
        s = routes[p]
        r = cnt[s]
        cnt[s] = r + 1
        dst[p] = s
        rnk[p] = r
        return 0

    lax.fori_loop(0, 32, place, 0, unroll=4)
    zero = jnp.zeros((8, LANES), F32)

    def wipe(d, _):
        for t in range(tiles):
            out[d, t] = zero
        return 0

    lax.fori_loop(0, 32, wipe, 0)

    def group(g, _):
        rows = pl.ds(pl.multiple_of(g * 64, 64), 64)
        lane = lax.broadcasted_iota(jnp.int32, (64, LANES), 1)
        blank = jnp.zeros((64, LANES), F32)
        parts = [blank if at_start else left[rows, :]]
        parts += [main[rows, t * LANES : (t + 1) * LANES] for t in range(nt)]
        parts += [blank if at_end else right[rows, :]]
        turned = [pltpu.roll(x, 64, 1) for x in parts]
        for t in range(nt + 1):
            v = jnp.where(lane < 64, turned[t], turned[t + 1])
            hi, lo = split(v)
            xs_hi[:, t * LANES : (t + 1) * LANES] = hi
            xs_lo[:, t * LANES : (t + 1) * LANES] = lo
        stack = lambda ref: jnp.concatenate(
            [ref[:, w * LANES : w * LANES + 256] for w in range(nt)], axis=0
        )
        x_hi, x_lo = stack(xs_hi), stack(xs_lo)

        lane = lax.broadcasted_iota(jnp.int32, (16, LANES), 1)
        left_hi, left_lo = [], []
        for i in range(4):
            p = g * 4 + i
            w = weights[p]
            pair = []
            for h in range(2):
                acc = None
                for a in range(5):
                    both = jnp.where(lane < 64, coeffs[a, 2 * h, p], coeffs[a, 2 * h + 1, p])
                    term = both * gt[a, :, h * LANES : (h + 1) * LANES]
                    acc = term if acc is None else acc + term
                acc = jnp.where((lane // 16) % 4 == i, acc * w, 0.0)
                pair.append(split(acc))
            left_hi.append(jnp.concatenate([pair[0][0], pair[1][0]], axis=1))
            left_lo.append(jnp.concatenate([pair[0][1], pair[1][1]], axis=1))
        l_hi = jnp.concatenate(left_hi, axis=0)
        l_both = jnp.concatenate(left_hi + left_lo, axis=0)

        cols = []
        for bp in range(2):
            y = mm3(x_hi, x_lo, whi[bp], wlo[bp])
            cols.append(split(y))

        for j0 in range(0, nt, 2):
            windows = range(j0, min(j0 + 2, nt))

            def operand(k):
                blocks = []
                for b in range(4):
                    src = cols[b // 2][k]
                    lanes = slice((b % 2) * LANES, (b % 2 + 1) * LANES)
                    pair = [src[64 * w : 64 * w + 64, lanes] for w in windows]
                    blocks.append(pair[0] if len(pair) == 1 else jnp.concatenate(pair, axis=1))
                return jnp.concatenate(blocks, axis=0)

            zz = mm(l_both, operand(0))
            z = zz[0:64] + (zz[64:128] + mm(l_hi, operand(1)))
            for i in range(4):
                p = g * 4 + i
                d = dst[p]
                base = 4 * j0 + rnk[p] * 2
                for h in range(2):
                    for w in range(len(windows)):
                        out[d, base + (4 * w + h)] = z[
                            16 * i + 8 * h : 16 * i + 8 * h + 8, w * LANES : (w + 1) * LANES
                        ]
        return 0

    lax.fori_loop(0, 8, group, 0)

    if has_meta:
        lane = lax.broadcasted_iota(jnp.int32, (1, LANES), 1)

        def note(p, _):
            k = offsets[p].astype(F32)
            row = jnp.where(lane == 0, k, weights[p])
            out[dst[p], tiles - 1, pl.ds(rnk[p], 1), :] = row
            return 0

        lax.fori_loop(0, 32, note, 0, unroll=4)


def full(shape):
    return pl.BlockSpec(shape, lambda i: (0,) * len(shape))


def match_chunk(pieces2d, routes, offsets, weights, coeffs, tables, first, nt, has_meta):
    gt, whi, wlo = tables
    tiles = 4 * nt + (1 if has_meta else 0)
    width = nt * LANES
    smem = pl.BlockSpec(memory_space=pltpu.SMEM)
    kernel = functools.partial(match_kernel, first == 0, first + nt == 8, nt, has_meta)
    return pl.pallas_call(
        kernel,
        grid=(1,),
        out_shape=jax.ShapeDtypeStruct((32, tiles, 8, LANES), F32),
        in_specs=[
            smem, smem, smem, smem,
            full(gt.shape), full(whi.shape), full(wlo.shape),
            pl.BlockSpec((512, LANES), lambda i: (0, max(first - 1, 0))),
            pl.BlockSpec((512, width), lambda i: (0, first // nt)),
            pl.BlockSpec((512, LANES), lambda i: (0, min(first + nt, 7))),
        ],
        out_specs=full((32, tiles, 8, LANES)),
        scratch_shapes=[
            pltpu.VMEM((64, width + LANES), BF),
            pltpu.VMEM((64, width + LANES), BF),
            pltpu.SMEM((32,), jnp.int32),
            pltpu.SMEM((32,), jnp.int32),
            pltpu.SMEM((32,), jnp.int32),
        ],
        compiler_params=pltpu.CompilerParams(
            vmem_limit_bytes=(60 << 20) if first == 0 else (24 << 20)
        ),
        cost_estimate=pl.CostEstimate(
            flops=10**9 * nt, bytes_accessed=(1 << 19) * nt, transcendentals=0
        ),
        name="match",
    )(routes, offsets, weights, coeffs, gt, whi, wlo, pieces2d, pieces2d, pieces2d)


def land_kernel(nt, has_meta, vis_ref, meta, recv, own, up, opp, down, acc, wsum, spot):
    me = vis_ref[0]
    per = 2 * nt
    zero = jnp.zeros((8, LANES), F32)

    def wipe(i, _):
        for t in range(per):
            acc[i, t] = zero
        return 0

    lax.fori_loop(0, 64, wipe, 0, unroll=4)
    lane = lax.broadcasted_iota(jnp.int32, (8, LANES), 1)
    if has_meta:
        wsum[...] = zero

    def address(s, _):
        for r in range(2):
            k = meta[s, r, 0].astype(jnp.int32)
            spot[2 * s + r] = (((k >> 4) - me) & 3) * 16 + (k & 15)
        return 0

    lax.fori_loop(0, 32, address, 0, unroll=4)

    def land(s, _):
        for r in range(2):
            at = spot[2 * s + r]
            got = [recv[s, (t // 2) * 4 + 2 * r + t % 2] for t in range(per)]
            for t in range(per):
                acc[at, t] += got[t]
            if has_meta:
                wsum[...] += jnp.where(lane == at, meta[s, r, 1], 0.0)
        return 0

    lax.fori_loop(0, 32, land, 0, unroll=4)

    for rel, ref in enumerate((own, up, opp, down)):
        def one(i, _, rel=rel, ref=ref):
            for t in range(per):
                ref[(t // 2) * 32 + i * 2 + t % 2] = acc[16 * rel + i, t]
            return 0

        lax.fori_loop(0, 16, one, 0, unroll=4)
        if has_meta:
            w = wsum[...]
            ref[16 * per] = w if rel == 0 else pltpu.roll(w, LANES - 16 * rel, 1)


def land_chunk(vis, meta, recv, nt, has_meta):
    per = 2 * nt
    shape = (16 * per + (1 if has_meta else 0), 8, LANES)
    smem = pl.BlockSpec(memory_space=pltpu.SMEM)
    return pl.pallas_call(
        functools.partial(land_kernel, nt, has_meta),
        grid=(1,),
        out_shape=[jax.ShapeDtypeStruct(shape, F32)] * 4,
        in_specs=[smem, smem, full(recv.shape)],
        out_specs=[full(shape)] * 4,
        scratch_shapes=[
            pltpu.VMEM((64, per, 8, LANES), F32),
            pltpu.VMEM((8, LANES), F32),
            pltpu.SMEM((64,), jnp.int32),
        ],
        compiler_params=pltpu.CompilerParams(vmem_limit_bytes=24 << 20),
        cost_estimate=pl.CostEstimate(
            flops=10**6, bytes_accessed=(2 << 20) * nt, transcendentals=0
        ),
        name="land",
    )(vis, meta, recv)


def coadd_kernel(nt, own, a, b, c, w0, w1, w2, w3, *refs):
    coadd, top, bottom = refs[-3:]
    lane = lax.broadcasted_iota(jnp.int32, (8, LANES), 1)
    weight = w0[0] + w1[0] + w2[0] + w3[0]

    def block(kk, _):
        total = jnp.sum(jnp.where(lane == kk, weight, 0.0), axis=1, keepdims=True)
        good = total > 0.0
        inverse = jnp.where(good, 1.0 / jnp.where(good, total, 1.0), 0.0)
        for ct in range(nt):
            for h in range(2):
                t = ct * 32 + kk * 2 + h
                v = ((own[t] + b[t]) + (a[t] + c[t])) * inverse
                rows = pl.ds(pl.multiple_of(kk * 16 + 8 * h, 8), 8)
                coadd[rows, ct * LANES : (ct + 1) * LANES] = v
        return 0

    lax.fori_loop(0, 16, block, 0, unroll=2)
    done = top.shape[1] - nt * LANES
    if done:
        for edge, old in ((top, refs[1]), (bottom, refs[2])):
            edge[:, :done] = old[...]
    top[:, done:] = coadd[0:16, :]
    bottom[:, done:] = coadd[240:256, :]


def coadd_chunk(group, wgroup, wat, first, nt, before, joined):
    wspec = pl.BlockSpec((1, 8, LANES), lambda i: (wat, 0, 0))
    in_specs = [pl.BlockSpec((32 * nt, 8, LANES), lambda i: (0, 0, 0))] * 4 + [wspec] * 4
    args = list(group) + list(wgroup)
    aliases = {}
    if before is not None:
        in_specs.append(pl.BlockSpec(memory_space=pl.ANY))
        args.append(before[0])
        aliases = {8: 0}
        if joined:
            in_specs += [full(x.shape) for x in before[1:]]
            args += list(before[1:])
    edge = (16, LANES * (nt + (first if joined else 0)))
    return pl.pallas_call(
        functools.partial(coadd_kernel, nt),
        grid=(1,),
        out_shape=[
            jax.ShapeDtypeStruct((256, 1024), F32),
            jax.ShapeDtypeStruct(edge, F32),
            jax.ShapeDtypeStruct(edge, F32),
        ],
        in_specs=in_specs,
        out_specs=[
            pl.BlockSpec((256, LANES * nt), lambda i: (0, first // nt)),
            full(edge),
            full(edge),
        ],
        input_output_aliases=aliases,
        compiler_params=pltpu.CompilerParams(vmem_limit_bytes=16 << 20),
        cost_estimate=pl.CostEstimate(
            flops=10**6, bytes_accessed=(5 << 17) * nt, transcendentals=0
        ),
        name="coadd",
    )(*args)


def shifted(rows, parts, store):
    lane = lax.broadcasted_iota(jnp.int32, (rows, LANES), 1)
    turned = [pltpu.roll(x, 64, 1) for x in parts]
    for t in range(len(parts) - 1):
        v = jnp.where(lane < 64, turned[t], turned[t + 1])
        store(slice(t * LANES, (t + 1) * LANES), *split(v))


def detect_kernel(high, split_at, dhi, dlo, bhi, blo, left, main, right, *refs):
    halos = [refs[0:1], refs[1:2]] if not high else [refs[0:2], refs[2:4]]
    out, xs_hi, xs_lo = refs[-3:]

    def filtered(rows, at, get):
        def store(lanes, hi, lo):
            xs_hi[at, lanes] = hi
            xs_lo[at, lanes] = lo

        shifted(rows, [get(t) for t in range(6)], store)

    for base, sources in ((0, halos[0]), (272, halos[1])):
        def tile(t, sources=sources):
            real = (4 if high else 0) + t - 1
            if real < 0 or real > 7:
                return jnp.zeros((16, LANES), F32)
            ref = sources[0] if real < split_at else sources[1]
            at = (real if real < split_at else real - split_at) * LANES
            return ref[:, at : at + LANES]

        filtered(16, slice(base, base + 16), tile)

    def own_rows(rb, _):
        rows = pl.ds(pl.multiple_of(rb * 32, 32), 32)
        at = pl.ds(pl.multiple_of(rb * 32 + 16, 16), 32)
        blank = jnp.zeros((32, LANES), F32)

        def tile(t):
            if t == 0:
                return left[rows, :] if high else blank
            if t == 5:
                return blank if high else right[rows, :]
            return main[rows, (t - 1) * LANES : t * LANES]

        filtered(32, at, tile)
        return 0

    lax.fori_loop(0, 8, own_rows, 0)
    for j in range(2):
        parts = []
        for w in range(2):
            win = slice((2 * j + w) * LANES, (2 * j + w) * LANES + 256)
            parts.append(mm3(xs_hi[:, win], xs_lo[:, win], dhi[...], dlo[...]))
        hi, lo = split(jnp.concatenate(parts, axis=1))
        out[:, j * 256 : (j + 1) * 256] = mm3(bhi[...], blo[...], hi, lo)


def detect_half(high, split_at, coadd, above, below, tables, before):
    halos = [*above, *below]
    args = [*tables, coadd, coadd, coadd, *halos]
    in_specs = [full(a.shape) for a in tables] + [
        pl.BlockSpec((256, LANES), lambda i: (0, 3)),
        pl.BlockSpec((256, 512), lambda i: (0, 1 if high else 0)),
        pl.BlockSpec((256, LANES), lambda i: (0, 4)),
    ]
    in_specs += [full(a.shape) for a in halos]
    aliases = {}
    if before is not None:
        aliases = {len(args): 0}
        args.append(before)
        in_specs.append(pl.BlockSpec(memory_space=pl.ANY))
    return pl.pallas_call(
        functools.partial(detect_kernel, high, split_at),
        grid=(1,),
        out_shape=jax.ShapeDtypeStruct(coadd.shape, F32),
        in_specs=in_specs,
        out_specs=pl.BlockSpec((256, 512), lambda i: (0, 1 if high else 0)),
        scratch_shapes=[pltpu.VMEM((288, 640 + LANES), BF), pltpu.VMEM((288, 640 + LANES), BF)],
        input_output_aliases=aliases,
        compiler_params=pltpu.CompilerParams(vmem_limit_bytes=(60 if high else 16) << 20),
        cost_estimate=pl.CostEstimate(
            flops=10**9, bytes_accessed=1 << 20, transcendentals=0
        ),
        name="detect",
    )(*args)


def detect_tables():
    dhi, dlo = halves(detect_taps(window_lags(128)))
    rows = np.arange(288, dtype=np.float64)[None, :] - 16
    bhi, blo = halves(detect_taps(rows - np.arange(256, dtype=np.float64)[:, None]))
    return dhi, dlo, bhi, blo


def shards(pieces, coeffs, weights, routes, offsets):
    count, rows, width = pieces.shape
    pieces2d = pieces.reshape(count * rows, width)
    route1 = routes.reshape(count)
    coeffs_t = jnp.transpose(coeffs, (1, 2, 0))
    whi, wlo = column_weights()
    tables = (jnp.asarray(row_tables()), jnp.asarray(whi), jnp.asarray(wlo))
    dtables = tuple(jnp.asarray(a) for a in detect_tables())
    vis = lax.axis_index("vis").reshape(1)
    nv = lax.axis_size("vis")
    n = lax.axis_size("tile") * nv
    shifts = [[(i, (i + d) % nv) for i in range(nv)] for d in (1, 2, 3)]
    axes = ("tile", "vis")

    first = 0
    meta = None
    before = detection = None
    above, below = [], []
    last = len(CHUNKS) - 1
    wgroup = None
    wat = 16 * 2 * CHUNKS[0]
    for c, nt in enumerate(CHUNKS):
        slots = match_chunk(pieces2d, route1, offsets, weights, coeffs_t, tables, first, nt, c == 0)
        recv = lax.all_to_all(slots, "tile", split_axis=0, concat_axis=0, tiled=True)
        if c == 0:
            meta = recv[:, 4 * nt, 0:2, 0:2]
        group = land_chunk(vis, meta, recv, nt, c == 0)
        moved = [group[0]]
        for d in range(3):
            moved.append(lax.ppermute(group[d + 1], "vis", shifts[d]))
        if c == 0:
            wgroup = moved
        joined = 0 < c < last
        before = coadd_chunk(moved, wgroup, wat, first, nt, before, joined)
        first += nt
        if c >= last - 1:
            coadd, top, bottom = before
            above.append(lax.ppermute(bottom, axes, [(i, i + 1) for i in range(n - 1)]))
            below.append(lax.ppermute(top, axes, [(i + 1, i) for i in range(n - 1)]))
            detection = detect_half(
                c == last, 8 - CHUNKS[-1], coadd, above, below, dtables, detection
            )
    return (coadd, detection)


def solution(mesh):
    placed = (
        P(("tile", "vis"), None, None),
        P(("tile", "vis"), None, None),
        P(("tile", "vis")),
        P(("tile", "vis"), None),
        P(("tile", "vis")),
    )
    return jax.shard_map(
        shards,
        mesh=mesh,
        in_specs=placed,
        out_specs=(P(("tile", "vis"), None), P(("tile", "vis"), None)),
        check_vma=False,
    )
```

```python
import functools
import math

import jax
import jax.numpy as jnp
import numpy as np
from jax import lax
from jax.experimental import pallas as pl
from jax.experimental.pallas import tpu as pltpu
from jax.sharding import PartitionSpec as P


TAPS = 10
REACH = 15
ROW_SHAPES = ((1.0, 0), (1.0, 1), (2.0, 0), (2.0, 2), (3.5, 0))
COLUMN_SHAPES = ((1.0, 0), (2.0, 0), (2.0, 1), (3.5, 0))
LANES = 128
CHUNKS = (4, 4)
BF = jnp.bfloat16
F32 = jnp.float32


def basis_taps(lags, shapes):
    spots = np.arange(-TAPS, TAPS + 1, dtype=np.float64)
    out = []
    for s, d in shapes:
        full = np.exp(-spots * spots / (2 * s * s)) * (spots / s) ** d
        scale = 1.0 / math.sqrt(np.sum(full * full))
        vals = np.exp(-lags * lags / (2 * s * s)) * (lags / s) ** d * scale
        out.append(np.where(np.abs(lags) <= TAPS, vals, 0.0))
    return np.stack(out)


def detect_taps(lags):
    spots = np.arange(-REACH, REACH + 1, dtype=np.float64)
    total = np.sum(np.exp(-spots * spots / 18.0))
    vals = np.exp(-lags * lags / 18.0) / total - 1.0 / (2 * REACH + 1)
    return np.where(np.abs(lags) <= REACH, vals, 0.0)


def halves(a):
    a = np.asarray(a, np.float32)
    hi = a.astype(jnp.bfloat16)
    lo = (a - hi.astype(np.float32)).astype(jnp.bfloat16)
    return hi, lo


def window_lags(n):
    k = np.arange(256, dtype=np.float64)[:, None] - 64
    return k - np.arange(n, dtype=np.float64)[None, :]


def column_weights():
    bank = basis_taps(window_lags(128), COLUMN_SHAPES)
    nt = np.stack(
        [np.concatenate([bank[0], bank[1]], 1), np.concatenate([bank[2], bank[3]], 1)]
    )
    return halves(nt)


def row_tables():
    lags = (np.arange(16)[None, :] - np.arange(16)[:, None]).astype(np.float64)
    bank = basis_taps(lags, ROW_SHAPES)
    return np.tile(bank, (1, 1, 16)).astype(np.float32)


def split(x):
    hi = x.astype(BF)
    lo = (x - hi.astype(F32)).astype(BF)
    return hi, lo


def mm(a, b):
    return jnp.dot(a, b, preferred_element_type=F32)


def mm3(ah, al, bh, bl):
    return mm(ah, bh) + (mm(al, bh) + mm(ah, bl))


def match_kernel(
    at_start, at_end, nt, has_meta,
    routes, offsets, weights, coeffs,
    gt, whi, wlo, left, main, right,
    out,
    xs_hi, xs_lo, cnt, dst, rnk,
):
    tiles = out.shape[1]

    def clear(i, _):
        cnt[i] = 0
        return 0

    lax.fori_loop(0, 32, clear, 0, unroll=8)

    def place(p, _):
        s = routes[p]
        r = cnt[s]
        cnt[s] = r + 1
        dst[p] = s
        rnk[p] = r
        return 0

    lax.fori_loop(0, 32, place, 0, unroll=4)
    zero = jnp.zeros((8, LANES), F32)

    def wipe(d, _):
        for t in range(tiles):
            out[d, t] = zero
        return 0

    lax.fori_loop(0, 32, wipe, 0)

    def group(g, _):
        rows = pl.ds(pl.multiple_of(g * 64, 64), 64)
        lane = lax.broadcasted_iota(jnp.int32, (64, LANES), 1)
        blank = jnp.zeros((64, LANES), F32)
        parts = [blank if at_start else left[rows, :]]
        parts += [main[rows, t * LANES : (t + 1) * LANES] for t in range(nt)]
        parts += [blank if at_end else right[rows, :]]
        turned = [pltpu.roll(x, 64, 1) for x in parts]
        for t in range(nt + 1):
            v = jnp.where(lane < 64, turned[t], turned[t + 1])
            hi, lo = split(v)
            xs_hi[:, t * LANES : (t + 1) * LANES] = hi
            xs_lo[:, t * LANES : (t + 1) * LANES] = lo
        stack = lambda ref: jnp.concatenate(
            [ref[:, w * LANES : w * LANES + 256] for w in range(nt)], axis=0
        )
        x_hi, x_lo = stack(xs_hi), stack(xs_lo)

        lane = lax.broadcasted_iota(jnp.int32, (16, LANES), 1)
        left_hi, left_lo = [], []
        for i in range(4):
            p = g * 4 + i
            w = weights[p]
            pair = []
            for h in range(2):
                acc = None
                for a in range(5):
                    both = jnp.where(lane < 64, coeffs[a, 2 * h, p], coeffs[a, 2 * h + 1, p])
                    term = both * gt[a, :, h * LANES : (h + 1) * LANES]
                    acc = term if acc is None else acc + term
                acc = jnp.where((lane // 16) % 4 == i, acc * w, 0.0)
                pair.append(split(acc))
            left_hi.append(jnp.concatenate([pair[0][0], pair[1][0]], axis=1))
            left_lo.append(jnp.concatenate([pair[0][1], pair[1][1]], axis=1))
        l_hi = jnp.concatenate(left_hi, axis=0)
        l_both = jnp.concatenate(left_hi + left_lo, axis=0)

        cols = []
        for bp in range(2):
            y = mm3(x_hi, x_lo, whi[bp], wlo[bp])
            cols.append(split(y))

        for j0 in range(0, nt, 2):
            windows = range(j0, min(j0 + 2, nt))

            def operand(k):
                blocks = []
                for b in range(4):
                    src = cols[b // 2][k]
                    lanes = slice((b % 2) * LANES, (b % 2 + 1) * LANES)
                    pair = [src[64 * w : 64 * w + 64, lanes] for w in windows]
                    blocks.append(pair[0] if len(pair) == 1 else jnp.concatenate(pair, axis=1))
                return jnp.concatenate(blocks, axis=0)

            zz = mm(l_both, operand(0))
            z = zz[0:64] + (zz[64:128] + mm(l_hi, operand(1)))
            for i in range(4):
                p = g * 4 + i
                d = dst[p]
                base = 4 * j0 + rnk[p] * 2
                for h in range(2):
                    for w in range(len(windows)):
                        out[d, base + (4 * w + h)] = z[
                            16 * i + 8 * h : 16 * i + 8 * h + 8, w * LANES : (w + 1) * LANES
                        ]
        return 0

    lax.fori_loop(0, 8, group, 0)

    if has_meta:
        lane = lax.broadcasted_iota(jnp.int32, (1, LANES), 1)

        def note(p, _):
            k = offsets[p].astype(F32)
            row = jnp.where(lane == 0, k, weights[p])
            out[dst[p], tiles - 1, pl.ds(rnk[p], 1), :] = row
            return 0

        lax.fori_loop(0, 32, note, 0, unroll=4)


def full(shape):
    return pl.BlockSpec(shape, lambda i: (0,) * len(shape))


def match_chunk(pieces2d, routes, offsets, weights, coeffs, tables, first, nt, has_meta):
    gt, whi, wlo = tables
    tiles = 4 * nt + (1 if has_meta else 0)
    width = nt * LANES
    smem = pl.BlockSpec(memory_space=pltpu.SMEM)
    kernel = functools.partial(match_kernel, first == 0, first + nt == 8, nt, has_meta)
    return pl.pallas_call(
        kernel,
        grid=(1,),
        out_shape=jax.ShapeDtypeStruct((32, tiles, 8, LANES), F32),
        in_specs=[
            smem, smem, smem, smem,
            full(gt.shape), full(whi.shape), full(wlo.shape),
            pl.BlockSpec((512, LANES), lambda i: (0, max(first - 1, 0))),
            pl.BlockSpec((512, width), lambda i: (0, first // nt)),
            pl.BlockSpec((512, LANES), lambda i: (0, min(first + nt, 7))),
        ],
        out_specs=full((32, tiles, 8, LANES)),
        scratch_shapes=[
            pltpu.VMEM((64, width + LANES), BF),
            pltpu.VMEM((64, width + LANES), BF),
            pltpu.SMEM((32,), jnp.int32),
            pltpu.SMEM((32,), jnp.int32),
            pltpu.SMEM((32,), jnp.int32),
        ],
        compiler_params=pltpu.CompilerParams(
            vmem_limit_bytes=(60 << 20) if first == 0 else (24 << 20)
        ),
        cost_estimate=pl.CostEstimate(
            flops=10**9 * nt, bytes_accessed=(1 << 19) * nt, transcendentals=0
        ),
        name="match",
    )(routes, offsets, weights, coeffs, gt, whi, wlo, pieces2d, pieces2d, pieces2d)


def land_kernel(nt, has_meta, edged, vis_ref, meta, recv, *refs):
    outs, (acc, wsum, spot) = refs[:-3], refs[-3:]
    me = vis_ref[0]
    per = 2 * nt
    zero = jnp.zeros((8, LANES), F32)

    def wipe(i, _):
        for t in range(per):
            acc[i, t] = zero
        return 0

    lax.fori_loop(0, 64, wipe, 0, unroll=4)
    lane = lax.broadcasted_iota(jnp.int32, (8, LANES), 1)
    if has_meta:
        wsum[...] = zero

    def address(s, _):
        for r in range(2):
            k = meta[s, r, 0].astype(jnp.int32)
            spot[2 * s + r] = (((k >> 4) - me) & 3) * 16 + (k & 15)
        return 0

    lax.fori_loop(0, 32, address, 0, unroll=4)

    def land(s, _):
        for r in range(2):
            at = spot[2 * s + r]
            got = [recv[s, (t // 2) * 4 + 2 * r + t % 2] for t in range(per)]
            for t in range(per):
                acc[at, t] += got[t]
            if has_meta:
                wsum[...] += jnp.where(lane == at, meta[s, r, 1], 0.0)
        return 0

    lax.fori_loop(0, 32, land, 0, unroll=4)

    def move(ref, rel, block, count, every):
        def one(i, _):
            for t in range(per):
                at = (t // 2) * (2 * count) + i * 2 + t % 2
                ref[at] = acc[16 * rel + block + i * every, t]
            return 0

        lax.fori_loop(0, count, one, 0, unroll=2)

    for rel in range(4):
        if edged:
            move(outs[rel], rel, 0, 2, 15)
            move(outs[4 + rel], rel, 1, 14, 1)
        else:
            move(outs[rel], rel, 0, 16, 1)
        if has_meta:
            w = wsum[...]
            outs[rel][16 * per] = w if rel == 0 else pltpu.roll(w, LANES - 16 * rel, 1)


def land_chunk(vis, meta, recv, nt, has_meta, edged):
    per = 2 * nt
    extra = 1 if has_meta else 0
    counts = [2 * per] * 4 + [14 * per] * 4 if edged else [16 * per + extra] * 4
    shapes = [(k, 8, LANES) for k in counts]
    smem = pl.BlockSpec(memory_space=pltpu.SMEM)
    return pl.pallas_call(
        functools.partial(land_kernel, nt, has_meta, edged),
        grid=(1,),
        out_shape=[jax.ShapeDtypeStruct(s, F32) for s in shapes],
        in_specs=[smem, smem, full(recv.shape)],
        out_specs=[full(s) for s in shapes],
        scratch_shapes=[
            pltpu.VMEM((64, per, 8, LANES), F32),
            pltpu.VMEM((8, LANES), F32),
            pltpu.SMEM((64,), jnp.int32),
        ],
        compiler_params=pltpu.CompilerParams(vmem_limit_bytes=24 << 20),
        cost_estimate=pl.CostEstimate(
            flops=10**6, bytes_accessed=(1 << 20) * nt, transcendentals=0
        ),
        name="land",
    )(vis, meta, recv)


def inverse_weight(weight, kk):
    lane = lax.broadcasted_iota(jnp.int32, (8, LANES), 1)
    total = jnp.sum(jnp.where(lane == kk, weight, 0.0), axis=1, keepdims=True)
    good = total > 0.0
    return jnp.where(good, 1.0 / jnp.where(good, total, 1.0), 0.0)


def summed(group, t):
    own, a, b, c = group
    return (own[t] + b[t]) + (a[t] + c[t])


def coadd_kernel(nt, *refs):
    group, wrefs = refs[:4], refs[4:8]
    coadd, top, bottom = refs[-3:]
    weight = (wrefs[0][0] + wrefs[2][0]) + (wrefs[1][0] + wrefs[3][0])

    def block(kk, _):
        inverse = inverse_weight(weight, kk)
        for ct in range(nt):
            for h in range(2):
                rows = pl.ds(pl.multiple_of(kk * 16 + 8 * h, 8), 8)
                v = summed(group, ct * 32 + kk * 2 + h) * inverse
                coadd[rows, ct * LANES : (ct + 1) * LANES] = v
        return 0

    lax.fori_loop(0, 16, block, 0, unroll=2)
    top[...] = coadd[0:16, :]
    bottom[...] = coadd[240:256, :]


def weight_specs(wat):
    return [pl.BlockSpec((1, 8, LANES), lambda i: (wat, 0, 0))] * 4


def first_coadd(group, wat, nt):
    edge = (16, LANES * nt)
    return pl.pallas_call(
        functools.partial(coadd_kernel, nt),
        grid=(1,),
        out_shape=[
            jax.ShapeDtypeStruct((256, 1024), F32),
            jax.ShapeDtypeStruct(edge, F32),
            jax.ShapeDtypeStruct(edge, F32),
        ],
        in_specs=[full((32 * nt, 8, LANES))] * 4 + weight_specs(wat),
        out_specs=[full((256, LANES * nt)), full(edge), full(edge)],
        compiler_params=pltpu.CompilerParams(vmem_limit_bytes=16 << 20),
        cost_estimate=pl.CostEstimate(
            flops=10**6, bytes_accessed=(5 << 17) * nt, transcendentals=0
        ),
        name="coadd",
    )(*group, *group)


def join_kernel(first, nt, *refs):
    group, wrefs, olds, outs = refs[:4], refs[4:8], refs[8:10], refs[10:]
    weight = (wrefs[0][0] + wrefs[2][0]) + (wrefs[1][0] + wrefs[3][0])
    for e in range(2):
        inverse = inverse_weight(weight, 15 * e)
        outs[e][:, : first * LANES] = olds[e][...]
        for ct in range(nt):
            for h in range(2):
                lanes = slice((first + ct) * LANES, (first + ct + 1) * LANES)
                outs[e][8 * h : 8 * h + 8, lanes] = summed(group, ct * 4 + e * 2 + h) * inverse


def join_edges(group, wgroup, wat, first, nt, top, bottom):
    edge = (16, LANES * (first + nt))
    return pl.pallas_call(
        functools.partial(join_kernel, first, nt),
        grid=(1,),
        out_shape=[jax.ShapeDtypeStruct(edge, F32)] * 2,
        in_specs=[full((4 * nt, 8, LANES))] * 4
        + weight_specs(wat)
        + [full(top.shape), full(bottom.shape)],
        out_specs=[full(edge)] * 2,
        compiler_params=pltpu.CompilerParams(vmem_limit_bytes=16 << 20),
        cost_estimate=pl.CostEstimate(flops=10**5, bytes_accessed=1 << 19, transcendentals=0),
        name="join",
    )(*group, *wgroup, top, bottom)


def filtered(parts, dhi, dlo):
    rows = parts[0].shape[0]
    lane = lax.broadcasted_iota(jnp.int32, (rows, LANES), 1)
    turned = [pltpu.roll(x, 64, 1) for x in parts]
    cut = [
        split(jnp.where(lane < 64, turned[t], turned[t + 1])) for t in range(len(parts) - 1)
    ]
    window = lambda k: jnp.concatenate(
        [
            jnp.concatenate([cut[j][k], cut[j + 1][k]], axis=1)
            for j in range(len(parts) - 2)
        ],
        axis=0,
    )
    return split(mm3(window(0), window(1), dhi[...], dlo[...]))


def detect_tiles(n, tile, halo_tile, tables, y_hi, y_lo, out, done):
    dhi, dlo, bhi, blo, ehi, elo = tables

    def group(g, _):
        rows = pl.ds(pl.multiple_of(g * 64, 64), 64)
        hi, lo = filtered([tile(t, rows) for t in range(n + 2)], dhi, dlo)
        for j in range(n):
            y_hi[rows, j * LANES : (j + 1) * LANES] = hi[64 * j : 64 * j + 64]
            y_lo[rows, j * LANES : (j + 1) * LANES] = lo[64 * j : 64 * j + 64]
        return 0

    lax.fori_loop(0, 4, group, 0)
    hi, lo = filtered([halo_tile(t) for t in range(n + 2)], dhi, dlo)
    for j0 in range(0, n, 2):
        tiles = range(j0, min(j0 + 2, n))
        lanes = slice(j0 * LANES, (tiles[-1] + 1) * LANES)
        side = lambda v: jnp.concatenate([v[32 * j : 32 * j + 32] for j in tiles], axis=1)
        out[:, lanes] = mm3(bhi[...], blo[...], y_hi[:, lanes], y_lo[:, lanes])
        delta = mm3(ehi[...], elo[...], side(hi), side(lo))
        out[0:16, lanes] += delta[0:16]
        out[240:256, lanes] += delta[16:32]
        done(j0, lanes)


def early_kernel(n, *refs):
    tables, (x, above, below, out, y_hi, y_lo) = refs[:6], refs[6:]

    def tile(t, rows):
        if t == 0:
            return jnp.zeros((64, LANES), F32)
        return x[rows, (t - 1) * LANES : t * LANES]

    def halo_tile(t):
        if t == 0:
            return jnp.zeros((32, LANES), F32)
        lanes = slice((t - 1) * LANES, t * LANES)
        return jnp.concatenate([above[:, lanes], below[:, lanes]], axis=0)

    detect_tiles(n, tile, halo_tile, tables, y_hi, y_lo, out, lambda j0, lanes: None)


def early_detect(n, coadd, above, below, tables):
    width = (n + 1) * LANES
    return pl.pallas_call(
        functools.partial(early_kernel, n),
        grid=(1,),
        out_shape=jax.ShapeDtypeStruct(coadd.shape, F32),
        in_specs=[full(a.shape) for a in tables]
        + [full((256, width)), full(above.shape), full(below.shape)],
        out_specs=full((256, n * LANES)),
        scratch_shapes=[pltpu.VMEM((256, n * LANES), BF), pltpu.VMEM((256, n * LANES), BF)],
        compiler_params=pltpu.CompilerParams(vmem_limit_bytes=16 << 20),
        cost_estimate=pl.CostEstimate(
            flops=10**9, bytes_accessed=1 << 20, transcendentals=0
        ),
        name="early",
    )(*tables, coadd, above, below)


def late_kernel(first, nt, n, *refs):
    tables, group, wrefs = refs[:6], refs[6:10], refs[10:14]
    top, bottom, above, below, left = refs[14:19]
    coadd, out, y_hi, y_lo, det, sems = refs[21:]
    weight = (wrefs[0][0] + wrefs[2][0]) + (wrefs[1][0] + wrefs[3][0])
    coadd[0:16, :] = top[:, first * LANES :]
    coadd[240:256, :] = bottom[:, first * LANES :]

    def block(i, _):
        inverse = inverse_weight(weight, i + 1)
        for ct in range(nt):
            for h in range(2):
                rows = pl.ds(pl.multiple_of(i * 16 + (16 + 8 * h), 8), 8)
                v = summed(group, ct * 28 + i * 2 + h) * inverse
                coadd[rows, ct * LANES : (ct + 1) * LANES] = v
        return 0

    lax.fori_loop(0, 14, block, 0, unroll=2)
    start = first + nt - n - 1

    def tile(t, rows):
        real = start + t
        if real >= first + nt:
            return jnp.zeros((64, LANES), F32)
        if real < first:
            return left[rows, t * LANES : (t + 1) * LANES]
        return coadd[rows, (real - first) * LANES : (real - first + 1) * LANES]

    def halo_tile(t):
        real = start + t
        if real >= first + nt:
            return jnp.zeros((32, LANES), F32)
        lanes = slice(real * LANES, (real + 1) * LANES)
        return jnp.concatenate([above[:, lanes], below[:, lanes]], axis=0)

    copies = []

    def done(j0, lanes):
        there = slice((start + 1) * LANES + lanes.start, (start + 1) * LANES + lanes.stop)
        copy = pltpu.make_async_copy(det.at[:, lanes], out.at[:, there], sems.at[j0 // 2])
        copy.start()
        copies.append(copy)

    detect_tiles(n, tile, halo_tile, tables, y_hi, y_lo, det, done)
    for copy in copies:
        copy.wait()


def late_detect(group, wgroup, wat, first, nt, n, edges, above, below, tables, coadd, before):
    start = (first + nt - n - 1) // (n + 1 - nt)
    any_spec = pl.BlockSpec(memory_space=pl.ANY)
    left = pl.BlockSpec((256, (n + 1 - nt) * LANES), lambda i: (0, start))
    args = [*tables, *group, *wgroup, *edges, above, below, coadd, coadd, before]
    in_specs = [full(a.shape) for a in [*tables, *group]] + weight_specs(wat)
    in_specs += [full(a.shape) for a in [*edges, above, below]] + [left, any_spec, any_spec]
    return pl.pallas_call(
        functools.partial(late_kernel, first, nt, n),
        grid=(1,),
        out_shape=[jax.ShapeDtypeStruct(coadd.shape, F32)] * 2,
        in_specs=in_specs,
        out_specs=[pl.BlockSpec((256, nt * LANES), lambda i: (0, first // nt)), any_spec],
        scratch_shapes=[
            pltpu.VMEM((256, n * LANES), BF),
            pltpu.VMEM((256, n * LANES), BF),
            pltpu.VMEM((256, n * LANES), F32),
            pltpu.SemaphoreType.DMA(((n + 1) // 2,)),
        ],
        input_output_aliases={len(args) - 2: 0, len(args) - 1: 1},
        compiler_params=pltpu.CompilerParams(vmem_limit_bytes=24 << 20),
        cost_estimate=pl.CostEstimate(
            flops=2 * 10**9, bytes_accessed=4 << 20, transcendentals=0
        ),
        name="late",
    )(*args)


def detect_tables():
    dhi, dlo = halves(detect_taps(window_lags(128)))
    idx = np.arange(256, dtype=np.float64)
    bhi, blo = halves(detect_taps(idx[None, :] - idx[:, None]))
    q = np.arange(16, dtype=np.float64)
    edge = np.zeros((32, 32))
    edge[0:16, 0:16] = detect_taps((q[None, :] - 16) - q[:, None])
    edge[16:32, 16:32] = detect_taps((q[None, :] + 16) - q[:, None])
    ehi, elo = halves(edge)
    return dhi, dlo, bhi, blo, ehi, elo


def shards(pieces, coeffs, weights, routes, offsets):
    count, rows, width = pieces.shape
    pieces2d = pieces.reshape(count * rows, width)
    route1 = routes.reshape(count)
    coeffs_t = jnp.transpose(coeffs, (1, 2, 0))
    whi, wlo = column_weights()
    tables = (jnp.asarray(row_tables()), jnp.asarray(whi), jnp.asarray(wlo))
    dtables = tuple(jnp.asarray(a) for a in detect_tables())
    vis = lax.axis_index("vis").reshape(1)
    nv = lax.axis_size("vis")
    n = lax.axis_size("tile") * nv
    shifts = [[(i, (i + d) % nv) for i in range(nv)] for d in (1, 2, 3)]
    axes = ("tile", "vis")

    first = 0
    meta = None
    wat = 16 * 2 * CHUNKS[0]
    landed = []
    for c, nt in enumerate(CHUNKS):
        slots = match_chunk(pieces2d, route1, offsets, weights, coeffs_t, tables, first, nt, c == 0)
        recv = lax.all_to_all(slots, "tile", split_axis=0, concat_axis=0, tiled=True)
        if c == 0:
            meta = recv[:, 4 * nt, 0:2, 0:2]
        landed.append(land_chunk(vis, meta, recv, nt, c == 0, c == 1))
        first += nt

    def over_vis(group):
        moved = [group[0]]
        for d in range(3):
            moved.append(lax.ppermute(group[d + 1], "vis", shifts[d]))
        return moved

    first, nt = CHUNKS
    start = over_vis(landed[0])
    rim = over_vis(landed[1][:4])
    bulk = over_vis(landed[1][4:])
    coadd, top, bottom = first_coadd(start, wat, first)
    edges = join_edges(rim, start, wat, first, nt, top, bottom)
    above = lax.ppermute(edges[1], axes, [(i, i + 1) for i in range(n - 1)])
    below = lax.ppermute(edges[0], axes, [(i + 1, i) for i in range(n - 1)])
    detection = early_detect(first - 1, coadd, above, below, dtables)
    coadd, detection = late_detect(
        bulk, start, wat, first, nt, nt + 1, edges, above, below, dtables, coadd, detection
    )
    return (coadd, detection)


def solution(mesh):
    placed = (
        P(("tile", "vis"), None, None),
        P(("tile", "vis"), None, None),
        P(("tile", "vis")),
        P(("tile", "vis"), None),
        P(("tile", "vis")),
    )
    return jax.shard_map(
        shards,
        mesh=mesh,
        in_specs=placed,
        out_specs=(P(("tile", "vis"), None), P(("tile", "vis"), None)),
        check_vma=False,
    )
```

```python
import functools
import math

import jax
import jax.numpy as jnp
import numpy as np
from jax import lax
from jax.experimental import pallas as pl
from jax.experimental.pallas import tpu as pltpu
from jax.sharding import PartitionSpec as P


TAPS = 10
REACH = 15
ROW_SHAPES = ((1.0, 0), (1.0, 1), (2.0, 0), (2.0, 2), (3.5, 0))
COLUMN_SHAPES = ((1.0, 0), (2.0, 0), (2.0, 1), (3.5, 0))
LANES = 128
CHUNKS = (4, 4)
BF = jnp.bfloat16
F32 = jnp.float32


def basis_taps(lags, shapes):
    spots = np.arange(-TAPS, TAPS + 1, dtype=np.float64)
    out = []
    for s, d in shapes:
        full = np.exp(-spots * spots / (2 * s * s)) * (spots / s) ** d
        scale = 1.0 / math.sqrt(np.sum(full * full))
        vals = np.exp(-lags * lags / (2 * s * s)) * (lags / s) ** d * scale
        out.append(np.where(np.abs(lags) <= TAPS, vals, 0.0))
    return np.stack(out)


def detect_taps(lags):
    spots = np.arange(-REACH, REACH + 1, dtype=np.float64)
    total = np.sum(np.exp(-spots * spots / 18.0))
    vals = np.exp(-lags * lags / 18.0) / total - 1.0 / (2 * REACH + 1)
    return np.where(np.abs(lags) <= REACH, vals, 0.0)


def halves(a):
    a = np.asarray(a, np.float32)
    hi = a.astype(jnp.bfloat16)
    lo = (a - hi.astype(np.float32)).astype(jnp.bfloat16)
    return hi, lo


def window_lags(n):
    k = np.arange(256, dtype=np.float64)[:, None] - 64
    return k - np.arange(n, dtype=np.float64)[None, :]


def column_weights():
    bank = basis_taps(window_lags(128), COLUMN_SHAPES)
    nt = np.stack(
        [np.concatenate([bank[0], bank[1]], 1), np.concatenate([bank[2], bank[3]], 1)]
    )
    return halves(nt)


def row_tables():
    lags = (np.arange(16)[None, :] - np.arange(16)[:, None]).astype(np.float64)
    bank = basis_taps(lags, ROW_SHAPES)
    return np.tile(bank, (1, 1, 16)).astype(np.float32)


def split(x):
    hi = x.astype(BF)
    lo = (x - hi.astype(F32)).astype(BF)
    return hi, lo


def mm(a, b):
    return jnp.dot(a, b, preferred_element_type=F32)


def mm3(ah, al, bh, bl):
    return mm(ah, bh) + (mm(al, bh) + mm(ah, bl))


def match_kernel(
    at_start, at_end, nt, has_meta,
    routes, offsets, weights, coeffs,
    gt, whi, wlo, left, main, right,
    out,
    xs_hi, xs_lo, cnt, dst, rnk,
):
    tiles = out.shape[1]

    def clear(i, _):
        cnt[i] = 0
        return 0

    lax.fori_loop(0, 32, clear, 0, unroll=8)

    def place(p, _):
        s = routes[p]
        r = cnt[s]
        cnt[s] = r + 1
        dst[p] = s
        rnk[p] = r
        return 0

    lax.fori_loop(0, 32, place, 0, unroll=4)
    zero = jnp.zeros((8, LANES), F32)

    def wipe(d, _):
        for t in range(tiles):
            out[d, t] = zero
        return 0

    lax.fori_loop(0, 32, wipe, 0)

    def group(g, _):
        rows = pl.ds(pl.multiple_of(g * 64, 64), 64)
        lane = lax.broadcasted_iota(jnp.int32, (64, LANES), 1)
        blank = jnp.zeros((64, LANES), F32)
        parts = [blank if at_start else left[rows, :]]
        parts += [main[rows, t * LANES : (t + 1) * LANES] for t in range(nt)]
        parts += [blank if at_end else right[rows, :]]
        turned = [pltpu.roll(x, 64, 1) for x in parts]
        for t in range(nt + 1):
            v = jnp.where(lane < 64, turned[t], turned[t + 1])
            hi, lo = split(v)
            xs_hi[:, t * LANES : (t + 1) * LANES] = hi
            xs_lo[:, t * LANES : (t + 1) * LANES] = lo
        stack = lambda ref: jnp.concatenate(
            [ref[:, w * LANES : w * LANES + 256] for w in range(nt)], axis=0
        )
        x_hi, x_lo = stack(xs_hi), stack(xs_lo)

        lane = lax.broadcasted_iota(jnp.int32, (16, LANES), 1)
        left_hi, left_lo = [], []
        for i in range(4):
            p = g * 4 + i
            w = weights[p]
            pair = []
            for h in range(2):
                acc = None
                for a in range(5):
                    both = jnp.where(lane < 64, coeffs[a, 2 * h, p], coeffs[a, 2 * h + 1, p])
                    term = both * gt[a, :, h * LANES : (h + 1) * LANES]
                    acc = term if acc is None else acc + term
                acc = jnp.where((lane // 16) % 4 == i, acc * w, 0.0)
                pair.append(split(acc))
            left_hi.append(jnp.concatenate([pair[0][0], pair[1][0]], axis=1))
            left_lo.append(jnp.concatenate([pair[0][1], pair[1][1]], axis=1))
        l_hi = jnp.concatenate(left_hi, axis=0)
        l_both = jnp.concatenate(left_hi + left_lo, axis=0)

        cols = []
        for bp in range(2):
            y = mm3(x_hi, x_lo, whi[bp], wlo[bp])
            cols.append(split(y))

        for j0 in range(0, nt, 2):
            windows = range(j0, min(j0 + 2, nt))

            def operand(k):
                blocks = []
                for b in range(4):
                    src = cols[b // 2][k]
                    lanes = slice((b % 2) * LANES, (b % 2 + 1) * LANES)
                    pair = [src[64 * w : 64 * w + 64, lanes] for w in windows]
                    blocks.append(pair[0] if len(pair) == 1 else jnp.concatenate(pair, axis=1))
                return jnp.concatenate(blocks, axis=0)

            zz = mm(l_both, operand(0))
            z = zz[0:64] + (zz[64:128] + mm(l_hi, operand(1)))
            for i in range(4):
                p = g * 4 + i
                d = dst[p]
                base = 4 * j0 + rnk[p] * 2
                for h in range(2):
                    for w in range(len(windows)):
                        out[d, base + (4 * w + h)] = z[
                            16 * i + 8 * h : 16 * i + 8 * h + 8, w * LANES : (w + 1) * LANES
                        ]
        return 0

    lax.fori_loop(0, 8, group, 0)

    if has_meta:
        lane = lax.broadcasted_iota(jnp.int32, (1, LANES), 1)

        def note(p, _):
            k = offsets[p].astype(F32)
            row = jnp.where(lane == 0, k, weights[p])
            out[dst[p], tiles - 1, pl.ds(rnk[p], 1), :] = row
            return 0

        lax.fori_loop(0, 32, note, 0, unroll=4)


def full(shape):
    return pl.BlockSpec(shape, lambda i: (0,) * len(shape))


def match_chunk(pieces2d, routes, offsets, weights, coeffs, tables, first, nt, has_meta):
    gt, whi, wlo = tables
    tiles = 4 * nt + (1 if has_meta else 0)
    width = nt * LANES
    smem = pl.BlockSpec(memory_space=pltpu.SMEM)
    kernel = functools.partial(match_kernel, first == 0, first + nt == 8, nt, has_meta)
    return pl.pallas_call(
        kernel,
        grid=(1,),
        out_shape=jax.ShapeDtypeStruct((32, tiles, 8, LANES), F32),
        in_specs=[
            smem, smem, smem, smem,
            full(gt.shape), full(whi.shape), full(wlo.shape),
            pl.BlockSpec((512, LANES), lambda i: (0, max(first - 1, 0))),
            pl.BlockSpec((512, width), lambda i: (0, first // nt)),
            pl.BlockSpec((512, LANES), lambda i: (0, min(first + nt, 7))),
        ],
        out_specs=full((32, tiles, 8, LANES)),
        scratch_shapes=[
            pltpu.VMEM((64, width + LANES), BF),
            pltpu.VMEM((64, width + LANES), BF),
            pltpu.SMEM((32,), jnp.int32),
            pltpu.SMEM((32,), jnp.int32),
            pltpu.SMEM((32,), jnp.int32),
        ],
        compiler_params=pltpu.CompilerParams(
            vmem_limit_bytes=(60 << 20) if first == 0 else (24 << 20)
        ),
        cost_estimate=pl.CostEstimate(
            flops=10**9 * nt, bytes_accessed=(1 << 19) * nt, transcendentals=0
        ),
        name="match",
    )(routes, offsets, weights, coeffs, gt, whi, wlo, pieces2d, pieces2d, pieces2d)


def land_kernel(nt, has_meta, edged, vis_ref, meta, recv, *refs):
    outs, (acc, wsum, spot) = refs[:-3], refs[-3:]
    me = vis_ref[0]
    per = 2 * nt
    zero = jnp.zeros((8, LANES), F32)

    def wipe(i, _):
        for t in range(per):
            acc[i, t] = zero
        return 0

    lax.fori_loop(0, 64, wipe, 0, unroll=4)
    lane = lax.broadcasted_iota(jnp.int32, (8, LANES), 1)
    if has_meta:
        wsum[...] = zero

    def address(s, _):
        for r in range(2):
            k = meta[s, r, 0].astype(jnp.int32)
            spot[2 * s + r] = (((k >> 4) - me) & 3) * 16 + (k & 15)
        return 0

    lax.fori_loop(0, 32, address, 0, unroll=4)

    def land(s, _):
        for r in range(2):
            at = spot[2 * s + r]
            got = [recv[s, (t // 2) * 4 + 2 * r + t % 2] for t in range(per)]
            for t in range(per):
                acc[at, t] += got[t]
            if has_meta:
                wsum[...] += jnp.where(lane == at, meta[s, r, 1], 0.0)
        return 0

    lax.fori_loop(0, 32, land, 0, unroll=4)

    def move(ref, rel, block, count, every):
        def one(i, _):
            for t in range(per):
                at = (t // 2) * (2 * count) + i * 2 + t % 2
                ref[at] = acc[16 * rel + block + i * every, t]
            return 0

        lax.fori_loop(0, count, one, 0, unroll=2)

    for rel in range(4):
        if edged:
            move(outs[rel], rel, 0, 2, 15)
            move(outs[4 + rel], rel, 1, 14, 1)
        else:
            move(outs[rel], rel, 0, 16, 1)
        if has_meta:
            w = wsum[...]
            outs[rel][16 * per] = w if rel == 0 else pltpu.roll(w, LANES - 16 * rel, 1)


def land_chunk(vis, meta, recv, nt, has_meta, edged):
    per = 2 * nt
    extra = 1 if has_meta else 0
    counts = [2 * per] * 4 + [14 * per] * 4 if edged else [16 * per + extra] * 4
    shapes = [(k, 8, LANES) for k in counts]
    smem = pl.BlockSpec(memory_space=pltpu.SMEM)
    return pl.pallas_call(
        functools.partial(land_kernel, nt, has_meta, edged),
        grid=(1,),
        out_shape=[jax.ShapeDtypeStruct(s, F32) for s in shapes],
        in_specs=[smem, smem, full(recv.shape)],
        out_specs=[full(s) for s in shapes],
        scratch_shapes=[
            pltpu.VMEM((64, per, 8, LANES), F32),
            pltpu.VMEM((8, LANES), F32),
            pltpu.SMEM((64,), jnp.int32),
        ],
        compiler_params=pltpu.CompilerParams(vmem_limit_bytes=24 << 20),
        cost_estimate=pl.CostEstimate(
            flops=10**6, bytes_accessed=(1 << 20) * nt, transcendentals=0
        ),
        name="land",
    )(vis, meta, recv)


def inverse_weight(weight, kk):
    lane = lax.broadcasted_iota(jnp.int32, (8, LANES), 1)
    total = jnp.sum(jnp.where(lane == kk, weight, 0.0), axis=1, keepdims=True)
    good = total > 0.0
    return jnp.where(good, 1.0 / jnp.where(good, total, 1.0), 0.0)


def summed(group, t):
    own, a, b, c = group
    return (own[t] + b[t]) + (a[t] + c[t])


def coadd_kernel(nt, *refs):
    group, wrefs = refs[:4], refs[4:8]
    coadd, top, bottom = refs[-3:]
    weight = (wrefs[0][0] + wrefs[2][0]) + (wrefs[1][0] + wrefs[3][0])

    def block(kk, _):
        inverse = inverse_weight(weight, kk)
        for ct in range(nt):
            for h in range(2):
                rows = pl.ds(pl.multiple_of(kk * 16 + 8 * h, 8), 8)
                v = summed(group, ct * 32 + kk * 2 + h) * inverse
                coadd[rows, ct * LANES : (ct + 1) * LANES] = v
        return 0

    lax.fori_loop(0, 16, block, 0, unroll=2)
    top[...] = coadd[0:16, :]
    bottom[...] = coadd[240:256, :]


def weight_specs(wat):
    return [pl.BlockSpec((1, 8, LANES), lambda i: (wat, 0, 0))] * 4


def first_coadd(group, wat, nt):
    edge = (16, LANES * nt)
    return pl.pallas_call(
        functools.partial(coadd_kernel, nt),
        grid=(1,),
        out_shape=[
            jax.ShapeDtypeStruct((256, 1024), F32),
            jax.ShapeDtypeStruct(edge, F32),
            jax.ShapeDtypeStruct(edge, F32),
        ],
        in_specs=[full((32 * nt, 8, LANES))] * 4 + weight_specs(wat),
        out_specs=[full((256, LANES * nt)), full(edge), full(edge)],
        compiler_params=pltpu.CompilerParams(vmem_limit_bytes=16 << 20),
        cost_estimate=pl.CostEstimate(
            flops=10**6, bytes_accessed=(5 << 17) * nt, transcendentals=0
        ),
        name="coadd",
    )(*group, *group)


def join_kernel(first, nt, *refs):
    group, wrefs, olds, outs = refs[:4], refs[4:8], refs[8:10], refs[10:]
    weight = (wrefs[0][0] + wrefs[2][0]) + (wrefs[1][0] + wrefs[3][0])
    for e in range(2):
        inverse = inverse_weight(weight, 15 * e)
        outs[e][:, : first * LANES] = olds[e][...]
        for ct in range(nt):
            for h in range(2):
                lanes = slice((first + ct) * LANES, (first + ct + 1) * LANES)
                outs[e][8 * h : 8 * h + 8, lanes] = summed(group, ct * 4 + e * 2 + h) * inverse


def join_edges(group, wgroup, wat, first, nt, top, bottom):
    edge = (16, LANES * (first + nt))
    return pl.pallas_call(
        functools.partial(join_kernel, first, nt),
        grid=(1,),
        out_shape=[jax.ShapeDtypeStruct(edge, F32)] * 2,
        in_specs=[full((4 * nt, 8, LANES))] * 4
        + weight_specs(wat)
        + [full(top.shape), full(bottom.shape)],
        out_specs=[full(edge)] * 2,
        compiler_params=pltpu.CompilerParams(vmem_limit_bytes=16 << 20),
        cost_estimate=pl.CostEstimate(flops=10**5, bytes_accessed=1 << 19, transcendentals=0),
        name="join",
    )(*group, *wgroup, top, bottom)


def filtered(parts, dhi, dlo):
    rows = parts[0].shape[0]
    lane = lax.broadcasted_iota(jnp.int32, (rows, LANES), 1)
    turned = [pltpu.roll(x, 64, 1) for x in parts]
    cut = [
        split(jnp.where(lane < 64, turned[t], turned[t + 1])) for t in range(len(parts) - 1)
    ]
    window = lambda k: jnp.concatenate(
        [
            jnp.concatenate([cut[j][k], cut[j + 1][k]], axis=1)
            for j in range(len(parts) - 2)
        ],
        axis=0,
    )
    return split(mm3(window(0), window(1), dhi[...], dlo[...]))


def detect_tiles(n, tile, tables, y_hi, y_lo, out, done):
    dhi, dlo, bhi, blo = tables[:4]

    def group(g, _):
        rows = pl.ds(pl.multiple_of(g * 64, 64), 64)
        hi, lo = filtered([tile(t, rows) for t in range(n + 2)], dhi, dlo)
        for j in range(n):
            y_hi[rows, j * LANES : (j + 1) * LANES] = hi[64 * j : 64 * j + 64]
            y_lo[rows, j * LANES : (j + 1) * LANES] = lo[64 * j : 64 * j + 64]
        return 0

    lax.fori_loop(0, 4, group, 0)
    for j0 in range(0, n, 2):
        lanes = slice(j0 * LANES, min(j0 + 2, n) * LANES)
        out[:, lanes] = mm3(bhi[...], blo[...], y_hi[:, lanes], y_lo[:, lanes])
        done(j0, lanes)


def early_kernel(n, *refs):
    tables, (x, out, rim, y_hi, y_lo) = refs[:4], refs[4:]

    def tile(t, rows):
        if t == 0:
            return jnp.zeros((64, LANES), F32)
        return x[rows, (t - 1) * LANES : t * LANES]

    detect_tiles(n, tile, tables, y_hi, y_lo, out, lambda j0, lanes: None)
    rim[0:16, :] = out[0:16, :]
    rim[16:32, :] = out[240:256, :]


def early_detect(n, coadd, tables):
    tables = tables[:4]
    width = (n + 1) * LANES
    return pl.pallas_call(
        functools.partial(early_kernel, n),
        grid=(1,),
        out_shape=[
            jax.ShapeDtypeStruct(coadd.shape, F32),
            jax.ShapeDtypeStruct((32, n * LANES), F32),
        ],
        in_specs=[full(a.shape) for a in tables] + [full((256, width))],
        out_specs=[full((256, n * LANES)), full((32, n * LANES))],
        scratch_shapes=[pltpu.VMEM((256, n * LANES), BF), pltpu.VMEM((256, n * LANES), BF)],
        compiler_params=pltpu.CompilerParams(vmem_limit_bytes=16 << 20),
        cost_estimate=pl.CostEstimate(
            flops=10**9, bytes_accessed=1 << 20, transcendentals=0
        ),
        name="early",
    )(*tables, coadd)


def late_kernel(first, nt, n, *refs):
    tables, group, wrefs = refs[:6], refs[6:10], refs[10:14]
    top, bottom, above, below, left, rim = refs[14:20]
    coadd, out, y_hi, y_lo, det, sides, sems = refs[22:]
    weight = (wrefs[0][0] + wrefs[2][0]) + (wrefs[1][0] + wrefs[3][0])
    last = first + nt
    start = last - n - 1
    copies = []

    def send(src, dst):
        copy = pltpu.make_async_copy(src, dst, sems.at[len(copies)])
        copy.start()
        copies.append(copy)

    strips = [jnp.zeros((32, LANES), F32)]
    for t in range(last):
        lanes = slice(t * LANES, (t + 1) * LANES)
        strips.append(jnp.concatenate([above[:, lanes], below[:, lanes]], axis=0))
    hi, lo = filtered(strips + strips[:1], tables[0], tables[1])
    side = lambda v: jnp.concatenate([v[32 * j : 32 * j + 32] for j in range(last)], axis=1)
    sides[...] = mm3(tables[4][...], tables[5][...], side(hi), side(lo))
    whole_left = slice(0, (start + 1) * LANES)
    sides[:, whole_left] += rim[...]
    send(sides.at[0:16, whole_left], out.at[0:16, whole_left])
    send(sides.at[16:32, whole_left], out.at[240:256, whole_left])

    coadd[0:16, :] = top[:, first * LANES :]
    coadd[240:256, :] = bottom[:, first * LANES :]

    def block(i, _):
        inverse = inverse_weight(weight, i + 1)
        for ct in range(nt):
            for h in range(2):
                rows = pl.ds(pl.multiple_of(i * 16 + (16 + 8 * h), 8), 8)
                v = summed(group, ct * 28 + i * 2 + h) * inverse
                coadd[rows, ct * LANES : (ct + 1) * LANES] = v
        return 0

    lax.fori_loop(0, 14, block, 0, unroll=2)

    def tile(t, rows):
        real = start + t
        if real >= last:
            return jnp.zeros((64, LANES), F32)
        if real < first:
            return left[rows, t * LANES : (t + 1) * LANES]
        return coadd[rows, (real - first) * LANES : (real - first + 1) * LANES]

    def done(j0, lanes):
        there = slice((start + 1) * LANES + lanes.start, (start + 1) * LANES + lanes.stop)
        det[0:16, lanes] += sides[0:16, there]
        det[240:256, lanes] += sides[16:32, there]
        send(det.at[:, lanes], out.at[:, there])

    detect_tiles(n, tile, tables, y_hi, y_lo, det, done)
    for copy in copies:
        copy.wait()


def late_detect(group, wgroup, wat, first, nt, n, edges, above, below, tables, coadd, before):
    start = (first + nt - n - 1) // (n + 1 - nt)
    detection, rim = before
    any_spec = pl.BlockSpec(memory_space=pl.ANY)
    left = pl.BlockSpec((256, (n + 1 - nt) * LANES), lambda i: (0, start))
    args = [*tables, *group, *wgroup, *edges, above, below, coadd, rim, coadd, detection]
    in_specs = [full(a.shape) for a in [*tables, *group]] + weight_specs(wat)
    in_specs += [full(a.shape) for a in [*edges, above, below]]
    in_specs += [left, full(rim.shape), any_spec, any_spec]
    return pl.pallas_call(
        functools.partial(late_kernel, first, nt, n),
        grid=(1,),
        out_shape=[jax.ShapeDtypeStruct(coadd.shape, F32)] * 2,
        in_specs=in_specs,
        out_specs=[pl.BlockSpec((256, nt * LANES), lambda i: (0, first // nt)), any_spec],
        scratch_shapes=[
            pltpu.VMEM((256, n * LANES), BF),
            pltpu.VMEM((256, n * LANES), BF),
            pltpu.VMEM((256, n * LANES), F32),
            pltpu.VMEM((32, (first + nt) * LANES), F32),
            pltpu.SemaphoreType.DMA((2 + (n + 1) // 2,)),
        ],
        input_output_aliases={len(args) - 2: 0, len(args) - 1: 1},
        compiler_params=pltpu.CompilerParams(vmem_limit_bytes=24 << 20),
        cost_estimate=pl.CostEstimate(
            flops=2 * 10**9, bytes_accessed=4 << 20, transcendentals=0
        ),
        name="late",
    )(*args)


def detect_tables():
    dhi, dlo = halves(detect_taps(window_lags(128)))
    idx = np.arange(256, dtype=np.float64)
    bhi, blo = halves(detect_taps(idx[None, :] - idx[:, None]))
    q = np.arange(16, dtype=np.float64)
    edge = np.zeros((32, 32))
    edge[0:16, 0:16] = detect_taps((q[None, :] - 16) - q[:, None])
    edge[16:32, 16:32] = detect_taps((q[None, :] + 16) - q[:, None])
    ehi, elo = halves(edge)
    return dhi, dlo, bhi, blo, ehi, elo


def shards(pieces, coeffs, weights, routes, offsets):
    count, rows, width = pieces.shape
    pieces2d = pieces.reshape(count * rows, width)
    route1 = routes.reshape(count)
    coeffs_t = jnp.transpose(coeffs, (1, 2, 0))
    whi, wlo = column_weights()
    tables = (jnp.asarray(row_tables()), jnp.asarray(whi), jnp.asarray(wlo))
    dtables = tuple(jnp.asarray(a) for a in detect_tables())
    vis = lax.axis_index("vis").reshape(1)
    nv = lax.axis_size("vis")
    n = lax.axis_size("tile") * nv
    shifts = [[(i, (i + d) % nv) for i in range(nv)] for d in (1, 2, 3)]
    axes = ("tile", "vis")

    first = 0
    meta = None
    wat = 16 * 2 * CHUNKS[0]
    landed = []
    for c, nt in enumerate(CHUNKS):
        slots = match_chunk(pieces2d, route1, offsets, weights, coeffs_t, tables, first, nt, c == 0)
        recv = lax.all_to_all(slots, "tile", split_axis=0, concat_axis=0, tiled=True)
        if c == 0:
            meta = recv[:, 4 * nt, 0:2, 0:2]
        landed.append(land_chunk(vis, meta, recv, nt, c == 0, c == 1))
        first += nt

    def over_vis(group):
        moved = [group[0]]
        for d in range(3):
            moved.append(lax.ppermute(group[d + 1], "vis", shifts[d]))
        return moved

    first, nt = CHUNKS
    start = over_vis(landed[0])
    rim = over_vis(landed[1][:4])
    bulk = over_vis(landed[1][4:])
    coadd, top, bottom = first_coadd(start, wat, first)
    edges = join_edges(rim, start, wat, first, nt, top, bottom)
    above = lax.ppermute(edges[1], axes, [(i, i + 1) for i in range(n - 1)])
    below = lax.ppermute(edges[0], axes, [(i + 1, i) for i in range(n - 1)])
    before = early_detect(first - 1, coadd, dtables)
    coadd, detection = late_detect(
        bulk, start, wat, first, nt, nt + 1, edges, above, below, dtables, coadd, before
    )
    return (coadd, detection)


def solution(mesh):
    placed = (
        P(("tile", "vis"), None, None),
        P(("tile", "vis"), None, None),
        P(("tile", "vis")),
        P(("tile", "vis"), None),
        P(("tile", "vis")),
    )
    return jax.shard_map(
        shards,
        mesh=mesh,
        in_specs=placed,
        out_specs=(P(("tile", "vis"), None), P(("tile", "vis"), None)),
        check_vma=False,
    )
```

```python
import functools
import math

import jax
import jax.numpy as jnp
import numpy as np
from jax import lax
from jax.experimental import pallas as pl
from jax.experimental.pallas import tpu as pltpu
from jax.sharding import PartitionSpec as P


TAPS = 10
REACH = 15
ROW_SHAPES = ((1.0, 0), (1.0, 1), (2.0, 0), (2.0, 2), (3.5, 0))
COLUMN_SHAPES = ((1.0, 0), (2.0, 0), (2.0, 1), (3.5, 0))
LANES = 128
CHUNKS = (4, 4)
BF = jnp.bfloat16
F32 = jnp.float32


def basis_taps(lags, shapes):
    spots = np.arange(-TAPS, TAPS + 1, dtype=np.float64)
    out = []
    for s, d in shapes:
        full = np.exp(-spots * spots / (2 * s * s)) * (spots / s) ** d
        scale = 1.0 / math.sqrt(np.sum(full * full))
        vals = np.exp(-lags * lags / (2 * s * s)) * (lags / s) ** d * scale
        out.append(np.where(np.abs(lags) <= TAPS, vals, 0.0))
    return np.stack(out)


def detect_taps(lags):
    spots = np.arange(-REACH, REACH + 1, dtype=np.float64)
    total = np.sum(np.exp(-spots * spots / 18.0))
    vals = np.exp(-lags * lags / 18.0) / total - 1.0 / (2 * REACH + 1)
    return np.where(np.abs(lags) <= REACH, vals, 0.0)


def halves(a):
    a = np.asarray(a, np.float32)
    hi = a.astype(jnp.bfloat16)
    lo = (a - hi.astype(np.float32)).astype(jnp.bfloat16)
    return hi, lo


def window_lags(n):
    k = np.arange(256, dtype=np.float64)[:, None] - 64
    return k - np.arange(n, dtype=np.float64)[None, :]


def column_weights():
    bank = basis_taps(window_lags(128), COLUMN_SHAPES)
    nt = np.stack(
        [np.concatenate([bank[0], bank[1]], 1), np.concatenate([bank[2], bank[3]], 1)]
    )
    return halves(nt)


def row_tables():
    lags = (np.arange(16)[None, :] - np.arange(16)[:, None]).astype(np.float64)
    bank = basis_taps(lags, ROW_SHAPES)
    return np.tile(bank, (1, 1, 16)).astype(np.float32)


def split(x):
    hi = x.astype(BF)
    lo = (x - hi.astype(F32)).astype(BF)
    return hi, lo


def mm(a, b):
    return jnp.dot(a, b, preferred_element_type=F32)


def mm3(ah, al, bh, bl):
    return mm(ah, bh) + (mm(al, bh) + mm(ah, bl))


def match_groups(
    at_start, at_end, nt, weights, coeffs, gt, whi, wlo, left, main, right,
    xs_hi, xs_lo, window_at, put,
):
    def group(g, _):
        rows = pl.ds(pl.multiple_of(g * 64, 64), 64)
        lane = lax.broadcasted_iota(jnp.int32, (64, LANES), 1)
        blank = jnp.zeros((64, LANES), F32)
        parts = [blank if at_start else left[rows, :]]
        parts += [main[rows, t * LANES : (t + 1) * LANES] for t in range(nt)]
        parts += [blank if at_end else right[rows, :]]
        turned = [pltpu.roll(x, 64, 1) for x in parts]
        for t in range(nt + 1):
            v = jnp.where(lane < 64, turned[t], turned[t + 1])
            hi, lo = split(v)
            xs_hi[:, t * LANES : (t + 1) * LANES] = hi
            xs_lo[:, t * LANES : (t + 1) * LANES] = lo
        stack = lambda ref: jnp.concatenate(
            [ref[:, pl.ds(window_at(w), 256)] for w in range(nt)], axis=0
        )
        x_hi, x_lo = stack(xs_hi), stack(xs_lo)

        lane = lax.broadcasted_iota(jnp.int32, (16, LANES), 1)
        left_hi, left_lo = [], []
        for i in range(4):
            p = g * 4 + i
            w = weights[p]
            pair = []
            for h in range(2):
                acc = None
                for a in range(5):
                    both = jnp.where(lane < 64, coeffs[a, 2 * h, p], coeffs[a, 2 * h + 1, p])
                    term = both * gt[a, :, h * LANES : (h + 1) * LANES]
                    acc = term if acc is None else acc + term
                acc = jnp.where((lane // 16) % 4 == i, acc * w, 0.0)
                pair.append(split(acc))
            left_hi.append(jnp.concatenate([pair[0][0], pair[1][0]], axis=1))
            left_lo.append(jnp.concatenate([pair[0][1], pair[1][1]], axis=1))
        l_hi = jnp.concatenate(left_hi, axis=0)
        l_both = jnp.concatenate(left_hi + left_lo, axis=0)

        cols = []
        for bp in range(2):
            y = mm3(x_hi, x_lo, whi[bp], wlo[bp])
            cols.append(split(y))

        for j0 in range(0, nt, 2):
            windows = range(j0, min(j0 + 2, nt))

            def operand(k):
                blocks = []
                for b in range(4):
                    src = cols[b // 2][k]
                    lanes = slice((b % 2) * LANES, (b % 2 + 1) * LANES)
                    pair = [src[64 * w : 64 * w + 64, lanes] for w in windows]
                    blocks.append(pair[0] if len(pair) == 1 else jnp.concatenate(pair, axis=1))
                return jnp.concatenate(blocks, axis=0)

            zz = mm(l_both, operand(0))
            z = zz[0:64] + (zz[64:128] + mm(l_hi, operand(1)))
            for i in range(4):
                for h in range(2):
                    for w in windows:
                        rows = slice(16 * i + 8 * h, 16 * i + 8 * h + 8)
                        lanes = slice((w - j0) * LANES, (w - j0 + 1) * LANES)
                        put(g * 4 + i, w, h, z[rows, lanes])
        return 0

    lax.fori_loop(0, 8, group, 0)


def slot_kernel(
    at_start, at_end, nt,
    routes, offsets, weights, coeffs,
    gt, whi, wlo, left, main, right,
    out,
    xs_hi, xs_lo, cnt, dst, rnk,
):
    tiles = out.shape[1]

    def clear(i, _):
        cnt[i] = 0
        return 0

    lax.fori_loop(0, 32, clear, 0, unroll=8)

    def place(p, _):
        s = routes[p]
        r = cnt[s]
        cnt[s] = r + 1
        dst[p] = s
        rnk[p] = r
        return 0

    lax.fori_loop(0, 32, place, 0, unroll=4)
    zero = jnp.zeros((8, LANES), F32)

    def wipe(d, _):
        for t in range(tiles):
            out[d, t] = zero
        return 0

    lax.fori_loop(0, 32, wipe, 0, unroll=2)

    def put(p, w, h, value):
        out[dst[p], rnk[p] * 2 + (4 * w + h)] = value

    match_groups(
        at_start, at_end, nt, weights, coeffs, gt, whi, wlo, left, main, right,
        xs_hi, xs_lo, lambda w: w * LANES, put,
    )
    lane = lax.broadcasted_iota(jnp.int32, (1, LANES), 1)

    def note(p, _):
        k = offsets[p].astype(F32)
        row = jnp.where(lane == 0, k, weights[p])
        out[dst[p], tiles - 1, pl.ds(rnk[p], 1), :] = row
        return 0

    lax.fori_loop(0, 32, note, 0, unroll=4)


def spread_kernel(
    at_start, at_end, nt,
    vis, weights, coeffs,
    gt, whi, wlo, left, main, right, meta,
    *refs,
):
    outs, (xs_hi, xs_lo) = refs[:4], refs[4:]
    me = vis[0]

    def put(p, w, h, value):
        outs[w][p * 2 + h] = value

    match_groups(
        at_start, at_end, nt, weights, coeffs, gt, whi, wlo, left, main, right,
        xs_hi, xs_lo, lambda w: pl.multiple_of(((me + w) & 3) * LANES, LANES), put,
    )
    for out in outs:
        out[64] = meta[...]


def full(shape):
    return pl.BlockSpec(shape, lambda i: (0,) * len(shape))


def match_call(kernel, scalars, tables, pieces2d, extra, first, nt, out_shapes, scratch):
    gt, whi, wlo = tables
    width = nt * LANES
    smem = pl.BlockSpec(memory_space=pltpu.SMEM)
    return pl.pallas_call(
        functools.partial(kernel, first == 0, first + nt == 8, nt),
        grid=(1,),
        out_shape=[jax.ShapeDtypeStruct(s, F32) for s in out_shapes],
        in_specs=[smem] * len(scalars)
        + [
            full(gt.shape), full(whi.shape), full(wlo.shape),
            pl.BlockSpec((512, LANES), lambda i: (0, max(first - 1, 0))),
            pl.BlockSpec((512, width), lambda i: (0, first // nt)),
            pl.BlockSpec((512, LANES), lambda i: (0, min(first + nt, 7))),
        ]
        + [full(x.shape) for x in extra],
        out_specs=[full(s) for s in out_shapes],
        scratch_shapes=[
            pltpu.VMEM((64, width + LANES), BF),
            pltpu.VMEM((64, width + LANES), BF),
            *scratch,
        ],
        compiler_params=pltpu.CompilerParams(
            vmem_limit_bytes=(60 << 20) if first == 0 else (24 << 20)
        ),
        cost_estimate=pl.CostEstimate(
            flops=10**9 * nt, bytes_accessed=(1 << 19) * nt, transcendentals=0
        ),
        name="match",
    )(*scalars, gt, whi, wlo, pieces2d, pieces2d, pieces2d, *extra)


def pack_kernel(meta, *refs):
    groups, (out, cnt, block) = refs[:4], refs[4:]
    zero = jnp.zeros((8, LANES), F32)

    def wipe(d, _):
        for t in range(17):
            out[d, t] = zero
        for v in range(4):
            cnt[v * 32 + d] = 0
        for j in range(8):
            block[d * 8 + j] = 0.0
        return 0

    lax.fori_loop(0, 32, wipe, 0, unroll=2)
    for v in range(4):
        def place(p, _, v=v):
            s = meta[v, 0, p].astype(jnp.int32)
            r = cnt[v * 32 + s]
            cnt[v * 32 + s] = r + 1
            j = 2 * v + r
            for h in range(2):
                out[s, 2 * j + h] = groups[v][p * 2 + h]
            block[s * 8 + j] = meta[v, 1, p]
            return 0

        lax.fori_loop(0, 32, place, 0, unroll=4)
    lane = lax.broadcasted_iota(jnp.int32, (1, LANES), 1)

    def note(d, _):
        row = jnp.zeros((1, LANES), F32)
        for j in range(8):
            row = jnp.where(lane == j, block[d * 8 + j], row)
        out[d, 16, 0:1, :] = row
        return 0

    lax.fori_loop(0, 32, note, 0, unroll=2)


def pack(meta, groups):
    shape = (32, 17, 8, LANES)
    return pl.pallas_call(
        pack_kernel,
        grid=(1,),
        out_shape=jax.ShapeDtypeStruct(shape, F32),
        in_specs=[pl.BlockSpec(memory_space=pltpu.SMEM)] + [full(x.shape) for x in groups],
        out_specs=full(shape),
        scratch_shapes=[pltpu.SMEM((128,), jnp.int32), pltpu.SMEM((256,), F32)],
        compiler_params=pltpu.CompilerParams(vmem_limit_bytes=24 << 20),
        cost_estimate=pl.CostEstimate(flops=10**6, bytes_accessed=4 << 20, transcendentals=0),
        name="pack",
    )(meta, *groups)


def land_kernel(nt, vis_ref, meta, recv, *refs):
    outs, (acc, wsum, spot) = refs[:-3], refs[-3:]
    me = vis_ref[0]
    per = 2 * nt
    zero = jnp.zeros((8, LANES), F32)

    def wipe(i, _):
        for t in range(per):
            acc[i, t] = zero
        return 0

    lax.fori_loop(0, 64, wipe, 0, unroll=4)
    lane = lax.broadcasted_iota(jnp.int32, (8, LANES), 1)
    wsum[...] = zero

    def address(s, _):
        for r in range(2):
            k = meta[s, r, 0].astype(jnp.int32)
            spot[2 * s + r] = (((k >> 4) - me) & 3) * 16 + (k & 15)
        return 0

    lax.fori_loop(0, 32, address, 0, unroll=4)

    def land(s, _):
        for r in range(2):
            at = spot[2 * s + r]
            got = [recv[s, (t // 2) * 4 + 2 * r + t % 2] for t in range(per)]
            for t in range(per):
                acc[at, t] += got[t]
            wsum[...] += jnp.where(lane == at, meta[s, r, 1], 0.0)
        return 0

    lax.fori_loop(0, 32, land, 0, unroll=4)
    for rel in range(4):
        def one(i, _, rel=rel):
            for t in range(per):
                outs[rel][(t // 2) * 32 + i * 2 + t % 2] = acc[16 * rel + i, t]
            return 0

        lax.fori_loop(0, 16, one, 0, unroll=4)
        w = wsum[...]
        outs[rel][16 * per] = w if rel == 0 else pltpu.roll(w, LANES - 16 * rel, 1)


def full_kernel(vis_ref, meta, recv, *refs):
    outs, (acc, spot) = refs[:-2], refs[-2:]
    me = vis_ref[0]
    zero = jnp.zeros((8, LANES), F32)

    def wipe(i, _):
        acc[i, 0] = zero
        acc[i, 1] = zero
        return 0

    lax.fori_loop(0, 64, wipe, 0, unroll=8)

    def address(s, _):
        for j in range(8):
            spot[8 * s + j] = meta[s, j].astype(jnp.int32)
        return 0

    lax.fori_loop(0, 32, address, 0, unroll=2)

    def land(s, _):
        for j in range(8):
            at = spot[8 * s + j]
            got = [recv[s, 2 * j + h] for h in range(2)]
            for h in range(2):
                acc[at, h] += got[h]
        return 0

    lax.fori_loop(0, 32, land, 0, unroll=2)
    for rel in range(4):
        base = ((me + rel) & 3) * 16
        for e in range(2):
            for h in range(2):
                outs[rel][e * 2 + h] = acc[base + 15 * e, h]

        def one(i, _, rel=rel, base=base):
            for h in range(2):
                outs[4 + rel][i * 2 + h] = acc[base + 1 + i, h]
            return 0

        lax.fori_loop(0, 14, one, 0, unroll=7)


def land_call(kernel, vis, meta, recv, counts, scratch):
    shapes = [(k, 8, LANES) for k in counts]
    smem = pl.BlockSpec(memory_space=pltpu.SMEM)
    return pl.pallas_call(
        kernel,
        grid=(1,),
        out_shape=[jax.ShapeDtypeStruct(s, F32) for s in shapes],
        in_specs=[smem, smem, full(recv.shape)],
        out_specs=[full(s) for s in shapes],
        scratch_shapes=scratch,
        compiler_params=pltpu.CompilerParams(vmem_limit_bytes=24 << 20),
        cost_estimate=pl.CostEstimate(flops=10**6, bytes_accessed=4 << 20, transcendentals=0),
        name="land",
    )(vis, meta, recv)


def inverse_weight(weight, kk):
    lane = lax.broadcasted_iota(jnp.int32, (8, LANES), 1)
    total = jnp.sum(jnp.where(lane == kk, weight, 0.0), axis=1, keepdims=True)
    good = total > 0.0
    return jnp.where(good, 1.0 / jnp.where(good, total, 1.0), 0.0)


def summed(group, t):
    own, a, b, c = group
    return (own[t] + b[t]) + (a[t] + c[t])


def coadd_kernel(nt, *refs):
    group, wrefs = refs[:4], refs[4:8]
    coadd, top, bottom = refs[-3:]
    weight = (wrefs[0][0] + wrefs[2][0]) + (wrefs[1][0] + wrefs[3][0])

    def block(kk, _):
        inverse = inverse_weight(weight, kk)
        for ct in range(nt):
            for h in range(2):
                rows = pl.ds(pl.multiple_of(kk * 16 + 8 * h, 8), 8)
                v = summed(group, ct * 32 + kk * 2 + h) * inverse
                coadd[rows, ct * LANES : (ct + 1) * LANES] = v
        return 0

    lax.fori_loop(0, 16, block, 0, unroll=2)
    top[...] = coadd[0:16, :]
    bottom[...] = coadd[240:256, :]


def weight_specs(wat):
    return [pl.BlockSpec((1, 8, LANES), lambda i: (wat, 0, 0))] * 4


def first_coadd(group, wat, nt):
    edge = (16, LANES * nt)
    return pl.pallas_call(
        functools.partial(coadd_kernel, nt),
        grid=(1,),
        out_shape=[
            jax.ShapeDtypeStruct((256, 1024), F32),
            jax.ShapeDtypeStruct(edge, F32),
            jax.ShapeDtypeStruct(edge, F32),
        ],
        in_specs=[full((32 * nt, 8, LANES))] * 4 + weight_specs(wat),
        out_specs=[full((256, LANES * nt)), full(edge), full(edge)],
        compiler_params=pltpu.CompilerParams(vmem_limit_bytes=16 << 20),
        cost_estimate=pl.CostEstimate(
            flops=10**6, bytes_accessed=(5 << 17) * nt, transcendentals=0
        ),
        name="coadd",
    )(*group, *group)


def join_kernel(first, vis_ref, *refs):
    group, wrefs, olds, outs = refs[:4], refs[4:8], refs[8:10], refs[10:]
    weight = (wrefs[0][0] + wrefs[2][0]) + (wrefs[1][0] + wrefs[3][0])
    for e in range(2):
        inverse = inverse_weight(weight, 15 * e)
        outs[e][:, : first * LANES] = olds[e][...]
        for d in range(4):
            tile = first + ((vis_ref[0] - d) & 3)
            lanes = pl.ds(pl.multiple_of(tile * LANES, LANES), LANES)
            for h in range(2):
                outs[e][8 * h : 8 * h + 8, lanes] = group[d][e * 2 + h] * inverse


def join_edges(vis, group, wgroup, wat, first, top, bottom):
    edge = (16, 1024)
    return pl.pallas_call(
        functools.partial(join_kernel, first),
        grid=(1,),
        out_shape=[jax.ShapeDtypeStruct(edge, F32)] * 2,
        in_specs=[pl.BlockSpec(memory_space=pltpu.SMEM)]
        + [full((4, 8, LANES))] * 4
        + weight_specs(wat)
        + [full(top.shape), full(bottom.shape)],
        out_specs=[full(edge)] * 2,
        compiler_params=pltpu.CompilerParams(vmem_limit_bytes=16 << 20),
        cost_estimate=pl.CostEstimate(flops=10**5, bytes_accessed=1 << 19, transcendentals=0),
        name="join",
    )(vis, *group, *wgroup, top, bottom)


def filtered(parts, dhi, dlo):
    rows = parts[0].shape[0]
    lane = lax.broadcasted_iota(jnp.int32, (rows, LANES), 1)
    turned = [pltpu.roll(x, 64, 1) for x in parts]
    cut = [
        split(jnp.where(lane < 64, turned[t], turned[t + 1])) for t in range(len(parts) - 1)
    ]
    window = lambda k: jnp.concatenate(
        [
            jnp.concatenate([cut[j][k], cut[j + 1][k]], axis=1)
            for j in range(len(parts) - 2)
        ],
        axis=0,
    )
    return split(mm3(window(0), window(1), dhi[...], dlo[...]))


def detect_tiles(n, tile, tables, y_hi, y_lo, out, done):
    dhi, dlo, bhi, blo = tables[:4]

    def group(g, _):
        rows = pl.ds(pl.multiple_of(g * 64, 64), 64)
        hi, lo = filtered([tile(t, rows) for t in range(n + 2)], dhi, dlo)
        for j in range(n):
            y_hi[rows, j * LANES : (j + 1) * LANES] = hi[64 * j : 64 * j + 64]
            y_lo[rows, j * LANES : (j + 1) * LANES] = lo[64 * j : 64 * j + 64]
        return 0

    lax.fori_loop(0, 4, group, 0)
    for j0 in range(0, n, 2):
        lanes = slice(j0 * LANES, min(j0 + 2, n) * LANES)
        out[:, lanes] = mm3(bhi[...], blo[...], y_hi[:, lanes], y_lo[:, lanes])
        done(j0, lanes)


def early_kernel(n, *refs):
    tables, (x, out, rim, y_hi, y_lo) = refs[:4], refs[4:]

    def tile(t, rows):
        if t == 0:
            return jnp.zeros((64, LANES), F32)
        return x[rows, (t - 1) * LANES : t * LANES]

    detect_tiles(n, tile, tables, y_hi, y_lo, out, lambda j0, lanes: None)
    rim[0:16, :] = out[0:16, :]
    rim[16:32, :] = out[240:256, :]


def early_detect(n, coadd, tables):
    tables = tables[:4]
    width = (n + 1) * LANES
    return pl.pallas_call(
        functools.partial(early_kernel, n),
        grid=(1,),
        out_shape=[
            jax.ShapeDtypeStruct(coadd.shape, F32),
            jax.ShapeDtypeStruct((32, n * LANES), F32),
        ],
        in_specs=[full(a.shape) for a in tables] + [full((256, width))],
        out_specs=[full((256, n * LANES)), full((32, n * LANES))],
        scratch_shapes=[pltpu.VMEM((256, n * LANES), BF), pltpu.VMEM((256, n * LANES), BF)],
        compiler_params=pltpu.CompilerParams(vmem_limit_bytes=16 << 20),
        cost_estimate=pl.CostEstimate(
            flops=10**9, bytes_accessed=1 << 20, transcendentals=0
        ),
        name="early",
    )(*tables, coadd)


def late_kernel(first, nt, n, vis_ref, *refs):
    tables, group, wrefs = refs[:6], refs[6:10], refs[10:14]
    top, bottom, above, below, left, rim = refs[14:20]
    coadd, out, y_hi, y_lo, det, sides, sems = refs[22:]
    weight = (wrefs[0][0] + wrefs[2][0]) + (wrefs[1][0] + wrefs[3][0])
    last = first + nt
    start = last - n - 1
    copies = []

    def send(src, dst):
        copy = pltpu.make_async_copy(src, dst, sems.at[len(copies)])
        copy.start()
        copies.append(copy)

    strips = [jnp.zeros((32, LANES), F32)]
    for t in range(last):
        lanes = slice(t * LANES, (t + 1) * LANES)
        strips.append(jnp.concatenate([above[:, lanes], below[:, lanes]], axis=0))
    hi, lo = filtered(strips + strips[:1], tables[0], tables[1])
    side = lambda v: jnp.concatenate([v[32 * j : 32 * j + 32] for j in range(last)], axis=1)
    sides[...] = mm3(tables[4][...], tables[5][...], side(hi), side(lo))
    whole_left = slice(0, (start + 1) * LANES)
    sides[:, whole_left] += rim[...]
    send(sides.at[0:16, whole_left], out.at[0:16, whole_left])
    send(sides.at[16:32, whole_left], out.at[240:256, whole_left])

    coadd[0:16, :] = top[:, first * LANES :]
    coadd[240:256, :] = bottom[:, first * LANES :]

    def block(i, _):
        inverse = inverse_weight(weight, i + 1)
        for d in range(4):
            lanes = pl.ds(pl.multiple_of(((vis_ref[0] - d) & 3) * LANES, LANES), LANES)
            for h in range(2):
                rows = pl.ds(pl.multiple_of(i * 16 + (16 + 8 * h), 8), 8)
                coadd[rows, lanes] = group[d][i * 2 + h] * inverse
        return 0

    lax.fori_loop(0, 14, block, 0, unroll=2)

    def tile(t, rows):
        real = start + t
        if real >= last:
            return jnp.zeros((64, LANES), F32)
        if real < first:
            return left[rows, t * LANES : (t + 1) * LANES]
        return coadd[rows, (real - first) * LANES : (real - first + 1) * LANES]

    def done(j0, lanes):
        there = slice((start + 1) * LANES + lanes.start, (start + 1) * LANES + lanes.stop)
        det[0:16, lanes] += sides[0:16, there]
        det[240:256, lanes] += sides[16:32, there]
        send(det.at[:, lanes], out.at[:, there])

    detect_tiles(n, tile, tables, y_hi, y_lo, det, done)
    for copy in copies:
        copy.wait()


def late_detect(vis, group, wgroup, wat, first, nt, n, edges, above, below, tables, coadd, before):
    start = (first + nt - n - 1) // (n + 1 - nt)
    detection, rim = before
    any_spec = pl.BlockSpec(memory_space=pl.ANY)
    left = pl.BlockSpec((256, (n + 1 - nt) * LANES), lambda i: (0, start))
    args = [vis, *tables, *group, *wgroup, *edges, above, below, coadd, rim, coadd, detection]
    in_specs = [pl.BlockSpec(memory_space=pltpu.SMEM)]
    in_specs += [full(a.shape) for a in [*tables, *group]] + weight_specs(wat)
    in_specs += [full(a.shape) for a in [*edges, above, below]]
    in_specs += [left, full(rim.shape), any_spec, any_spec]
    return pl.pallas_call(
        functools.partial(late_kernel, first, nt, n),
        grid=(1,),
        out_shape=[jax.ShapeDtypeStruct(coadd.shape, F32)] * 2,
        in_specs=in_specs,
        out_specs=[pl.BlockSpec((256, nt * LANES), lambda i: (0, first // nt)), any_spec],
        scratch_shapes=[
            pltpu.VMEM((256, n * LANES), BF),
            pltpu.VMEM((256, n * LANES), BF),
            pltpu.VMEM((256, n * LANES), F32),
            pltpu.VMEM((32, (first + nt) * LANES), F32),
            pltpu.SemaphoreType.DMA((2 + (n + 1) // 2,)),
        ],
        input_output_aliases={len(args) - 2: 0, len(args) - 1: 1},
        compiler_params=pltpu.CompilerParams(vmem_limit_bytes=24 << 20),
        cost_estimate=pl.CostEstimate(
            flops=2 * 10**9, bytes_accessed=4 << 20, transcendentals=0
        ),
        name="late",
    )(*args)


def detect_tables():
    dhi, dlo = halves(detect_taps(window_lags(128)))
    idx = np.arange(256, dtype=np.float64)
    bhi, blo = halves(detect_taps(idx[None, :] - idx[:, None]))
    q = np.arange(16, dtype=np.float64)
    edge = np.zeros((32, 32))
    edge[0:16, 0:16] = detect_taps((q[None, :] - 16) - q[:, None])
    edge[16:32, 16:32] = detect_taps((q[None, :] + 16) - q[:, None])
    ehi, elo = halves(edge)
    return dhi, dlo, bhi, blo, ehi, elo


def shards(pieces, coeffs, weights, routes, offsets):
    count, rows, width = pieces.shape
    pieces2d = pieces.reshape(count * rows, width)
    route1 = routes.reshape(count)
    coeffs_t = jnp.transpose(coeffs, (1, 2, 0))
    whi, wlo = column_weights()
    tables = (jnp.asarray(row_tables()), jnp.asarray(whi), jnp.asarray(wlo))
    dtables = tuple(jnp.asarray(a) for a in detect_tables())
    vis = lax.axis_index("vis").reshape(1)
    nv = lax.axis_size("vis")
    n = lax.axis_size("tile") * nv
    shifts = [[(i, (i + d) % nv) for i in range(nv)] for d in (1, 2, 3)]
    axes = ("tile", "vis")

    first, nt = CHUNKS
    per = 2 * first
    wat = 16 * per
    ints = [pltpu.SMEM((32,), jnp.int32)] * 3

    def over_vis(group):
        moved = [group[0]]
        for d in range(3):
            moved.append(lax.ppermute(group[d + 1], "vis", shifts[d]))
        return moved

    def over_tile(slots):
        return lax.all_to_all(slots, "tile", split_axis=0, concat_axis=0, tiled=True)

    (slots,) = match_call(
        slot_kernel, (route1, offsets, weights, coeffs_t), tables, pieces2d, (), 0, first,
        [(32, 4 * first + 1, 8, LANES)], ints,
    )
    recv = over_tile(slots)
    meta = recv[:, 4 * first, 0:2, 0:2]
    landed = land_call(
        functools.partial(land_kernel, first), vis, meta, recv, [16 * per + 1] * 4,
        [
            pltpu.VMEM((64, per, 8, LANES), F32),
            pltpu.VMEM((8, LANES), F32),
            pltpu.SMEM((64,), jnp.int32),
        ],
    )
    start = over_vis(landed)

    facts = jnp.stack([route1.astype(F32), offsets.astype(F32)])
    facts = jnp.pad(facts, ((0, 6), (0, LANES - count)))
    spread = match_call(
        spread_kernel, (vis, weights, coeffs_t), tables, pieces2d, (facts,), first, nt,
        [(2 * count + 1, 8, LANES)] * 4, [],
    )
    traded = over_vis(spread)
    notes = jnp.stack([x[2 * count, 0:2, 0:count] for x in traded])
    slots = pack(notes, traded)
    recv = over_tile(slots)
    landed = land_call(
        full_kernel, vis, recv[:, 16, 0, 0:8], recv, [4] * 4 + [28] * 4,
        [pltpu.VMEM((64, 2, 8, LANES), F32), pltpu.SMEM((256,), jnp.int32)],
    )
    rim = over_vis(landed[:4])
    bulk = over_vis(landed[4:])

    coadd, top, bottom = first_coadd(start, wat, first)
    edges = join_edges(vis, rim, start, wat, first, top, bottom)
    above = lax.ppermute(edges[1], axes, [(i, i + 1) for i in range(n - 1)])
    below = lax.ppermute(edges[0], axes, [(i + 1, i) for i in range(n - 1)])
    before = early_detect(first - 1, coadd, dtables)
    coadd, detection = late_detect(
        vis, bulk, start, wat, first, nt, nt + 1, edges, above, below, dtables, coadd, before
    )
    return (coadd, detection)


def solution(mesh):
    placed = (
        P(("tile", "vis"), None, None),
        P(("tile", "vis"), None, None),
        P(("tile", "vis")),
        P(("tile", "vis"), None),
        P(("tile", "vis")),
    )
    return jax.shard_map(
        shards,
        mesh=mesh,
        in_specs=placed,
        out_specs=(P(("tile", "vis"), None), P(("tile", "vis"), None)),
        check_vma=False,
    )
```

```python
import functools
import math

import jax
import jax.numpy as jnp
import numpy as np
from jax import lax
from jax.experimental import pallas as pl
from jax.experimental.pallas import tpu as pltpu
from jax.sharding import PartitionSpec as P


TAPS = 10
REACH = 15
ROW_SHAPES = ((1.0, 0), (1.0, 1), (2.0, 0), (2.0, 2), (3.5, 0))
COLUMN_SHAPES = ((1.0, 0), (2.0, 0), (2.0, 1), (3.5, 0))
LANES = 128
CHUNKS = (4, 4)
BF = jnp.bfloat16
F32 = jnp.float32


def basis_taps(lags, shapes):
    spots = np.arange(-TAPS, TAPS + 1, dtype=np.float64)
    out = []
    for s, d in shapes:
        full = np.exp(-spots * spots / (2 * s * s)) * (spots / s) ** d
        scale = 1.0 / math.sqrt(np.sum(full * full))
        vals = np.exp(-lags * lags / (2 * s * s)) * (lags / s) ** d * scale
        out.append(np.where(np.abs(lags) <= TAPS, vals, 0.0))
    return np.stack(out)


def detect_taps(lags):
    spots = np.arange(-REACH, REACH + 1, dtype=np.float64)
    total = np.sum(np.exp(-spots * spots / 18.0))
    vals = np.exp(-lags * lags / 18.0) / total - 1.0 / (2 * REACH + 1)
    return np.where(np.abs(lags) <= REACH, vals, 0.0)


def halves(a):
    a = np.asarray(a, np.float32)
    hi = a.astype(jnp.bfloat16)
    lo = (a - hi.astype(np.float32)).astype(jnp.bfloat16)
    return hi, lo


def window_lags(n):
    k = np.arange(256, dtype=np.float64)[:, None] - 64
    return k - np.arange(n, dtype=np.float64)[None, :]


def column_weights():
    bank = basis_taps(window_lags(128), COLUMN_SHAPES)
    nt = np.stack(
        [np.concatenate([bank[0], bank[1]], 1), np.concatenate([bank[2], bank[3]], 1)]
    )
    return halves(nt)


def row_tables():
    lags = (np.arange(16)[None, :] - np.arange(16)[:, None]).astype(np.float64)
    bank = basis_taps(lags, ROW_SHAPES)
    return np.tile(bank, (1, 1, 16)).astype(np.float32)


def split(x):
    hi = x.astype(BF)
    lo = (x - hi.astype(F32)).astype(BF)
    return hi, lo


def mm(a, b):
    return jnp.dot(a, b, preferred_element_type=F32)


def mm3(ah, al, bh, bl):
    return mm(ah, bh) + (mm(al, bh) + mm(ah, bl))


def match_groups(
    at_start, at_end, nt, weights, coeffs, gt, whi, wlo, left, main, right,
    xs_hi, xs_lo, window_at, put,
):
    def group(g, _):
        rows = pl.ds(pl.multiple_of(g * 64, 64), 64)
        lane = lax.broadcasted_iota(jnp.int32, (64, LANES), 1)
        blank = jnp.zeros((64, LANES), F32)
        parts = [blank if at_start else left[rows, :]]
        parts += [main[rows, t * LANES : (t + 1) * LANES] for t in range(nt)]
        parts += [blank if at_end else right[rows, :]]
        turned = [pltpu.roll(x, 64, 1) for x in parts]
        for t in range(nt + 1):
            v = jnp.where(lane < 64, turned[t], turned[t + 1])
            hi, lo = split(v)
            xs_hi[:, t * LANES : (t + 1) * LANES] = hi
            xs_lo[:, t * LANES : (t + 1) * LANES] = lo
        stack = lambda ref: jnp.concatenate(
            [ref[:, pl.ds(window_at(w), 256)] for w in range(nt)], axis=0
        )
        x_hi, x_lo = stack(xs_hi), stack(xs_lo)

        lane = lax.broadcasted_iota(jnp.int32, (16, LANES), 1)
        left_hi, left_lo = [], []
        for i in range(4):
            p = g * 4 + i
            w = weights[p]
            pair = []
            for h in range(2):
                acc = None
                for a in range(5):
                    both = jnp.where(lane < 64, coeffs[a, 2 * h, p], coeffs[a, 2 * h + 1, p])
                    term = both * gt[a, :, h * LANES : (h + 1) * LANES]
                    acc = term if acc is None else acc + term
                acc = jnp.where((lane // 16) % 4 == i, acc * w, 0.0)
                pair.append(split(acc))
            left_hi.append(jnp.concatenate([pair[0][0], pair[1][0]], axis=1))
            left_lo.append(jnp.concatenate([pair[0][1], pair[1][1]], axis=1))
        l_hi = jnp.concatenate(left_hi, axis=0)
        l_both = jnp.concatenate(left_hi + left_lo, axis=0)

        cols = []
        for bp in range(2):
            y = mm3(x_hi, x_lo, whi[bp], wlo[bp])
            cols.append(split(y))

        for j0 in range(0, nt, 2):
            windows = range(j0, min(j0 + 2, nt))

            def operand(k):
                blocks = []
                for b in range(4):
                    src = cols[b // 2][k]
                    lanes = slice((b % 2) * LANES, (b % 2 + 1) * LANES)
                    pair = [src[64 * w : 64 * w + 64, lanes] for w in windows]
                    blocks.append(pair[0] if len(pair) == 1 else jnp.concatenate(pair, axis=1))
                return jnp.concatenate(blocks, axis=0)

            zz = mm(l_both, operand(0))
            z = zz[0:64] + (zz[64:128] + mm(l_hi, operand(1)))
            for i in range(4):
                for h in range(2):
                    for w in windows:
                        rows = slice(16 * i + 8 * h, 16 * i + 8 * h + 8)
                        lanes = slice((w - j0) * LANES, (w - j0 + 1) * LANES)
                        put(g * 4 + i, w, h, z[rows, lanes])
        return 0

    lax.fori_loop(0, 8, group, 0)


def slot_kernel(
    at_start, at_end, nt,
    routes, offsets, weights, coeffs,
    gt, whi, wlo, left, main, right,
    out,
    xs_hi, xs_lo, cnt, dst, rnk,
):
    tiles = out.shape[1]

    def clear(i, _):
        cnt[i] = 0
        return 0

    lax.fori_loop(0, 32, clear, 0, unroll=8)

    def place(p, _):
        s = routes[p]
        r = cnt[s]
        cnt[s] = r + 1
        dst[p] = s
        rnk[p] = r
        return 0

    lax.fori_loop(0, 32, place, 0, unroll=4)
    zero = jnp.zeros((8, LANES), F32)

    def wipe(d, _):
        for t in range(tiles):
            out[d, t] = zero
        return 0

    lax.fori_loop(0, 32, wipe, 0, unroll=2)

    def put(p, w, h, value):
        out[dst[p], rnk[p] * 2 + (4 * w + h)] = value

    match_groups(
        at_start, at_end, nt, weights, coeffs, gt, whi, wlo, left, main, right,
        xs_hi, xs_lo, lambda w: w * LANES, put,
    )
    lane = lax.broadcasted_iota(jnp.int32, (1, LANES), 1)

    def note(p, _):
        k = offsets[p].astype(F32)
        row = jnp.where(lane == 0, k, weights[p])
        out[dst[p], tiles - 1, pl.ds(rnk[p], 1), :] = row
        return 0

    lax.fori_loop(0, 32, note, 0, unroll=4)


def spread_kernel(
    at_start, at_end, nt,
    vis, weights, coeffs,
    gt, whi, wlo, left, main, right, meta,
    *refs,
):
    outs, (xs_hi, xs_lo) = refs[:4], refs[4:]
    me = vis[0]

    def put(p, w, h, value):
        outs[w][p * 2 + h] = value

    match_groups(
        at_start, at_end, nt, weights, coeffs, gt, whi, wlo, left, main, right,
        xs_hi, xs_lo, lambda w: pl.multiple_of(((me + w) & 3) * LANES, LANES), put,
    )
    for out in outs:
        out[64] = meta[...]


def full(shape):
    return pl.BlockSpec(shape, lambda i: (0,) * len(shape))


def match_call(kernel, scalars, tables, pieces2d, extra, first, nt, out_shapes, scratch):
    gt, whi, wlo = tables
    width = nt * LANES
    smem = pl.BlockSpec(memory_space=pltpu.SMEM)
    return pl.pallas_call(
        functools.partial(kernel, first == 0, first + nt == 8, nt),
        grid=(1,),
        out_shape=[jax.ShapeDtypeStruct(s, F32) for s in out_shapes],
        in_specs=[smem] * len(scalars)
        + [
            full(gt.shape), full(whi.shape), full(wlo.shape),
            pl.BlockSpec((512, LANES), lambda i: (0, max(first - 1, 0))),
            pl.BlockSpec((512, width), lambda i: (0, first // nt)),
            pl.BlockSpec((512, LANES), lambda i: (0, min(first + nt, 7))),
        ]
        + [full(x.shape) for x in extra],
        out_specs=[full(s) for s in out_shapes],
        scratch_shapes=[
            pltpu.VMEM((64, width + LANES), BF),
            pltpu.VMEM((64, width + LANES), BF),
            *scratch,
        ],
        compiler_params=pltpu.CompilerParams(
            vmem_limit_bytes=(60 << 20) if first == 0 else (24 << 20)
        ),
        cost_estimate=pl.CostEstimate(
            flops=10**9 * nt, bytes_accessed=(1 << 19) * nt, transcendentals=0
        ),
        name="match",
    )(*scalars, gt, whi, wlo, pieces2d, pieces2d, pieces2d, *extra)


def pack_kernel(meta, *refs):
    groups, (out, cnt, block) = refs[:4], refs[4:]
    zero = jnp.zeros((8, LANES), F32)

    def wipe(d, _):
        for t in range(17):
            out[d, t] = zero
        for v in range(4):
            cnt[v * 32 + d] = 0
        for j in range(8):
            block[d * 8 + j] = 0.0
        return 0

    lax.fori_loop(0, 32, wipe, 0, unroll=2)
    for v in range(4):
        def place(p, _, v=v):
            s = meta[v, 0, p].astype(jnp.int32)
            r = cnt[v * 32 + s]
            cnt[v * 32 + s] = r + 1
            j = 2 * v + r
            for h in range(2):
                out[s, 2 * j + h] = groups[v][p * 2 + h]
            block[s * 8 + j] = meta[v, 1, p]
            return 0

        lax.fori_loop(0, 32, place, 0, unroll=4)
    lane = lax.broadcasted_iota(jnp.int32, (1, LANES), 1)

    def note(d, _):
        row = jnp.zeros((1, LANES), F32)
        for j in range(8):
            row = jnp.where(lane == j, block[d * 8 + j], row)
        out[d, 16, 0:1, :] = row
        return 0

    lax.fori_loop(0, 32, note, 0, unroll=2)


def pack(meta, groups):
    shape = (32, 17, 8, LANES)
    return pl.pallas_call(
        pack_kernel,
        grid=(1,),
        out_shape=jax.ShapeDtypeStruct(shape, F32),
        in_specs=[pl.BlockSpec(memory_space=pltpu.SMEM)] + [full(x.shape) for x in groups],
        out_specs=full(shape),
        scratch_shapes=[pltpu.SMEM((128,), jnp.int32), pltpu.SMEM((256,), F32)],
        compiler_params=pltpu.CompilerParams(vmem_limit_bytes=24 << 20),
        cost_estimate=pl.CostEstimate(flops=10**6, bytes_accessed=4 << 20, transcendentals=0),
        name="pack",
    )(meta, *groups)


def land_kernel(nt, vis_ref, meta, recv, *refs):
    outs, (acc, wsum, spot) = refs[:-3], refs[-3:]
    me = vis_ref[0]
    per = 2 * nt
    zero = jnp.zeros((8, LANES), F32)

    def wipe(i, _):
        for t in range(per):
            acc[i, t] = zero
        return 0

    lax.fori_loop(0, 64, wipe, 0, unroll=4)
    lane = lax.broadcasted_iota(jnp.int32, (8, LANES), 1)
    wsum[...] = zero

    def address(s, _):
        for r in range(2):
            k = meta[s, r, 0].astype(jnp.int32)
            spot[2 * s + r] = (((k >> 4) - me) & 3) * 16 + (k & 15)
        return 0

    lax.fori_loop(0, 32, address, 0, unroll=4)

    def land(s, _):
        for r in range(2):
            at = spot[2 * s + r]
            got = [recv[s, (t // 2) * 4 + 2 * r + t % 2] for t in range(per)]
            for t in range(per):
                acc[at, t] += got[t]
            wsum[...] += jnp.where(lane == at, meta[s, r, 1], 0.0)
        return 0

    lax.fori_loop(0, 32, land, 0, unroll=4)
    for rel in range(4):
        def one(i, _, rel=rel):
            for t in range(per):
                outs[rel][(t // 2) * 32 + i * 2 + t % 2] = acc[16 * rel + i, t]
            return 0

        lax.fori_loop(0, 16, one, 0, unroll=4)
        w = wsum[...]
        outs[rel][16 * per] = w if rel == 0 else pltpu.roll(w, LANES - 16 * rel, 1)


def full_kernel(vis_ref, spot, recv, *refs):
    outs, acc = refs[:-1], refs[-1]
    me = vis_ref[0]
    zero = jnp.zeros((8, LANES), F32)

    def wipe(i, _):
        acc[i, 0] = zero
        acc[i, 1] = zero
        return 0

    lax.fori_loop(0, 64, wipe, 0, unroll=8)

    def land(s, _):
        for j in range(8):
            at = spot[s, j]
            got = [recv[s, 2 * j + h] for h in range(2)]
            for h in range(2):
                acc[at, h] += got[h]
        return 0

    lax.fori_loop(0, 32, land, 0, unroll=4)
    for rel in range(4):
        base = ((me + rel) & 3) * 16

        def one(i, _, rel=rel, base=base):
            for h in range(2):
                outs[rel][i * 2 + h] = acc[base + i, h]
            return 0

        lax.fori_loop(0, 16, one, 0, unroll=8)


def land_call(kernel, vis, meta, recv, counts, scratch):
    shapes = [(k, 8, LANES) for k in counts]
    smem = pl.BlockSpec(memory_space=pltpu.SMEM)
    return pl.pallas_call(
        kernel,
        grid=(1,),
        out_shape=[jax.ShapeDtypeStruct(s, F32) for s in shapes],
        in_specs=[smem, smem, full(recv.shape)],
        out_specs=[full(s) for s in shapes],
        scratch_shapes=scratch,
        compiler_params=pltpu.CompilerParams(vmem_limit_bytes=24 << 20),
        cost_estimate=pl.CostEstimate(flops=10**6, bytes_accessed=4 << 20, transcendentals=0),
        name="land",
    )(vis, meta, recv)


def inverse_weight(weight, kk):
    lane = lax.broadcasted_iota(jnp.int32, (8, LANES), 1)
    total = jnp.sum(jnp.where(lane == kk, weight, 0.0), axis=1, keepdims=True)
    good = total > 0.0
    return jnp.where(good, 1.0 / jnp.where(good, total, 1.0), 0.0)


def summed(group, t):
    own, a, b, c = group
    return (own[t] + b[t]) + (a[t] + c[t])


def coadd_kernel(nt, *refs):
    group, wrefs = refs[:4], refs[4:8]
    coadd, top, bottom = refs[-3:]
    weight = (wrefs[0][0] + wrefs[2][0]) + (wrefs[1][0] + wrefs[3][0])

    def block(kk, _):
        inverse = inverse_weight(weight, kk)
        for ct in range(nt):
            for h in range(2):
                rows = pl.ds(pl.multiple_of(kk * 16 + 8 * h, 8), 8)
                v = summed(group, ct * 32 + kk * 2 + h) * inverse
                coadd[rows, ct * LANES : (ct + 1) * LANES] = v
        return 0

    lax.fori_loop(0, 16, block, 0, unroll=2)
    top[...] = coadd[0:16, :]
    bottom[...] = coadd[240:256, :]


def weight_specs(wat):
    return [pl.BlockSpec((1, 8, LANES), lambda i: (wat, 0, 0))] * 4


def first_coadd(group, wat, nt):
    edge = (16, LANES * nt)
    return pl.pallas_call(
        functools.partial(coadd_kernel, nt),
        grid=(1,),
        out_shape=[
            jax.ShapeDtypeStruct((256, 1024), F32),
            jax.ShapeDtypeStruct(edge, F32),
            jax.ShapeDtypeStruct(edge, F32),
        ],
        in_specs=[full((32 * nt, 8, LANES))] * 4 + weight_specs(wat),
        out_specs=[full((256, LANES * nt)), full(edge), full(edge)],
        compiler_params=pltpu.CompilerParams(vmem_limit_bytes=16 << 20),
        cost_estimate=pl.CostEstimate(
            flops=10**6, bytes_accessed=(5 << 17) * nt, transcendentals=0
        ),
        name="coadd",
    )(*group, *group)


def join_kernel(first, vis_ref, *refs):
    heads, feet, wrefs = refs[:4], refs[4:8], refs[8:12]
    olds, outs = refs[12:14], refs[14:]
    weight = (wrefs[0][0] + wrefs[2][0]) + (wrefs[1][0] + wrefs[3][0])
    for e, group in enumerate((heads, feet)):
        inverse = inverse_weight(weight, 15 * e)
        outs[e][:, : first * LANES] = olds[e][...]
        for d in range(4):
            tile = first + ((vis_ref[0] - d) & 3)
            lanes = pl.ds(pl.multiple_of(tile * LANES, LANES), LANES)
            for h in range(2):
                outs[e][8 * h : 8 * h + 8, lanes] = group[d][h] * inverse


def join_edges(vis, group, wgroup, wat, first, top, bottom):
    edge = (16, 1024)
    end = lambda k: [pl.BlockSpec((2, 8, LANES), lambda i: (k, 0, 0))] * 4
    return pl.pallas_call(
        functools.partial(join_kernel, first),
        grid=(1,),
        out_shape=[jax.ShapeDtypeStruct(edge, F32)] * 2,
        in_specs=[pl.BlockSpec(memory_space=pltpu.SMEM)]
        + end(0)
        + end(15)
        + weight_specs(wat)
        + [full(top.shape), full(bottom.shape)],
        out_specs=[full(edge)] * 2,
        compiler_params=pltpu.CompilerParams(vmem_limit_bytes=16 << 20),
        cost_estimate=pl.CostEstimate(flops=10**5, bytes_accessed=1 << 19, transcendentals=0),
        name="join",
    )(vis, *group, *group, *wgroup, top, bottom)


def filtered(parts, dhi, dlo):
    rows = parts[0].shape[0]
    lane = lax.broadcasted_iota(jnp.int32, (rows, LANES), 1)
    turned = [pltpu.roll(x, 64, 1) for x in parts]
    cut = [
        split(jnp.where(lane < 64, turned[t], turned[t + 1])) for t in range(len(parts) - 1)
    ]
    window = lambda k: jnp.concatenate(
        [
            jnp.concatenate([cut[j][k], cut[j + 1][k]], axis=1)
            for j in range(len(parts) - 2)
        ],
        axis=0,
    )
    return split(mm3(window(0), window(1), dhi[...], dlo[...]))


def detect_tiles(n, tile, tables, y_hi, y_lo, out, done, between):
    dhi, dlo, bhi, blo = tables[:4]

    def group(g, _):
        rows = pl.ds(pl.multiple_of(g * 64, 64), 64)
        hi, lo = filtered([tile(t, rows) for t in range(n + 2)], dhi, dlo)
        for j in range(n):
            y_hi[rows, j * LANES : (j + 1) * LANES] = hi[64 * j : 64 * j + 64]
            y_lo[rows, j * LANES : (j + 1) * LANES] = lo[64 * j : 64 * j + 64]
        return 0

    lax.fori_loop(0, 4, group, 0, unroll=2)
    between()
    for j0 in range(0, n, 2):
        lanes = slice(j0 * LANES, min(j0 + 2, n) * LANES)
        out[:, lanes] = mm3(bhi[...], blo[...], y_hi[:, lanes], y_lo[:, lanes])
        done(j0, lanes)


def early_kernel(n, *refs):
    tables, (x, out, rim, y_hi, y_lo) = refs[:4], refs[4:]

    def tile(t, rows):
        if t == 0:
            return jnp.zeros((64, LANES), F32)
        return x[rows, (t - 1) * LANES : t * LANES]

    detect_tiles(n, tile, tables, y_hi, y_lo, out, lambda *_: None, lambda: None)
    rim[0:16, :] = out[0:16, :]
    rim[16:32, :] = out[240:256, :]


def early_detect(n, coadd, tables):
    tables = tables[:4]
    width = (n + 1) * LANES
    return pl.pallas_call(
        functools.partial(early_kernel, n),
        grid=(1,),
        out_shape=[
            jax.ShapeDtypeStruct(coadd.shape, F32),
            jax.ShapeDtypeStruct((32, n * LANES), F32),
        ],
        in_specs=[full(a.shape) for a in tables] + [full((256, width))],
        out_specs=[full((256, n * LANES)), full((32, n * LANES))],
        scratch_shapes=[pltpu.VMEM((256, n * LANES), BF), pltpu.VMEM((256, n * LANES), BF)],
        compiler_params=pltpu.CompilerParams(vmem_limit_bytes=16 << 20),
        cost_estimate=pl.CostEstimate(
            flops=10**9, bytes_accessed=1 << 20, transcendentals=0
        ),
        name="early",
    )(*tables, coadd)


def late_kernel(first, nt, n, vis_ref, *refs):
    tables, group, wrefs = refs[:6], refs[6:10], refs[10:14]
    above, below, left, rim = refs[14:18]
    coadd, out, y_hi, y_lo, det, sides, sems = refs[20:]
    weight = (wrefs[0][0] + wrefs[2][0]) + (wrefs[1][0] + wrefs[3][0])
    last = first + nt
    start = last - n - 1
    copies = []

    def send(src, dst):
        copy = pltpu.make_async_copy(src, dst, sems.at[len(copies)])
        copy.start()
        copies.append(copy)

    def block(i, _):
        inverse = inverse_weight(weight, i)
        for d in range(4):
            lanes = pl.ds(pl.multiple_of(((vis_ref[0] - d) & 3) * LANES, LANES), LANES)
            for h in range(2):
                rows = pl.ds(pl.multiple_of(i * 16 + 8 * h, 8), 8)
                coadd[rows, lanes] = group[d][i * 2 + h] * inverse
        return 0

    lax.fori_loop(0, 16, block, 0, unroll=4)

    def tile(t, rows):
        real = start + t
        if real >= last:
            return jnp.zeros((64, LANES), F32)
        if real < first:
            return left[rows, t * LANES : (t + 1) * LANES]
        return coadd[rows, (real - first) * LANES : (real - first + 1) * LANES]

    whole_left = slice(0, (start + 1) * LANES)

    def between():
        strips = [jnp.zeros((32, LANES), F32)]
        for t in range(last):
            lanes = slice(t * LANES, (t + 1) * LANES)
            strips.append(jnp.concatenate([above[:, lanes], below[:, lanes]], axis=0))
        hi, lo = filtered(strips + strips[:1], tables[0], tables[1])
        side = lambda v: jnp.concatenate([v[32 * j : 32 * j + 32] for j in range(last)], axis=1)
        sides[...] = mm3(tables[4][...], tables[5][...], side(hi), side(lo))
        sides[:, whole_left] += rim[...]

    def done(j0, lanes):
        there = slice((start + 1) * LANES + lanes.start, (start + 1) * LANES + lanes.stop)
        det[0:16, lanes] += sides[0:16, there]
        det[240:256, lanes] += sides[16:32, there]
        send(det.at[:, lanes], out.at[:, there])

    detect_tiles(n, tile, tables, y_hi, y_lo, det, done, between)
    send(sides.at[0:16, whole_left], out.at[0:16, whole_left])
    send(sides.at[16:32, whole_left], out.at[240:256, whole_left])
    for copy in copies:
        copy.wait()


def late_detect(vis, group, wgroup, wat, first, nt, n, above, below, tables, coadd, before):
    start = (first + nt - n - 1) // (n + 1 - nt)
    detection, rim = before
    any_spec = pl.BlockSpec(memory_space=pl.ANY)
    left = pl.BlockSpec((256, (n + 1 - nt) * LANES), lambda i: (0, start))
    args = [vis, *tables, *group, *wgroup, above, below, coadd, rim, coadd, detection]
    in_specs = [pl.BlockSpec(memory_space=pltpu.SMEM)]
    in_specs += [full(a.shape) for a in [*tables, *group]] + weight_specs(wat)
    in_specs += [full(a.shape) for a in [above, below]]
    in_specs += [left, full(rim.shape), any_spec, any_spec]
    return pl.pallas_call(
        functools.partial(late_kernel, first, nt, n),
        grid=(1,),
        out_shape=[jax.ShapeDtypeStruct(coadd.shape, F32)] * 2,
        in_specs=in_specs,
        out_specs=[pl.BlockSpec((256, nt * LANES), lambda i: (0, first // nt)), any_spec],
        scratch_shapes=[
            pltpu.VMEM((256, n * LANES), BF),
            pltpu.VMEM((256, n * LANES), BF),
            pltpu.VMEM((256, n * LANES), F32),
            pltpu.VMEM((32, (first + nt) * LANES), F32),
            pltpu.SemaphoreType.DMA((2 + (n + 1) // 2,)),
        ],
        input_output_aliases={len(args) - 2: 0, len(args) - 1: 1},
        compiler_params=pltpu.CompilerParams(vmem_limit_bytes=24 << 20),
        cost_estimate=pl.CostEstimate(
            flops=2 * 10**9, bytes_accessed=4 << 20, transcendentals=0
        ),
        name="late",
    )(*args)


def detect_tables():
    dhi, dlo = halves(detect_taps(window_lags(128)))
    idx = np.arange(256, dtype=np.float64)
    bhi, blo = halves(detect_taps(idx[None, :] - idx[:, None]))
    q = np.arange(16, dtype=np.float64)
    edge = np.zeros((32, 32))
    edge[0:16, 0:16] = detect_taps((q[None, :] - 16) - q[:, None])
    edge[16:32, 16:32] = detect_taps((q[None, :] + 16) - q[:, None])
    ehi, elo = halves(edge)
    return dhi, dlo, bhi, blo, ehi, elo


def shards(pieces, coeffs, weights, routes, offsets):
    count, rows, width = pieces.shape
    pieces2d = pieces.reshape(count * rows, width)
    route1 = routes.reshape(count)
    coeffs_t = jnp.transpose(coeffs, (1, 2, 0))
    whi, wlo = column_weights()
    tables = (jnp.asarray(row_tables()), jnp.asarray(whi), jnp.asarray(wlo))
    dtables = tuple(jnp.asarray(a) for a in detect_tables())
    vis = lax.axis_index("vis").reshape(1)
    nv = lax.axis_size("vis")
    n = lax.axis_size("tile") * nv
    shifts = [[(i, (i + d) % nv) for i in range(nv)] for d in (1, 2, 3)]
    axes = ("tile", "vis")

    first, nt = CHUNKS
    per = 2 * first
    wat = 16 * per
    ints = [pltpu.SMEM((32,), jnp.int32)] * 3

    def over_vis(group):
        moved = [group[0]]
        for d in range(3):
            moved.append(lax.ppermute(group[d + 1], "vis", shifts[d]))
        return moved

    def over_tile(slots):
        return lax.all_to_all(slots, "tile", split_axis=0, concat_axis=0, tiled=True)

    (slots,) = match_call(
        slot_kernel, (route1, offsets, weights, coeffs_t), tables, pieces2d, (), 0, first,
        [(32, 4 * first + 1, 8, LANES)], ints,
    )
    recv = over_tile(slots)
    meta = recv[:, 4 * first, 0:2, 0:2]
    landed = land_call(
        functools.partial(land_kernel, first), vis, meta, recv, [16 * per + 1] * 4,
        [
            pltpu.VMEM((64, per, 8, LANES), F32),
            pltpu.VMEM((8, LANES), F32),
            pltpu.SMEM((64,), jnp.int32),
        ],
    )
    start = over_vis(landed)

    facts = jnp.stack([route1.astype(F32), offsets.astype(F32)])
    facts = jnp.pad(facts, ((0, 6), (0, LANES - count)))
    spread = match_call(
        spread_kernel, (vis, weights, coeffs_t), tables, pieces2d, (facts,), first, nt,
        [(2 * count + 1, 8, LANES)] * 4, [],
    )
    traded = over_vis(spread)
    notes = jnp.stack([x[2 * count, 0:2, 0:count] for x in traded])
    slots = pack(notes, traded)
    recv = over_tile(slots)
    landed = land_call(
        full_kernel, vis, recv[:, 16, 0, 0:8].astype(jnp.int32), recv, [32] * 4,
        [pltpu.VMEM((64, 2, 8, LANES), F32)],
    )
    bulk = over_vis(landed)

    coadd, top, bottom = first_coadd(start, wat, first)
    edges = join_edges(vis, bulk, start, wat, first, top, bottom)
    above = lax.ppermute(edges[1], axes, [(i, i + 1) for i in range(n - 1)])
    below = lax.ppermute(edges[0], axes, [(i + 1, i) for i in range(n - 1)])
    before = early_detect(first - 1, coadd, dtables)
    coadd, detection = late_detect(
        vis, bulk, start, wat, first, nt, nt + 1, above, below, dtables, coadd, before
    )
    return (coadd, detection)


def solution(mesh):
    placed = (
        P(("tile", "vis"), None, None),
        P(("tile", "vis"), None, None),
        P(("tile", "vis")),
        P(("tile", "vis"), None),
        P(("tile", "vis")),
    )
    return jax.shard_map(
        shards,
        mesh=mesh,
        in_specs=placed,
        out_specs=(P(("tile", "vis"), None), P(("tile", "vis"), None)),
        check_vma=False,
    )
```

```python
import functools
import math

import jax
import jax.numpy as jnp
import numpy as np
from jax import lax
from jax.experimental import pallas as pl
from jax.experimental.pallas import tpu as pltpu
from jax.sharding import PartitionSpec as P


TAPS = 10
REACH = 15
ROW_SHAPES = ((1.0, 0), (1.0, 1), (2.0, 0), (2.0, 2), (3.5, 0))
COLUMN_SHAPES = ((1.0, 0), (2.0, 0), (2.0, 1), (3.5, 0))
LANES = 128
CHUNKS = (4, 4)
BF = jnp.bfloat16
F32 = jnp.float32


def basis_taps(lags, shapes):
    spots = np.arange(-TAPS, TAPS + 1, dtype=np.float64)
    out = []
    for s, d in shapes:
        full = np.exp(-spots * spots / (2 * s * s)) * (spots / s) ** d
        scale = 1.0 / math.sqrt(np.sum(full * full))
        vals = np.exp(-lags * lags / (2 * s * s)) * (lags / s) ** d * scale
        out.append(np.where(np.abs(lags) <= TAPS, vals, 0.0))
    return np.stack(out)


def detect_taps(lags):
    spots = np.arange(-REACH, REACH + 1, dtype=np.float64)
    total = np.sum(np.exp(-spots * spots / 18.0))
    vals = np.exp(-lags * lags / 18.0) / total - 1.0 / (2 * REACH + 1)
    return np.where(np.abs(lags) <= REACH, vals, 0.0)


def halves(a):
    a = np.asarray(a, np.float32)
    hi = a.astype(jnp.bfloat16)
    lo = (a - hi.astype(np.float32)).astype(jnp.bfloat16)
    return hi, lo


def window_lags(n):
    k = np.arange(256, dtype=np.float64)[:, None] - 64
    return k - np.arange(n, dtype=np.float64)[None, :]


def column_weights():
    bank = basis_taps(window_lags(128), COLUMN_SHAPES)
    nt = np.stack(
        [np.concatenate([bank[0], bank[1]], 1), np.concatenate([bank[2], bank[3]], 1)]
    )
    return halves(nt)


def row_tables():
    lags = (np.arange(16)[None, :] - np.arange(16)[:, None]).astype(np.float64)
    bank = basis_taps(lags, ROW_SHAPES)
    return np.tile(bank, (1, 1, 16)).astype(np.float32)


def split(x):
    hi = x.astype(BF)
    lo = (x - hi.astype(F32)).astype(BF)
    return hi, lo


def mm(a, b):
    return jnp.dot(a, b, preferred_element_type=F32)


def mm3(ah, al, bh, bl):
    return mm(ah, bh) + (mm(al, bh) + mm(ah, bl))


def match_groups(
    at_start, at_end, nt, weights, coeffs, gt, whi, wlo, left, main, right,
    xs_hi, xs_lo, window_at, put,
):
    def group(g, _):
        rows = pl.ds(pl.multiple_of(g * 64, 64), 64)
        lane = lax.broadcasted_iota(jnp.int32, (64, LANES), 1)
        blank = jnp.zeros((64, LANES), F32)
        parts = [blank if at_start else left[rows, :]]
        parts += [main[rows, t * LANES : (t + 1) * LANES] for t in range(nt)]
        parts += [blank if at_end else right[rows, :]]
        turned = [pltpu.roll(x, 64, 1) for x in parts]
        for t in range(nt + 1):
            v = jnp.where(lane < 64, turned[t], turned[t + 1])
            hi, lo = split(v)
            xs_hi[:, t * LANES : (t + 1) * LANES] = hi
            xs_lo[:, t * LANES : (t + 1) * LANES] = lo
        stack = lambda ref: jnp.concatenate(
            [ref[:, pl.ds(window_at(w), 256)] for w in range(nt)], axis=0
        )
        x_hi, x_lo = stack(xs_hi), stack(xs_lo)

        lane = lax.broadcasted_iota(jnp.int32, (16, LANES), 1)
        left_hi, left_lo = [], []
        for i in range(4):
            p = g * 4 + i
            w = weights[p]
            pair = []
            for h in range(2):
                acc = None
                for a in range(5):
                    both = jnp.where(lane < 64, coeffs[a, 2 * h, p], coeffs[a, 2 * h + 1, p])
                    term = both * gt[a, :, h * LANES : (h + 1) * LANES]
                    acc = term if acc is None else acc + term
                acc = jnp.where((lane // 16) % 4 == i, acc * w, 0.0)
                pair.append(split(acc))
            left_hi.append(jnp.concatenate([pair[0][0], pair[1][0]], axis=1))
            left_lo.append(jnp.concatenate([pair[0][1], pair[1][1]], axis=1))
        l_hi = jnp.concatenate(left_hi, axis=0)
        l_both = jnp.concatenate(left_hi + left_lo, axis=0)

        cols = []
        for bp in range(2):
            y = mm3(x_hi, x_lo, whi[bp], wlo[bp])
            cols.append(split(y))

        for j0 in range(0, nt, 2):
            windows = range(j0, min(j0 + 2, nt))

            def operand(k):
                blocks = []
                for b in range(4):
                    src = cols[b // 2][k]
                    lanes = slice((b % 2) * LANES, (b % 2 + 1) * LANES)
                    pair = [src[64 * w : 64 * w + 64, lanes] for w in windows]
                    blocks.append(pair[0] if len(pair) == 1 else jnp.concatenate(pair, axis=1))
                return jnp.concatenate(blocks, axis=0)

            zz = mm(l_both, operand(0))
            z = zz[0:64] + (zz[64:128] + mm(l_hi, operand(1)))
            for i in range(4):
                for h in range(2):
                    for w in windows:
                        rows = slice(16 * i + 8 * h, 16 * i + 8 * h + 8)
                        lanes = slice((w - j0) * LANES, (w - j0 + 1) * LANES)
                        put(g * 4 + i, w, h, z[rows, lanes])
        return 0

    lax.fori_loop(0, 8, group, 0)


def slot_kernel(
    nt,
    routes, offsets, weights, coeffs,
    gt_any, whi_any, wlo_any, pieces,
    out,
    xs_hi, xs_lo, gt, whi, wlo, main, cnt, dst, rnk, sems,
):
    tiles = out.shape[1]
    moves = [
        (pieces.at[:, 0 : (nt + 1) * LANES], main),
        (whi_any, whi),
        (wlo_any, wlo),
        (gt_any, gt),
    ]
    fetches = [pltpu.make_async_copy(a, b, sems.at[i]) for i, (a, b) in enumerate(moves)]
    for fetch in fetches:
        fetch.start()

    def clear(i, _):
        cnt[i] = 0
        return 0

    lax.fori_loop(0, 32, clear, 0, unroll=8)

    def place(p, _):
        s = routes[p]
        r = cnt[s]
        cnt[s] = r + 1
        dst[p] = s
        rnk[p] = r
        return 0

    lax.fori_loop(0, 32, place, 0, unroll=4)
    zero = jnp.zeros((8, LANES), F32)

    def wipe(d, _):
        for t in range(tiles):
            out[d, t] = zero
        return 0

    lax.fori_loop(0, 32, wipe, 0, unroll=2)

    def put(p, w, h, value):
        out[dst[p], rnk[p] * 2 + (4 * w + h)] = value

    for fetch in fetches:
        fetch.wait()
    match_groups(
        True, False, nt, weights, coeffs, gt, whi, wlo,
        None, main, main.at[:, nt * LANES : (nt + 1) * LANES],
        xs_hi, xs_lo, lambda w: w * LANES, put,
    )
    lane = lax.broadcasted_iota(jnp.int32, (1, LANES), 1)

    def note(p, _):
        k = offsets[p].astype(F32)
        row = jnp.where(lane == 0, k, weights[p])
        out[dst[p], tiles - 1, pl.ds(rnk[p], 1), :] = row
        return 0

    lax.fori_loop(0, 32, note, 0, unroll=4)


def spread_kernel(
    at_start, at_end, nt,
    vis, weights, coeffs,
    gt, whi, wlo, left, main, right, meta,
    *refs,
):
    outs, (xs_hi, xs_lo) = refs[:4], refs[4:]
    me = vis[0]

    def put(p, w, h, value):
        outs[w][p * 2 + h] = value

    match_groups(
        at_start, at_end, nt, weights, coeffs, gt, whi, wlo, left, main, right,
        xs_hi, xs_lo, lambda w: pl.multiple_of(((me + w) & 3) * LANES, LANES), put,
    )
    for out in outs:
        out[64] = meta[...]


def full(shape):
    return pl.BlockSpec(shape, lambda i: (0,) * len(shape))


def match_call(kernel, scalars, tables, pieces2d, extra, first, nt, out_shapes, scratch):
    gt, whi, wlo = tables
    width = nt * LANES
    smem = pl.BlockSpec(memory_space=pltpu.SMEM)
    return pl.pallas_call(
        functools.partial(kernel, first == 0, first + nt == 8, nt),
        grid=(1,),
        out_shape=[jax.ShapeDtypeStruct(s, F32) for s in out_shapes],
        in_specs=[smem] * len(scalars)
        + [
            full(gt.shape), full(whi.shape), full(wlo.shape),
            pl.BlockSpec((512, LANES), lambda i: (0, max(first - 1, 0))),
            pl.BlockSpec((512, width), lambda i: (0, first // nt)),
            pl.BlockSpec((512, LANES), lambda i: (0, min(first + nt, 7))),
        ]
        + [full(x.shape) for x in extra],
        out_specs=[full(s) for s in out_shapes],
        scratch_shapes=[
            pltpu.VMEM((64, width + LANES), BF),
            pltpu.VMEM((64, width + LANES), BF),
            *scratch,
        ],
        compiler_params=pltpu.CompilerParams(
            vmem_limit_bytes=(60 << 20) if first == 0 else (24 << 20)
        ),
        cost_estimate=pl.CostEstimate(
            flops=10**9 * nt, bytes_accessed=(1 << 19) * nt, transcendentals=0
        ),
        name="match",
    )(*scalars, gt, whi, wlo, pieces2d, pieces2d, pieces2d, *extra)


def match_slots(scalars, tables, pieces2d, nt):
    smem = pl.BlockSpec(memory_space=pltpu.SMEM)
    any_spec = pl.BlockSpec(memory_space=pl.ANY)
    shape = (32, 4 * nt + 1, 8, LANES)
    width = (nt + 1) * LANES
    return pl.pallas_call(
        functools.partial(slot_kernel, nt),
        grid=(1,),
        out_shape=jax.ShapeDtypeStruct(shape, F32),
        in_specs=[smem] * 4 + [any_spec] * 4,
        out_specs=full(shape),
        scratch_shapes=[
            pltpu.VMEM((64, width), BF),
            pltpu.VMEM((64, width), BF),
            *[pltpu.VMEM(x.shape, x.dtype) for x in tables],
            pltpu.VMEM((512, width), F32),
            *[pltpu.SMEM((32,), jnp.int32)] * 3,
            pltpu.SemaphoreType.DMA((4,)),
        ],
        compiler_params=pltpu.CompilerParams(vmem_limit_bytes=60 << 20),
        cost_estimate=pl.CostEstimate(
            flops=10**9 * nt, bytes_accessed=(1 << 19) * nt, transcendentals=0
        ),
        name="match",
    )(*scalars, *tables, pieces2d)


def pack_kernel(meta, *refs):
    groups, (out, cnt) = refs[:4], refs[4:]
    zero = jnp.zeros((8, LANES), F32)

    def wipe(d, _):
        for t in range(16):
            out[d, t] = zero
        for v in range(4):
            cnt[v * 32 + d] = 0
        return 0

    lax.fori_loop(0, 32, wipe, 0, unroll=2)
    for v in range(4):
        def place(p, _, v=v):
            s = meta[v, 0, p].astype(jnp.int32)
            r = cnt[v * 32 + s]
            cnt[v * 32 + s] = r + 1
            j = 2 * v + r
            for h in range(2):
                out[s, 2 * j + h] = groups[v][p * 2 + h]
            return 0

        lax.fori_loop(0, 32, place, 0, unroll=4)


def pack(meta, groups):
    shape = (32, 16, 8, LANES)
    return pl.pallas_call(
        pack_kernel,
        grid=(1,),
        out_shape=jax.ShapeDtypeStruct(shape, F32),
        in_specs=[pl.BlockSpec(memory_space=pltpu.SMEM)] + [full(x.shape) for x in groups],
        out_specs=full(shape),
        scratch_shapes=[pltpu.SMEM((128,), jnp.int32)],
        compiler_params=pltpu.CompilerParams(vmem_limit_bytes=24 << 20),
        cost_estimate=pl.CostEstimate(flops=10**6, bytes_accessed=4 << 20, transcendentals=0),
        name="pack",
    )(meta, *groups)


def land_kernel(nt, vis_ref, meta, recv, *refs):
    outs, (acc, wsum, spot) = refs[:-3], refs[-3:]
    me = vis_ref[0]
    per = 2 * nt
    zero = jnp.zeros((8, LANES), F32)

    def wipe(i, _):
        for t in range(per):
            acc[i, t] = zero
        return 0

    lax.fori_loop(0, 64, wipe, 0, unroll=4)
    lane = lax.broadcasted_iota(jnp.int32, (8, LANES), 1)
    wsum[...] = zero

    def address(s, _):
        for r in range(2):
            k = meta[s, r, 0].astype(jnp.int32)
            spot[2 * s + r] = (((k >> 4) - me) & 3) * 16 + (k & 15)
        return 0

    lax.fori_loop(0, 32, address, 0, unroll=4)

    def land(s, _):
        for r in range(2):
            at = spot[2 * s + r]
            got = [recv[s, (t // 2) * 4 + 2 * r + t % 2] for t in range(per)]
            for t in range(per):
                acc[at, t] += got[t]
            wsum[...] += jnp.where(lane == at, meta[s, r, 1], 0.0)
        return 0

    lax.fori_loop(0, 32, land, 0, unroll=4)
    for rel in range(4):
        def one(i, _, rel=rel):
            for t in range(per):
                outs[rel][(t // 2) * 32 + i * 2 + t % 2] = acc[16 * rel + i, t]
            return 0

        lax.fori_loop(0, 16, one, 0, unroll=4)
        w = wsum[...]
        outs[rel][16 * per] = w if rel == 0 else pltpu.roll(w, LANES - 16 * rel, 1)


def full_kernel(vis_ref, spot, recv, *refs):
    outs, acc = refs[:-1], refs[-1]
    me = vis_ref[0]
    zero = jnp.zeros((8, LANES), F32)

    def wipe(i, _):
        acc[i, 0] = zero
        acc[i, 1] = zero
        return 0

    lax.fori_loop(0, 64, wipe, 0, unroll=8)

    def land(s, _):
        for j in range(8):
            at = spot[j // 2, s, j % 2]
            got = [recv[s, 2 * j + h] for h in range(2)]
            for h in range(2):
                acc[at, h] += got[h]
        return 0

    lax.fori_loop(0, 32, land, 0, unroll=4)
    for rel in range(4):
        base = ((me + rel) & 3) * 16

        def one(i, _, rel=rel, base=base):
            for h in range(2):
                outs[rel][i * 2 + h] = acc[base + i, h]
            return 0

        lax.fori_loop(0, 16, one, 0, unroll=8)


def land_right(vis, spot, recv):
    smem = pl.BlockSpec(memory_space=pltpu.SMEM)
    vmem = pl.BlockSpec(memory_space=pltpu.VMEM)
    return pl.pallas_call(
        full_kernel,
        out_shape=[jax.ShapeDtypeStruct((32, 8, LANES), F32)] * 4,
        in_specs=[smem, smem, vmem],
        out_specs=[vmem] * 4,
        scratch_shapes=[pltpu.VMEM((64, 2, 8, LANES), F32)],
        compiler_params=pltpu.CompilerParams(vmem_limit_bytes=8 << 20),
        cost_estimate=pl.CostEstimate(flops=10**6, bytes_accessed=4 << 20, transcendentals=0),
        name="land",
    )(vis, spot, recv)


def land_call(kernel, vis, meta, recv, counts, scratch):
    shapes = [(k, 8, LANES) for k in counts]
    smem = pl.BlockSpec(memory_space=pltpu.SMEM)
    return pl.pallas_call(
        kernel,
        grid=(1,),
        out_shape=[jax.ShapeDtypeStruct(s, F32) for s in shapes],
        in_specs=[smem, smem, full(recv.shape)],
        out_specs=[full(s) for s in shapes],
        scratch_shapes=scratch,
        compiler_params=pltpu.CompilerParams(vmem_limit_bytes=24 << 20),
        cost_estimate=pl.CostEstimate(flops=10**6, bytes_accessed=4 << 20, transcendentals=0),
        name="land",
    )(vis, meta, recv)


def inverse_weight(weight, kk):
    lane = lax.broadcasted_iota(jnp.int32, (8, LANES), 1)
    total = jnp.sum(jnp.where(lane == kk, weight, 0.0), axis=1, keepdims=True)
    good = total > 0.0
    return jnp.where(good, 1.0 / jnp.where(good, total, 1.0), 0.0)


def summed(group, t):
    own, a, b, c = group
    return (own[t] + b[t]) + (a[t] + c[t])


def coadd_kernel(nt, *refs):
    group, wrefs = refs[:4], refs[4:8]
    coadd, top, bottom, mass = refs[-4:]
    weight = (wrefs[0][0] + wrefs[2][0]) + (wrefs[1][0] + wrefs[3][0])
    mass[...] = weight

    def block(kk, _):
        inverse = inverse_weight(weight, kk)
        for ct in range(nt):
            for h in range(2):
                rows = pl.ds(pl.multiple_of(kk * 16 + 8 * h, 8), 8)
                v = summed(group, ct * 32 + kk * 2 + h) * inverse
                coadd[rows, ct * LANES : (ct + 1) * LANES] = v
        return 0

    lax.fori_loop(0, 16, block, 0, unroll=2)
    top[...] = coadd[0:16, :]
    bottom[...] = coadd[240:256, :]


def weight_specs(wat):
    return [pl.BlockSpec((1, 8, LANES), lambda i: (wat, 0, 0))] * 4


def first_coadd(group, wat, nt):
    edge = (16, LANES * nt)
    return pl.pallas_call(
        functools.partial(coadd_kernel, nt),
        grid=(1,),
        out_shape=[
            jax.ShapeDtypeStruct((256, 1024), F32),
            jax.ShapeDtypeStruct(edge, F32),
            jax.ShapeDtypeStruct(edge, F32),
            jax.ShapeDtypeStruct((8, LANES), F32),
        ],
        in_specs=[full((32 * nt, 8, LANES))] * 4 + weight_specs(wat),
        out_specs=[full((256, LANES * nt)), full(edge), full(edge), full((8, LANES))],
        compiler_params=pltpu.CompilerParams(vmem_limit_bytes=16 << 20),
        cost_estimate=pl.CostEstimate(
            flops=10**6, bytes_accessed=(5 << 17) * nt, transcendentals=0
        ),
        name="coadd",
    )(*group, *group)


def join_kernel(first, vis_ref, mass, *refs):
    group, olds, outs = refs[:4], refs[4:6], refs[6:]
    for e in range(2):
        inverse = inverse_weight(mass[...], 15 * e)
        outs[e][:, : first * LANES] = olds[e][...]
        for d in range(4):
            tile = first + ((vis_ref[0] - d) & 3)
            lanes = pl.ds(pl.multiple_of(tile * LANES, LANES), LANES)
            for h in range(2):
                outs[e][8 * h : 8 * h + 8, lanes] = group[d][30 * e + h] * inverse


def join_edges(vis, mass, group, first, top, bottom):
    vmem = pl.BlockSpec(memory_space=pltpu.VMEM)
    return pl.pallas_call(
        functools.partial(join_kernel, first),
        out_shape=[jax.ShapeDtypeStruct((16, 1024), F32)] * 2,
        in_specs=[pl.BlockSpec(memory_space=pltpu.SMEM)] + [vmem] * 7,
        out_specs=[vmem] * 2,
        compiler_params=pltpu.CompilerParams(vmem_limit_bytes=4 << 20),
        cost_estimate=pl.CostEstimate(flops=10**5, bytes_accessed=1 << 19, transcendentals=0),
        name="join",
    )(vis, mass, *group, top, bottom)


def filtered(parts, dhi, dlo):
    rows = parts[0].shape[0]
    lane = lax.broadcasted_iota(jnp.int32, (rows, LANES), 1)
    turned = [pltpu.roll(x, 64, 1) for x in parts]
    cut = [
        split(jnp.where(lane < 64, turned[t], turned[t + 1])) for t in range(len(parts) - 1)
    ]
    window = lambda k: jnp.concatenate(
        [
            jnp.concatenate([cut[j][k], cut[j + 1][k]], axis=1)
            for j in range(len(parts) - 2)
        ],
        axis=0,
    )
    return split(mm3(window(0), window(1), dhi[...], dlo[...]))


def detect_tiles(n, tile, tables, y_hi, y_lo, out, done, between):
    dhi, dlo, bhi, blo = tables[:4]

    def group(g, _):
        rows = pl.ds(pl.multiple_of(g * 64, 64), 64)
        hi, lo = filtered([tile(t, rows) for t in range(n + 2)], dhi, dlo)
        for j in range(n):
            y_hi[rows, j * LANES : (j + 1) * LANES] = hi[64 * j : 64 * j + 64]
            y_lo[rows, j * LANES : (j + 1) * LANES] = lo[64 * j : 64 * j + 64]
        return 0

    lax.fori_loop(0, 4, group, 0, unroll=2)
    between()
    for j0 in range(0, n, 2):
        lanes = slice(j0 * LANES, min(j0 + 2, n) * LANES)
        out[:, lanes] = mm3(bhi[...], blo[...], y_hi[:, lanes], y_lo[:, lanes])
        done(j0, lanes)


def early_kernel(n, *refs):
    tables, (x, out, rim, context, y_hi, y_lo) = refs[:4], refs[4:]
    context[...] = x[:, (n - 1) * LANES : (n + 1) * LANES]

    def tile(t, rows):
        if t == 0:
            return jnp.zeros((64, LANES), F32)
        return x[rows, (t - 1) * LANES : t * LANES]

    detect_tiles(n, tile, tables, y_hi, y_lo, out, lambda *_: None, lambda: None)
    rim[0:16, :] = out[0:16, :]
    rim[16:32, :] = out[240:256, :]


def early_detect(n, coadd, tables):
    tables = tables[:4]
    width = (n + 1) * LANES
    return pl.pallas_call(
        functools.partial(early_kernel, n),
        grid=(1,),
        out_shape=[
            jax.ShapeDtypeStruct(coadd.shape, F32),
            jax.ShapeDtypeStruct((32, n * LANES), F32),
            jax.ShapeDtypeStruct((256, 2 * LANES), F32),
        ],
        in_specs=[full(a.shape) for a in tables] + [full((256, width))],
        out_specs=[full((256, n * LANES)), full((32, n * LANES)), full((256, 2 * LANES))],
        scratch_shapes=[pltpu.VMEM((256, n * LANES), BF), pltpu.VMEM((256, n * LANES), BF)],
        compiler_params=pltpu.CompilerParams(vmem_limit_bytes=16 << 20),
        cost_estimate=pl.CostEstimate(
            flops=10**9, bytes_accessed=1 << 20, transcendentals=0
        ),
        name="early",
    )(*tables, coadd)


def late_kernel(first, nt, n, vis_ref, mass, *refs):
    tables, group, (above, below, left, rim) = refs[:6], refs[6:10], refs[10:14]
    coadd_out, out, coadd, y_hi, y_lo, det, sides, sems = refs[16:]
    weight = mass[...]
    last = first + nt
    start = last - n - 1
    copies = []

    def send(src, dst):
        copy = pltpu.make_async_copy(src, dst, sems.at[len(copies)])
        copy.start()
        copies.append(copy)

    def block(i, _):
        inverse = inverse_weight(weight, i)
        for d in range(4):
            lanes = pl.ds(pl.multiple_of(((vis_ref[0] - d) & 3) * LANES, LANES), LANES)
            for h in range(2):
                rows = pl.ds(pl.multiple_of(i * 16 + 8 * h, 8), 8)
                coadd[rows, lanes] = group[d][i * 2 + h] * inverse
        return 0

    lax.fori_loop(0, 16, block, 0, unroll=4)
    send(coadd, coadd_out.at[:, first * LANES : last * LANES])

    def tile(t, rows):
        real = start + t
        if real >= last:
            return jnp.zeros((64, LANES), F32)
        if real < first:
            return left[rows, t * LANES : (t + 1) * LANES]
        return coadd[rows, (real - first) * LANES : (real - first + 1) * LANES]

    whole_left = slice(0, (start + 1) * LANES)

    def between():
        strips = [jnp.zeros((32, LANES), F32)]
        for t in range(last):
            lanes = slice(t * LANES, (t + 1) * LANES)
            strips.append(jnp.concatenate([above[:, lanes], below[:, lanes]], axis=0))
        hi, lo = filtered(strips + strips[:1], tables[0], tables[1])
        side = lambda v: jnp.concatenate([v[32 * j : 32 * j + 32] for j in range(last)], axis=1)
        sides[...] = mm3(tables[4][...], tables[5][...], side(hi), side(lo))
        sides[:, whole_left] += rim[...]

    def done(j0, lanes):
        there = slice((start + 1) * LANES + lanes.start, (start + 1) * LANES + lanes.stop)
        det[0:16, lanes] += sides[0:16, there]
        det[240:256, lanes] += sides[16:32, there]
        send(det.at[:, lanes], out.at[:, there])

    detect_tiles(n, tile, tables, y_hi, y_lo, det, done, between)
    send(sides.at[0:16, whole_left], out.at[0:16, whole_left])
    send(sides.at[16:32, whole_left], out.at[240:256, whole_left])
    for copy in copies:
        copy.wait()


def late_detect(vis, mass, group, first, nt, n, above, below, tables, left, coadd, before):
    detection, rim = before
    any_spec = pl.BlockSpec(memory_space=pl.ANY)
    vmem = pl.BlockSpec(memory_space=pltpu.VMEM)
    args = [vis, mass, *tables, *group, above, below, left, rim, coadd, detection]
    return pl.pallas_call(
        functools.partial(late_kernel, first, nt, n),
        out_shape=[jax.ShapeDtypeStruct(coadd.shape, F32)] * 2,
        in_specs=[pl.BlockSpec(memory_space=pltpu.SMEM)]
        + [vmem] * (len(args) - 3)
        + [any_spec] * 2,
        out_specs=[any_spec] * 2,
        scratch_shapes=[
            pltpu.VMEM((256, nt * LANES), F32),
            pltpu.VMEM((256, n * LANES), BF),
            pltpu.VMEM((256, n * LANES), BF),
            pltpu.VMEM((256, n * LANES), F32),
            pltpu.VMEM((32, (first + nt) * LANES), F32),
            pltpu.SemaphoreType.DMA((3 + (n + 1) // 2,)),
        ],
        input_output_aliases={len(args) - 2: 0, len(args) - 1: 1},
        compiler_params=pltpu.CompilerParams(vmem_limit_bytes=12 << 20),
        cost_estimate=pl.CostEstimate(
            flops=2 * 10**9, bytes_accessed=4 << 20, transcendentals=0
        ),
        name="late",
    )(*args)


def detect_tables():
    dhi, dlo = halves(detect_taps(window_lags(128)))
    idx = np.arange(256, dtype=np.float64)
    bhi, blo = halves(detect_taps(idx[None, :] - idx[:, None]))
    q = np.arange(16, dtype=np.float64)
    edge = np.zeros((32, 32))
    edge[0:16, 0:16] = detect_taps((q[None, :] - 16) - q[:, None])
    edge[16:32, 16:32] = detect_taps((q[None, :] + 16) - q[:, None])
    ehi, elo = halves(edge)
    return dhi, dlo, bhi, blo, ehi, elo


def shards(pieces, coeffs, weights, routes, offsets):
    count, rows, width = pieces.shape
    pieces2d = pieces.reshape(count * rows, width)
    route1 = routes.reshape(count)
    coeffs_t = jnp.transpose(coeffs, (1, 2, 0))
    whi, wlo = column_weights()
    tables = (jnp.asarray(row_tables()), jnp.asarray(whi), jnp.asarray(wlo))
    dtables = tuple(jnp.asarray(a) for a in detect_tables())
    vis = lax.axis_index("vis").reshape(1)
    nv = lax.axis_size("vis")
    n = lax.axis_size("tile") * nv
    shifts = [[(i, (i + d) % nv) for i in range(nv)] for d in (1, 2, 3)]
    axes = ("tile", "vis")

    first, nt = CHUNKS
    per = 2 * first
    wat = 16 * per

    def over_vis(group):
        moved = [group[0]]
        for d in (0, 2, 1):
            moved.append(lax.ppermute(group[d + 1], "vis", shifts[d]))
        return [moved[0], moved[1], moved[3], moved[2]]

    def over_tile(slots):
        return lax.all_to_all(slots, "tile", split_axis=0, concat_axis=0, tiled=True)

    slots = match_slots((route1, offsets, weights, coeffs_t), tables, pieces2d, first)
    recv = over_tile(slots)
    meta = recv[:, 4 * first, 0:2, 0:2]
    landed = land_call(
        functools.partial(land_kernel, first), vis, meta, recv, [16 * per + 1] * 4,
        [
            pltpu.VMEM((64, per, 8, LANES), F32),
            pltpu.VMEM((8, LANES), F32),
            pltpu.SMEM((64,), jnp.int32),
        ],
    )
    blocks = jnp.pad(meta[:, :, 0].T, ((0, 6), (0, LANES - count)))
    told = over_vis([blocks] * nv)
    spot = jnp.stack([x[0:2, 0:count] for x in told]).astype(jnp.int32)
    spot = jnp.transpose(spot, (0, 2, 1))
    start = over_vis(landed)

    facts = jnp.stack([route1.astype(F32), offsets.astype(F32)])
    facts = jnp.pad(facts, ((0, 6), (0, LANES - count)))
    spread = match_call(
        spread_kernel, (vis, weights, coeffs_t), tables, pieces2d, (facts,), first, nt,
        [(2 * count + 1, 8, LANES)] * 4, [],
    )
    traded = over_vis(spread)
    notes = jnp.stack([x[2 * count, 0:2, 0:count] for x in traded])
    slots = pack(notes, traded)
    recv = over_tile(slots)
    landed = land_right(vis, spot, recv)
    bulk = over_vis(landed)

    coadd, top, bottom, mass = first_coadd(start, wat, first)
    edges = join_edges(vis, mass, bulk, first, top, bottom)
    above = lax.ppermute(edges[1], axes, [(i, i + 1) for i in range(n - 1)])
    below = lax.ppermute(edges[0], axes, [(i + 1, i) for i in range(n - 1)])
    *before, left = early_detect(first - 1, coadd, dtables)
    coadd, detection = late_detect(
        vis, mass, bulk, first, nt, nt + 1, above, below, dtables, left, coadd, before
    )
    return (coadd, detection)


def solution(mesh):
    placed = (
        P(("tile", "vis"), None, None),
        P(("tile", "vis"), None, None),
        P(("tile", "vis")),
        P(("tile", "vis"), None),
        P(("tile", "vis")),
    )
    return jax.shard_map(
        shards,
        mesh=mesh,
        in_specs=placed,
        out_specs=(P(("tile", "vis"), None), P(("tile", "vis"), None)),
        check_vma=False,
    )
```

```python
import functools
import math

import jax
import jax.numpy as jnp
import numpy as np
from jax import lax
from jax.experimental import pallas as pl
from jax.experimental.pallas import tpu as pltpu
from jax.sharding import PartitionSpec as P


TAPS = 10
REACH = 15
ROW_SHAPES = ((1.0, 0), (1.0, 1), (2.0, 0), (2.0, 2), (3.5, 0))
COLUMN_SHAPES = ((1.0, 0), (2.0, 0), (2.0, 1), (3.5, 0))
LANES = 128
SPAN = 18
CHUNKS = (4, 4)
BF = jnp.bfloat16
F32 = jnp.float32


def basis_taps(lags, shapes):
    spots = np.arange(-TAPS, TAPS + 1, dtype=np.float64)
    out = []
    for s, d in shapes:
        full = np.exp(-spots * spots / (2 * s * s)) * (spots / s) ** d
        scale = 1.0 / math.sqrt(np.sum(full * full))
        vals = np.exp(-lags * lags / (2 * s * s)) * (lags / s) ** d * scale
        out.append(np.where(np.abs(lags) <= TAPS, vals, 0.0))
    return np.stack(out)


def detect_taps(lags):
    spots = np.arange(-REACH, REACH + 1, dtype=np.float64)
    total = np.sum(np.exp(-spots * spots / 18.0))
    vals = np.exp(-lags * lags / 18.0) / total - 1.0 / (2 * REACH + 1)
    return np.where(np.abs(lags) <= REACH, vals, 0.0)


def halves(a):
    a = np.asarray(a, np.float32)
    hi = a.astype(jnp.bfloat16)
    lo = (a - hi.astype(np.float32)).astype(jnp.bfloat16)
    return hi, lo


def window_lags(n):
    k = np.arange(256, dtype=np.float64)[:, None] - 64
    return k - np.arange(n, dtype=np.float64)[None, :]


def column_weights():
    bank = basis_taps(window_lags(128), COLUMN_SHAPES)
    nt = np.stack(
        [np.concatenate([bank[0], bank[1]], 1), np.concatenate([bank[2], bank[3]], 1)]
    )
    return halves(nt)


def row_tables():
    lags = (np.arange(16)[None, :] - np.arange(16)[:, None]).astype(np.float64)
    bank = basis_taps(lags, ROW_SHAPES)
    return np.tile(bank, (1, 1, 16)).astype(np.float32)


def split(x):
    hi = x.astype(BF)
    lo = (x - hi.astype(F32)).astype(BF)
    return hi, lo


def mm(a, b):
    return jnp.dot(a, b, preferred_element_type=F32)


def mm3(ah, al, bh, bl):
    return mm(ah, bh) + (mm(al, bh) + mm(ah, bl))


def match_groups(
    at_start, at_end, nt, weights, coeffs, gt, whi, wlo, left, main, right,
    xs_hi, xs_lo, window_at, put,
):
    def group(g, _):
        rows = pl.ds(pl.multiple_of(g * 64, 64), 64)
        lane = lax.broadcasted_iota(jnp.int32, (64, LANES), 1)
        blank = jnp.zeros((64, LANES), F32)
        parts = [blank if at_start else left[rows, :]]
        parts += [main[rows, t * LANES : (t + 1) * LANES] for t in range(nt)]
        parts += [blank if at_end else right[rows, :]]
        turned = [pltpu.roll(x, 64, 1) for x in parts]
        for t in range(nt + 1):
            v = jnp.where(lane < 64, turned[t], turned[t + 1])
            hi, lo = split(v)
            xs_hi[:, t * LANES : (t + 1) * LANES] = hi
            xs_lo[:, t * LANES : (t + 1) * LANES] = lo
        stack = lambda ref: jnp.concatenate(
            [ref[:, pl.ds(window_at(w), 256)] for w in range(nt)], axis=0
        )
        x_hi, x_lo = stack(xs_hi), stack(xs_lo)

        lane = lax.broadcasted_iota(jnp.int32, (16, LANES), 1)
        left_hi, left_lo = [], []
        for i in range(4):
            p = g * 4 + i
            w = weights[p]
            pair = []
            for h in range(2):
                acc = None
                for a in range(5):
                    both = jnp.where(lane < 64, coeffs[a, 2 * h, p], coeffs[a, 2 * h + 1, p])
                    term = both * gt[a, :, h * LANES : (h + 1) * LANES]
                    acc = term if acc is None else acc + term
                acc = jnp.where((lane // 16) % 4 == i, acc * w, 0.0)
                pair.append(split(acc))
            left_hi.append(jnp.concatenate([pair[0][0], pair[1][0]], axis=1))
            left_lo.append(jnp.concatenate([pair[0][1], pair[1][1]], axis=1))
        l_hi = jnp.concatenate(left_hi, axis=0)
        l_both = jnp.concatenate(left_hi + left_lo, axis=0)

        cols = []
        for bp in range(2):
            y = mm3(x_hi, x_lo, whi[bp], wlo[bp])
            cols.append(split(y))

        for j0 in range(0, nt, 2):
            windows = range(j0, min(j0 + 2, nt))

            def operand(k):
                blocks = []
                for b in range(4):
                    src = cols[b // 2][k]
                    lanes = slice((b % 2) * LANES, (b % 2 + 1) * LANES)
                    pair = [src[64 * w : 64 * w + 64, lanes] for w in windows]
                    blocks.append(pair[0] if len(pair) == 1 else jnp.concatenate(pair, axis=1))
                return jnp.concatenate(blocks, axis=0)

            zz = mm(l_both, operand(0))
            z = zz[0:64] + (zz[64:128] + mm(l_hi, operand(1)))
            for i in range(4):
                for h in range(2):
                    for w in windows:
                        rows = slice(16 * i + 8 * h, 16 * i + 8 * h + 8)
                        lanes = slice((w - j0) * LANES, (w - j0 + 1) * LANES)
                        put(g * 4 + i, w, h, z[rows, lanes])
        return 0

    lax.fori_loop(0, 8, group, 0)


def slot_kernel(
    nt,
    routes, offsets, weights, coeffs,
    gt_any, whi_any, wlo_any, pieces,
    out,
    xs_hi, xs_lo, gt, whi, wlo, main, cnt, dst, rnk, sems,
):
    tiles = out.shape[1]
    moves = [
        (pieces.at[:, 0 : (nt + 1) * LANES], main),
        (whi_any, whi),
        (wlo_any, wlo),
        (gt_any, gt),
    ]
    fetches = [pltpu.make_async_copy(a, b, sems.at[i]) for i, (a, b) in enumerate(moves)]
    for fetch in fetches:
        fetch.start()

    def clear(i, _):
        cnt[i] = 0
        return 0

    lax.fori_loop(0, 32, clear, 0, unroll=8)

    def place(p, _):
        s = routes[p]
        r = cnt[s]
        cnt[s] = r + 1
        dst[p] = s
        rnk[p] = r
        return 0

    lax.fori_loop(0, 32, place, 0, unroll=4)
    zero = jnp.zeros((8, LANES), F32)

    def wipe(d, _):
        for t in range(tiles):
            out[d, t] = zero
        return 0

    lax.fori_loop(0, 32, wipe, 0, unroll=2)

    def put(p, w, h, value):
        out[dst[p], rnk[p] * 2 + (4 * w + h)] = value

    for fetch in fetches:
        fetch.wait()
    match_groups(
        True, False, nt, weights, coeffs, gt, whi, wlo,
        None, main, main.at[:, nt * LANES : (nt + 1) * LANES],
        xs_hi, xs_lo, lambda w: w * LANES, put,
    )
    lane = lax.broadcasted_iota(jnp.int32, (1, LANES), 1)

    def note(p, _):
        k = offsets[p].astype(F32)
        row = jnp.where(lane == 0, k, weights[p])
        out[dst[p], tiles - 1, pl.ds(rnk[p], 1), :] = row
        return 0

    lax.fori_loop(0, 32, note, 0, unroll=4)


def spread_kernel(
    at_start, at_end, nt,
    vis, weights, coeffs,
    gt, whi, wlo, left, main, right, meta,
    *refs,
):
    outs, (xs_hi, xs_lo) = refs[:4], refs[4:]
    me = vis[0]

    def put(p, w, h, value):
        outs[w][p * 2 + h] = value

    match_groups(
        at_start, at_end, nt, weights, coeffs, gt, whi, wlo, left, main, right,
        xs_hi, xs_lo, lambda w: pl.multiple_of(((me + w) & 3) * LANES, LANES), put,
    )
    for out in outs:
        out[64] = meta[...]


def full(shape):
    return pl.BlockSpec(shape, lambda i: (0,) * len(shape))


def match_call(kernel, scalars, tables, pieces2d, extra, first, nt, out_shapes, scratch):
    gt, whi, wlo = tables
    width = nt * LANES
    smem = pl.BlockSpec(memory_space=pltpu.SMEM)
    return pl.pallas_call(
        functools.partial(kernel, first == 0, first + nt == 8, nt),
        grid=(1,),
        out_shape=[jax.ShapeDtypeStruct(s, F32) for s in out_shapes],
        in_specs=[smem] * len(scalars)
        + [
            full(gt.shape), full(whi.shape), full(wlo.shape),
            pl.BlockSpec((512, LANES), lambda i: (0, max(first - 1, 0))),
            pl.BlockSpec((512, width), lambda i: (0, first // nt)),
            pl.BlockSpec((512, LANES), lambda i: (0, min(first + nt, 7))),
        ]
        + [full(x.shape) for x in extra],
        out_specs=[full(s) for s in out_shapes],
        scratch_shapes=[
            pltpu.VMEM((64, width + LANES), BF),
            pltpu.VMEM((64, width + LANES), BF),
            *scratch,
        ],
        compiler_params=pltpu.CompilerParams(
            vmem_limit_bytes=(60 << 20) if first == 0 else (24 << 20)
        ),
        cost_estimate=pl.CostEstimate(
            flops=10**9 * nt, bytes_accessed=(1 << 19) * nt, transcendentals=0
        ),
        name="match",
    )(*scalars, gt, whi, wlo, pieces2d, pieces2d, pieces2d, *extra)


def match_slots(scalars, tables, pieces2d, nt):
    smem = pl.BlockSpec(memory_space=pltpu.SMEM)
    any_spec = pl.BlockSpec(memory_space=pl.ANY)
    shape = (32, 4 * nt + 1, 8, LANES)
    width = (nt + 1) * LANES
    return pl.pallas_call(
        functools.partial(slot_kernel, nt),
        grid=(1,),
        out_shape=jax.ShapeDtypeStruct(shape, F32),
        in_specs=[smem] * 4 + [any_spec] * 4,
        out_specs=full(shape),
        scratch_shapes=[
            pltpu.VMEM((64, width), BF),
            pltpu.VMEM((64, width), BF),
            *[pltpu.VMEM(x.shape, x.dtype) for x in tables],
            pltpu.VMEM((512, width), F32),
            *[pltpu.SMEM((32,), jnp.int32)] * 3,
            pltpu.SemaphoreType.DMA((4,)),
        ],
        compiler_params=pltpu.CompilerParams(vmem_limit_bytes=60 << 20),
        cost_estimate=pl.CostEstimate(
            flops=10**9 * nt, bytes_accessed=(1 << 19) * nt, transcendentals=0
        ),
        name="match",
    )(*scalars, *tables, pieces2d)


def pack_kernel(meta, *refs):
    groups, (out, cnt) = refs[:4], refs[4:]
    zero = jnp.zeros((8, LANES), F32)

    def wipe(d, _):
        for t in range(16):
            out[d, t] = zero
        for v in range(4):
            cnt[v * 32 + d] = 0
        return 0

    lax.fori_loop(0, 32, wipe, 0, unroll=2)
    for v in range(4):
        def place(p, _, v=v):
            s = meta[v, 0, p].astype(jnp.int32)
            r = cnt[v * 32 + s]
            cnt[v * 32 + s] = r + 1
            j = 2 * v + r
            for h in range(2):
                out[s, 2 * j + h] = groups[v][p * 2 + h]
            return 0

        lax.fori_loop(0, 32, place, 0, unroll=4)


def pack(meta, groups):
    shape = (32, 16, 8, LANES)
    return pl.pallas_call(
        pack_kernel,
        grid=(1,),
        out_shape=jax.ShapeDtypeStruct(shape, F32),
        in_specs=[pl.BlockSpec(memory_space=pltpu.SMEM)] + [full(x.shape) for x in groups],
        out_specs=full(shape),
        scratch_shapes=[pltpu.SMEM((128,), jnp.int32)],
        compiler_params=pltpu.CompilerParams(vmem_limit_bytes=24 << 20),
        cost_estimate=pl.CostEstimate(flops=10**6, bytes_accessed=4 << 20, transcendentals=0),
        name="pack",
    )(meta, *groups)


def land_kernel(nt, vis_ref, meta, recv, *refs):
    outs, (acc, wsum, spot) = refs[:-3], refs[-3:]
    per = 2 * nt
    zero = jnp.zeros((8, LANES), F32)

    def wipe(i, _):
        for t in range(per):
            acc[i, t] = zero
        return 0

    lax.fori_loop(0, 66, wipe, 0, unroll=3)
    lane = lax.broadcasted_iota(jnp.int32, (8, LANES), 1)
    wsum[...] = zero

    def address(s, _):
        for r in range(2):
            spot[2 * s + r] = meta[s, r, 0].astype(jnp.int32) + 1
        return 0

    lax.fori_loop(0, 32, address, 0, unroll=4)

    def land(s, _):
        for r in range(2):
            at = spot[2 * s + r]
            got = [recv[s, (t // 2) * 4 + 2 * r + t % 2] for t in range(per)]
            for t in range(per):
                acc[at, t] += got[t]
            wsum[...] += jnp.where(lane == at, meta[s, r, 1], 0.0)
        return 0

    lax.fori_loop(0, 32, land, 0, unroll=4)
    for rel in range(4):
        base = ((vis_ref[0] + rel) & 3) * 16

        def one(i, _, rel=rel, base=base):
            for t in range(per):
                outs[rel][(t // 2) * (2 * SPAN) + i * 2 + t % 2] = acc[base + i, t]
            return 0

        lax.fori_loop(0, SPAN, one, 0, unroll=3)
        outs[rel][SPAN * per] = pltpu.roll(wsum[...], (LANES - base) & (LANES - 1), 1)


def full_kernel(vis_ref, spot, recv, *refs):
    outs, acc = refs[:-1], refs[-1]
    zero = jnp.zeros((8, LANES), F32)

    def wipe(i, _):
        acc[i, 0] = zero
        acc[i, 1] = zero
        return 0

    lax.fori_loop(0, 66, wipe, 0, unroll=6)

    def land(s, _):
        for j in range(8):
            at = spot[j // 2, s, j % 2] + 1
            got = [recv[s, 2 * j + h] for h in range(2)]
            for h in range(2):
                acc[at, h] += got[h]
        return 0

    lax.fori_loop(0, 32, land, 0, unroll=4)
    for rel in range(4):
        base = ((vis_ref[0] + rel) & 3) * 16

        def one(i, _, rel=rel, base=base):
            for h in range(2):
                outs[rel][i * 2 + h] = acc[base + i, h]
            return 0

        lax.fori_loop(0, SPAN, one, 0, unroll=9)


def land_right(vis, spot, recv):
    smem = pl.BlockSpec(memory_space=pltpu.SMEM)
    vmem = pl.BlockSpec(memory_space=pltpu.VMEM)
    return pl.pallas_call(
        full_kernel,
        out_shape=[jax.ShapeDtypeStruct((2 * SPAN, 8, LANES), F32)] * 4,
        in_specs=[smem, smem, vmem],
        out_specs=[vmem] * 4,
        scratch_shapes=[pltpu.VMEM((66, 2, 8, LANES), F32)],
        compiler_params=pltpu.CompilerParams(vmem_limit_bytes=8 << 20),
        cost_estimate=pl.CostEstimate(flops=10**6, bytes_accessed=4 << 20, transcendentals=0),
        name="land",
    )(vis, spot, recv)


def land_call(kernel, vis, meta, recv, counts, scratch):
    shapes = [(k, 8, LANES) for k in counts]
    smem = pl.BlockSpec(memory_space=pltpu.SMEM)
    return pl.pallas_call(
        kernel,
        grid=(1,),
        out_shape=[jax.ShapeDtypeStruct(s, F32) for s in shapes],
        in_specs=[smem, smem, full(recv.shape)],
        out_specs=[full(s) for s in shapes],
        scratch_shapes=scratch,
        compiler_params=pltpu.CompilerParams(vmem_limit_bytes=24 << 20),
        cost_estimate=pl.CostEstimate(flops=10**6, bytes_accessed=4 << 20, transcendentals=0),
        name="land",
    )(vis, meta, recv)


def inverse_weight(weight, kk):
    lane = lax.broadcasted_iota(jnp.int32, (8, LANES), 1)
    total = jnp.sum(jnp.where(lane == kk, weight, 0.0), axis=1, keepdims=True)
    good = total > 0.0
    return jnp.where(good, 1.0 / jnp.where(good, total, 1.0), 0.0)


def summed(group, t):
    own, a, b, c = group
    return (own[t] + b[t]) + (a[t] + c[t])


def coadd_kernel(nt, *refs):
    group, wrefs = refs[:4], refs[4:8]
    coadd, mass, *edges = refs[8:]
    weight = (wrefs[0][0] + wrefs[2][0]) + (wrefs[1][0] + wrefs[3][0])
    mass[...] = weight

    def block(kk, _):
        inverse = inverse_weight(weight, kk + 1)
        for ct in range(nt):
            for h in range(2):
                rows = pl.ds(pl.multiple_of(kk * 16 + 8 * h, 8), 8)
                v = summed(group, ct * (2 * SPAN) + (kk + 1) * 2 + h) * inverse
                coadd[rows, ct * LANES : (ct + 1) * LANES] = v
        return 0

    lax.fori_loop(0, 16, block, 0, unroll=2)
    edges[0][...] = coadd[0:16, :]
    edges[1][...] = coadd[240:256, :]
    for e in range(2):
        at = (SPAN - 1) * e
        inverse = inverse_weight(weight, at)
        for ct in range(nt):
            for h in range(2):
                v = summed(group, ct * (2 * SPAN) + at * 2 + h) * inverse
                edges[2 + e][8 * h : 8 * h + 8, ct * LANES : (ct + 1) * LANES] = v


def weight_specs(wat):
    return [pl.BlockSpec((1, 8, LANES), lambda i: (wat, 0, 0))] * 4


def first_coadd(group, wat, nt):
    shapes = [(256, 1024), (8, LANES)] + [(16, LANES * nt)] * 4
    blocks = [(256, LANES * nt)] + shapes[1:]
    return pl.pallas_call(
        functools.partial(coadd_kernel, nt),
        grid=(1,),
        out_shape=[jax.ShapeDtypeStruct(s, F32) for s in shapes],
        in_specs=[full((2 * SPAN * nt, 8, LANES))] * 4 + weight_specs(wat),
        out_specs=[full(s) for s in blocks],
        compiler_params=pltpu.CompilerParams(vmem_limit_bytes=16 << 20),
        cost_estimate=pl.CostEstimate(
            flops=10**6, bytes_accessed=(5 << 17) * nt, transcendentals=0
        ),
        name="coadd",
    )(*group, *group)


def join_kernel(first, vis_ref, mass, *refs):
    group, olds, outs = refs[:4], refs[4:6], refs[6:]
    for e in range(2):
        inverse = inverse_weight(mass[...], 1 + 15 * e)
        outs[e][:, : first * LANES] = olds[e][...]
        for d in range(4):
            tile = first + ((vis_ref[0] - d) & 3)
            lanes = pl.ds(pl.multiple_of(tile * LANES, LANES), LANES)
            for h in range(2):
                outs[e][8 * h : 8 * h + 8, lanes] = group[d][2 + 30 * e + h] * inverse


def join_edges(vis, mass, group, first, top, bottom):
    vmem = pl.BlockSpec(memory_space=pltpu.VMEM)
    return pl.pallas_call(
        functools.partial(join_kernel, first),
        out_shape=[jax.ShapeDtypeStruct((16, 1024), F32)] * 2,
        in_specs=[pl.BlockSpec(memory_space=pltpu.SMEM)] + [vmem] * 7,
        out_specs=[vmem] * 2,
        compiler_params=pltpu.CompilerParams(vmem_limit_bytes=4 << 20),
        cost_estimate=pl.CostEstimate(flops=10**5, bytes_accessed=1 << 19, transcendentals=0),
        name="join",
    )(vis, mass, *group, top, bottom)


def filtered(parts, dhi, dlo):
    rows = parts[0].shape[0]
    lane = lax.broadcasted_iota(jnp.int32, (rows, LANES), 1)
    turned = [pltpu.roll(x, 64, 1) for x in parts]
    cut = [
        split(jnp.where(lane < 64, turned[t], turned[t + 1])) for t in range(len(parts) - 1)
    ]
    window = lambda k: jnp.concatenate(
        [
            jnp.concatenate([cut[j][k], cut[j + 1][k]], axis=1)
            for j in range(len(parts) - 2)
        ],
        axis=0,
    )
    return split(mm3(window(0), window(1), dhi[...], dlo[...]))


def detect_tiles(n, tile, tables, y_hi, y_lo, out, done, between):
    dhi, dlo, bhi, blo = tables[:4]

    def group(g, _):
        rows = pl.ds(pl.multiple_of(g * 64, 64), 64)
        hi, lo = filtered([tile(t, rows) for t in range(n + 2)], dhi, dlo)
        for j in range(n):
            y_hi[rows, j * LANES : (j + 1) * LANES] = hi[64 * j : 64 * j + 64]
            y_lo[rows, j * LANES : (j + 1) * LANES] = lo[64 * j : 64 * j + 64]
        return 0

    lax.fori_loop(0, 4, group, 0, unroll=2)
    between()
    for j0 in range(0, n, 2):
        lanes = slice(j0 * LANES, min(j0 + 2, n) * LANES)
        out[:, lanes] = mm3(bhi[...], blo[...], y_hi[:, lanes], y_lo[:, lanes])
        done(j0, lanes)


def early_kernel(n, *refs):
    tables, (x, out, rim, context, y_hi, y_lo) = refs[:4], refs[4:]
    context[...] = x[:, (n - 1) * LANES : (n + 1) * LANES]

    def tile(t, rows):
        if t == 0:
            return jnp.zeros((64, LANES), F32)
        return x[rows, (t - 1) * LANES : t * LANES]

    detect_tiles(n, tile, tables, y_hi, y_lo, out, lambda *_: None, lambda: None)
    rim[0:16, :] = out[0:16, :]
    rim[16:32, :] = out[240:256, :]


def early_detect(n, coadd, tables):
    tables = tables[:4]
    width = (n + 1) * LANES
    return pl.pallas_call(
        functools.partial(early_kernel, n),
        grid=(1,),
        out_shape=[
            jax.ShapeDtypeStruct(coadd.shape, F32),
            jax.ShapeDtypeStruct((32, n * LANES), F32),
            jax.ShapeDtypeStruct((256, 2 * LANES), F32),
        ],
        in_specs=[full(a.shape) for a in tables] + [full((256, width))],
        out_specs=[full((256, n * LANES)), full((32, n * LANES)), full((256, 2 * LANES))],
        scratch_shapes=[pltpu.VMEM((256, n * LANES), BF), pltpu.VMEM((256, n * LANES), BF)],
        compiler_params=pltpu.CompilerParams(vmem_limit_bytes=16 << 20),
        cost_estimate=pl.CostEstimate(
            flops=10**9, bytes_accessed=1 << 20, transcendentals=0
        ),
        name="early",
    )(*tables, coadd)


def late_kernel(first, nt, n, vis_ref, mass, *refs):
    tables, group, (above, below, before, after, left, rim) = refs[:6], refs[6:10], refs[10:16]
    coadd_out, out, coadd, y_hi, y_lo, det, sides, near, sems = refs[18:]
    weight = mass[...]
    last = first + nt
    start = last - n - 1
    copies = []

    def send(src, dst):
        copy = pltpu.make_async_copy(src, dst, sems.at[len(copies)])
        copy.start()
        copies.append(copy)

    def block(i, _):
        inverse = inverse_weight(weight, i + 1)
        for d in range(4):
            lanes = pl.ds(pl.multiple_of(((vis_ref[0] - d) & 3) * LANES, LANES), LANES)
            for h in range(2):
                rows = pl.ds(pl.multiple_of(i * 16 + 8 * h, 8), 8)
                coadd[rows, lanes] = group[d][i * 2 + (2 + h)] * inverse
        return 0

    lax.fori_loop(0, 16, block, 0, unroll=4)
    send(coadd, coadd_out.at[:, first * LANES : last * LANES])

    def tile(t, rows):
        real = start + t
        if real >= last:
            return jnp.zeros((64, LANES), F32)
        if real < first:
            return left[rows, t * LANES : (t + 1) * LANES]
        return coadd[rows, (real - first) * LANES : (real - first + 1) * LANES]

    whole_left = slice(0, (start + 1) * LANES)

    def between():
        for e in range(2):
            inverse = inverse_weight(weight, (SPAN - 1) * e)
            for d in range(4):
                lanes = pl.ds(pl.multiple_of(((vis_ref[0] - d) & 3) * LANES, LANES), LANES)
                for h in range(2):
                    rows = slice(16 * e + 8 * h, 16 * e + 8 * h + 8)
                    near[rows, lanes] = group[d][2 * (SPAN - 1) * e + h] * inverse
        strips = [jnp.zeros((32, LANES), F32)]
        for t in range(last):
            lanes = slice(t * LANES, (t + 1) * LANES)
            far = jnp.concatenate([above[:, lanes], below[:, lanes]], axis=0)
            if t < first:
                own = jnp.concatenate([before[:, lanes], after[:, lanes]], axis=0)
            else:
                own = near[:, (t - first) * LANES : (t - first + 1) * LANES]
            strips.append(far + own)
        hi, lo = filtered(strips + strips[:1], tables[0], tables[1])
        side = lambda v: jnp.concatenate([v[32 * j : 32 * j + 32] for j in range(last)], axis=1)
        sides[...] = mm3(tables[4][...], tables[5][...], side(hi), side(lo))
        sides[:, whole_left] += rim[...]

    def done(j0, lanes):
        there = slice((start + 1) * LANES + lanes.start, (start + 1) * LANES + lanes.stop)
        det[0:16, lanes] += sides[0:16, there]
        det[240:256, lanes] += sides[16:32, there]
        send(det.at[:, lanes], out.at[:, there])

    detect_tiles(n, tile, tables, y_hi, y_lo, det, done, between)
    send(sides.at[0:16, whole_left], out.at[0:16, whole_left])
    send(sides.at[16:32, whole_left], out.at[240:256, whole_left])
    for copy in copies:
        copy.wait()


def late_detect(vis, mass, group, first, nt, n, halos, tables, left, coadd, before):
    detection, rim = before
    any_spec = pl.BlockSpec(memory_space=pl.ANY)
    vmem = pl.BlockSpec(memory_space=pltpu.VMEM)
    args = [vis, mass, *tables, *group, *halos, left, rim, coadd, detection]
    return pl.pallas_call(
        functools.partial(late_kernel, first, nt, n),
        out_shape=[jax.ShapeDtypeStruct(coadd.shape, F32)] * 2,
        in_specs=[pl.BlockSpec(memory_space=pltpu.SMEM)]
        + [vmem] * (len(args) - 3)
        + [any_spec] * 2,
        out_specs=[any_spec] * 2,
        scratch_shapes=[
            pltpu.VMEM((256, nt * LANES), F32),
            pltpu.VMEM((256, n * LANES), BF),
            pltpu.VMEM((256, n * LANES), BF),
            pltpu.VMEM((256, n * LANES), F32),
            pltpu.VMEM((32, (first + nt) * LANES), F32),
            pltpu.VMEM((32, nt * LANES), F32),
            pltpu.SemaphoreType.DMA((3 + (n + 1) // 2,)),
        ],
        input_output_aliases={len(args) - 2: 0, len(args) - 1: 1},
        compiler_params=pltpu.CompilerParams(vmem_limit_bytes=12 << 20),
        cost_estimate=pl.CostEstimate(
            flops=2 * 10**9, bytes_accessed=4 << 20, transcendentals=0
        ),
        name="late",
    )(*args)


def detect_tables():
    dhi, dlo = halves(detect_taps(window_lags(128)))
    idx = np.arange(256, dtype=np.float64)
    bhi, blo = halves(detect_taps(idx[None, :] - idx[:, None]))
    q = np.arange(16, dtype=np.float64)
    edge = np.zeros((32, 32))
    edge[0:16, 0:16] = detect_taps((q[None, :] - 16) - q[:, None])
    edge[16:32, 16:32] = detect_taps((q[None, :] + 16) - q[:, None])
    ehi, elo = halves(edge)
    return dhi, dlo, bhi, blo, ehi, elo


def shards(pieces, coeffs, weights, routes, offsets):
    count, rows, width = pieces.shape
    pieces2d = pieces.reshape(count * rows, width)
    route1 = routes.reshape(count)
    coeffs_t = jnp.transpose(coeffs, (1, 2, 0))
    whi, wlo = column_weights()
    tables = (jnp.asarray(row_tables()), jnp.asarray(whi), jnp.asarray(wlo))
    dtables = tuple(jnp.asarray(a) for a in detect_tables())
    vis = lax.axis_index("vis").reshape(1)
    nv = lax.axis_size("vis")
    n = lax.axis_size("tile") * nv
    shifts = [[(i, (i + d) % nv) for i in range(nv)] for d in (1, 2, 3)]
    axes = ("tile", "vis")

    first, nt = CHUNKS
    per = 2 * first
    wat = SPAN * per

    def over_vis(group):
        moved = [group[0]]
        for d in (0, 2, 1):
            moved.append(lax.ppermute(group[d + 1], "vis", shifts[d]))
        return [moved[0], moved[1], moved[3], moved[2]]

    def over_tile(slots):
        return lax.all_to_all(slots, "tile", split_axis=0, concat_axis=0, tiled=True)

    slots = match_slots((route1, offsets, weights, coeffs_t), tables, pieces2d, first)
    recv = over_tile(slots)
    meta = recv[:, 4 * first, 0:2, 0:2]
    landed = land_call(
        functools.partial(land_kernel, first), vis, meta, recv, [SPAN * per + 1] * 4,
        [
            pltpu.VMEM((66, per, 8, LANES), F32),
            pltpu.VMEM((8, LANES), F32),
            pltpu.SMEM((64,), jnp.int32),
        ],
    )
    blocks = jnp.pad(meta[:, :, 0].T, ((0, 6), (0, LANES - count)))
    told = over_vis([blocks] * nv)
    spot = jnp.stack([x[0:2, 0:count] for x in told]).astype(jnp.int32)
    spot = jnp.transpose(spot, (0, 2, 1))
    start = over_vis(landed)

    facts = jnp.stack([route1.astype(F32), offsets.astype(F32)])
    facts = jnp.pad(facts, ((0, 6), (0, LANES - count)))
    spread = match_call(
        spread_kernel, (vis, weights, coeffs_t), tables, pieces2d, (facts,), first, nt,
        [(2 * count + 1, 8, LANES)] * 4, [],
    )
    traded = over_vis(spread)
    notes = jnp.stack([x[2 * count, 0:2, 0:count] for x in traded])
    slots = pack(notes, traded)
    recv = over_tile(slots)
    landed = land_right(vis, spot, recv)
    bulk = over_vis(landed)

    coadd, mass, top, bottom, *outside = first_coadd(start, wat, first)
    edges = join_edges(vis, mass, bulk, first, top, bottom)
    above = lax.ppermute(edges[1], axes, [(i - 1, i) for i in range(nv, n, nv)])
    below = lax.ppermute(edges[0], axes, [(i, i - 1) for i in range(nv, n, nv)])
    *before, left = early_detect(first - 1, coadd, dtables)
    coadd, detection = late_detect(
        vis, mass, bulk, first, nt, nt + 1, (above, below, *outside), dtables, left, coadd,
        before,
    )
    return (coadd, detection)


def solution(mesh):
    placed = (
        P(("tile", "vis"), None, None),
        P(("tile", "vis"), None, None),
        P(("tile", "vis")),
        P(("tile", "vis"), None),
        P(("tile", "vis")),
    )
    return jax.shard_map(
        shards,
        mesh=mesh,
        in_specs=placed,
        out_specs=(P(("tile", "vis"), None), P(("tile", "vis"), None)),
        check_vma=False,
    )
```

```python
import functools
import math

import jax
import jax.numpy as jnp
import numpy as np
from jax import lax
from jax.experimental import pallas as pl
from jax.experimental.pallas import tpu as pltpu
from jax.sharding import PartitionSpec as P


TAPS = 10
REACH = 15
ROW_SHAPES = ((1.0, 0), (1.0, 1), (2.0, 0), (2.0, 2), (3.5, 0))
COLUMN_SHAPES = ((1.0, 0), (2.0, 0), (2.0, 1), (3.5, 0))
LANES = 128
SPAN = 18
CHUNKS = (4, 4)
BF = jnp.bfloat16
F32 = jnp.float32


def basis_taps(lags, shapes):
    spots = np.arange(-TAPS, TAPS + 1, dtype=np.float64)
    out = []
    for s, d in shapes:
        full = np.exp(-spots * spots / (2 * s * s)) * (spots / s) ** d
        scale = 1.0 / math.sqrt(np.sum(full * full))
        vals = np.exp(-lags * lags / (2 * s * s)) * (lags / s) ** d * scale
        out.append(np.where(np.abs(lags) <= TAPS, vals, 0.0))
    return np.stack(out)


def detect_taps(lags):
    spots = np.arange(-REACH, REACH + 1, dtype=np.float64)
    total = np.sum(np.exp(-spots * spots / 18.0))
    vals = np.exp(-lags * lags / 18.0) / total - 1.0 / (2 * REACH + 1)
    return np.where(np.abs(lags) <= REACH, vals, 0.0)


def halves(a):
    a = np.asarray(a, np.float32)
    hi = a.astype(jnp.bfloat16)
    lo = (a - hi.astype(np.float32)).astype(jnp.bfloat16)
    return hi, lo


def window_lags(n):
    k = np.arange(256, dtype=np.float64)[:, None] - 64
    return k - np.arange(n, dtype=np.float64)[None, :]


def column_weights():
    bank = basis_taps(window_lags(128), COLUMN_SHAPES)
    nt = np.stack(
        [np.concatenate([bank[0], bank[1]], 1), np.concatenate([bank[2], bank[3]], 1)]
    )
    return halves(nt)


def row_tables():
    lags = (np.arange(16)[None, :] - np.arange(16)[:, None]).astype(np.float64)
    bank = basis_taps(lags, ROW_SHAPES)
    return np.tile(bank, (1, 1, 16)).astype(np.float32)


def split(x):
    hi = x.astype(BF)
    lo = (x - hi.astype(F32)).astype(BF)
    return hi, lo


def mm(a, b):
    return jnp.dot(a, b, preferred_element_type=F32)


def mm3(ah, al, bh, bl):
    return mm(ah, bh) + (mm(al, bh) + mm(ah, bl))


def match_groups(
    at_start, at_end, nt, weights, coeffs, gt, whi, wlo, left, main, right,
    xs_hi, xs_lo, window_at, put,
):
    def group(g, _):
        rows = pl.ds(pl.multiple_of(g * 64, 64), 64)
        lane = lax.broadcasted_iota(jnp.int32, (64, LANES), 1)
        blank = jnp.zeros((64, LANES), F32)
        parts = [blank if at_start else left[rows, :]]
        parts += [main[rows, t * LANES : (t + 1) * LANES] for t in range(nt)]
        parts += [blank if at_end else right[rows, :]]
        turned = [pltpu.roll(x, 64, 1) for x in parts]
        for t in range(nt + 1):
            v = jnp.where(lane < 64, turned[t], turned[t + 1])
            hi, lo = split(v)
            xs_hi[:, t * LANES : (t + 1) * LANES] = hi
            xs_lo[:, t * LANES : (t + 1) * LANES] = lo
        stack = lambda ref: jnp.concatenate(
            [ref[:, pl.ds(window_at(w), 256)] for w in range(nt)], axis=0
        )
        x_hi, x_lo = stack(xs_hi), stack(xs_lo)

        lane = lax.broadcasted_iota(jnp.int32, (16, LANES), 1)
        left_hi, left_lo = [], []
        for i in range(4):
            p = g * 4 + i
            w = weights[p]
            pair = []
            for h in range(2):
                acc = None
                for a in range(5):
                    both = jnp.where(lane < 64, coeffs[a, 2 * h, p], coeffs[a, 2 * h + 1, p])
                    term = both * gt[a, :, h * LANES : (h + 1) * LANES]
                    acc = term if acc is None else acc + term
                acc = jnp.where((lane // 16) % 4 == i, acc * w, 0.0)
                pair.append(split(acc))
            left_hi.append(jnp.concatenate([pair[0][0], pair[1][0]], axis=1))
            left_lo.append(jnp.concatenate([pair[0][1], pair[1][1]], axis=1))
        l_hi = jnp.concatenate(left_hi, axis=0)
        l_both = jnp.concatenate(left_hi + left_lo, axis=0)

        cols = []
        for bp in range(2):
            y = mm3(x_hi, x_lo, whi[bp], wlo[bp])
            cols.append(split(y))

        for j0 in range(0, nt, 2):
            windows = range(j0, min(j0 + 2, nt))

            def operand(k):
                blocks = []
                for b in range(4):
                    src = cols[b // 2][k]
                    lanes = slice((b % 2) * LANES, (b % 2 + 1) * LANES)
                    pair = [src[64 * w : 64 * w + 64, lanes] for w in windows]
                    blocks.append(pair[0] if len(pair) == 1 else jnp.concatenate(pair, axis=1))
                return jnp.concatenate(blocks, axis=0)

            zz = mm(l_both, operand(0))
            z = zz[0:64] + (zz[64:128] + mm(l_hi, operand(1)))
            for i in range(4):
                for h in range(2):
                    for w in windows:
                        rows = slice(16 * i + 8 * h, 16 * i + 8 * h + 8)
                        lanes = slice((w - j0) * LANES, (w - j0 + 1) * LANES)
                        put(g * 4 + i, w, h, z[rows, lanes])
        return 0

    lax.fori_loop(0, 8, group, 0)


def slot_kernel(
    nt,
    routes, offsets, weights, coeffs,
    gt_any, whi_any, wlo_any, pieces,
    out,
    xs_hi, xs_lo, gt, whi, wlo, main, cnt, dst, rnk, sems,
):
    tiles = out.shape[1]
    moves = [
        (pieces.at[:, 0 : (nt + 1) * LANES], main),
        (whi_any, whi),
        (wlo_any, wlo),
        (gt_any, gt),
    ]
    fetches = [pltpu.make_async_copy(a, b, sems.at[i]) for i, (a, b) in enumerate(moves)]
    for fetch in fetches:
        fetch.start()

    def clear(i, _):
        cnt[i] = 0
        return 0

    lax.fori_loop(0, 32, clear, 0, unroll=8)

    def place(p, _):
        s = routes[p]
        r = cnt[s]
        cnt[s] = r + 1
        dst[p] = s
        rnk[p] = r
        return 0

    lax.fori_loop(0, 32, place, 0, unroll=4)
    zero = jnp.zeros((8, LANES), F32)

    def wipe(d, _):
        for t in range(tiles):
            out[d, t] = zero
        return 0

    lax.fori_loop(0, 32, wipe, 0, unroll=2)

    def put(p, w, h, value):
        out[dst[p], rnk[p] * 2 + (4 * w + h)] = value

    for fetch in fetches:
        fetch.wait()
    match_groups(
        True, False, nt, weights, coeffs, gt, whi, wlo,
        None, main, main.at[:, nt * LANES : (nt + 1) * LANES],
        xs_hi, xs_lo, lambda w: w * LANES, put,
    )
    lane = lax.broadcasted_iota(jnp.int32, (1, LANES), 1)

    def note(p, _):
        k = offsets[p].astype(F32)
        row = jnp.where(lane == 0, k, weights[p])
        out[dst[p], tiles - 1, pl.ds(rnk[p], 1), :] = row
        return 0

    lax.fori_loop(0, 32, note, 0, unroll=4)


def spread_kernel(
    at_start, at_end, nt,
    vis, weights, coeffs,
    gt, whi, wlo, left, main, right, meta,
    *refs,
):
    outs, (xs_hi, xs_lo) = refs[:4], refs[4:]
    me = vis[0]

    def put(p, w, h, value):
        outs[w][p * 2 + h] = value

    match_groups(
        at_start, at_end, nt, weights, coeffs, gt, whi, wlo, left, main, right,
        xs_hi, xs_lo, lambda w: pl.multiple_of(((me + w) & 3) * LANES, LANES), put,
    )
    for out in outs:
        out[64] = meta[...]


def full(shape):
    return pl.BlockSpec(shape, lambda i: (0,) * len(shape))


def match_call(kernel, scalars, tables, pieces2d, extra, first, nt, out_shapes, scratch):
    gt, whi, wlo = tables
    width = nt * LANES
    smem = pl.BlockSpec(memory_space=pltpu.SMEM)
    return pl.pallas_call(
        functools.partial(kernel, first == 0, first + nt == 8, nt),
        grid=(1,),
        out_shape=[jax.ShapeDtypeStruct(s, F32) for s in out_shapes],
        in_specs=[smem] * len(scalars)
        + [
            full(gt.shape), full(whi.shape), full(wlo.shape),
            pl.BlockSpec((512, LANES), lambda i: (0, max(first - 1, 0))),
            pl.BlockSpec((512, width), lambda i: (0, first // nt)),
            pl.BlockSpec((512, LANES), lambda i: (0, min(first + nt, 7))),
        ]
        + [full(x.shape) for x in extra],
        out_specs=[full(s) for s in out_shapes],
        scratch_shapes=[
            pltpu.VMEM((64, width + LANES), BF),
            pltpu.VMEM((64, width + LANES), BF),
            *scratch,
        ],
        compiler_params=pltpu.CompilerParams(
            vmem_limit_bytes=(60 << 20) if first == 0 else (24 << 20)
        ),
        cost_estimate=pl.CostEstimate(
            flops=10**9 * nt, bytes_accessed=(1 << 19) * nt, transcendentals=0
        ),
        name="match",
    )(*scalars, gt, whi, wlo, pieces2d, pieces2d, pieces2d, *extra)


def match_slots(scalars, tables, pieces2d, nt):
    smem = pl.BlockSpec(memory_space=pltpu.SMEM)
    any_spec = pl.BlockSpec(memory_space=pl.ANY)
    shape = (32, 4 * nt + 1, 8, LANES)
    width = (nt + 1) * LANES
    return pl.pallas_call(
        functools.partial(slot_kernel, nt),
        grid=(1,),
        out_shape=jax.ShapeDtypeStruct(shape, F32),
        in_specs=[smem] * 4 + [any_spec] * 4,
        out_specs=full(shape),
        scratch_shapes=[
            pltpu.VMEM((64, width), BF),
            pltpu.VMEM((64, width), BF),
            *[pltpu.VMEM(x.shape, x.dtype) for x in tables],
            pltpu.VMEM((512, width), F32),
            *[pltpu.SMEM((32,), jnp.int32)] * 3,
            pltpu.SemaphoreType.DMA((4,)),
        ],
        compiler_params=pltpu.CompilerParams(vmem_limit_bytes=60 << 20),
        cost_estimate=pl.CostEstimate(
            flops=10**9 * nt, bytes_accessed=(1 << 19) * nt, transcendentals=0
        ),
        name="match",
    )(*scalars, *tables, pieces2d)


def pack_kernel(meta, *refs):
    groups, (out, cnt) = refs[:4], refs[4:]
    zero = jnp.zeros((8, LANES), F32)

    def wipe(d, _):
        for t in range(16):
            out[d, t] = zero
        for v in range(4):
            cnt[v * 32 + d] = 0
        return 0

    lax.fori_loop(0, 32, wipe, 0, unroll=2)
    for v in range(4):
        def place(p, _, v=v):
            s = meta[v, 0, p].astype(jnp.int32)
            r = cnt[v * 32 + s]
            cnt[v * 32 + s] = r + 1
            j = 2 * v + r
            for h in range(2):
                out[s, 2 * j + h] = groups[v][p * 2 + h]
            return 0

        lax.fori_loop(0, 32, place, 0, unroll=4)


def pack(meta, groups):
    shape = (32, 16, 8, LANES)
    return pl.pallas_call(
        pack_kernel,
        grid=(1,),
        out_shape=jax.ShapeDtypeStruct(shape, F32),
        in_specs=[pl.BlockSpec(memory_space=pltpu.SMEM)] + [full(x.shape) for x in groups],
        out_specs=full(shape),
        scratch_shapes=[pltpu.SMEM((128,), jnp.int32)],
        compiler_params=pltpu.CompilerParams(vmem_limit_bytes=24 << 20),
        cost_estimate=pl.CostEstimate(flops=10**6, bytes_accessed=4 << 20, transcendentals=0),
        name="pack",
    )(meta, *groups)


def land_kernel(nt, vis_ref, meta, recv, *refs):
    outs, (acc, wsum, spot) = refs[:-3], refs[-3:]
    per = 2 * nt
    zero = jnp.zeros((8, LANES), F32)

    def wipe(i, _):
        for t in range(per):
            acc[i, t] = zero
        return 0

    lax.fori_loop(0, 66, wipe, 0, unroll=3)
    lane = lax.broadcasted_iota(jnp.int32, (8, LANES), 1)
    wsum[...] = zero

    def address(s, _):
        for r in range(2):
            spot[2 * s + r] = meta[s, r, 0].astype(jnp.int32) + 1
        return 0

    lax.fori_loop(0, 32, address, 0, unroll=4)

    def land(s, _):
        for r in range(2):
            at = spot[2 * s + r]
            got = [recv[s, (t // 2) * 4 + 2 * r + t % 2] for t in range(per)]
            for t in range(per):
                acc[at, t] += got[t]
            wsum[...] += jnp.where(lane == at, meta[s, r, 1], 0.0)
        return 0

    lax.fori_loop(0, 32, land, 0, unroll=4)
    own, p1, m1, p2, m2 = outs
    half = SPAN * nt

    def move(ref, start, rel, first):
        base = ((vis_ref[0] + rel) & 3) * 16

        def one(i, _):
            for t in range(per // 2):
                ref[start + (t // 2) * (2 * SPAN) + i * 2 + t % 2] = acc[base + i, first + t]
            return 0

        lax.fori_loop(0, SPAN, one, 0, unroll=3)

    def mass(rel):
        base = ((vis_ref[0] + rel) & 3) * 16
        return pltpu.roll(wsum[...], (LANES - base) & (LANES - 1), 1)

    move(p1, 0, 2, 0)
    p1[half] = zero
    move(p1, half + 1, 1, per // 2)
    move(m1, 0, 2, per // 2)
    m1[half] = mass(2)
    move(m1, half + 1, 3, 0)
    move(p2, 0, 1, 0)
    p2[half] = mass(1)
    move(m2, 0, 3, per // 2)
    m2[half] = mass(3)
    move(own, 0, 0, 0)
    move(own, half, 0, per // 2)
    own[2 * half] = mass(0)


def full_kernel(vis_ref, spot, recv, *refs):
    outs, acc = refs[:-1], refs[-1]
    zero = jnp.zeros((8, LANES), F32)

    def wipe(i, _):
        acc[i, 0] = zero
        acc[i, 1] = zero
        return 0

    lax.fori_loop(0, 66, wipe, 0, unroll=6)

    def land(s, _):
        for j in range(8):
            at = spot[j // 2, s, j % 2] + 1
            got = [recv[s, 2 * j + h] for h in range(2)]
            for h in range(2):
                acc[at, h] += got[h]
        return 0

    lax.fori_loop(0, 32, land, 0, unroll=4)
    for rel in range(4):
        base = ((vis_ref[0] + rel) & 3) * 16

        def one(i, _, rel=rel, base=base):
            for h in range(2):
                outs[rel][i * 2 + h] = acc[base + i, h]
            return 0

        lax.fori_loop(0, SPAN, one, 0, unroll=9)


def land_right(vis, spot, recv):
    smem = pl.BlockSpec(memory_space=pltpu.SMEM)
    vmem = pl.BlockSpec(memory_space=pltpu.VMEM)
    return pl.pallas_call(
        full_kernel,
        out_shape=[jax.ShapeDtypeStruct((2 * SPAN, 8, LANES), F32)] * 4,
        in_specs=[smem, smem, vmem],
        out_specs=[vmem] * 4,
        scratch_shapes=[pltpu.VMEM((66, 2, 8, LANES), F32)],
        compiler_params=pltpu.CompilerParams(vmem_limit_bytes=8 << 20),
        cost_estimate=pl.CostEstimate(flops=10**6, bytes_accessed=4 << 20, transcendentals=0),
        name="land",
    )(vis, spot, recv)


def land_call(kernel, vis, meta, recv, counts, scratch):
    shapes = [(k, 8, LANES) for k in counts]
    smem = pl.BlockSpec(memory_space=pltpu.SMEM)
    return pl.pallas_call(
        kernel,
        grid=(1,),
        out_shape=[jax.ShapeDtypeStruct(s, F32) for s in shapes],
        in_specs=[smem, smem, full(recv.shape)],
        out_specs=[full(s) for s in shapes],
        scratch_shapes=scratch,
        compiler_params=pltpu.CompilerParams(vmem_limit_bytes=24 << 20),
        cost_estimate=pl.CostEstimate(flops=10**6, bytes_accessed=4 << 20, transcendentals=0),
        name="land",
    )(vis, meta, recv)


def inverse_weight(weight, kk):
    lane = lax.broadcasted_iota(jnp.int32, (8, LANES), 1)
    total = jnp.sum(jnp.where(lane == kk, weight, 0.0), axis=1, keepdims=True)
    good = total > 0.0
    return jnp.where(good, 1.0 / jnp.where(good, total, 1.0), 0.0)


def coadd_kernel(nt, own, p1, m1, p2, m2, coadd, mass, *edges):
    half = SPAN * nt
    weight = own[2 * half] + (p2[half] + m2[half])
    mass[...] = weight

    def value(ct, at, h, inverse):
        t = ct * (2 * SPAN) + at * 2 + h
        if ct < nt // 2:
            return (own[t] + (p2[t] + m1[half + 1 + t])) * inverse
        near = t - half
        return (own[t] + (p1[half + 1 + near] + m2[near])) * inverse

    def block(kk, _):
        inverse = inverse_weight(weight, kk + 1)
        for ct in range(nt):
            for h in range(2):
                rows = pl.ds(pl.multiple_of(kk * 16 + 8 * h, 8), 8)
                coadd[rows, ct * LANES : (ct + 1) * LANES] = value(ct, kk + 1, h, inverse)
        return 0

    lax.fori_loop(0, 16, block, 0, unroll=2)
    edges[0][...] = coadd[0:16, :]
    edges[1][...] = coadd[240:256, :]
    for e in range(2):
        at = (SPAN - 1) * e
        inverse = inverse_weight(weight, at)
        for ct in range(nt):
            for h in range(2):
                lanes = slice(ct * LANES, (ct + 1) * LANES)
                edges[2 + e][8 * h : 8 * h + 8, lanes] = value(ct, at, h, inverse)


def first_coadd(group, nt):
    shapes = [(256, 1024), (8, LANES)] + [(16, LANES * nt)] * 4
    blocks = [(256, LANES * nt)] + shapes[1:]
    return pl.pallas_call(
        functools.partial(coadd_kernel, nt),
        grid=(1,),
        out_shape=[jax.ShapeDtypeStruct(s, F32) for s in shapes],
        in_specs=[full(x.shape) for x in group],
        out_specs=[full(s) for s in blocks],
        compiler_params=pltpu.CompilerParams(vmem_limit_bytes=16 << 20),
        cost_estimate=pl.CostEstimate(
            flops=10**6, bytes_accessed=(5 << 17) * nt, transcendentals=0
        ),
        name="coadd",
    )(*group)


def join_kernel(first, vis_ref, mass, *refs):
    group, (top, bottom), out = refs[:4], refs[4:6], refs[6]
    end = vis_ref[0] == 3
    at = jnp.where(end, SPAN - 2, 1)
    inverse = inverse_weight(mass[...], at)
    out[:, : first * LANES] = jnp.where(end, bottom[...], top[...])
    for d in range(4):
        tile = first + ((vis_ref[0] - d) & 3)
        lanes = pl.ds(pl.multiple_of(tile * LANES, LANES), LANES)
        for h in range(2):
            out[8 * h : 8 * h + 8, lanes] = group[d][2 * at + h] * inverse


def join_edges(vis, mass, group, first, top, bottom):
    vmem = pl.BlockSpec(memory_space=pltpu.VMEM)
    return pl.pallas_call(
        functools.partial(join_kernel, first),
        out_shape=jax.ShapeDtypeStruct((16, 1024), F32),
        in_specs=[pl.BlockSpec(memory_space=pltpu.SMEM)] + [vmem] * 7,
        out_specs=vmem,
        compiler_params=pltpu.CompilerParams(vmem_limit_bytes=4 << 20),
        cost_estimate=pl.CostEstimate(flops=10**5, bytes_accessed=1 << 19, transcendentals=0),
        name="join",
    )(vis, mass, *group, top, bottom)


def filtered(parts, dhi, dlo):
    rows = parts[0].shape[0]
    lane = lax.broadcasted_iota(jnp.int32, (rows, LANES), 1)
    turned = [pltpu.roll(x, 64, 1) for x in parts]
    cut = [
        split(jnp.where(lane < 64, turned[t], turned[t + 1])) for t in range(len(parts) - 1)
    ]
    window = lambda k: jnp.concatenate(
        [
            jnp.concatenate([cut[j][k], cut[j + 1][k]], axis=1)
            for j in range(len(parts) - 2)
        ],
        axis=0,
    )
    return split(mm3(window(0), window(1), dhi[...], dlo[...]))


def detect_tiles(n, tile, tables, y_hi, y_lo, out, done, between):
    dhi, dlo, bhi, blo = tables[:4]

    def group(g, _):
        rows = pl.ds(pl.multiple_of(g * 64, 64), 64)
        hi, lo = filtered([tile(t, rows) for t in range(n + 2)], dhi, dlo)
        for j in range(n):
            y_hi[rows, j * LANES : (j + 1) * LANES] = hi[64 * j : 64 * j + 64]
            y_lo[rows, j * LANES : (j + 1) * LANES] = lo[64 * j : 64 * j + 64]
        return 0

    lax.fori_loop(0, 4, group, 0, unroll=2)
    between()
    for j0 in range(0, n, 2):
        lanes = slice(j0 * LANES, min(j0 + 2, n) * LANES)
        out[:, lanes] = mm3(bhi[...], blo[...], y_hi[:, lanes], y_lo[:, lanes])
        done(j0, lanes)


def early_kernel(n, *refs):
    tables, (x, out, rim, context, y_hi, y_lo) = refs[:4], refs[4:]
    context[...] = x[:, (n - 1) * LANES : (n + 1) * LANES]

    def tile(t, rows):
        if t == 0:
            return jnp.zeros((64, LANES), F32)
        return x[rows, (t - 1) * LANES : t * LANES]

    detect_tiles(n, tile, tables, y_hi, y_lo, out, lambda *_: None, lambda: None)
    rim[0:16, :] = out[0:16, :]
    rim[16:32, :] = out[240:256, :]


def early_detect(n, coadd, tables):
    tables = tables[:4]
    width = (n + 1) * LANES
    return pl.pallas_call(
        functools.partial(early_kernel, n),
        grid=(1,),
        out_shape=[
            jax.ShapeDtypeStruct(coadd.shape, F32),
            jax.ShapeDtypeStruct((32, n * LANES), F32),
            jax.ShapeDtypeStruct((256, 2 * LANES), F32),
        ],
        in_specs=[full(a.shape) for a in tables] + [full((256, width))],
        out_specs=[full((256, n * LANES)), full((32, n * LANES)), full((256, 2 * LANES))],
        scratch_shapes=[pltpu.VMEM((256, n * LANES), BF), pltpu.VMEM((256, n * LANES), BF)],
        compiler_params=pltpu.CompilerParams(vmem_limit_bytes=16 << 20),
        cost_estimate=pl.CostEstimate(
            flops=10**9, bytes_accessed=1 << 20, transcendentals=0
        ),
        name="early",
    )(*tables, coadd)


def late_kernel(first, nt, n, vis_ref, mass, *refs):
    tables, group, (other, before, after, left, rim) = refs[:6], refs[6:10], refs[10:15]
    coadd_out, out, coadd, y_hi, y_lo, det, sides, near, sems = refs[17:]
    weight = mass[...]
    last = first + nt
    start = last - n - 1
    copies = []

    def send(src, dst):
        copy = pltpu.make_async_copy(src, dst, sems.at[len(copies)])
        copy.start()
        copies.append(copy)

    def block(i, _):
        inverse = inverse_weight(weight, i + 1)
        for d in range(4):
            lanes = pl.ds(pl.multiple_of(((vis_ref[0] - d) & 3) * LANES, LANES), LANES)
            for h in range(2):
                rows = pl.ds(pl.multiple_of(i * 16 + 8 * h, 8), 8)
                coadd[rows, lanes] = group[d][i * 2 + (2 + h)] * inverse
        return 0

    lax.fori_loop(0, 16, block, 0, unroll=4)
    send(coadd, coadd_out.at[:, first * LANES : last * LANES])

    def tile(t, rows):
        real = start + t
        if real >= last:
            return jnp.zeros((64, LANES), F32)
        if real < first:
            return left[rows, t * LANES : (t + 1) * LANES]
        return coadd[rows, (real - first) * LANES : (real - first + 1) * LANES]

    whole_left = slice(0, (start + 1) * LANES)

    def between():
        for e in range(2):
            inverse = inverse_weight(weight, (SPAN - 1) * e)
            for d in range(4):
                lanes = pl.ds(pl.multiple_of(((vis_ref[0] - d) & 3) * LANES, LANES), LANES)
                for h in range(2):
                    rows = slice(16 * e + 8 * h, 16 * e + 8 * h + 8)
                    near[rows, lanes] = group[d][2 * (SPAN - 1) * e + h] * inverse
        strips = [jnp.zeros((32, LANES), F32)]
        for t in range(last):
            lanes = slice(t * LANES, (t + 1) * LANES)
            rows = other[:, lanes]
            above = jnp.where(vis_ref[0] == 0, rows, 0.0)
            below = jnp.where(vis_ref[0] == 3, rows, 0.0)
            far = jnp.concatenate([above, below], axis=0)
            if t < first:
                own = jnp.concatenate([before[:, lanes], after[:, lanes]], axis=0)
            else:
                own = near[:, (t - first) * LANES : (t - first + 1) * LANES]
            strips.append(far + own)
        hi, lo = filtered(strips + strips[:1], tables[0], tables[1])
        side = lambda v: jnp.concatenate([v[32 * j : 32 * j + 32] for j in range(last)], axis=1)
        sides[...] = mm3(tables[4][...], tables[5][...], side(hi), side(lo))
        sides[:, whole_left] += rim[...]

    def done(j0, lanes):
        there = slice((start + 1) * LANES + lanes.start, (start + 1) * LANES + lanes.stop)
        det[0:16, lanes] += sides[0:16, there]
        det[240:256, lanes] += sides[16:32, there]
        send(det.at[:, lanes], out.at[:, there])

    detect_tiles(n, tile, tables, y_hi, y_lo, det, done, between)
    send(sides.at[0:16, whole_left], out.at[0:16, whole_left])
    send(sides.at[16:32, whole_left], out.at[240:256, whole_left])
    for copy in copies:
        copy.wait()


def late_detect(vis, mass, group, first, nt, n, halos, tables, left, coadd, before):
    detection, rim = before
    any_spec = pl.BlockSpec(memory_space=pl.ANY)
    vmem = pl.BlockSpec(memory_space=pltpu.VMEM)
    args = [vis, mass, *tables, *group, *halos, left, rim, coadd, detection]
    return pl.pallas_call(
        functools.partial(late_kernel, first, nt, n),
        out_shape=[jax.ShapeDtypeStruct(coadd.shape, F32)] * 2,
        in_specs=[pl.BlockSpec(memory_space=pltpu.SMEM)]
        + [vmem] * (len(args) - 3)
        + [any_spec] * 2,
        out_specs=[any_spec] * 2,
        scratch_shapes=[
            pltpu.VMEM((256, nt * LANES), F32),
            pltpu.VMEM((256, n * LANES), BF),
            pltpu.VMEM((256, n * LANES), BF),
            pltpu.VMEM((256, n * LANES), F32),
            pltpu.VMEM((32, (first + nt) * LANES), F32),
            pltpu.VMEM((32, nt * LANES), F32),
            pltpu.SemaphoreType.DMA((3 + (n + 1) // 2,)),
        ],
        input_output_aliases={len(args) - 2: 0, len(args) - 1: 1},
        compiler_params=pltpu.CompilerParams(vmem_limit_bytes=12 << 20),
        cost_estimate=pl.CostEstimate(
            flops=2 * 10**9, bytes_accessed=4 << 20, transcendentals=0
        ),
        name="late",
    )(*args)


def detect_tables():
    dhi, dlo = halves(detect_taps(window_lags(128)))
    idx = np.arange(256, dtype=np.float64)
    bhi, blo = halves(detect_taps(idx[None, :] - idx[:, None]))
    q = np.arange(16, dtype=np.float64)
    edge = np.zeros((32, 32))
    edge[0:16, 0:16] = detect_taps((q[None, :] - 16) - q[:, None])
    edge[16:32, 16:32] = detect_taps((q[None, :] + 16) - q[:, None])
    ehi, elo = halves(edge)
    return dhi, dlo, bhi, blo, ehi, elo


def shards(pieces, coeffs, weights, routes, offsets):
    count, rows, width = pieces.shape
    pieces2d = pieces.reshape(count * rows, width)
    route1 = routes.reshape(count)
    coeffs_t = jnp.transpose(coeffs, (1, 2, 0))
    whi, wlo = column_weights()
    tables = (jnp.asarray(row_tables()), jnp.asarray(whi), jnp.asarray(wlo))
    dtables = tuple(jnp.asarray(a) for a in detect_tables())
    vis = lax.axis_index("vis").reshape(1)
    nv = lax.axis_size("vis")
    n = lax.axis_size("tile") * nv
    shifts = [[(i, (i + d) % nv) for i in range(nv)] for d in (1, 2, 3)]
    axes = ("tile", "vis")

    first, nt = CHUNKS
    per = 2 * first

    def over_vis(group):
        moved = [group[0]]
        for d in (0, 2, 1):
            moved.append(lax.ppermute(group[d + 1], "vis", shifts[d]))
        return [moved[0], moved[1], moved[3], moved[2]]

    def over_tile(slots):
        return lax.all_to_all(slots, "tile", split_axis=0, concat_axis=0, tiled=True)

    slots = match_slots((route1, offsets, weights, coeffs_t), tables, pieces2d, first)
    recv = over_tile(slots)
    meta = recv[:, 4 * first, 0:2, 0:2]
    landed = land_call(
        functools.partial(land_kernel, first), vis, meta, recv, [SPAN * per + 1] * 3 + [SPAN * first + 1] * 2,
        [
            pltpu.VMEM((66, per, 8, LANES), F32),
            pltpu.VMEM((8, LANES), F32),
            pltpu.SMEM((64,), jnp.int32),
        ],
    )
    blocks = jnp.pad(meta[:, :, 0].T, ((0, 6), (0, LANES - count)))
    told = over_vis([blocks] * nv)
    spot = jnp.stack([x[0:2, 0:count] for x in told]).astype(jnp.int32)
    spot = jnp.transpose(spot, (0, 2, 1))
    own, p1, m1, p2, m2 = landed
    head = p2.shape[0]
    p1 = lax.ppermute(p1, "vis", shifts[0])
    m1 = lax.ppermute(m1, "vis", shifts[2])
    p2 = lax.ppermute(p2 + p1[:head], "vis", shifts[0])
    m2 = lax.ppermute(m2 + m1[:head], "vis", shifts[2])

    facts = jnp.stack([route1.astype(F32), offsets.astype(F32)])
    facts = jnp.pad(facts, ((0, 6), (0, LANES - count)))
    spread = match_call(
        spread_kernel, (vis, weights, coeffs_t), tables, pieces2d, (facts,), first, nt,
        [(2 * count + 1, 8, LANES)] * 4, [],
    )
    traded = over_vis(spread)
    notes = jnp.stack([x[2 * count, 0:2, 0:count] for x in traded])
    slots = pack(notes, traded)
    recv = over_tile(slots)
    landed = land_right(vis, spot, recv)
    bulk = over_vis(landed)

    coadd, mass, top, bottom, *outside = first_coadd((own, p1, m1, p2, m2), first)
    edge = join_edges(vis, mass, bulk, first, top, bottom)
    swaps = [(i - 1, i) for i in range(nv, n, nv)] + [(i, i - 1) for i in range(nv, n, nv)]
    other = lax.ppermute(edge, axes, swaps)
    *before, left = early_detect(first - 1, coadd, dtables)
    coadd, detection = late_detect(
        vis, mass, bulk, first, nt, nt + 1, (other, *outside), dtables, left, coadd,
        before,
    )
    return (coadd, detection)


def solution(mesh):
    placed = (
        P(("tile", "vis"), None, None),
        P(("tile", "vis"), None, None),
        P(("tile", "vis")),
        P(("tile", "vis"), None),
        P(("tile", "vis")),
    )
    return jax.shard_map(
        shards,
        mesh=mesh,
        in_specs=placed,
        out_specs=(P(("tile", "vis"), None), P(("tile", "vis"), None)),
        check_vma=False,
    )
```

```python
import functools
import math

import jax
import jax.numpy as jnp
import numpy as np
from jax import lax
from jax.experimental import pallas as pl
from jax.experimental.pallas import tpu as pltpu
from jax.sharding import PartitionSpec as P


TAPS = 10
REACH = 15
ROW_SHAPES = ((1.0, 0), (1.0, 1), (2.0, 0), (2.0, 2), (3.5, 0))
COLUMN_SHAPES = ((1.0, 0), (2.0, 0), (2.0, 1), (3.5, 0))
LANES = 128
SPAN = 18
CHUNKS = (4, 4)
BF = jnp.bfloat16
F32 = jnp.float32


def basis_taps(lags, shapes):
    spots = np.arange(-TAPS, TAPS + 1, dtype=np.float64)
    out = []
    for s, d in shapes:
        full = np.exp(-spots * spots / (2 * s * s)) * (spots / s) ** d
        scale = 1.0 / math.sqrt(np.sum(full * full))
        vals = np.exp(-lags * lags / (2 * s * s)) * (lags / s) ** d * scale
        out.append(np.where(np.abs(lags) <= TAPS, vals, 0.0))
    return np.stack(out)


def detect_taps(lags):
    spots = np.arange(-REACH, REACH + 1, dtype=np.float64)
    total = np.sum(np.exp(-spots * spots / 18.0))
    vals = np.exp(-lags * lags / 18.0) / total - 1.0 / (2 * REACH + 1)
    return np.where(np.abs(lags) <= REACH, vals, 0.0)


def halves(a):
    a = np.asarray(a, np.float32)
    hi = a.astype(jnp.bfloat16)
    lo = (a - hi.astype(np.float32)).astype(jnp.bfloat16)
    return hi, lo


def window_lags(n):
    k = np.arange(256, dtype=np.float64)[:, None] - 64
    return k - np.arange(n, dtype=np.float64)[None, :]


def column_weights():
    bank = basis_taps(window_lags(128), COLUMN_SHAPES)
    nt = np.stack(
        [np.concatenate([bank[0], bank[1]], 1), np.concatenate([bank[2], bank[3]], 1)]
    )
    return halves(nt)


def row_tables():
    lags = (np.arange(16)[None, :] - np.arange(16)[:, None]).astype(np.float64)
    bank = basis_taps(lags, ROW_SHAPES)
    return np.tile(bank, (1, 1, 16)).astype(np.float32)


def split(x):
    hi = x.astype(BF)
    lo = (x - hi.astype(F32)).astype(BF)
    return hi, lo


def mm(a, b):
    return jnp.dot(a, b, preferred_element_type=F32)


def mm3(ah, al, bh, bl):
    return mm(ah, bh) + (mm(al, bh) + mm(ah, bl))


def match_groups(
    at_start, at_end, nt, weights, coeffs, gt, whi, wlo, left, main, right,
    xs_hi, xs_lo, window_at, put, ready=lambda g: None,
):
    def group(g, _):
        ready(g)
        rows = pl.ds(pl.multiple_of(g * 64, 64), 64)
        lane = lax.broadcasted_iota(jnp.int32, (64, LANES), 1)
        blank = jnp.zeros((64, LANES), F32)
        parts = [blank if at_start else left[rows, :]]
        parts += [main[rows, t * LANES : (t + 1) * LANES] for t in range(nt)]
        parts += [blank if at_end else right[rows, :]]
        turned = [pltpu.roll(x, 64, 1) for x in parts]
        for t in range(nt + 1):
            v = jnp.where(lane < 64, turned[t], turned[t + 1])
            hi, lo = split(v)
            xs_hi[:, t * LANES : (t + 1) * LANES] = hi
            xs_lo[:, t * LANES : (t + 1) * LANES] = lo
        stack = lambda ref: jnp.concatenate(
            [ref[:, pl.ds(window_at(w), 256)] for w in range(nt)], axis=0
        )
        x_hi, x_lo = stack(xs_hi), stack(xs_lo)

        lane = lax.broadcasted_iota(jnp.int32, (16, LANES), 1)
        left_hi, left_lo = [], []
        for i in range(4):
            p = g * 4 + i
            w = weights[p]
            pair = []
            for h in range(2):
                acc = None
                for a in range(5):
                    both = jnp.where(lane < 64, coeffs[a, 2 * h, p], coeffs[a, 2 * h + 1, p])
                    term = both * gt[a, :, h * LANES : (h + 1) * LANES]
                    acc = term if acc is None else acc + term
                acc = jnp.where((lane // 16) % 4 == i, acc * w, 0.0)
                pair.append(split(acc))
            left_hi.append(jnp.concatenate([pair[0][0], pair[1][0]], axis=1))
            left_lo.append(jnp.concatenate([pair[0][1], pair[1][1]], axis=1))
        l_hi = jnp.concatenate(left_hi, axis=0)
        l_both = jnp.concatenate(left_hi + left_lo, axis=0)

        cols = []
        for bp in range(2):
            y = mm3(x_hi, x_lo, whi[bp], wlo[bp])
            cols.append(split(y))

        for j0 in range(0, nt, 2):
            windows = range(j0, min(j0 + 2, nt))

            def operand(k):
                blocks = []
                for b in range(4):
                    src = cols[b // 2][k]
                    lanes = slice((b % 2) * LANES, (b % 2 + 1) * LANES)
                    pair = [src[64 * w : 64 * w + 64, lanes] for w in windows]
                    blocks.append(pair[0] if len(pair) == 1 else jnp.concatenate(pair, axis=1))
                return jnp.concatenate(blocks, axis=0)

            zz = mm(l_both, operand(0))
            z = zz[0:64] + (zz[64:128] + mm(l_hi, operand(1)))
            for i in range(4):
                for h in range(2):
                    for w in windows:
                        rows = slice(16 * i + 8 * h, 16 * i + 8 * h + 8)
                        lanes = slice((w - j0) * LANES, (w - j0 + 1) * LANES)
                        put(g * 4 + i, w, h, z[rows, lanes])
        return 0

    lax.fori_loop(0, 8, group, 0)


def slot_kernel(
    nt,
    routes, offsets, weights, coeffs,
    gt_any, whi_any, wlo_any, pieces,
    out,
    xs_hi, xs_lo, gt, whi, wlo, main, cnt, dst, rnk, sems,
):
    tiles = out.shape[1]
    moves = [(whi_any, whi), (wlo_any, wlo), (gt_any, gt)]
    fetches = [pltpu.make_async_copy(a, b, sems.at[i]) for i, (a, b) in enumerate(moves)]

    def rows_of(g):
        rows = pl.ds(pl.multiple_of(g * 64, 64), 64)
        src = pieces.at[rows, 0 : (nt + 1) * LANES]
        return pltpu.make_async_copy(src, main.at[rows, :], sems.at[3 + g])

    rows_of(0).start()
    for fetch in fetches:
        fetch.start()
    for g in range(1, 8):
        rows_of(g).start()

    def clear(i, _):
        cnt[i] = 0
        return 0

    lax.fori_loop(0, 32, clear, 0, unroll=8)

    def place(p, _):
        s = routes[p]
        r = cnt[s]
        cnt[s] = r + 1
        dst[p] = s
        rnk[p] = r
        return 0

    lax.fori_loop(0, 32, place, 0, unroll=4)
    zero = jnp.zeros((8, LANES), F32)

    def wipe(d, _):
        for t in range(tiles):
            out[d, t] = zero
        return 0

    lax.fori_loop(0, 32, wipe, 0, unroll=2)

    def put(p, w, h, value):
        out[dst[p], rnk[p] * 2 + (4 * w + h)] = value

    for fetch in fetches:
        fetch.wait()
    match_groups(
        True, False, nt, weights, coeffs, gt, whi, wlo,
        None, main, main.at[:, nt * LANES : (nt + 1) * LANES],
        xs_hi, xs_lo, lambda w: w * LANES, put, lambda g: rows_of(g).wait(),
    )
    lane = lax.broadcasted_iota(jnp.int32, (1, LANES), 1)

    def note(p, _):
        k = offsets[p].astype(F32)
        row = jnp.where(lane == 0, k, weights[p])
        out[dst[p], tiles - 1, pl.ds(rnk[p], 1), :] = row
        return 0

    lax.fori_loop(0, 32, note, 0, unroll=4)


def spread_kernel(
    at_start, at_end, nt,
    vis, weights, coeffs,
    gt, whi, wlo, left, main, right, meta,
    *refs,
):
    outs, (xs_hi, xs_lo) = refs[:4], refs[4:]
    me = vis[0]

    def put(p, w, h, value):
        outs[w][p * 2 + h] = value

    match_groups(
        at_start, at_end, nt, weights, coeffs, gt, whi, wlo, left, main, right,
        xs_hi, xs_lo, lambda w: pl.multiple_of(((me + w) & 3) * LANES, LANES), put,
    )
    for out in outs:
        out[64] = meta[...]


def full(shape):
    return pl.BlockSpec(shape, lambda i: (0,) * len(shape))


def match_call(kernel, scalars, tables, pieces2d, extra, first, nt, out_shapes, scratch):
    gt, whi, wlo = tables
    width = nt * LANES
    smem = pl.BlockSpec(memory_space=pltpu.SMEM)
    return pl.pallas_call(
        functools.partial(kernel, first == 0, first + nt == 8, nt),
        grid=(1,),
        out_shape=[jax.ShapeDtypeStruct(s, F32) for s in out_shapes],
        in_specs=[smem] * len(scalars)
        + [
            full(gt.shape), full(whi.shape), full(wlo.shape),
            pl.BlockSpec((512, LANES), lambda i: (0, max(first - 1, 0))),
            pl.BlockSpec((512, width), lambda i: (0, first // nt)),
            pl.BlockSpec((512, LANES), lambda i: (0, min(first + nt, 7))),
        ]
        + [full(x.shape) for x in extra],
        out_specs=[full(s) for s in out_shapes],
        scratch_shapes=[
            pltpu.VMEM((64, width + LANES), BF),
            pltpu.VMEM((64, width + LANES), BF),
            *scratch,
        ],
        compiler_params=pltpu.CompilerParams(
            vmem_limit_bytes=(60 << 20) if first == 0 else (24 << 20)
        ),
        cost_estimate=pl.CostEstimate(
            flops=10**9 * nt, bytes_accessed=(1 << 19) * nt, transcendentals=0
        ),
        name="match",
    )(*scalars, gt, whi, wlo, pieces2d, pieces2d, pieces2d, *extra)


def match_slots(scalars, tables, pieces2d, nt):
    smem = pl.BlockSpec(memory_space=pltpu.SMEM)
    any_spec = pl.BlockSpec(memory_space=pl.ANY)
    shape = (32, 4 * nt + 1, 8, LANES)
    width = (nt + 1) * LANES
    return pl.pallas_call(
        functools.partial(slot_kernel, nt),
        grid=(1,),
        out_shape=jax.ShapeDtypeStruct(shape, F32),
        in_specs=[smem] * 4 + [any_spec] * 4,
        out_specs=full(shape),
        scratch_shapes=[
            pltpu.VMEM((64, width), BF),
            pltpu.VMEM((64, width), BF),
            *[pltpu.VMEM(x.shape, x.dtype) for x in tables],
            pltpu.VMEM((512, width), F32),
            *[pltpu.SMEM((32,), jnp.int32)] * 3,
            pltpu.SemaphoreType.DMA((11,)),
        ],
        compiler_params=pltpu.CompilerParams(vmem_limit_bytes=60 << 20),
        cost_estimate=pl.CostEstimate(
            flops=10**9 * nt, bytes_accessed=(1 << 19) * nt, transcendentals=0
        ),
        name="match",
    )(*scalars, *tables, pieces2d)


def pack_kernel(meta, *refs):
    groups, (out, cnt) = refs[:4], refs[4:]
    zero = jnp.zeros((8, LANES), F32)

    def wipe(d, _):
        for t in range(16):
            out[d, t] = zero
        for v in range(4):
            cnt[v * 32 + d] = 0
        return 0

    lax.fori_loop(0, 32, wipe, 0, unroll=2)
    for v in range(4):
        def place(p, _, v=v):
            s = meta[v, 0, p].astype(jnp.int32)
            r = cnt[v * 32 + s]
            cnt[v * 32 + s] = r + 1
            j = 2 * v + r
            for h in range(2):
                out[s, 2 * j + h] = groups[v][p * 2 + h]
            return 0

        lax.fori_loop(0, 32, place, 0, unroll=4)


def pack(meta, groups):
    shape = (32, 16, 8, LANES)
    return pl.pallas_call(
        pack_kernel,
        grid=(1,),
        out_shape=jax.ShapeDtypeStruct(shape, F32),
        in_specs=[pl.BlockSpec(memory_space=pltpu.SMEM)] + [full(x.shape) for x in groups],
        out_specs=full(shape),
        scratch_shapes=[pltpu.SMEM((128,), jnp.int32)],
        compiler_params=pltpu.CompilerParams(vmem_limit_bytes=24 << 20),
        cost_estimate=pl.CostEstimate(flops=10**6, bytes_accessed=4 << 20, transcendentals=0),
        name="pack",
    )(meta, *groups)


def land_kernel(nt, vis_ref, meta, recv, *refs):
    outs, (acc, wsum, spot) = refs[:-3], refs[-3:]
    per = 2 * nt
    zero = jnp.zeros((8, LANES), F32)

    def wipe(i, _):
        for t in range(per):
            acc[i, t] = zero
        return 0

    lax.fori_loop(0, 66, wipe, 0, unroll=3)
    lane = lax.broadcasted_iota(jnp.int32, (8, LANES), 1)
    wsum[...] = zero

    def address(s, _):
        for r in range(2):
            spot[2 * s + r] = meta[s, r, 0].astype(jnp.int32) + 1
        return 0

    lax.fori_loop(0, 32, address, 0, unroll=4)

    def land(s, _):
        for r in range(2):
            at = spot[2 * s + r]
            got = [recv[s, (t // 2) * 4 + 2 * r + t % 2] for t in range(per)]
            for t in range(per):
                acc[at, t] += got[t]
            wsum[...] += jnp.where(lane == at, meta[s, r, 1], 0.0)
        return 0

    lax.fori_loop(0, 32, land, 0, unroll=4)
    own, p1, m1, p2, m2 = outs
    half = SPAN * nt

    def move(ref, start, rel, first):
        base = ((vis_ref[0] + rel) & 3) * 16

        def one(i, _):
            for t in range(per // 2):
                ref[start + (t // 2) * (2 * SPAN) + i * 2 + t % 2] = acc[base + i, first + t]
            return 0

        lax.fori_loop(0, SPAN, one, 0, unroll=3)

    def mass(rel):
        base = ((vis_ref[0] + rel) & 3) * 16
        return pltpu.roll(wsum[...], (LANES - base) & (LANES - 1), 1)

    move(p1, 0, 2, 0)
    p1[half] = zero
    move(p1, half + 1, 1, per // 2)
    move(m1, 0, 2, per // 2)
    m1[half] = mass(2)
    move(m1, half + 1, 3, 0)
    move(p2, 0, 1, 0)
    p2[half] = mass(1)
    move(m2, 0, 3, per // 2)
    m2[half] = mass(3)
    move(own, 0, 0, 0)
    move(own, half, 0, per // 2)
    own[2 * half] = mass(0)


def full_kernel(vis_ref, spot, recv_any, *refs):
    outs, (acc, recv, sems) = refs[:-3], refs[-3:]
    zero = jnp.zeros((8, LANES), F32)
    fetches = [
        pltpu.make_async_copy(
            recv_any.at[8 * c : 8 * c + 8], recv.at[8 * c : 8 * c + 8], sems.at[c]
        )
        for c in range(4)
    ]
    for fetch in fetches:
        fetch.start()

    def wipe(i, _):
        acc[i, 0] = zero
        acc[i, 1] = zero
        return 0

    lax.fori_loop(0, 66, wipe, 0, unroll=6)

    def land(s, _):
        for j in range(8):
            at = spot[j // 2, s, j % 2] + 1
            got = [recv[s, 2 * j + h] for h in range(2)]
            for h in range(2):
                acc[at, h] += got[h]
        return 0

    for c in range(4):
        fetches[c].wait()
        lax.fori_loop(8 * c, 8 * c + 8, land, 0, unroll=4)
    for rel in range(4):
        base = ((vis_ref[0] + rel) & 3) * 16

        def one(i, _, rel=rel, base=base):
            for h in range(2):
                outs[rel][i * 2 + h] = acc[base + i, h]
            return 0

        lax.fori_loop(0, SPAN, one, 0, unroll=9)


def land_right(vis, spot, recv):
    smem = pl.BlockSpec(memory_space=pltpu.SMEM)
    vmem = pl.BlockSpec(memory_space=pltpu.VMEM)
    return pl.pallas_call(
        full_kernel,
        out_shape=[jax.ShapeDtypeStruct((2 * SPAN, 8, LANES), F32)] * 4,
        in_specs=[smem, smem, pl.BlockSpec(memory_space=pl.ANY)],
        out_specs=[vmem] * 4,
        scratch_shapes=[
            pltpu.VMEM((66, 2, 8, LANES), F32),
            pltpu.VMEM(recv.shape, F32),
            pltpu.SemaphoreType.DMA((4,)),
        ],
        compiler_params=pltpu.CompilerParams(vmem_limit_bytes=8 << 20),
        cost_estimate=pl.CostEstimate(flops=10**6, bytes_accessed=4 << 20, transcendentals=0),
        name="land",
    )(vis, spot, recv)


def land_call(kernel, vis, meta, recv, counts, scratch):
    shapes = [(k, 8, LANES) for k in counts]
    smem = pl.BlockSpec(memory_space=pltpu.SMEM)
    return pl.pallas_call(
        kernel,
        grid=(1,),
        out_shape=[jax.ShapeDtypeStruct(s, F32) for s in shapes],
        in_specs=[smem, smem, full(recv.shape)],
        out_specs=[full(s) for s in shapes],
        scratch_shapes=scratch,
        compiler_params=pltpu.CompilerParams(vmem_limit_bytes=24 << 20),
        cost_estimate=pl.CostEstimate(flops=10**6, bytes_accessed=4 << 20, transcendentals=0),
        name="land",
    )(vis, meta, recv)


def inverse_weight(weight, kk):
    lane = lax.broadcasted_iota(jnp.int32, (8, LANES), 1)
    total = jnp.sum(jnp.where(lane == kk, weight, 0.0), axis=1, keepdims=True)
    good = total > 0.0
    return jnp.where(good, 1.0 / jnp.where(good, total, 1.0), 0.0)


def coadd_kernel(nt, own, p1, m1, p2, m2, coadd, mass, *edges):
    half = SPAN * nt
    weight = own[2 * half] + (p2[half] + m2[half])
    mass[...] = weight

    def value(ct, at, h, inverse):
        t = ct * (2 * SPAN) + at * 2 + h
        if ct < nt // 2:
            return (own[t] + (p2[t] + m1[half + 1 + t])) * inverse
        near = t - half
        return (own[t] + (p1[half + 1 + near] + m2[near])) * inverse

    def block(kk, _):
        inverse = inverse_weight(weight, kk + 1)
        for ct in range(nt):
            for h in range(2):
                rows = pl.ds(pl.multiple_of(kk * 16 + 8 * h, 8), 8)
                coadd[rows, ct * LANES : (ct + 1) * LANES] = value(ct, kk + 1, h, inverse)
        return 0

    lax.fori_loop(0, 16, block, 0, unroll=2)
    edges[0][...] = coadd[0:16, :]
    edges[1][...] = coadd[240:256, :]
    for e in range(2):
        at = (SPAN - 1) * e
        inverse = inverse_weight(weight, at)
        for ct in range(nt):
            for h in range(2):
                lanes = slice(ct * LANES, (ct + 1) * LANES)
                edges[2 + e][8 * h : 8 * h + 8, lanes] = value(ct, at, h, inverse)


def first_coadd(group, nt):
    shapes = [(256, 1024), (8, LANES)] + [(16, LANES * nt)] * 4
    blocks = [(256, LANES * nt)] + shapes[1:]
    return pl.pallas_call(
        functools.partial(coadd_kernel, nt),
        grid=(1,),
        out_shape=[jax.ShapeDtypeStruct(s, F32) for s in shapes],
        in_specs=[full(x.shape) for x in group],
        out_specs=[full(s) for s in blocks],
        compiler_params=pltpu.CompilerParams(vmem_limit_bytes=16 << 20),
        cost_estimate=pl.CostEstimate(
            flops=10**6, bytes_accessed=(5 << 17) * nt, transcendentals=0
        ),
        name="coadd",
    )(*group)


def join_kernel(first, vis_ref, mass, *refs):
    group, (top, bottom), out = refs[:4], refs[4:6], refs[6]
    end = vis_ref[0] == 3
    at = jnp.where(end, SPAN - 2, 1)
    inverse = inverse_weight(mass[...], at)
    out[:, : first * LANES] = jnp.where(end, bottom[...], top[...])
    for d in range(4):
        tile = first + ((vis_ref[0] - d) & 3)
        lanes = pl.ds(pl.multiple_of(tile * LANES, LANES), LANES)
        for h in range(2):
            out[8 * h : 8 * h + 8, lanes] = group[d][2 * at + h] * inverse


def join_edges(vis, mass, group, first, top, bottom):
    vmem = pl.BlockSpec(memory_space=pltpu.VMEM)
    return pl.pallas_call(
        functools.partial(join_kernel, first),
        out_shape=jax.ShapeDtypeStruct((16, 1024), F32),
        in_specs=[pl.BlockSpec(memory_space=pltpu.SMEM)] + [vmem] * 7,
        out_specs=vmem,
        compiler_params=pltpu.CompilerParams(vmem_limit_bytes=4 << 20),
        cost_estimate=pl.CostEstimate(flops=10**5, bytes_accessed=1 << 19, transcendentals=0),
        name="join",
    )(vis, mass, *group, top, bottom)


def filtered(parts, dhi, dlo):
    rows = parts[0].shape[0]
    lane = lax.broadcasted_iota(jnp.int32, (rows, LANES), 1)
    turned = [pltpu.roll(x, 64, 1) for x in parts]
    cut = [
        split(jnp.where(lane < 64, turned[t], turned[t + 1])) for t in range(len(parts) - 1)
    ]
    window = lambda k: jnp.concatenate(
        [
            jnp.concatenate([cut[j][k], cut[j + 1][k]], axis=1)
            for j in range(len(parts) - 2)
        ],
        axis=0,
    )
    return split(mm3(window(0), window(1), dhi[...], dlo[...]))


def detect_tiles(n, tile, tables, y_hi, y_lo, out, done, between):
    dhi, dlo, bhi, blo = tables[:4]

    def group(g, _):
        rows = pl.ds(pl.multiple_of(g * 64, 64), 64)
        hi, lo = filtered([tile(t, rows) for t in range(n + 2)], dhi, dlo)
        for j in range(n):
            y_hi[rows, j * LANES : (j + 1) * LANES] = hi[64 * j : 64 * j + 64]
            y_lo[rows, j * LANES : (j + 1) * LANES] = lo[64 * j : 64 * j + 64]
        return 0

    lax.fori_loop(0, 4, group, 0, unroll=2)
    between()
    for j0 in range(0, n, 2):
        lanes = slice(j0 * LANES, min(j0 + 2, n) * LANES)
        out[:, lanes] = mm3(bhi[...], blo[...], y_hi[:, lanes], y_lo[:, lanes])
        done(j0, lanes)


def early_kernel(n, *refs):
    tables, (x, out, rim, context, y_hi, y_lo) = refs[:4], refs[4:]
    context[...] = x[:, (n - 1) * LANES : (n + 1) * LANES]

    def tile(t, rows):
        if t == 0:
            return jnp.zeros((64, LANES), F32)
        return x[rows, (t - 1) * LANES : t * LANES]

    detect_tiles(n, tile, tables, y_hi, y_lo, out, lambda *_: None, lambda: None)
    rim[0:16, :] = out[0:16, :]
    rim[16:32, :] = out[240:256, :]


def early_detect(n, coadd, tables):
    tables = tables[:4]
    width = (n + 1) * LANES
    return pl.pallas_call(
        functools.partial(early_kernel, n),
        grid=(1,),
        out_shape=[
            jax.ShapeDtypeStruct(coadd.shape, F32),
            jax.ShapeDtypeStruct((32, n * LANES), F32),
            jax.ShapeDtypeStruct((256, 2 * LANES), F32),
        ],
        in_specs=[full(a.shape) for a in tables] + [full((256, width))],
        out_specs=[full((256, n * LANES)), full((32, n * LANES)), full((256, 2 * LANES))],
        scratch_shapes=[pltpu.VMEM((256, n * LANES), BF), pltpu.VMEM((256, n * LANES), BF)],
        compiler_params=pltpu.CompilerParams(vmem_limit_bytes=16 << 20),
        cost_estimate=pl.CostEstimate(
            flops=10**9, bytes_accessed=1 << 20, transcendentals=0
        ),
        name="early",
    )(*tables, coadd)


def late_kernel(first, nt, n, vis_ref, mass, *refs):
    tables, group, (before, after, left, rim) = refs[:6], refs[6:10], refs[10:14]
    coadd_out, out, sides, coadd, y_hi, y_lo, det, near, sems = refs[16:]
    weight = mass[...]
    last = first + nt
    start = last - n - 1
    copies = []

    def send(src, dst):
        copy = pltpu.make_async_copy(src, dst, sems.at[len(copies)])
        copy.start()
        copies.append(copy)

    def block(i, _):
        inverse = inverse_weight(weight, i + 1)
        for d in range(4):
            lanes = pl.ds(pl.multiple_of(((vis_ref[0] - d) & 3) * LANES, LANES), LANES)
            for h in range(2):
                rows = pl.ds(pl.multiple_of(i * 16 + 8 * h, 8), 8)
                coadd[rows, lanes] = group[d][i * 2 + (2 + h)] * inverse
        return 0

    lax.fori_loop(0, 16, block, 0, unroll=4)
    send(coadd, coadd_out.at[:, first * LANES : last * LANES])

    def tile(t, rows):
        real = start + t
        if real >= last:
            return jnp.zeros((64, LANES), F32)
        if real < first:
            return left[rows, t * LANES : (t + 1) * LANES]
        return coadd[rows, (real - first) * LANES : (real - first + 1) * LANES]

    whole_left = slice(0, (start + 1) * LANES)

    def between():
        for e in range(2):
            inverse = inverse_weight(weight, (SPAN - 1) * e)
            for d in range(4):
                lanes = pl.ds(pl.multiple_of(((vis_ref[0] - d) & 3) * LANES, LANES), LANES)
                for h in range(2):
                    rows = slice(16 * e + 8 * h, 16 * e + 8 * h + 8)
                    near[rows, lanes] = group[d][2 * (SPAN - 1) * e + h] * inverse
        strips = [jnp.zeros((32, LANES), F32)]
        for t in range(last):
            lanes = slice(t * LANES, (t + 1) * LANES)
            if t < first:
                own = jnp.concatenate([before[:, lanes], after[:, lanes]], axis=0)
            else:
                own = near[:, (t - first) * LANES : (t - first + 1) * LANES]
            strips.append(own)
        hi, lo = filtered(strips + strips[:1], tables[0], tables[1])
        side = lambda v: jnp.concatenate([v[32 * j : 32 * j + 32] for j in range(last)], axis=1)
        sides[...] = mm3(tables[4][...], tables[5][...], side(hi), side(lo))
        sides[:, whole_left] += rim[...]

    def done(j0, lanes):
        there = slice((start + 1) * LANES + lanes.start, (start + 1) * LANES + lanes.stop)
        sides[0:16, there] += det[0:16, lanes]
        sides[16:32, there] += det[240:256, lanes]
        det[0:16, lanes] = sides[0:16, there]
        det[240:256, lanes] = sides[16:32, there]
        send(det.at[:, lanes], out.at[:, there])

    detect_tiles(n, tile, tables, y_hi, y_lo, det, done, between)
    send(sides.at[0:16, whole_left], out.at[0:16, whole_left])
    send(sides.at[16:32, whole_left], out.at[240:256, whole_left])
    for copy in copies:
        copy.wait()


def late_detect(vis, mass, group, first, nt, n, halos, tables, left, coadd, before):
    detection, rim = before
    any_spec = pl.BlockSpec(memory_space=pl.ANY)
    vmem = pl.BlockSpec(memory_space=pltpu.VMEM)
    args = [vis, mass, *tables, *group, *halos, left, rim, coadd, detection]
    return pl.pallas_call(
        functools.partial(late_kernel, first, nt, n),
        out_shape=[jax.ShapeDtypeStruct(coadd.shape, F32)] * 2
        + [jax.ShapeDtypeStruct((32, (first + nt) * LANES), F32)],
        in_specs=[pl.BlockSpec(memory_space=pltpu.SMEM)]
        + [vmem] * (len(args) - 3)
        + [any_spec] * 2,
        out_specs=[any_spec] * 2 + [vmem],
        scratch_shapes=[
            pltpu.VMEM((256, nt * LANES), F32),
            pltpu.VMEM((256, n * LANES), BF),
            pltpu.VMEM((256, n * LANES), BF),
            pltpu.VMEM((256, n * LANES), F32),
            pltpu.VMEM((32, nt * LANES), F32),
            pltpu.SemaphoreType.DMA((3 + (n + 1) // 2,)),
        ],
        input_output_aliases={len(args) - 2: 0, len(args) - 1: 1},
        compiler_params=pltpu.CompilerParams(vmem_limit_bytes=12 << 20),
        cost_estimate=pl.CostEstimate(
            flops=2 * 10**9, bytes_accessed=4 << 20, transcendentals=0
        ),
        name="late",
    )(*args)


def end_kernel(vis_ref, dhi, dlo, ehi, elo, other, sides, unused, out, rows, sem):
    me = vis_ref[0]
    n = other.shape[1] // LANES

    @pl.when((me == 0) | (me == 3))
    def _():
        strips = [jnp.zeros((32, LANES), F32)]
        for t in range(n):
            got = other[:, t * LANES : (t + 1) * LANES]
            above = jnp.where(me == 0, got, 0.0)
            below = jnp.where(me == 3, got, 0.0)
            strips.append(jnp.concatenate([above, below], axis=0))
        hi, lo = filtered(strips + strips[:1], dhi, dlo)
        side = lambda v: jnp.concatenate([v[32 * j : 32 * j + 32] for j in range(n)], axis=1)
        both = sides[...] + mm3(ehi[...], elo[...], side(hi), side(lo))
        rows[...] = jnp.where(me == 0, both[0:16], both[16:32])
        at = pl.ds(pl.multiple_of(jnp.where(me == 0, 0, 240), 16), 16)
        copy = pltpu.make_async_copy(rows, out.at[at, :], sem)
        copy.start()
        copy.wait()


def end_detect(vis, tables, other, sides, detection):
    any_spec = pl.BlockSpec(memory_space=pl.ANY)
    vmem = pl.BlockSpec(memory_space=pltpu.VMEM)
    dhi, dlo, _, _, ehi, elo = tables
    return pl.pallas_call(
        end_kernel,
        out_shape=jax.ShapeDtypeStruct(detection.shape, F32),
        in_specs=[pl.BlockSpec(memory_space=pltpu.SMEM)] + [vmem] * 6 + [any_spec],
        out_specs=any_spec,
        scratch_shapes=[pltpu.VMEM(other.shape, F32), pltpu.SemaphoreType.DMA],
        input_output_aliases={7: 0},
        compiler_params=pltpu.CompilerParams(vmem_limit_bytes=4 << 20),
        cost_estimate=pl.CostEstimate(flops=10**8, bytes_accessed=1 << 18, transcendentals=0),
        name="end",
    )(vis, dhi, dlo, ehi, elo, other, sides, detection)


def detect_tables():
    dhi, dlo = halves(detect_taps(window_lags(128)))
    idx = np.arange(256, dtype=np.float64)
    bhi, blo = halves(detect_taps(idx[None, :] - idx[:, None]))
    q = np.arange(16, dtype=np.float64)
    edge = np.zeros((32, 32))
    edge[0:16, 0:16] = detect_taps((q[None, :] - 16) - q[:, None])
    edge[16:32, 16:32] = detect_taps((q[None, :] + 16) - q[:, None])
    ehi, elo = halves(edge)
    return dhi, dlo, bhi, blo, ehi, elo


def shards(pieces, coeffs, weights, routes, offsets):
    count, rows, width = pieces.shape
    pieces2d = pieces.reshape(count * rows, width)
    route1 = routes.reshape(count)
    coeffs_t = jnp.transpose(coeffs, (1, 2, 0))
    whi, wlo = column_weights()
    tables = (jnp.asarray(row_tables()), jnp.asarray(whi), jnp.asarray(wlo))
    dtables = tuple(jnp.asarray(a) for a in detect_tables())
    vis = lax.axis_index("vis").reshape(1)
    nv = lax.axis_size("vis")
    n = lax.axis_size("tile") * nv
    shifts = [[(i, (i + d) % nv) for i in range(nv)] for d in (1, 2, 3)]
    axes = ("tile", "vis")

    first, nt = CHUNKS
    per = 2 * first

    def over_vis(group):
        moved = [group[0]]
        for d in (0, 2, 1):
            moved.append(lax.ppermute(group[d + 1], "vis", shifts[d]))
        return [moved[0], moved[1], moved[3], moved[2]]

    def over_tile(slots):
        return lax.all_to_all(slots, "tile", split_axis=0, concat_axis=0, tiled=True)

    slots = match_slots((route1, offsets, weights, coeffs_t), tables, pieces2d, first)
    recv = over_tile(slots)
    meta = recv[:, 4 * first, 0:2, 0:2]
    landed = land_call(
        functools.partial(land_kernel, first), vis, meta, recv, [SPAN * per + 1] * 3 + [SPAN * first + 1] * 2,
        [
            pltpu.VMEM((66, per, 8, LANES), F32),
            pltpu.VMEM((8, LANES), F32),
            pltpu.SMEM((64,), jnp.int32),
        ],
    )
    blocks = jnp.pad(meta[:, :, 0].T, ((0, 6), (0, LANES - count)))
    told = over_vis([blocks] * nv)
    spot = jnp.stack([x[0:2, 0:count] for x in told]).astype(jnp.int32)
    spot = jnp.transpose(spot, (0, 2, 1))
    own, p1, m1, p2, m2 = landed
    head = p2.shape[0]
    p1 = lax.ppermute(p1, "vis", shifts[0])
    m1 = lax.ppermute(m1, "vis", shifts[2])
    p2 = lax.ppermute(p2 + p1[:head], "vis", shifts[0])
    m2 = lax.ppermute(m2 + m1[:head], "vis", shifts[2])

    facts = jnp.stack([route1.astype(F32), offsets.astype(F32)])
    facts = jnp.pad(facts, ((0, 6), (0, LANES - count)))
    spread = match_call(
        spread_kernel, (vis, weights, coeffs_t), tables, pieces2d, (facts,), first, nt,
        [(2 * count + 1, 8, LANES)] * 4, [],
    )
    traded = over_vis(spread)
    notes = jnp.stack([x[2 * count, 0:2, 0:count] for x in traded])
    slots = pack(notes, traded)
    recv = over_tile(slots)
    landed = land_right(vis, spot, recv)
    bulk = over_vis(landed)

    coadd, mass, top, bottom, *outside = first_coadd((own, p1, m1, p2, m2), first)
    edge = join_edges(vis, mass, bulk, first, top, bottom)
    swaps = [(i - 1, i) for i in range(nv, n, nv)] + [(i, i - 1) for i in range(nv, n, nv)]
    other = lax.ppermute(edge, axes, swaps)
    *before, left = early_detect(first - 1, coadd, dtables)
    coadd, detection, sides = late_detect(
        vis, mass, bulk, first, nt, nt + 1, outside, dtables, left, coadd, before
    )
    detection = end_detect(vis, dtables, other, sides, detection)
    return (coadd, detection)


def solution(mesh):
    placed = (
        P(("tile", "vis"), None, None),
        P(("tile", "vis"), None, None),
        P(("tile", "vis")),
        P(("tile", "vis"), None),
        P(("tile", "vis")),
    )
    return jax.shard_map(
        shards,
        mesh=mesh,
        in_specs=placed,
        out_specs=(P(("tile", "vis"), None), P(("tile", "vis"), None)),
        check_vma=False,
    )
```

```python
import functools
import math

import jax
import jax.numpy as jnp
import numpy as np
from jax import lax
from jax.experimental import pallas as pl
from jax.experimental.pallas import tpu as pltpu
from jax.sharding import PartitionSpec as P


TAPS = 10
REACH = 15
ROW_SHAPES = ((1.0, 0), (1.0, 1), (2.0, 0), (2.0, 2), (3.5, 0))
COLUMN_SHAPES = ((1.0, 0), (2.0, 0), (2.0, 1), (3.5, 0))
LANES = 128
SPAN = 18
CHUNKS = (4, 4)
BF = jnp.bfloat16
F32 = jnp.float32


def basis_taps(lags, shapes):
    spots = np.arange(-TAPS, TAPS + 1, dtype=np.float64)
    out = []
    for s, d in shapes:
        full = np.exp(-spots * spots / (2 * s * s)) * (spots / s) ** d
        scale = 1.0 / math.sqrt(np.sum(full * full))
        vals = np.exp(-lags * lags / (2 * s * s)) * (lags / s) ** d * scale
        out.append(np.where(np.abs(lags) <= TAPS, vals, 0.0))
    return np.stack(out)


def detect_taps(lags):
    spots = np.arange(-REACH, REACH + 1, dtype=np.float64)
    total = np.sum(np.exp(-spots * spots / 18.0))
    vals = np.exp(-lags * lags / 18.0) / total - 1.0 / (2 * REACH + 1)
    return np.where(np.abs(lags) <= REACH, vals, 0.0)


def halves(a):
    a = np.asarray(a, np.float32)
    hi = a.astype(jnp.bfloat16)
    lo = (a - hi.astype(np.float32)).astype(jnp.bfloat16)
    return hi, lo


def window_lags(n):
    k = np.arange(256, dtype=np.float64)[:, None] - 64
    return k - np.arange(n, dtype=np.float64)[None, :]


def column_weights():
    bank = basis_taps(window_lags(128), COLUMN_SHAPES)
    nt = np.stack(
        [np.concatenate([bank[0], bank[1]], 1), np.concatenate([bank[2], bank[3]], 1)]
    )
    return halves(nt)


def row_tables():
    lags = (np.arange(16)[None, :] - np.arange(16)[:, None]).astype(np.float64)
    bank = basis_taps(lags, ROW_SHAPES)
    return np.tile(bank, (1, 1, 16)).astype(np.float32)


def split(x):
    hi = x.astype(BF)
    lo = (x - hi.astype(F32)).astype(BF)
    return hi, lo


def mm(a, b):
    return jnp.dot(a, b, preferred_element_type=F32)


def mm3(ah, al, bh, bl):
    return mm(ah, bh) + (mm(al, bh) + mm(ah, bl))


def match_groups(
    at_start, at_end, nt, weights, coeffs, gt, whi, wlo, left, main, right,
    xs_hi, xs_lo, window_at, put, ready=lambda g: None,
):
    def group(g, _):
        ready(g)
        rows = pl.ds(pl.multiple_of(g * 64, 64), 64)
        lane = lax.broadcasted_iota(jnp.int32, (64, LANES), 1)
        blank = jnp.zeros((64, LANES), F32)
        parts = [blank if at_start else left[rows, :]]
        parts += [main[rows, t * LANES : (t + 1) * LANES] for t in range(nt)]
        parts += [blank if at_end else right[rows, :]]
        turned = [pltpu.roll(x, 64, 1) for x in parts]
        for t in range(nt + 1):
            v = jnp.where(lane < 64, turned[t], turned[t + 1])
            hi, lo = split(v)
            xs_hi[:, t * LANES : (t + 1) * LANES] = hi
            xs_lo[:, t * LANES : (t + 1) * LANES] = lo
        stack = lambda ref: jnp.concatenate(
            [ref[:, pl.ds(window_at(w), 256)] for w in range(nt)], axis=0
        )
        x_hi, x_lo = stack(xs_hi), stack(xs_lo)

        lane = lax.broadcasted_iota(jnp.int32, (16, LANES), 1)
        left_hi, left_lo = [], []
        for i in range(4):
            p = g * 4 + i
            w = weights[p]
            pair = []
            for h in range(2):
                acc = None
                for a in range(5):
                    both = jnp.where(lane < 64, coeffs[a, 2 * h, p], coeffs[a, 2 * h + 1, p])
                    term = both * gt[a, :, h * LANES : (h + 1) * LANES]
                    acc = term if acc is None else acc + term
                acc = jnp.where((lane // 16) % 4 == i, acc * w, 0.0)
                pair.append(split(acc))
            left_hi.append(jnp.concatenate([pair[0][0], pair[1][0]], axis=1))
            left_lo.append(jnp.concatenate([pair[0][1], pair[1][1]], axis=1))
        l_hi = jnp.concatenate(left_hi, axis=0)
        l_both = jnp.concatenate(left_hi + left_lo, axis=0)

        cols = []
        for bp in range(2):
            y = mm3(x_hi, x_lo, whi[bp], wlo[bp])
            cols.append(split(y))

        for j0 in range(0, nt, 2):
            windows = range(j0, min(j0 + 2, nt))

            def operand(k):
                blocks = []
                for b in range(4):
                    src = cols[b // 2][k]
                    lanes = slice((b % 2) * LANES, (b % 2 + 1) * LANES)
                    pair = [src[64 * w : 64 * w + 64, lanes] for w in windows]
                    blocks.append(pair[0] if len(pair) == 1 else jnp.concatenate(pair, axis=1))
                return jnp.concatenate(blocks, axis=0)

            zz = mm(l_both, operand(0))
            z = zz[0:64] + (zz[64:128] + mm(l_hi, operand(1)))
            for i in range(4):
                for h in range(2):
                    for w in windows:
                        rows = slice(16 * i + 8 * h, 16 * i + 8 * h + 8)
                        lanes = slice((w - j0) * LANES, (w - j0 + 1) * LANES)
                        put(g * 4 + i, w, h, z[rows, lanes])
        return 0

    lax.fori_loop(0, 8, group, 0)


def slot_kernel(
    nt,
    routes, offsets, weights, coeffs,
    gt_any, whi_any, wlo_any, pieces,
    out,
    xs_hi, xs_lo, gt, whi, wlo, main, cnt, dst, rnk, sems,
):
    tiles = out.shape[1]
    moves = [(whi_any, whi), (wlo_any, wlo), (gt_any, gt)]
    fetches = [pltpu.make_async_copy(a, b, sems.at[i]) for i, (a, b) in enumerate(moves)]

    def rows_of(g):
        rows = pl.ds(pl.multiple_of(g * 64, 64), 64)
        src = pieces.at[rows, 0 : (nt + 1) * LANES]
        return pltpu.make_async_copy(src, main.at[rows, :], sems.at[3 + g])

    rows_of(0).start()
    for fetch in fetches:
        fetch.start()
    for g in range(1, 8):
        rows_of(g).start()

    def clear(i, _):
        cnt[i] = 0
        return 0

    lax.fori_loop(0, 32, clear, 0, unroll=8)

    def place(p, _):
        s = routes[p]
        r = cnt[s]
        cnt[s] = r + 1
        dst[p] = s
        rnk[p] = r
        return 0

    lax.fori_loop(0, 32, place, 0, unroll=4)
    zero = jnp.zeros((8, LANES), F32)

    def wipe(d, _):
        for t in range(tiles):
            out[d, t] = zero
        return 0

    lax.fori_loop(0, 32, wipe, 0, unroll=2)

    def put(p, w, h, value):
        out[dst[p], rnk[p] * 2 + (4 * w + h)] = value

    for fetch in fetches:
        fetch.wait()
    match_groups(
        True, False, nt, weights, coeffs, gt, whi, wlo,
        None, main, main.at[:, nt * LANES : (nt + 1) * LANES],
        xs_hi, xs_lo, lambda w: w * LANES, put, lambda g: rows_of(g).wait(),
    )
    lane = lax.broadcasted_iota(jnp.int32, (1, LANES), 1)

    def note(p, _):
        k = offsets[p].astype(F32)
        row = jnp.where(lane == 0, k, weights[p])
        out[dst[p], tiles - 1, pl.ds(rnk[p], 1), :] = row
        return 0

    lax.fori_loop(0, 32, note, 0, unroll=4)


def spread_kernel(
    at_start, at_end, nt,
    vis, weights, coeffs,
    gt, whi, wlo, left, main, right, meta, unused,
    *refs,
):
    outs, (xs_hi, xs_lo) = refs[:4], refs[4:]
    me = vis[0]

    def put(p, w, h, value):
        outs[w][p * 2 + h] = value

    match_groups(
        at_start, at_end, nt, weights, coeffs, gt, whi, wlo, left, main, right,
        xs_hi, xs_lo, lambda w: pl.multiple_of(((me + w) & 3) * LANES, LANES), put,
    )
    for out in outs:
        out[64] = meta[...]


def full(shape):
    return pl.BlockSpec(shape, lambda i: (0,) * len(shape))


def match_call(kernel, scalars, tables, pieces2d, extra, first, nt, out_shapes, scratch):
    gt, whi, wlo = tables
    width = nt * LANES
    smem = pl.BlockSpec(memory_space=pltpu.SMEM)
    return pl.pallas_call(
        functools.partial(kernel, first == 0, first + nt == 8, nt),
        grid=(1,),
        out_shape=[jax.ShapeDtypeStruct(s, F32) for s in out_shapes],
        in_specs=[smem] * len(scalars)
        + [
            full(gt.shape), full(whi.shape), full(wlo.shape),
            pl.BlockSpec((512, LANES), lambda i: (0, max(first - 1, 0))),
            pl.BlockSpec((512, width), lambda i: (0, first // nt)),
            pl.BlockSpec((512, LANES), lambda i: (0, min(first + nt, 7))),
        ]
        + [full(x.shape) for x in extra],
        out_specs=[full(s) for s in out_shapes],
        scratch_shapes=[
            pltpu.VMEM((64, width + LANES), BF),
            pltpu.VMEM((64, width + LANES), BF),
            *scratch,
        ],
        compiler_params=pltpu.CompilerParams(
            vmem_limit_bytes=(60 << 20) if first == 0 else (24 << 20)
        ),
        cost_estimate=pl.CostEstimate(
            flops=10**9 * nt, bytes_accessed=(1 << 19) * nt, transcendentals=0
        ),
        name="match",
    )(*scalars, gt, whi, wlo, pieces2d, pieces2d, pieces2d, *extra)


def match_slots(scalars, tables, pieces2d, nt):
    smem = pl.BlockSpec(memory_space=pltpu.SMEM)
    any_spec = pl.BlockSpec(memory_space=pl.ANY)
    shape = (32, 4 * nt + 1, 8, LANES)
    width = (nt + 1) * LANES
    return pl.pallas_call(
        functools.partial(slot_kernel, nt),
        grid=(1,),
        out_shape=jax.ShapeDtypeStruct(shape, F32),
        in_specs=[smem] * 4 + [any_spec] * 4,
        out_specs=full(shape),
        scratch_shapes=[
            pltpu.VMEM((64, width), BF),
            pltpu.VMEM((64, width), BF),
            *[pltpu.VMEM(x.shape, x.dtype) for x in tables],
            pltpu.VMEM((512, width), F32),
            *[pltpu.SMEM((32,), jnp.int32)] * 3,
            pltpu.SemaphoreType.DMA((11,)),
        ],
        compiler_params=pltpu.CompilerParams(vmem_limit_bytes=60 << 20),
        cost_estimate=pl.CostEstimate(
            flops=10**9 * nt, bytes_accessed=(1 << 19) * nt, transcendentals=0
        ),
        name="match",
    )(*scalars, *tables, pieces2d)


def pack_kernel(meta, *refs):
    groups, (out, cnt) = refs[:4], refs[4:]
    zero = jnp.zeros((8, LANES), F32)

    def wipe(d, _):
        for t in range(16):
            out[d, t] = zero
        for v in range(4):
            cnt[v * 32 + d] = 0
        return 0

    lax.fori_loop(0, 32, wipe, 0, unroll=2)
    for v in range(4):
        def place(p, _, v=v):
            s = meta[v, 0, p].astype(jnp.int32)
            r = cnt[v * 32 + s]
            cnt[v * 32 + s] = r + 1
            j = 2 * v + r
            for h in range(2):
                out[s, 2 * j + h] = groups[v][p * 2 + h]
            return 0

        lax.fori_loop(0, 32, place, 0, unroll=4)


def pack(meta, groups):
    shape = (32, 16, 8, LANES)
    return pl.pallas_call(
        pack_kernel,
        grid=(1,),
        out_shape=jax.ShapeDtypeStruct(shape, F32),
        in_specs=[pl.BlockSpec(memory_space=pltpu.SMEM)] + [full(x.shape) for x in groups],
        out_specs=full(shape),
        scratch_shapes=[pltpu.SMEM((128,), jnp.int32)],
        compiler_params=pltpu.CompilerParams(vmem_limit_bytes=24 << 20),
        cost_estimate=pl.CostEstimate(flops=10**6, bytes_accessed=4 << 20, transcendentals=0),
        name="pack",
    )(meta, *groups)


def land_kernel(nt, vis_ref, meta, recv, *refs):
    outs, (acc, wsum, spot) = refs[:-3], refs[-3:]
    per = 2 * nt
    zero = jnp.zeros((8, LANES), F32)

    def wipe(i, _):
        for t in range(per):
            acc[i, t] = zero
        return 0

    lax.fori_loop(0, 66, wipe, 0, unroll=3)
    lane = lax.broadcasted_iota(jnp.int32, (8, LANES), 1)
    wsum[...] = zero

    def address(s, _):
        for r in range(2):
            spot[2 * s + r] = meta[s, r, 0].astype(jnp.int32) + 1
        return 0

    lax.fori_loop(0, 32, address, 0, unroll=4)

    def land(s, _):
        for r in range(2):
            at = spot[2 * s + r]
            got = [recv[s, (t // 2) * 4 + 2 * r + t % 2] for t in range(per)]
            for t in range(per):
                acc[at, t] += got[t]
            wsum[...] += jnp.where(lane == at, meta[s, r, 1], 0.0)
        return 0

    lax.fori_loop(0, 32, land, 0, unroll=4)
    own, p1, m1, p2, m2 = outs
    half = SPAN * nt

    def move(ref, start, rel, first):
        base = ((vis_ref[0] + rel) & 3) * 16

        def one(i, _):
            for t in range(per // 2):
                ref[start + (t // 2) * (2 * SPAN) + i * 2 + t % 2] = acc[base + i, first + t]
            return 0

        lax.fori_loop(0, SPAN, one, 0, unroll=3)

    def mass(rel):
        base = ((vis_ref[0] + rel) & 3) * 16
        return pltpu.roll(wsum[...], (LANES - base) & (LANES - 1), 1)

    move(p1, 0, 2, 0)
    p1[half] = zero
    move(p1, half + 1, 1, per // 2)
    move(m1, 0, 2, per // 2)
    m1[half] = mass(2)
    move(m1, half + 1, 3, 0)
    move(p2, 0, 1, 0)
    p2[half] = mass(1)
    move(m2, 0, 3, per // 2)
    m2[half] = mass(3)
    move(own, 0, 0, 0)
    move(own, half, 0, per // 2)
    own[2 * half] = mass(0)


def full_kernel(vis_ref, spot, recv, *refs):
    outs, acc = refs[:-1], refs[-1]
    zero = jnp.zeros((8, LANES), F32)

    def wipe(i, _):
        acc[i, 0] = zero
        acc[i, 1] = zero
        return 0

    lax.fori_loop(0, 66, wipe, 0, unroll=6)

    def land(s, _):
        for j in range(8):
            at = spot[j // 2, s, j % 2] + 1
            got = [recv[s, 2 * j + h] for h in range(2)]
            for h in range(2):
                acc[at, h] += got[h]
        return 0

    lax.fori_loop(0, 32, land, 0, unroll=4)
    for rel in range(4):
        base = ((vis_ref[0] + rel) & 3) * 16

        def one(i, _, rel=rel, base=base):
            for h in range(2):
                outs[rel][i * 2 + h] = acc[base + i, h]
            return 0

        lax.fori_loop(0, SPAN, one, 0, unroll=9)


def land_right(vis, spot, recv):
    smem = pl.BlockSpec(memory_space=pltpu.SMEM)
    vmem = pl.BlockSpec(memory_space=pltpu.VMEM)
    return pl.pallas_call(
        full_kernel,
        out_shape=[jax.ShapeDtypeStruct((2 * SPAN, 8, LANES), F32)] * 4,
        in_specs=[smem, smem, vmem],
        out_specs=[vmem] * 4,
        scratch_shapes=[pltpu.VMEM((66, 2, 8, LANES), F32)],
        compiler_params=pltpu.CompilerParams(vmem_limit_bytes=8 << 20),
        cost_estimate=pl.CostEstimate(flops=10**6, bytes_accessed=4 << 20, transcendentals=0),
        name="land",
    )(vis, spot, recv)


def land_call(kernel, vis, meta, recv, counts, scratch):
    shapes = [(k, 8, LANES) for k in counts]
    smem = pl.BlockSpec(memory_space=pltpu.SMEM)
    return pl.pallas_call(
        kernel,
        grid=(1,),
        out_shape=[jax.ShapeDtypeStruct(s, F32) for s in shapes],
        in_specs=[smem, smem, full(recv.shape)],
        out_specs=[full(s) for s in shapes],
        scratch_shapes=scratch,
        compiler_params=pltpu.CompilerParams(vmem_limit_bytes=24 << 20),
        cost_estimate=pl.CostEstimate(flops=10**6, bytes_accessed=4 << 20, transcendentals=0),
        name="land",
    )(vis, meta, recv)


def inverse_weight(weight, kk):
    lane = lax.broadcasted_iota(jnp.int32, (8, LANES), 1)
    total = jnp.sum(jnp.where(lane == kk, weight, 0.0), axis=1, keepdims=True)
    good = total > 0.0
    return jnp.where(good, 1.0 / jnp.where(good, total, 1.0), 0.0)


def coadd_kernel(nt, own, p1, m1, p2, m2, coadd, mass, *edges):
    half = SPAN * nt
    weight = own[2 * half] + (p2[half] + m2[half])
    mass[...] = weight

    def value(ct, at, h, inverse):
        t = ct * (2 * SPAN) + at * 2 + h
        if ct < nt // 2:
            return (own[t] + (p2[t] + m1[half + 1 + t])) * inverse
        near = t - half
        return (own[t] + (p1[half + 1 + near] + m2[near])) * inverse

    def block(kk, _):
        inverse = inverse_weight(weight, kk + 1)
        for ct in range(nt):
            for h in range(2):
                rows = pl.ds(pl.multiple_of(kk * 16 + 8 * h, 8), 8)
                coadd[rows, ct * LANES : (ct + 1) * LANES] = value(ct, kk + 1, h, inverse)
        return 0

    lax.fori_loop(0, 16, block, 0, unroll=2)
    edges[0][...] = coadd[0:16, :]
    edges[1][...] = coadd[240:256, :]
    for e in range(2):
        at = (SPAN - 1) * e
        inverse = inverse_weight(weight, at)
        for ct in range(nt):
            for h in range(2):
                lanes = slice(ct * LANES, (ct + 1) * LANES)
                edges[2 + e][8 * h : 8 * h + 8, lanes] = value(ct, at, h, inverse)


def first_coadd(group, nt):
    shapes = [(256, 1024), (8, LANES)] + [(16, LANES * nt)] * 4
    blocks = [(256, LANES * nt)] + shapes[1:]
    return pl.pallas_call(
        functools.partial(coadd_kernel, nt),
        grid=(1,),
        out_shape=[jax.ShapeDtypeStruct(s, F32) for s in shapes],
        in_specs=[full(x.shape) for x in group],
        out_specs=[full(s) for s in blocks],
        compiler_params=pltpu.CompilerParams(vmem_limit_bytes=16 << 20),
        cost_estimate=pl.CostEstimate(
            flops=10**6, bytes_accessed=(5 << 17) * nt, transcendentals=0
        ),
        name="coadd",
    )(*group)


def join_kernel(first, vis_ref, mass, *refs):
    group, (top, bottom), out = refs[:4], refs[4:6], refs[6]
    end = vis_ref[0] == 3
    at = jnp.where(end, SPAN - 2, 1)
    inverse = inverse_weight(mass[...], at)
    out[:, : first * LANES] = jnp.where(end, bottom[...], top[...])
    for d in range(4):
        tile = first + ((vis_ref[0] - d) & 3)
        lanes = pl.ds(pl.multiple_of(tile * LANES, LANES), LANES)
        for h in range(2):
            out[8 * h : 8 * h + 8, lanes] = group[d][2 * at + h] * inverse


def join_edges(vis, mass, group, first, top, bottom):
    vmem = pl.BlockSpec(memory_space=pltpu.VMEM)
    return pl.pallas_call(
        functools.partial(join_kernel, first),
        out_shape=jax.ShapeDtypeStruct((16, 1024), F32),
        in_specs=[pl.BlockSpec(memory_space=pltpu.SMEM)] + [vmem] * 7,
        out_specs=vmem,
        compiler_params=pltpu.CompilerParams(vmem_limit_bytes=4 << 20),
        cost_estimate=pl.CostEstimate(flops=10**5, bytes_accessed=1 << 19, transcendentals=0),
        name="join",
    )(vis, mass, *group, top, bottom)


def filtered(parts, dhi, dlo):
    rows = parts[0].shape[0]
    lane = lax.broadcasted_iota(jnp.int32, (rows, LANES), 1)
    turned = [pltpu.roll(x, 64, 1) for x in parts]
    cut = [
        split(jnp.where(lane < 64, turned[t], turned[t + 1])) for t in range(len(parts) - 1)
    ]
    window = lambda k: jnp.concatenate(
        [
            jnp.concatenate([cut[j][k], cut[j + 1][k]], axis=1)
            for j in range(len(parts) - 2)
        ],
        axis=0,
    )
    return split(mm3(window(0), window(1), dhi[...], dlo[...]))


def detect_tiles(n, tile, tables, y_hi, y_lo, out, done, between):
    dhi, dlo, bhi, blo = tables[:4]

    def group(g, _):
        rows = pl.ds(pl.multiple_of(g * 64, 64), 64)
        hi, lo = filtered([tile(t, rows) for t in range(n + 2)], dhi, dlo)
        for j in range(n):
            y_hi[rows, j * LANES : (j + 1) * LANES] = hi[64 * j : 64 * j + 64]
            y_lo[rows, j * LANES : (j + 1) * LANES] = lo[64 * j : 64 * j + 64]
        return 0

    lax.fori_loop(0, 4, group, 0, unroll=2)
    between()
    for j0 in range(0, n, 2):
        lanes = slice(j0 * LANES, min(j0 + 2, n) * LANES)
        out[:, lanes] = mm3(bhi[...], blo[...], y_hi[:, lanes], y_lo[:, lanes])
        done(j0, lanes)


def early_kernel(n, *refs):
    tables, (x, out, rim, context, y_hi, y_lo) = refs[:4], refs[4:]
    context[...] = x[:, (n - 1) * LANES : (n + 1) * LANES]

    def tile(t, rows):
        if t == 0:
            return jnp.zeros((64, LANES), F32)
        return x[rows, (t - 1) * LANES : t * LANES]

    detect_tiles(n, tile, tables, y_hi, y_lo, out, lambda *_: None, lambda: None)
    rim[0:16, :] = out[0:16, :]
    rim[16:32, :] = out[240:256, :]


def early_detect(n, coadd, tables):
    tables = tables[:4]
    width = (n + 1) * LANES
    return pl.pallas_call(
        functools.partial(early_kernel, n),
        grid=(1,),
        out_shape=[
            jax.ShapeDtypeStruct(coadd.shape, F32),
            jax.ShapeDtypeStruct((32, n * LANES), F32),
            jax.ShapeDtypeStruct((256, 2 * LANES), F32),
        ],
        in_specs=[full(a.shape) for a in tables] + [full((256, width))],
        out_specs=[full((256, n * LANES)), full((32, n * LANES)), full((256, 2 * LANES))],
        scratch_shapes=[pltpu.VMEM((256, n * LANES), BF), pltpu.VMEM((256, n * LANES), BF)],
        compiler_params=pltpu.CompilerParams(vmem_limit_bytes=16 << 20),
        cost_estimate=pl.CostEstimate(
            flops=10**9, bytes_accessed=1 << 20, transcendentals=0
        ),
        name="early",
    )(*tables, coadd)


def late_kernel(first, nt, n, vis_ref, mass, *refs):
    tables, group, (before, after, left, rim) = refs[:6], refs[6:10], refs[10:14]
    coadd_out, out, sides, coadd, y_hi, y_lo, det, near, sems = refs[16:]
    weight = mass[...]
    last = first + nt
    start = last - n - 1
    copies = []

    def send(src, dst):
        copy = pltpu.make_async_copy(src, dst, sems.at[len(copies)])
        copy.start()
        copies.append(copy)

    def block(i, _):
        inverse = inverse_weight(weight, i + 1)
        for d in range(4):
            lanes = pl.ds(pl.multiple_of(((vis_ref[0] - d) & 3) * LANES, LANES), LANES)
            for h in range(2):
                rows = pl.ds(pl.multiple_of(i * 16 + 8 * h, 8), 8)
                coadd[rows, lanes] = group[d][i * 2 + (2 + h)] * inverse
        return 0

    lax.fori_loop(0, 16, block, 0, unroll=4)
    send(coadd, coadd_out.at[:, first * LANES : last * LANES])

    def tile(t, rows):
        real = start + t
        if real >= last:
            return jnp.zeros((64, LANES), F32)
        if real < first:
            return left[rows, t * LANES : (t + 1) * LANES]
        return coadd[rows, (real - first) * LANES : (real - first + 1) * LANES]

    whole_left = slice(0, (start + 1) * LANES)

    def between():
        for e in range(2):
            inverse = inverse_weight(weight, (SPAN - 1) * e)
            for d in range(4):
                lanes = pl.ds(pl.multiple_of(((vis_ref[0] - d) & 3) * LANES, LANES), LANES)
                for h in range(2):
                    rows = slice(16 * e + 8 * h, 16 * e + 8 * h + 8)
                    near[rows, lanes] = group[d][2 * (SPAN - 1) * e + h] * inverse
        strips = [jnp.zeros((32, LANES), F32)]
        for t in range(last):
            lanes = slice(t * LANES, (t + 1) * LANES)
            if t < first:
                own = jnp.concatenate([before[:, lanes], after[:, lanes]], axis=0)
            else:
                own = near[:, (t - first) * LANES : (t - first + 1) * LANES]
            strips.append(own)
        hi, lo = filtered(strips + strips[:1], tables[0], tables[1])
        side = lambda v: jnp.concatenate([v[32 * j : 32 * j + 32] for j in range(last)], axis=1)
        sides[...] = mm3(tables[4][...], tables[5][...], side(hi), side(lo))
        sides[:, whole_left] += rim[...]

    def done(j0, lanes):
        there = slice((start + 1) * LANES + lanes.start, (start + 1) * LANES + lanes.stop)
        sides[0:16, there] += det[0:16, lanes]
        sides[16:32, there] += det[240:256, lanes]
        det[0:16, lanes] = sides[0:16, there]
        det[240:256, lanes] = sides[16:32, there]
        send(det.at[:, lanes], out.at[:, there])

    detect_tiles(n, tile, tables, y_hi, y_lo, det, done, between)
    send(sides.at[0:16, whole_left], out.at[0:16, whole_left])
    send(sides.at[16:32, whole_left], out.at[240:256, whole_left])
    for copy in copies:
        copy.wait()


def late_detect(vis, mass, group, first, nt, n, halos, tables, left, coadd, before):
    detection, rim = before
    any_spec = pl.BlockSpec(memory_space=pl.ANY)
    vmem = pl.BlockSpec(memory_space=pltpu.VMEM)
    args = [vis, mass, *tables, *group, *halos, left, rim, coadd, detection]
    return pl.pallas_call(
        functools.partial(late_kernel, first, nt, n),
        out_shape=[jax.ShapeDtypeStruct(coadd.shape, F32)] * 2
        + [jax.ShapeDtypeStruct((32, (first + nt) * LANES), F32)],
        in_specs=[pl.BlockSpec(memory_space=pltpu.SMEM)]
        + [vmem] * (len(args) - 3)
        + [any_spec] * 2,
        out_specs=[any_spec] * 2 + [vmem],
        scratch_shapes=[
            pltpu.VMEM((256, nt * LANES), F32),
            pltpu.VMEM((256, n * LANES), BF),
            pltpu.VMEM((256, n * LANES), BF),
            pltpu.VMEM((256, n * LANES), F32),
            pltpu.VMEM((32, nt * LANES), F32),
            pltpu.SemaphoreType.DMA((3 + (n + 1) // 2,)),
        ],
        input_output_aliases={len(args) - 2: 0, len(args) - 1: 1},
        compiler_params=pltpu.CompilerParams(vmem_limit_bytes=12 << 20),
        cost_estimate=pl.CostEstimate(
            flops=2 * 10**9, bytes_accessed=4 << 20, transcendentals=0
        ),
        name="late",
    )(*args)


def end_kernel(vis_ref, dhi, dlo, ehi, elo, other, sides, unused, out, rows, sem):
    me = vis_ref[0]
    n = other.shape[1] // LANES

    @pl.when((me == 0) | (me == 3))
    def _():
        strips = [jnp.zeros((32, LANES), F32)]
        for t in range(n):
            got = other[:, t * LANES : (t + 1) * LANES]
            above = jnp.where(me == 0, got, 0.0)
            below = jnp.where(me == 3, got, 0.0)
            strips.append(jnp.concatenate([above, below], axis=0))
        hi, lo = filtered(strips + strips[:1], dhi, dlo)
        side = lambda v: jnp.concatenate([v[32 * j : 32 * j + 32] for j in range(n)], axis=1)
        both = sides[...] + mm3(ehi[...], elo[...], side(hi), side(lo))
        rows[...] = jnp.where(me == 0, both[0:16], both[16:32])
        at = pl.ds(pl.multiple_of(jnp.where(me == 0, 0, 240), 16), 16)
        copy = pltpu.make_async_copy(rows, out.at[at, :], sem)
        copy.start()
        copy.wait()


def end_detect(vis, tables, other, sides, detection):
    any_spec = pl.BlockSpec(memory_space=pl.ANY)
    vmem = pl.BlockSpec(memory_space=pltpu.VMEM)
    dhi, dlo, _, _, ehi, elo = tables
    return pl.pallas_call(
        end_kernel,
        out_shape=jax.ShapeDtypeStruct(detection.shape, F32),
        in_specs=[pl.BlockSpec(memory_space=pltpu.SMEM)] + [vmem] * 6 + [any_spec],
        out_specs=any_spec,
        scratch_shapes=[pltpu.VMEM(other.shape, F32), pltpu.SemaphoreType.DMA],
        input_output_aliases={7: 0},
        compiler_params=pltpu.CompilerParams(vmem_limit_bytes=4 << 20),
        cost_estimate=pl.CostEstimate(flops=10**8, bytes_accessed=1 << 18, transcendentals=0),
        name="end",
    )(vis, dhi, dlo, ehi, elo, other, sides, detection)


def detect_tables():
    dhi, dlo = halves(detect_taps(window_lags(128)))
    idx = np.arange(256, dtype=np.float64)
    bhi, blo = halves(detect_taps(idx[None, :] - idx[:, None]))
    q = np.arange(16, dtype=np.float64)
    edge = np.zeros((32, 32))
    edge[0:16, 0:16] = detect_taps((q[None, :] - 16) - q[:, None])
    edge[16:32, 16:32] = detect_taps((q[None, :] + 16) - q[:, None])
    ehi, elo = halves(edge)
    return dhi, dlo, bhi, blo, ehi, elo


def shards(pieces, coeffs, weights, routes, offsets):
    count, rows, width = pieces.shape
    pieces2d = pieces.reshape(count * rows, width)
    route1 = routes.reshape(count)
    coeffs_t = jnp.transpose(coeffs, (1, 2, 0))
    whi, wlo = column_weights()
    tables = (jnp.asarray(row_tables()), jnp.asarray(whi), jnp.asarray(wlo))
    dtables = tuple(jnp.asarray(a) for a in detect_tables())
    vis = lax.axis_index("vis").reshape(1)
    nv = lax.axis_size("vis")
    n = lax.axis_size("tile") * nv
    shifts = [[(i, (i + d) % nv) for i in range(nv)] for d in (1, 2, 3)]
    axes = ("tile", "vis")

    first, nt = CHUNKS
    per = 2 * first

    def over_vis(group):
        moved = [group[0]]
        for d in (0, 2, 1):
            moved.append(lax.ppermute(group[d + 1], "vis", shifts[d]))
        return [moved[0], moved[1], moved[3], moved[2]]

    def over_tile(slots):
        return lax.all_to_all(slots, "tile", split_axis=0, concat_axis=0, tiled=True)

    pairs = [(i, i ^ 1) for i in range(lax.axis_size("tile"))]
    woken = lax.ppermute(weights, "tile", pairs)

    slots = match_slots((route1, offsets, weights, coeffs_t), tables, pieces2d, first)
    recv = over_tile(slots)
    meta = recv[:, 4 * first, 0:2, 0:2]
    landed = land_call(
        functools.partial(land_kernel, first), vis, meta, recv, [SPAN * per + 1] * 3 + [SPAN * first + 1] * 2,
        [
            pltpu.VMEM((66, per, 8, LANES), F32),
            pltpu.VMEM((8, LANES), F32),
            pltpu.SMEM((64,), jnp.int32),
        ],
    )
    blocks = jnp.pad(meta[:, :, 0].T, ((0, 6), (0, LANES - count)))
    told = over_vis([blocks] * nv)
    spot = jnp.stack([x[0:2, 0:count] for x in told]).astype(jnp.int32)
    spot = jnp.transpose(spot, (0, 2, 1))
    own, p1, m1, p2, m2 = landed
    head = p2.shape[0]
    p1 = lax.ppermute(p1, "vis", shifts[0])
    m1 = lax.ppermute(m1, "vis", shifts[2])
    p2 = lax.ppermute(p2 + p1[:head], "vis", shifts[0])
    m2 = lax.ppermute(m2 + m1[:head], "vis", shifts[2])

    facts = jnp.stack([route1.astype(F32), offsets.astype(F32)])
    facts = jnp.pad(facts, ((0, 6), (0, LANES - count)))
    spread = match_call(
        spread_kernel, (vis, weights, coeffs_t), tables, pieces2d, (facts, woken), first, nt,
        [(2 * count + 1, 8, LANES)] * 4, [],
    )
    traded = over_vis(spread)
    notes = jnp.stack([x[2 * count, 0:2, 0:count] for x in traded])
    slots = pack(notes, traded)
    recv = over_tile(slots)
    landed = land_right(vis, spot, recv)
    bulk = over_vis(landed)

    coadd, mass, top, bottom, *outside = first_coadd((own, p1, m1, p2, m2), first)
    edge = join_edges(vis, mass, bulk, first, top, bottom)
    swaps = [(i - 1, i) for i in range(nv, n, nv)] + [(i, i - 1) for i in range(nv, n, nv)]
    other = lax.ppermute(edge, axes, swaps)
    *before, left = early_detect(first - 1, coadd, dtables)
    coadd, detection, sides = late_detect(
        vis, mass, bulk, first, nt, nt + 1, outside, dtables, left, coadd, before
    )
    detection = end_detect(vis, dtables, other, sides, detection)
    return (coadd, detection)


def solution(mesh):
    placed = (
        P(("tile", "vis"), None, None),
        P(("tile", "vis"), None, None),
        P(("tile", "vis")),
        P(("tile", "vis"), None),
        P(("tile", "vis")),
    )
    return jax.shard_map(
        shards,
        mesh=mesh,
        in_specs=placed,
        out_specs=(P(("tile", "vis"), None), P(("tile", "vis"), None)),
        check_vma=False,
    )
```

```python
import functools
import math

import jax
import jax.numpy as jnp
import numpy as np
from jax import lax
from jax.experimental import pallas as pl
from jax.experimental.pallas import tpu as pltpu
from jax.sharding import PartitionSpec as P


TAPS = 10
REACH = 15
ROW_SHAPES = ((1.0, 0), (1.0, 1), (2.0, 0), (2.0, 2), (3.5, 0))
COLUMN_SHAPES = ((1.0, 0), (2.0, 0), (2.0, 1), (3.5, 0))
LANES = 128
SPAN = 18
CHUNKS = (4, 4)
BF = jnp.bfloat16
F32 = jnp.float32


def basis_taps(lags, shapes):
    spots = np.arange(-TAPS, TAPS + 1, dtype=np.float64)
    out = []
    for s, d in shapes:
        full = np.exp(-spots * spots / (2 * s * s)) * (spots / s) ** d
        scale = 1.0 / math.sqrt(np.sum(full * full))
        vals = np.exp(-lags * lags / (2 * s * s)) * (lags / s) ** d * scale
        out.append(np.where(np.abs(lags) <= TAPS, vals, 0.0))
    return np.stack(out)


def detect_taps(lags):
    spots = np.arange(-REACH, REACH + 1, dtype=np.float64)
    total = np.sum(np.exp(-spots * spots / 18.0))
    vals = np.exp(-lags * lags / 18.0) / total - 1.0 / (2 * REACH + 1)
    return np.where(np.abs(lags) <= REACH, vals, 0.0)


def halves(a):
    a = np.asarray(a, np.float32)
    hi = a.astype(jnp.bfloat16)
    lo = (a - hi.astype(np.float32)).astype(jnp.bfloat16)
    return hi, lo


def window_lags(n):
    k = np.arange(256, dtype=np.float64)[:, None] - 64
    return k - np.arange(n, dtype=np.float64)[None, :]


def column_weights():
    bank = basis_taps(window_lags(128), COLUMN_SHAPES)
    nt = np.stack(
        [np.concatenate([bank[0], bank[1]], 1), np.concatenate([bank[2], bank[3]], 1)]
    )
    return halves(nt)


def row_tables():
    lags = (np.arange(16)[None, :] - np.arange(16)[:, None]).astype(np.float64)
    bank = basis_taps(lags, ROW_SHAPES)
    return np.tile(bank, (1, 1, 16)).astype(np.float32)


def split(x):
    hi = x.astype(BF)
    lo = (x - hi.astype(F32)).astype(BF)
    return hi, lo


def mm(a, b):
    return jnp.dot(a, b, preferred_element_type=F32)


def mm3(ah, al, bh, bl):
    return mm(ah, bh) + (mm(al, bh) + mm(ah, bl))


def match_groups(
    at_start, at_end, nt, weights, coeffs, gt, whi, wlo, left, main, right,
    xs_hi, xs_lo, window_at, put, ready=lambda g: None,
):
    def group(g, _):
        ready(g)
        rows = pl.ds(pl.multiple_of(g * 64, 64), 64)
        lane = lax.broadcasted_iota(jnp.int32, (64, LANES), 1)
        blank = jnp.zeros((64, LANES), F32)
        parts = [blank if at_start else left[rows, :]]
        parts += [main[rows, t * LANES : (t + 1) * LANES] for t in range(nt)]
        parts += [blank if at_end else right[rows, :]]
        turned = [pltpu.roll(x, 64, 1) for x in parts]
        for t in range(nt + 1):
            v = jnp.where(lane < 64, turned[t], turned[t + 1])
            hi, lo = split(v)
            xs_hi[:, t * LANES : (t + 1) * LANES] = hi
            xs_lo[:, t * LANES : (t + 1) * LANES] = lo
        stack = lambda ref: jnp.concatenate(
            [ref[:, pl.ds(window_at(w), 256)] for w in range(nt)], axis=0
        )
        x_hi, x_lo = stack(xs_hi), stack(xs_lo)

        lane = lax.broadcasted_iota(jnp.int32, (16, LANES), 1)
        left_hi, left_lo = [], []
        for i in range(4):
            p = g * 4 + i
            w = weights[p]
            pair = []
            for h in range(2):
                acc = None
                for a in range(5):
                    both = jnp.where(lane < 64, coeffs[a, 2 * h, p], coeffs[a, 2 * h + 1, p])
                    term = both * gt[a, :, h * LANES : (h + 1) * LANES]
                    acc = term if acc is None else acc + term
                acc = jnp.where((lane // 16) % 4 == i, acc * w, 0.0)
                pair.append(split(acc))
            left_hi.append(jnp.concatenate([pair[0][0], pair[1][0]], axis=1))
            left_lo.append(jnp.concatenate([pair[0][1], pair[1][1]], axis=1))
        l_hi = jnp.concatenate(left_hi, axis=0)
        l_both = jnp.concatenate(left_hi + left_lo, axis=0)

        cols = []
        for bp in range(2):
            y = mm3(x_hi, x_lo, whi[bp], wlo[bp])
            cols.append(split(y))

        for j0 in range(0, nt, 2):
            windows = range(j0, min(j0 + 2, nt))

            def operand(k):
                blocks = []
                for b in range(4):
                    src = cols[b // 2][k]
                    lanes = slice((b % 2) * LANES, (b % 2 + 1) * LANES)
                    pair = [src[64 * w : 64 * w + 64, lanes] for w in windows]
                    blocks.append(pair[0] if len(pair) == 1 else jnp.concatenate(pair, axis=1))
                return jnp.concatenate(blocks, axis=0)

            zz = mm(l_both, operand(0))
            z = zz[0:64] + (zz[64:128] + mm(l_hi, operand(1)))
            for i in range(4):
                for h in range(2):
                    for w in windows:
                        rows = slice(16 * i + 8 * h, 16 * i + 8 * h + 8)
                        lanes = slice((w - j0) * LANES, (w - j0 + 1) * LANES)
                        put(g * 4 + i, w, h, z[rows, lanes])
        return 0

    lax.fori_loop(0, 8, group, 0)


def slot_kernel(
    nt,
    routes, offsets, weights, coeffs,
    gt_any, whi_any, wlo_any, pieces,
    out,
    xs_hi, xs_lo, gt, whi, wlo, main, cnt, dst, rnk, sems,
):
    tiles = out.shape[1]
    moves = [(whi_any, whi), (wlo_any, wlo), (gt_any, gt)]
    fetches = [pltpu.make_async_copy(a, b, sems.at[i]) for i, (a, b) in enumerate(moves)]

    def rows_of(g):
        rows = pl.ds(pl.multiple_of(g * 64, 64), 64)
        src = pieces.at[rows, 0 : (nt + 1) * LANES]
        return pltpu.make_async_copy(src, main.at[rows, :], sems.at[3 + g])

    rows_of(0).start()
    for fetch in fetches:
        fetch.start()
    for g in range(1, 8):
        rows_of(g).start()

    def clear(i, _):
        cnt[i] = 0
        return 0

    lax.fori_loop(0, 32, clear, 0, unroll=8)

    def place(p, _):
        s = routes[p]
        r = cnt[s]
        cnt[s] = r + 1
        dst[p] = s
        rnk[p] = r
        return 0

    lax.fori_loop(0, 32, place, 0, unroll=4)
    zero = jnp.zeros((8, LANES), F32)

    def wipe(d, _):
        for t in range(tiles):
            out[d, t] = zero
        return 0

    lax.fori_loop(0, 32, wipe, 0, unroll=2)

    lane = lax.broadcasted_iota(jnp.int32, (1, LANES), 1)

    def note(p, _):
        k = offsets[p].astype(F32)
        row = jnp.where(lane == 0, k, weights[p])
        out[dst[p], tiles - 1, pl.ds(rnk[p], 1), :] = row
        return 0

    lax.fori_loop(0, 32, note, 0, unroll=4)

    def put(p, w, h, value):
        out[dst[p], rnk[p] * 2 + (4 * w + h)] = value

    for fetch in fetches:
        fetch.wait()
    match_groups(
        True, False, nt, weights, coeffs, gt, whi, wlo,
        None, main, main.at[:, nt * LANES : (nt + 1) * LANES],
        xs_hi, xs_lo, lambda w: w * LANES, put, lambda g: rows_of(g).wait(),
    )


def spread_kernel(
    at_start, at_end, nt,
    vis, weights, coeffs,
    gt, whi, wlo, left, main, right, meta,
    *refs,
):
    outs, (xs_hi, xs_lo) = refs[:4], refs[4:]
    me = vis[0]

    def put(p, w, h, value):
        outs[w][p * 2 + h] = value

    match_groups(
        at_start, at_end, nt, weights, coeffs, gt, whi, wlo, left, main, right,
        xs_hi, xs_lo, lambda w: pl.multiple_of(((me + w) & 3) * LANES, LANES), put,
    )
    for out in outs:
        out[64] = meta[...]


def full(shape):
    return pl.BlockSpec(shape, lambda i: (0,) * len(shape))


def match_call(kernel, scalars, tables, pieces2d, extra, first, nt, out_shapes, scratch):
    gt, whi, wlo = tables
    width = nt * LANES
    smem = pl.BlockSpec(memory_space=pltpu.SMEM)
    return pl.pallas_call(
        functools.partial(kernel, first == 0, first + nt == 8, nt),
        grid=(1,),
        out_shape=[jax.ShapeDtypeStruct(s, F32) for s in out_shapes],
        in_specs=[smem] * len(scalars)
        + [
            full(gt.shape), full(whi.shape), full(wlo.shape),
            pl.BlockSpec((512, LANES), lambda i: (0, max(first - 1, 0))),
            pl.BlockSpec((512, width), lambda i: (0, first // nt)),
            pl.BlockSpec((512, LANES), lambda i: (0, min(first + nt, 7))),
        ]
        + [full(x.shape) for x in extra],
        out_specs=[full(s) for s in out_shapes],
        scratch_shapes=[
            pltpu.VMEM((64, width + LANES), BF),
            pltpu.VMEM((64, width + LANES), BF),
            *scratch,
        ],
        compiler_params=pltpu.CompilerParams(
            vmem_limit_bytes=(60 << 20) if first == 0 else (24 << 20)
        ),
        cost_estimate=pl.CostEstimate(
            flops=10**9 * nt, bytes_accessed=(1 << 19) * nt, transcendentals=0
        ),
        name="match",
    )(*scalars, gt, whi, wlo, pieces2d, pieces2d, pieces2d, *extra)


def match_slots(scalars, tables, pieces2d, nt):
    smem = pl.BlockSpec(memory_space=pltpu.SMEM)
    any_spec = pl.BlockSpec(memory_space=pl.ANY)
    shape = (32, 4 * nt + 1, 8, LANES)
    width = (nt + 1) * LANES
    return pl.pallas_call(
        functools.partial(slot_kernel, nt),
        grid=(1,),
        out_shape=jax.ShapeDtypeStruct(shape, F32),
        in_specs=[smem] * 4 + [any_spec] * 4,
        out_specs=full(shape),
        scratch_shapes=[
            pltpu.VMEM((64, width), BF),
            pltpu.VMEM((64, width), BF),
            *[pltpu.VMEM(x.shape, x.dtype) for x in tables],
            pltpu.VMEM((512, width), F32),
            *[pltpu.SMEM((32,), jnp.int32)] * 3,
            pltpu.SemaphoreType.DMA((11,)),
        ],
        compiler_params=pltpu.CompilerParams(vmem_limit_bytes=60 << 20),
        cost_estimate=pl.CostEstimate(
            flops=10**9 * nt, bytes_accessed=(1 << 19) * nt, transcendentals=0
        ),
        name="match",
    )(*scalars, *tables, pieces2d)


def pack_kernel(meta, *refs):
    groups, (out, cnt) = refs[:4], refs[4:]
    zero = jnp.zeros((8, LANES), F32)

    def wipe(d, _):
        for t in range(16):
            out[d, t] = zero
        for v in range(4):
            cnt[v * 32 + d] = 0
        return 0

    lax.fori_loop(0, 32, wipe, 0, unroll=2)
    for v in range(4):
        def place(p, _, v=v):
            s = meta[v, 0, p].astype(jnp.int32)
            r = cnt[v * 32 + s]
            cnt[v * 32 + s] = r + 1
            j = 2 * v + r
            for h in range(2):
                out[s, 2 * j + h] = groups[v][p * 2 + h]
            return 0

        lax.fori_loop(0, 32, place, 0, unroll=4)


def pack(meta, groups):
    shape = (32, 16, 8, LANES)
    return pl.pallas_call(
        pack_kernel,
        grid=(1,),
        out_shape=jax.ShapeDtypeStruct(shape, F32),
        in_specs=[pl.BlockSpec(memory_space=pltpu.SMEM)] + [full(x.shape) for x in groups],
        out_specs=full(shape),
        scratch_shapes=[pltpu.SMEM((128,), jnp.int32)],
        compiler_params=pltpu.CompilerParams(vmem_limit_bytes=24 << 20),
        cost_estimate=pl.CostEstimate(flops=10**6, bytes_accessed=4 << 20, transcendentals=0),
        name="pack",
    )(meta, *groups)


def land_kernel(nt, vis_ref, meta, recv, *refs):
    outs, (acc, wsum, spot) = refs[:-3], refs[-3:]
    per = 2 * nt
    zero = jnp.zeros((8, LANES), F32)

    def wipe(i, _):
        for t in range(per):
            acc[i, t] = zero
        return 0

    lax.fori_loop(0, 66, wipe, 0, unroll=3)
    lane = lax.broadcasted_iota(jnp.int32, (8, LANES), 1)
    wsum[...] = zero

    def address(s, _):
        for r in range(2):
            spot[2 * s + r] = meta[s, r, 0].astype(jnp.int32) + 1
        return 0

    lax.fori_loop(0, 32, address, 0, unroll=4)

    def land(s, _):
        for r in range(2):
            at = spot[2 * s + r]
            got = [recv[s, (t // 2) * 4 + 2 * r + t % 2] for t in range(per)]
            for t in range(per):
                acc[at, t] += got[t]
            wsum[...] += jnp.where(lane == at, meta[s, r, 1], 0.0)
        return 0

    lax.fori_loop(0, 32, land, 0, unroll=4)
    own, p1, m1, p2, m2 = outs
    half = SPAN * nt

    def move(ref, start, rel, first):
        base = ((vis_ref[0] + rel) & 3) * 16

        def one(i, _):
            for t in range(per // 2):
                ref[start + (t // 2) * (2 * SPAN) + i * 2 + t % 2] = acc[base + i, first + t]
            return 0

        lax.fori_loop(0, SPAN, one, 0, unroll=3)

    def mass(rel):
        base = ((vis_ref[0] + rel) & 3) * 16
        return pltpu.roll(wsum[...], (LANES - base) & (LANES - 1), 1)

    move(p1, 0, 2, 0)
    p1[half] = zero
    move(p1, half + 1, 1, per // 2)
    move(m1, 0, 2, per // 2)
    m1[half] = mass(2)
    move(m1, half + 1, 3, 0)
    move(p2, 0, 1, 0)
    p2[half] = mass(1)
    move(m2, 0, 3, per // 2)
    m2[half] = mass(3)
    move(own, 0, 0, 0)
    move(own, half, 0, per // 2)
    own[2 * half] = mass(0)


def full_kernel(vis_ref, spot, recv, *refs):
    outs, acc = refs[:-1], refs[-1]
    zero = jnp.zeros((8, LANES), F32)

    def wipe(i, _):
        acc[i, 0] = zero
        acc[i, 1] = zero
        return 0

    lax.fori_loop(0, 66, wipe, 0, unroll=6)

    def land(s, _):
        for j in range(8):
            at = spot[j // 2, s, j % 2] + 1
            got = [recv[s, 2 * j + h] for h in range(2)]
            for h in range(2):
                acc[at, h] += got[h]
        return 0

    lax.fori_loop(0, 32, land, 0, unroll=4)
    for rel in range(4):
        base = ((vis_ref[0] + rel) & 3) * 16

        def one(i, _, rel=rel, base=base):
            for h in range(2):
                outs[rel][i * 2 + h] = acc[base + i, h]
            return 0

        lax.fori_loop(0, SPAN, one, 0, unroll=9)


def land_right(vis, spot, recv):
    smem = pl.BlockSpec(memory_space=pltpu.SMEM)
    vmem = pl.BlockSpec(memory_space=pltpu.VMEM)
    return pl.pallas_call(
        full_kernel,
        out_shape=[jax.ShapeDtypeStruct((2 * SPAN, 8, LANES), F32)] * 4,
        in_specs=[smem, smem, vmem],
        out_specs=[vmem] * 4,
        scratch_shapes=[pltpu.VMEM((66, 2, 8, LANES), F32)],
        compiler_params=pltpu.CompilerParams(vmem_limit_bytes=8 << 20),
        cost_estimate=pl.CostEstimate(flops=10**6, bytes_accessed=4 << 20, transcendentals=0),
        name="land",
    )(vis, spot, recv)


def land_call(kernel, vis, meta, recv, counts, scratch):
    shapes = [(k, 8, LANES) for k in counts]
    smem = pl.BlockSpec(memory_space=pltpu.SMEM)
    return pl.pallas_call(
        kernel,
        grid=(1,),
        out_shape=[jax.ShapeDtypeStruct(s, F32) for s in shapes],
        in_specs=[smem, smem, full(recv.shape)],
        out_specs=[full(s) for s in shapes],
        scratch_shapes=scratch,
        compiler_params=pltpu.CompilerParams(vmem_limit_bytes=24 << 20),
        cost_estimate=pl.CostEstimate(flops=10**6, bytes_accessed=4 << 20, transcendentals=0),
        name="land",
    )(vis, meta, recv)


def inverse_weight(weight, kk):
    lane = lax.broadcasted_iota(jnp.int32, (8, LANES), 1)
    total = jnp.sum(jnp.where(lane == kk, weight, 0.0), axis=1, keepdims=True)
    good = total > 0.0
    return jnp.where(good, 1.0 / jnp.where(good, total, 1.0), 0.0)


def coadd_kernel(nt, own, p1, m1, p2, m2, coadd, mass, *edges):
    half = SPAN * nt
    weight = own[2 * half] + (p2[half] + m2[half])
    mass[...] = weight

    def value(ct, at, h, inverse):
        t = ct * (2 * SPAN) + at * 2 + h
        if ct < nt // 2:
            return (own[t] + (p2[t] + m1[half + 1 + t])) * inverse
        near = t - half
        return (own[t] + (p1[half + 1 + near] + m2[near])) * inverse

    def block(kk, _):
        inverse = inverse_weight(weight, kk + 1)
        for ct in range(nt):
            for h in range(2):
                rows = pl.ds(pl.multiple_of(kk * 16 + 8 * h, 8), 8)
                coadd[rows, ct * LANES : (ct + 1) * LANES] = value(ct, kk + 1, h, inverse)
        return 0

    lax.fori_loop(0, 16, block, 0, unroll=2)
    edges[0][...] = coadd[0:16, :]
    edges[1][...] = coadd[240:256, :]
    for e in range(2):
        at = (SPAN - 1) * e
        inverse = inverse_weight(weight, at)
        for ct in range(nt):
            for h in range(2):
                lanes = slice(ct * LANES, (ct + 1) * LANES)
                edges[2 + e][8 * h : 8 * h + 8, lanes] = value(ct, at, h, inverse)


def first_coadd(group, nt):
    shapes = [(256, 1024), (8, LANES)] + [(16, LANES * nt)] * 4
    blocks = [(256, LANES * nt)] + shapes[1:]
    return pl.pallas_call(
        functools.partial(coadd_kernel, nt),
        grid=(1,),
        out_shape=[jax.ShapeDtypeStruct(s, F32) for s in shapes],
        in_specs=[full(x.shape) for x in group],
        out_specs=[full(s) for s in blocks],
        compiler_params=pltpu.CompilerParams(vmem_limit_bytes=16 << 20),
        cost_estimate=pl.CostEstimate(
            flops=10**6, bytes_accessed=(5 << 17) * nt, transcendentals=0
        ),
        name="coadd",
    )(*group)


def join_kernel(first, vis_ref, mass, *refs):
    group, (top, bottom), out = refs[:4], refs[4:6], refs[6]
    end = vis_ref[0] == 3
    at = jnp.where(end, SPAN - 2, 1)
    inverse = inverse_weight(mass[...], at)
    out[:, : first * LANES] = jnp.where(end, bottom[...], top[...])
    for d in range(4):
        tile = first + ((vis_ref[0] - d) & 3)
        lanes = pl.ds(pl.multiple_of(tile * LANES, LANES), LANES)
        for h in range(2):
            out[8 * h : 8 * h + 8, lanes] = group[d][2 * at + h] * inverse


def join_edges(vis, mass, group, first, top, bottom):
    vmem = pl.BlockSpec(memory_space=pltpu.VMEM)
    return pl.pallas_call(
        functools.partial(join_kernel, first),
        out_shape=jax.ShapeDtypeStruct((16, 1024), F32),
        in_specs=[pl.BlockSpec(memory_space=pltpu.SMEM)] + [vmem] * 7,
        out_specs=vmem,
        compiler_params=pltpu.CompilerParams(vmem_limit_bytes=4 << 20),
        cost_estimate=pl.CostEstimate(flops=10**5, bytes_accessed=1 << 19, transcendentals=0),
        name="join",
    )(vis, mass, *group, top, bottom)


def filtered(parts, dhi, dlo):
    rows = parts[0].shape[0]
    lane = lax.broadcasted_iota(jnp.int32, (rows, LANES), 1)
    turned = [pltpu.roll(x, 64, 1) for x in parts]
    cut = [
        split(jnp.where(lane < 64, turned[t], turned[t + 1])) for t in range(len(parts) - 1)
    ]
    window = lambda k: jnp.concatenate(
        [
            jnp.concatenate([cut[j][k], cut[j + 1][k]], axis=1)
            for j in range(len(parts) - 2)
        ],
        axis=0,
    )
    return split(mm3(window(0), window(1), dhi[...], dlo[...]))


def detect_tiles(n, tile, tables, y_hi, y_lo, out, done, between):
    dhi, dlo, bhi, blo = tables[:4]

    def group(g, _):
        rows = pl.ds(pl.multiple_of(g * 64, 64), 64)
        hi, lo = filtered([tile(t, rows) for t in range(n + 2)], dhi, dlo)
        for j in range(n):
            y_hi[rows, j * LANES : (j + 1) * LANES] = hi[64 * j : 64 * j + 64]
            y_lo[rows, j * LANES : (j + 1) * LANES] = lo[64 * j : 64 * j + 64]
        return 0

    lax.fori_loop(0, 4, group, 0, unroll=2)
    between()
    for j0 in range(0, n, 2):
        lanes = slice(j0 * LANES, min(j0 + 2, n) * LANES)
        out[:, lanes] = mm3(bhi[...], blo[...], y_hi[:, lanes], y_lo[:, lanes])
        done(j0, lanes)


def early_kernel(n, *refs):
    tables, (x, out, rim, context, y_hi, y_lo) = refs[:4], refs[4:]
    context[...] = x[:, (n - 1) * LANES : (n + 1) * LANES]

    def tile(t, rows):
        if t == 0:
            return jnp.zeros((64, LANES), F32)
        return x[rows, (t - 1) * LANES : t * LANES]

    detect_tiles(n, tile, tables, y_hi, y_lo, out, lambda *_: None, lambda: None)
    rim[0:16, :] = out[0:16, :]
    rim[16:32, :] = out[240:256, :]


def early_detect(n, coadd, tables):
    tables = tables[:4]
    width = (n + 1) * LANES
    return pl.pallas_call(
        functools.partial(early_kernel, n),
        grid=(1,),
        out_shape=[
            jax.ShapeDtypeStruct(coadd.shape, F32),
            jax.ShapeDtypeStruct((32, n * LANES), F32),
            jax.ShapeDtypeStruct((256, 2 * LANES), F32),
        ],
        in_specs=[full(a.shape) for a in tables] + [full((256, width))],
        out_specs=[full((256, n * LANES)), full((32, n * LANES)), full((256, 2 * LANES))],
        scratch_shapes=[pltpu.VMEM((256, n * LANES), BF), pltpu.VMEM((256, n * LANES), BF)],
        compiler_params=pltpu.CompilerParams(vmem_limit_bytes=16 << 20),
        cost_estimate=pl.CostEstimate(
            flops=10**9, bytes_accessed=1 << 20, transcendentals=0
        ),
        name="early",
    )(*tables, coadd)


def late_kernel(first, nt, n, vis_ref, mass, *refs):
    tables, group, (before, after, left, rim) = refs[:6], refs[6:10], refs[10:14]
    coadd_out, out, sides, coadd, y_hi, y_lo, det, near, sems = refs[16:]
    weight = mass[...]
    last = first + nt
    start = last - n - 1
    copies = []

    def send(src, dst):
        copy = pltpu.make_async_copy(src, dst, sems.at[len(copies)])
        copy.start()
        copies.append(copy)

    def block(i, _):
        inverse = inverse_weight(weight, i + 1)
        for d in range(4):
            lanes = pl.ds(pl.multiple_of(((vis_ref[0] - d) & 3) * LANES, LANES), LANES)
            for h in range(2):
                rows = pl.ds(pl.multiple_of(i * 16 + 8 * h, 8), 8)
                coadd[rows, lanes] = group[d][i * 2 + (2 + h)] * inverse
        return 0

    lax.fori_loop(0, 16, block, 0, unroll=4)
    send(coadd, coadd_out.at[:, first * LANES : last * LANES])

    def tile(t, rows):
        real = start + t
        if real >= last:
            return jnp.zeros((64, LANES), F32)
        if real < first:
            return left[rows, t * LANES : (t + 1) * LANES]
        return coadd[rows, (real - first) * LANES : (real - first + 1) * LANES]

    whole_left = slice(0, (start + 1) * LANES)

    def between():
        for e in range(2):
            inverse = inverse_weight(weight, (SPAN - 1) * e)
            for d in range(4):
                lanes = pl.ds(pl.multiple_of(((vis_ref[0] - d) & 3) * LANES, LANES), LANES)
                for h in range(2):
                    rows = slice(16 * e + 8 * h, 16 * e + 8 * h + 8)
                    near[rows, lanes] = group[d][2 * (SPAN - 1) * e + h] * inverse
        strips = [jnp.zeros((32, LANES), F32)]
        for t in range(last):
            lanes = slice(t * LANES, (t + 1) * LANES)
            if t < first:
                own = jnp.concatenate([before[:, lanes], after[:, lanes]], axis=0)
            else:
                own = near[:, (t - first) * LANES : (t - first + 1) * LANES]
            strips.append(own)
        hi, lo = filtered(strips + strips[:1], tables[0], tables[1])
        side = lambda v: jnp.concatenate([v[32 * j : 32 * j + 32] for j in range(last)], axis=1)
        sides[...] = mm3(tables[4][...], tables[5][...], side(hi), side(lo))
        sides[:, whole_left] += rim[...]

    def done(j0, lanes):
        there = slice((start + 1) * LANES + lanes.start, (start + 1) * LANES + lanes.stop)
        sides[0:16, there] += det[0:16, lanes]
        sides[16:32, there] += det[240:256, lanes]
        det[0:16, lanes] = sides[0:16, there]
        det[240:256, lanes] = sides[16:32, there]
        send(det.at[:, lanes], out.at[:, there])

    detect_tiles(n, tile, tables, y_hi, y_lo, det, done, between)
    send(sides.at[0:16, whole_left], out.at[0:16, whole_left])
    send(sides.at[16:32, whole_left], out.at[240:256, whole_left])
    for copy in copies:
        copy.wait()


def late_detect(vis, mass, group, first, nt, n, halos, tables, left, coadd, before):
    detection, rim = before
    any_spec = pl.BlockSpec(memory_space=pl.ANY)
    vmem = pl.BlockSpec(memory_space=pltpu.VMEM)
    args = [vis, mass, *tables, *group, *halos, left, rim, coadd, detection]
    return pl.pallas_call(
        functools.partial(late_kernel, first, nt, n),
        out_shape=[jax.ShapeDtypeStruct(coadd.shape, F32)] * 2
        + [jax.ShapeDtypeStruct((32, (first + nt) * LANES), F32)],
        in_specs=[pl.BlockSpec(memory_space=pltpu.SMEM)]
        + [vmem] * (len(args) - 3)
        + [any_spec] * 2,
        out_specs=[any_spec] * 2 + [vmem],
        scratch_shapes=[
            pltpu.VMEM((256, nt * LANES), F32),
            pltpu.VMEM((256, n * LANES), BF),
            pltpu.VMEM((256, n * LANES), BF),
            pltpu.VMEM((256, n * LANES), F32),
            pltpu.VMEM((32, nt * LANES), F32),
            pltpu.SemaphoreType.DMA((3 + (n + 1) // 2,)),
        ],
        input_output_aliases={len(args) - 2: 0, len(args) - 1: 1},
        compiler_params=pltpu.CompilerParams(vmem_limit_bytes=12 << 20),
        cost_estimate=pl.CostEstimate(
            flops=2 * 10**9, bytes_accessed=4 << 20, transcendentals=0
        ),
        name="late",
    )(*args)


def end_kernel(vis_ref, dhi, dlo, ehi, elo, other, sides, unused, out, rows, sem):
    me = vis_ref[0]
    n = other.shape[1] // LANES

    @pl.when((me == 0) | (me == 3))
    def _():
        strips = [jnp.zeros((16, LANES), F32)]
        strips += [other[:, t * LANES : (t + 1) * LANES] for t in range(n)]
        hi, lo = filtered(strips + strips[:1], dhi, dlo)
        side = lambda v: jnp.concatenate([v[16 * j : 16 * j + 16] for j in range(n)], axis=1)
        both = mm3(ehi[...], elo[...], side(hi), side(lo))
        rows[...] = jnp.where(
            me == 0, sides[0:16] + both[0:16], sides[16:32] + both[16:32]
        )
        at = pl.ds(pl.multiple_of(jnp.where(me == 0, 0, 240), 16), 16)
        copy = pltpu.make_async_copy(rows, out.at[at, :], sem)
        copy.start()
        copy.wait()


def end_detect(vis, tables, other, sides, detection):
    any_spec = pl.BlockSpec(memory_space=pl.ANY)
    vmem = pl.BlockSpec(memory_space=pltpu.VMEM)
    dhi, dlo = tables[:2]
    ehi, elo = tables[6:]
    return pl.pallas_call(
        end_kernel,
        out_shape=jax.ShapeDtypeStruct(detection.shape, F32),
        in_specs=[pl.BlockSpec(memory_space=pltpu.SMEM)] + [vmem] * 6 + [any_spec],
        out_specs=any_spec,
        scratch_shapes=[pltpu.VMEM(other.shape, F32), pltpu.SemaphoreType.DMA],
        input_output_aliases={7: 0},
        compiler_params=pltpu.CompilerParams(vmem_limit_bytes=4 << 20),
        cost_estimate=pl.CostEstimate(flops=10**8, bytes_accessed=1 << 18, transcendentals=0),
        name="end",
    )(vis, dhi, dlo, ehi, elo, other, sides, detection)


def detect_tables():
    dhi, dlo = halves(detect_taps(window_lags(128)))
    idx = np.arange(256, dtype=np.float64)
    bhi, blo = halves(detect_taps(idx[None, :] - idx[:, None]))
    q = np.arange(16, dtype=np.float64)
    edge = np.zeros((32, 32))
    edge[0:16, 0:16] = detect_taps((q[None, :] - 16) - q[:, None])
    edge[16:32, 16:32] = detect_taps((q[None, :] + 16) - q[:, None])
    ehi, elo = halves(edge)
    fhi, flo = halves(edge[:, 0:16] + edge[:, 16:32])
    return dhi, dlo, bhi, blo, ehi, elo, fhi, flo


def shards(pieces, coeffs, weights, routes, offsets):
    count, rows, width = pieces.shape
    pieces2d = pieces.reshape(count * rows, width)
    route1 = routes.reshape(count)
    coeffs_t = jnp.transpose(coeffs, (1, 2, 0))
    whi, wlo = column_weights()
    tables = (jnp.asarray(row_tables()), jnp.asarray(whi), jnp.asarray(wlo))
    dtables = tuple(jnp.asarray(a) for a in detect_tables())
    vis = lax.axis_index("vis").reshape(1)
    nv = lax.axis_size("vis")
    n = lax.axis_size("tile") * nv
    shifts = [[(i, (i + d) % nv) for i in range(nv)] for d in (1, 2, 3)]
    axes = ("tile", "vis")

    first, nt = CHUNKS
    per = 2 * first

    def over_vis(group):
        moved = [group[0]]
        for d in (0, 2, 1):
            moved.append(lax.ppermute(group[d + 1], "vis", shifts[d]))
        return [moved[0], moved[1], moved[3], moved[2]]

    def over_tile(slots):
        return lax.all_to_all(slots, "tile", split_axis=0, concat_axis=0, tiled=True)

    slots = match_slots((route1, offsets, weights, coeffs_t), tables, pieces2d, first)
    recv = over_tile(slots)
    meta = recv[:, 4 * first, 0:2, 0:2]
    landed = land_call(
        functools.partial(land_kernel, first), vis, meta, recv, [SPAN * per + 1] * 3 + [SPAN * first + 1] * 2,
        [
            pltpu.VMEM((66, per, 8, LANES), F32),
            pltpu.VMEM((8, LANES), F32),
            pltpu.SMEM((64,), jnp.int32),
        ],
    )
    blocks = jnp.pad(meta[:, :, 0].T, ((0, 6), (0, LANES - count)))
    told = over_vis([blocks] * nv)
    spot = jnp.stack([x[0:2, 0:count] for x in told]).astype(jnp.int32)
    spot = jnp.transpose(spot, (0, 2, 1))
    own, p1, m1, p2, m2 = landed
    head = p2.shape[0]
    p1 = lax.ppermute(p1, "vis", shifts[0])
    m1 = lax.ppermute(m1, "vis", shifts[2])
    p2 = lax.ppermute(p2 + p1[:head], "vis", shifts[0])
    m2 = lax.ppermute(m2 + m1[:head], "vis", shifts[2])

    facts = jnp.stack([route1.astype(F32), offsets.astype(F32)])
    facts = jnp.pad(facts, ((0, 6), (0, LANES - count)))
    spread = match_call(
        spread_kernel, (vis, weights, coeffs_t), tables, pieces2d, (facts,), first, nt,
        [(2 * count + 1, 8, LANES)] * 4, [],
    )
    traded = over_vis(spread)
    notes = jnp.stack([x[2 * count, 0:2, 0:count] for x in traded])
    slots = pack(notes, traded)
    recv = over_tile(slots)
    landed = land_right(vis, spot, recv)
    bulk = over_vis(landed)

    coadd, mass, top, bottom, *outside = first_coadd((own, p1, m1, p2, m2), first)
    edge = join_edges(vis, mass, bulk, first, top, bottom)
    swaps = [(i - 1, i) for i in range(nv, n, nv)] + [(i, i - 1) for i in range(nv, n, nv)]
    other = lax.ppermute(edge, axes, swaps)
    *before, left = early_detect(first - 1, coadd, dtables)
    coadd, detection, sides = late_detect(
        vis, mass, bulk, first, nt, nt + 1, outside, dtables[:6], left, coadd, before
    )
    detection = end_detect(vis, dtables, other, sides, detection)
    return (coadd, detection)


def solution(mesh):
    placed = (
        P(("tile", "vis"), None, None),
        P(("tile", "vis"), None, None),
        P(("tile", "vis")),
        P(("tile", "vis"), None),
        P(("tile", "vis")),
    )
    return jax.shard_map(
        shards,
        mesh=mesh,
        in_specs=placed,
        out_specs=(P(("tile", "vis"), None), P(("tile", "vis"), None)),
        check_vma=False,
    )
```

```python
import functools
import math

import jax
import jax.numpy as jnp
import numpy as np
from jax import lax
from jax.experimental import pallas as pl
from jax.experimental.pallas import tpu as pltpu
from jax.sharding import PartitionSpec as P


TAPS = 10
REACH = 15
ROW_SHAPES = ((1.0, 0), (1.0, 1), (2.0, 0), (2.0, 2), (3.5, 0))
COLUMN_SHAPES = ((1.0, 0), (2.0, 0), (2.0, 1), (3.5, 0))
LANES = 128
SPAN = 18
CHUNKS = (4, 4)
BF = jnp.bfloat16
F32 = jnp.float32


def basis_taps(lags, shapes):
    spots = np.arange(-TAPS, TAPS + 1, dtype=np.float64)
    out = []
    for s, d in shapes:
        full = np.exp(-spots * spots / (2 * s * s)) * (spots / s) ** d
        scale = 1.0 / math.sqrt(np.sum(full * full))
        vals = np.exp(-lags * lags / (2 * s * s)) * (lags / s) ** d * scale
        out.append(np.where(np.abs(lags) <= TAPS, vals, 0.0))
    return np.stack(out)


def detect_taps(lags):
    spots = np.arange(-REACH, REACH + 1, dtype=np.float64)
    total = np.sum(np.exp(-spots * spots / 18.0))
    vals = np.exp(-lags * lags / 18.0) / total - 1.0 / (2 * REACH + 1)
    return np.where(np.abs(lags) <= REACH, vals, 0.0)


def halves(a):
    a = np.asarray(a, np.float32)
    hi = a.astype(jnp.bfloat16)
    lo = (a - hi.astype(np.float32)).astype(jnp.bfloat16)
    return hi, lo


def window_lags(n):
    k = np.arange(256, dtype=np.float64)[:, None] - 64
    return k - np.arange(n, dtype=np.float64)[None, :]


def column_weights():
    bank = basis_taps(window_lags(128), COLUMN_SHAPES)
    nt = np.stack(
        [np.concatenate([bank[0], bank[1]], 1), np.concatenate([bank[2], bank[3]], 1)]
    )
    return halves(nt)


def row_tables():
    lags = (np.arange(16)[None, :] - np.arange(16)[:, None]).astype(np.float64)
    bank = basis_taps(lags, ROW_SHAPES)
    return np.tile(bank, (1, 1, 16)).astype(np.float32)


def split(x):
    hi = x.astype(BF)
    lo = (x - hi.astype(F32)).astype(BF)
    return hi, lo


def mm(a, b):
    return jnp.dot(a, b, preferred_element_type=F32)


def mm3(ah, al, bh, bl):
    return mm(ah, bh) + (mm(al, bh) + mm(ah, bl))


def match_groups(
    at_start, at_end, nt, weights, coeffs, gt, whi, wlo, left, main, right,
    xs_hi, xs_lo, window_at, put, ready=lambda g: None,
):
    def group(g, _):
        ready(g)
        rows = pl.ds(pl.multiple_of(g * 64, 64), 64)
        lane = lax.broadcasted_iota(jnp.int32, (64, LANES), 1)
        blank = jnp.zeros((64, LANES), F32)
        parts = [blank if at_start else left[rows, :]]
        parts += [main[rows, t * LANES : (t + 1) * LANES] for t in range(nt)]
        parts += [blank if at_end else right[rows, :]]
        turned = [pltpu.roll(x, 64, 1) for x in parts]
        for t in range(nt + 1):
            v = jnp.where(lane < 64, turned[t], turned[t + 1])
            hi, lo = split(v)
            xs_hi[:, t * LANES : (t + 1) * LANES] = hi
            xs_lo[:, t * LANES : (t + 1) * LANES] = lo
        stack = lambda ref: jnp.concatenate(
            [ref[:, pl.ds(window_at(w), 256)] for w in range(nt)], axis=0
        )
        x_hi, x_lo = stack(xs_hi), stack(xs_lo)

        lane = lax.broadcasted_iota(jnp.int32, (16, LANES), 1)
        left_hi, left_lo = [], []
        for i in range(4):
            p = g * 4 + i
            w = weights[p]
            pair = []
            for h in range(2):
                acc = None
                for a in range(5):
                    both = jnp.where(lane < 64, coeffs[a, 2 * h, p], coeffs[a, 2 * h + 1, p])
                    term = both * gt[a, :, h * LANES : (h + 1) * LANES]
                    acc = term if acc is None else acc + term
                acc = jnp.where((lane // 16) % 4 == i, acc * w, 0.0)
                pair.append(split(acc))
            left_hi.append(jnp.concatenate([pair[0][0], pair[1][0]], axis=1))
            left_lo.append(jnp.concatenate([pair[0][1], pair[1][1]], axis=1))
        l_hi = jnp.concatenate(left_hi, axis=0)
        l_both = jnp.concatenate(left_hi + left_lo, axis=0)

        cols = []
        for bp in range(2):
            y = mm3(x_hi, x_lo, whi[bp], wlo[bp])
            cols.append(split(y))

        for j0 in range(0, nt, 2):
            windows = range(j0, min(j0 + 2, nt))

            def operand(k):
                blocks = []
                for b in range(4):
                    src = cols[b // 2][k]
                    lanes = slice((b % 2) * LANES, (b % 2 + 1) * LANES)
                    pair = [src[64 * w : 64 * w + 64, lanes] for w in windows]
                    blocks.append(pair[0] if len(pair) == 1 else jnp.concatenate(pair, axis=1))
                return jnp.concatenate(blocks, axis=0)

            zz = mm(l_both, operand(0))
            z = zz[0:64] + (zz[64:128] + mm(l_hi, operand(1)))
            for i in range(4):
                for h in range(2):
                    for w in windows:
                        rows = slice(16 * i + 8 * h, 16 * i + 8 * h + 8)
                        lanes = slice((w - j0) * LANES, (w - j0 + 1) * LANES)
                        put(g * 4 + i, w, h, z[rows, lanes])
        return 0

    lax.fori_loop(0, 8, group, 0)


def slot_kernel(
    nt,
    routes, offsets, weights, coeffs,
    gt_any, whi_any, wlo_any, pieces,
    out,
    xs_hi, xs_lo, gt, whi, wlo, main, cnt, dst, rnk, sems,
):
    tiles = out.shape[1]
    moves = [(whi_any, whi), (wlo_any, wlo), (gt_any, gt)]
    fetches = [pltpu.make_async_copy(a, b, sems.at[i]) for i, (a, b) in enumerate(moves)]

    def rows_of(g):
        rows = pl.ds(pl.multiple_of(g * 64, 64), 64)
        src = pieces.at[rows, 0 : (nt + 1) * LANES]
        return pltpu.make_async_copy(src, main.at[rows, :], sems.at[3 + g])

    rows_of(0).start()
    for fetch in fetches:
        fetch.start()
    for g in range(1, 8):
        rows_of(g).start()

    def clear(i, _):
        cnt[i] = 0
        return 0

    lax.fori_loop(0, 32, clear, 0, unroll=8)

    def place(p, _):
        s = routes[p]
        r = cnt[s]
        cnt[s] = r + 1
        dst[p] = s
        rnk[p] = r
        return 0

    lax.fori_loop(0, 32, place, 0, unroll=4)
    zero = jnp.zeros((8, LANES), F32)

    def wipe(d, _):
        for t in range(tiles):
            out[d, t] = zero
        return 0

    lax.fori_loop(0, 32, wipe, 0, unroll=2)

    lane = lax.broadcasted_iota(jnp.int32, (1, LANES), 1)

    def note(p, _):
        k = offsets[p].astype(F32)
        row = jnp.where(lane == 0, k, weights[p])
        out[dst[p], tiles - 1, pl.ds(rnk[p], 1), :] = row
        return 0

    lax.fori_loop(0, 32, note, 0, unroll=4)

    def put(p, w, h, value):
        out[dst[p], rnk[p] * 2 + (4 * w + h)] = value

    for fetch in fetches:
        fetch.wait()
    match_groups(
        True, False, nt, weights, coeffs, gt, whi, wlo,
        None, main, main.at[:, nt * LANES : (nt + 1) * LANES],
        xs_hi, xs_lo, lambda w: w * LANES, put, lambda g: rows_of(g).wait(),
    )


def spread_kernel(
    at_start, at_end, nt,
    vis, weights, coeffs,
    gt, whi, wlo, left, main, right, meta,
    *refs,
):
    outs, (xs_hi, xs_lo) = refs[:4], refs[4:]
    me = vis[0]

    def put(p, w, h, value):
        outs[w][p * 2 + h] = value

    match_groups(
        at_start, at_end, nt, weights, coeffs, gt, whi, wlo, left, main, right,
        xs_hi, xs_lo, lambda w: pl.multiple_of(((me + w) & 3) * LANES, LANES), put,
    )
    for out in outs:
        out[64] = meta[...]


def full(shape):
    return pl.BlockSpec(shape, lambda i: (0,) * len(shape))


def match_call(kernel, scalars, tables, pieces2d, extra, first, nt, out_shapes, scratch):
    gt, whi, wlo = tables
    width = nt * LANES
    smem = pl.BlockSpec(memory_space=pltpu.SMEM)
    return pl.pallas_call(
        functools.partial(kernel, first == 0, first + nt == 8, nt),
        grid=(1,),
        out_shape=[jax.ShapeDtypeStruct(s, F32) for s in out_shapes],
        in_specs=[smem] * len(scalars)
        + [
            full(gt.shape), full(whi.shape), full(wlo.shape),
            pl.BlockSpec((512, LANES), lambda i: (0, max(first - 1, 0))),
            pl.BlockSpec((512, width), lambda i: (0, first // nt)),
            pl.BlockSpec((512, LANES), lambda i: (0, min(first + nt, 7))),
        ]
        + [full(x.shape) for x in extra],
        out_specs=[full(s) for s in out_shapes],
        scratch_shapes=[
            pltpu.VMEM((64, width + LANES), BF),
            pltpu.VMEM((64, width + LANES), BF),
            *scratch,
        ],
        compiler_params=pltpu.CompilerParams(
            vmem_limit_bytes=(60 << 20) if first == 0 else (24 << 20)
        ),
        cost_estimate=pl.CostEstimate(
            flops=10**9 * nt, bytes_accessed=(1 << 19) * nt, transcendentals=0
        ),
        name="match",
    )(*scalars, gt, whi, wlo, pieces2d, pieces2d, pieces2d, *extra)


def match_slots(scalars, tables, pieces2d, nt):
    smem = pl.BlockSpec(memory_space=pltpu.SMEM)
    any_spec = pl.BlockSpec(memory_space=pl.ANY)
    shape = (32, 4 * nt + 1, 8, LANES)
    width = (nt + 1) * LANES
    return pl.pallas_call(
        functools.partial(slot_kernel, nt),
        grid=(1,),
        out_shape=jax.ShapeDtypeStruct(shape, F32),
        in_specs=[smem] * 4 + [any_spec] * 4,
        out_specs=full(shape),
        scratch_shapes=[
            pltpu.VMEM((64, width), BF),
            pltpu.VMEM((64, width), BF),
            *[pltpu.VMEM(x.shape, x.dtype) for x in tables],
            pltpu.VMEM((512, width), F32),
            *[pltpu.SMEM((32,), jnp.int32)] * 3,
            pltpu.SemaphoreType.DMA((11,)),
        ],
        compiler_params=pltpu.CompilerParams(vmem_limit_bytes=60 << 20),
        cost_estimate=pl.CostEstimate(
            flops=10**9 * nt, bytes_accessed=(1 << 19) * nt, transcendentals=0
        ),
        name="match",
    )(*scalars, *tables, pieces2d)


def pack_kernel(meta, *refs):
    groups, (out, cnt) = refs[:4], refs[4:]
    zero = jnp.zeros((8, LANES), F32)

    def wipe(d, _):
        for t in range(16):
            out[d, t] = zero
        for v in range(4):
            cnt[v * 32 + d] = 0
        return 0

    lax.fori_loop(0, 32, wipe, 0, unroll=2)
    for v in range(4):
        def place(p, _, v=v):
            s = meta[v, 0, p].astype(jnp.int32)
            r = cnt[v * 32 + s]
            cnt[v * 32 + s] = r + 1
            j = 2 * v + r
            for h in range(2):
                out[s, 2 * j + h] = groups[v][p * 2 + h]
            return 0

        lax.fori_loop(0, 32, place, 0, unroll=4)


def pack(meta, groups):
    shape = (32, 16, 8, LANES)
    return pl.pallas_call(
        pack_kernel,
        grid=(1,),
        out_shape=jax.ShapeDtypeStruct(shape, F32),
        in_specs=[pl.BlockSpec(memory_space=pltpu.SMEM)] + [full(x.shape) for x in groups],
        out_specs=full(shape),
        scratch_shapes=[pltpu.SMEM((128,), jnp.int32)],
        compiler_params=pltpu.CompilerParams(vmem_limit_bytes=24 << 20),
        cost_estimate=pl.CostEstimate(flops=10**6, bytes_accessed=4 << 20, transcendentals=0),
        name="pack",
    )(meta, *groups)


def land_kernel(nt, vis_ref, meta, recv, *refs):
    outs, (acc, wsum, spot) = refs[:-3], refs[-3:]
    per = 2 * nt
    zero = jnp.zeros((8, LANES), F32)

    def wipe(i, _):
        for t in range(per):
            acc[i, t] = zero
        return 0

    lax.fori_loop(0, 66, wipe, 0, unroll=3)
    lane = lax.broadcasted_iota(jnp.int32, (8, LANES), 1)
    wsum[...] = zero

    def address(s, _):
        for r in range(2):
            spot[2 * s + r] = meta[s, r, 0].astype(jnp.int32) + 1
        return 0

    lax.fori_loop(0, 32, address, 0, unroll=4)

    def land(s, _):
        for r in range(2):
            at = spot[2 * s + r]
            got = [recv[s, (t // 2) * 4 + 2 * r + t % 2] for t in range(per)]
            for t in range(per):
                acc[at, t] += got[t]
            wsum[...] += jnp.where(lane == at, meta[s, r, 1], 0.0)
        return 0

    lax.fori_loop(0, 32, land, 0, unroll=4)
    own, p1, m1, p2, m2 = outs
    half = SPAN * nt

    def move(ref, start, rel, first):
        base = ((vis_ref[0] + rel) & 3) * 16

        def one(i, _):
            for t in range(per // 2):
                ref[start + (t // 2) * (2 * SPAN) + i * 2 + t % 2] = acc[base + i, first + t]
            return 0

        lax.fori_loop(0, SPAN, one, 0, unroll=3)

    def mass(rel):
        base = ((vis_ref[0] + rel) & 3) * 16
        return pltpu.roll(wsum[...], (LANES - base) & (LANES - 1), 1)

    move(p1, 0, 2, 0)
    p1[half] = zero
    move(p1, half + 1, 1, per // 2)
    move(m1, 0, 2, per // 2)
    m1[half] = mass(2)
    move(m1, half + 1, 3, 0)
    move(p2, 0, 1, 0)
    p2[half] = mass(1)
    move(m2, 0, 3, per // 2)
    m2[half] = mass(3)
    move(own, 0, 0, 0)
    move(own, half, 0, per // 2)
    own[2 * half] = mass(0)


def full_kernel(vis_ref, spot, recv, *refs):
    outs, accs = refs[:-2], refs[-2:]
    zero = jnp.zeros((8, LANES), F32)

    def wipe(i, _):
        for acc in accs:
            acc[i, 0] = zero
            acc[i, 1] = zero
        return 0

    lax.fori_loop(0, 66, wipe, 0, unroll=6)

    def land(s, _):
        for j in range(8):
            at = spot[j // 2, s, j % 2] + 1
            got = [recv[s, 2 * j + h] for h in range(2)]
            for h in range(2):
                accs[j % 2][at, h] += got[h]
        return 0

    lax.fori_loop(0, 32, land, 0, unroll=4)
    for rel in range(4):
        base = ((vis_ref[0] + rel) & 3) * 16

        def one(i, _, rel=rel, base=base):
            for h in range(2):
                outs[rel][i * 2 + h] = accs[0][base + i, h] + accs[1][base + i, h]
            return 0

        lax.fori_loop(0, SPAN, one, 0, unroll=9)


def land_right(vis, spot, recv):
    smem = pl.BlockSpec(memory_space=pltpu.SMEM)
    vmem = pl.BlockSpec(memory_space=pltpu.VMEM)
    return pl.pallas_call(
        full_kernel,
        out_shape=[jax.ShapeDtypeStruct((2 * SPAN, 8, LANES), F32)] * 4,
        in_specs=[smem, smem, vmem],
        out_specs=[vmem] * 4,
        scratch_shapes=[pltpu.VMEM((66, 2, 8, LANES), F32)] * 2,
        compiler_params=pltpu.CompilerParams(vmem_limit_bytes=8 << 20),
        cost_estimate=pl.CostEstimate(flops=10**6, bytes_accessed=4 << 20, transcendentals=0),
        name="land",
    )(vis, spot, recv)


def land_call(kernel, vis, meta, recv, counts, scratch):
    shapes = [(k, 8, LANES) for k in counts]
    smem = pl.BlockSpec(memory_space=pltpu.SMEM)
    return pl.pallas_call(
        kernel,
        grid=(1,),
        out_shape=[jax.ShapeDtypeStruct(s, F32) for s in shapes],
        in_specs=[smem, smem, full(recv.shape)],
        out_specs=[full(s) for s in shapes],
        scratch_shapes=scratch,
        compiler_params=pltpu.CompilerParams(vmem_limit_bytes=24 << 20),
        cost_estimate=pl.CostEstimate(flops=10**6, bytes_accessed=4 << 20, transcendentals=0),
        name="land",
    )(vis, meta, recv)


def inverse_weight(weight, kk):
    lane = lax.broadcasted_iota(jnp.int32, (8, LANES), 1)
    total = jnp.sum(jnp.where(lane == kk, weight, 0.0), axis=1, keepdims=True)
    good = total > 0.0
    return jnp.where(good, 1.0 / jnp.where(good, total, 1.0), 0.0)


def coadd_kernel(nt, own, p1, m1, p2, m2, coadd, mass, *edges):
    half = SPAN * nt
    weight = own[2 * half] + (p2[half] + m2[half])
    mass[...] = weight

    def value(ct, at, h, inverse):
        t = ct * (2 * SPAN) + at * 2 + h
        if ct < nt // 2:
            return (own[t] + (p2[t] + m1[half + 1 + t])) * inverse
        near = t - half
        return (own[t] + (p1[half + 1 + near] + m2[near])) * inverse

    def block(kk, _):
        inverse = inverse_weight(weight, kk + 1)
        for ct in range(nt):
            for h in range(2):
                rows = pl.ds(pl.multiple_of(kk * 16 + 8 * h, 8), 8)
                coadd[rows, ct * LANES : (ct + 1) * LANES] = value(ct, kk + 1, h, inverse)
        return 0

    lax.fori_loop(0, 16, block, 0, unroll=2)
    edges[0][...] = coadd[0:16, :]
    edges[1][...] = coadd[240:256, :]
    for e in range(2):
        at = (SPAN - 1) * e
        inverse = inverse_weight(weight, at)
        for ct in range(nt):
            for h in range(2):
                lanes = slice(ct * LANES, (ct + 1) * LANES)
                edges[2 + e][8 * h : 8 * h + 8, lanes] = value(ct, at, h, inverse)


def first_coadd(group, nt):
    shapes = [(256, 1024), (8, LANES)] + [(16, LANES * nt)] * 4
    blocks = [(256, LANES * nt)] + shapes[1:]
    return pl.pallas_call(
        functools.partial(coadd_kernel, nt),
        grid=(1,),
        out_shape=[jax.ShapeDtypeStruct(s, F32) for s in shapes],
        in_specs=[full(x.shape) for x in group],
        out_specs=[full(s) for s in blocks],
        compiler_params=pltpu.CompilerParams(vmem_limit_bytes=16 << 20),
        cost_estimate=pl.CostEstimate(
            flops=10**6, bytes_accessed=(5 << 17) * nt, transcendentals=0
        ),
        name="coadd",
    )(*group)


def join_kernel(first, vis_ref, mass, *refs):
    group, (top, bottom), out = refs[:4], refs[4:6], refs[6]
    end = vis_ref[0] == 3
    at = jnp.where(end, SPAN - 2, 1)
    inverse = inverse_weight(mass[...], at)
    out[:, : first * LANES] = jnp.where(end, bottom[...], top[...])
    for d in range(4):
        tile = first + ((vis_ref[0] - d) & 3)
        lanes = pl.ds(pl.multiple_of(tile * LANES, LANES), LANES)
        for h in range(2):
            out[8 * h : 8 * h + 8, lanes] = group[d][2 * at + h] * inverse


def join_edges(vis, mass, group, first, top, bottom):
    vmem = pl.BlockSpec(memory_space=pltpu.VMEM)
    return pl.pallas_call(
        functools.partial(join_kernel, first),
        out_shape=jax.ShapeDtypeStruct((16, 1024), F32),
        in_specs=[pl.BlockSpec(memory_space=pltpu.SMEM)] + [vmem] * 7,
        out_specs=vmem,
        compiler_params=pltpu.CompilerParams(vmem_limit_bytes=4 << 20),
        cost_estimate=pl.CostEstimate(flops=10**5, bytes_accessed=1 << 19, transcendentals=0),
        name="join",
    )(vis, mass, *group, top, bottom)


def filtered(parts, dhi, dlo):
    rows = parts[0].shape[0]
    lane = lax.broadcasted_iota(jnp.int32, (rows, LANES), 1)
    turned = [pltpu.roll(x, 64, 1) for x in parts]
    cut = [
        split(jnp.where(lane < 64, turned[t], turned[t + 1])) for t in range(len(parts) - 1)
    ]
    window = lambda k: jnp.concatenate(
        [
            jnp.concatenate([cut[j][k], cut[j + 1][k]], axis=1)
            for j in range(len(parts) - 2)
        ],
        axis=0,
    )
    return split(mm3(window(0), window(1), dhi[...], dlo[...]))


def detect_tiles(n, tile, tables, y_hi, y_lo, out, done, between):
    dhi, dlo, bhi, blo = tables[:4]

    def group(g, _):
        rows = pl.ds(pl.multiple_of(g * 64, 64), 64)
        hi, lo = filtered([tile(t, rows) for t in range(n + 2)], dhi, dlo)
        for j in range(n):
            y_hi[rows, j * LANES : (j + 1) * LANES] = hi[64 * j : 64 * j + 64]
            y_lo[rows, j * LANES : (j + 1) * LANES] = lo[64 * j : 64 * j + 64]
        return 0

    lax.fori_loop(0, 4, group, 0, unroll=2)
    between()
    for j0 in range(0, n, 2):
        lanes = slice(j0 * LANES, min(j0 + 2, n) * LANES)
        out[:, lanes] = mm3(bhi[...], blo[...], y_hi[:, lanes], y_lo[:, lanes])
        done(j0, lanes)


def early_kernel(n, *refs):
    tables, (x, out, rim, context, y_hi, y_lo) = refs[:4], refs[4:]
    context[...] = x[:, (n - 1) * LANES : (n + 1) * LANES]

    def tile(t, rows):
        if t == 0:
            return jnp.zeros((64, LANES), F32)
        return x[rows, (t - 1) * LANES : t * LANES]

    detect_tiles(n, tile, tables, y_hi, y_lo, out, lambda *_: None, lambda: None)
    rim[0:16, :] = out[0:16, :]
    rim[16:32, :] = out[240:256, :]


def early_detect(n, coadd, tables):
    tables = tables[:4]
    width = (n + 1) * LANES
    return pl.pallas_call(
        functools.partial(early_kernel, n),
        grid=(1,),
        out_shape=[
            jax.ShapeDtypeStruct(coadd.shape, F32),
            jax.ShapeDtypeStruct((32, n * LANES), F32),
            jax.ShapeDtypeStruct((256, 2 * LANES), F32),
        ],
        in_specs=[full(a.shape) for a in tables] + [full((256, width))],
        out_specs=[full((256, n * LANES)), full((32, n * LANES)), full((256, 2 * LANES))],
        scratch_shapes=[pltpu.VMEM((256, n * LANES), BF), pltpu.VMEM((256, n * LANES), BF)],
        compiler_params=pltpu.CompilerParams(vmem_limit_bytes=16 << 20),
        cost_estimate=pl.CostEstimate(
            flops=10**9, bytes_accessed=1 << 20, transcendentals=0
        ),
        name="early",
    )(*tables, coadd)


def late_kernel(first, nt, n, vis_ref, mass, *refs):
    tables, group, (before, after, left, rim) = refs[:6], refs[6:10], refs[10:14]
    coadd_out, out, sides, coadd, y_hi, y_lo, det, near, sems = refs[16:]
    weight = mass[...]
    last = first + nt
    start = last - n - 1
    copies = []

    def send(src, dst):
        copy = pltpu.make_async_copy(src, dst, sems.at[len(copies)])
        copy.start()
        copies.append(copy)

    def block(i, _):
        inverse = inverse_weight(weight, i + 1)
        for d in range(4):
            lanes = pl.ds(pl.multiple_of(((vis_ref[0] - d) & 3) * LANES, LANES), LANES)
            for h in range(2):
                rows = pl.ds(pl.multiple_of(i * 16 + 8 * h, 8), 8)
                coadd[rows, lanes] = group[d][i * 2 + (2 + h)] * inverse
        return 0

    lax.fori_loop(0, 16, block, 0, unroll=4)
    send(coadd, coadd_out.at[:, first * LANES : last * LANES])

    def tile(t, rows):
        real = start + t
        if real >= last:
            return jnp.zeros((64, LANES), F32)
        if real < first:
            return left[rows, t * LANES : (t + 1) * LANES]
        return coadd[rows, (real - first) * LANES : (real - first + 1) * LANES]

    whole_left = slice(0, (start + 1) * LANES)

    def between():
        for e in range(2):
            inverse = inverse_weight(weight, (SPAN - 1) * e)
            for d in range(4):
                lanes = pl.ds(pl.multiple_of(((vis_ref[0] - d) & 3) * LANES, LANES), LANES)
                for h in range(2):
                    rows = slice(16 * e + 8 * h, 16 * e + 8 * h + 8)
                    near[rows, lanes] = group[d][2 * (SPAN - 1) * e + h] * inverse
        strips = [jnp.zeros((32, LANES), F32)]
        for t in range(last):
            lanes = slice(t * LANES, (t + 1) * LANES)
            if t < first:
                own = jnp.concatenate([before[:, lanes], after[:, lanes]], axis=0)
            else:
                own = near[:, (t - first) * LANES : (t - first + 1) * LANES]
            strips.append(own)
        hi, lo = filtered(strips + strips[:1], tables[0], tables[1])
        side = lambda v: jnp.concatenate([v[32 * j : 32 * j + 32] for j in range(last)], axis=1)
        sides[...] = mm3(tables[4][...], tables[5][...], side(hi), side(lo))
        sides[:, whole_left] += rim[...]

    def done(j0, lanes):
        there = slice((start + 1) * LANES + lanes.start, (start + 1) * LANES + lanes.stop)
        sides[0:16, there] += det[0:16, lanes]
        sides[16:32, there] += det[240:256, lanes]
        det[0:16, lanes] = sides[0:16, there]
        det[240:256, lanes] = sides[16:32, there]
        send(det.at[:, lanes], out.at[:, there])

    detect_tiles(n, tile, tables, y_hi, y_lo, det, done, between)
    send(sides.at[0:16, whole_left], out.at[0:16, whole_left])
    send(sides.at[16:32, whole_left], out.at[240:256, whole_left])
    for copy in copies:
        copy.wait()


def late_detect(vis, mass, group, first, nt, n, halos, tables, left, coadd, before):
    detection, rim = before
    any_spec = pl.BlockSpec(memory_space=pl.ANY)
    vmem = pl.BlockSpec(memory_space=pltpu.VMEM)
    args = [vis, mass, *tables, *group, *halos, left, rim, coadd, detection]
    return pl.pallas_call(
        functools.partial(late_kernel, first, nt, n),
        out_shape=[jax.ShapeDtypeStruct(coadd.shape, F32)] * 2
        + [jax.ShapeDtypeStruct((32, (first + nt) * LANES), F32)],
        in_specs=[pl.BlockSpec(memory_space=pltpu.SMEM)]
        + [vmem] * (len(args) - 3)
        + [any_spec] * 2,
        out_specs=[any_spec] * 2 + [vmem],
        scratch_shapes=[
            pltpu.VMEM((256, nt * LANES), F32),
            pltpu.VMEM((256, n * LANES), BF),
            pltpu.VMEM((256, n * LANES), BF),
            pltpu.VMEM((256, n * LANES), F32),
            pltpu.VMEM((32, nt * LANES), F32),
            pltpu.SemaphoreType.DMA((3 + (n + 1) // 2,)),
        ],
        input_output_aliases={len(args) - 2: 0, len(args) - 1: 1},
        compiler_params=pltpu.CompilerParams(vmem_limit_bytes=12 << 20),
        cost_estimate=pl.CostEstimate(
            flops=2 * 10**9, bytes_accessed=4 << 20, transcendentals=0
        ),
        name="late",
    )(*args)


def end_kernel(vis_ref, dhi, dlo, ehi, elo, other, sides, unused, out, rows, sem):
    me = vis_ref[0]
    n = other.shape[1] // LANES

    @pl.when((me == 0) | (me == 3))
    def _():
        strips = [jnp.zeros((16, LANES), F32)]
        strips += [other[:, t * LANES : (t + 1) * LANES] for t in range(n)]
        hi, lo = filtered(strips + strips[:1], dhi, dlo)
        side = lambda v: jnp.concatenate([v[16 * j : 16 * j + 16] for j in range(n)], axis=1)
        both = mm3(ehi[...], elo[...], side(hi), side(lo))
        rows[...] = jnp.where(
            me == 0, sides[0:16] + both[0:16], sides[16:32] + both[16:32]
        )
        at = pl.ds(pl.multiple_of(jnp.where(me == 0, 0, 240), 16), 16)
        copy = pltpu.make_async_copy(rows, out.at[at, :], sem)
        copy.start()
        copy.wait()


def end_detect(vis, tables, other, sides, detection):
    any_spec = pl.BlockSpec(memory_space=pl.ANY)
    vmem = pl.BlockSpec(memory_space=pltpu.VMEM)
    dhi, dlo = tables[:2]
    ehi, elo = tables[6:]
    return pl.pallas_call(
        end_kernel,
        out_shape=jax.ShapeDtypeStruct(detection.shape, F32),
        in_specs=[pl.BlockSpec(memory_space=pltpu.SMEM)] + [vmem] * 6 + [any_spec],
        out_specs=any_spec,
        scratch_shapes=[pltpu.VMEM(other.shape, F32), pltpu.SemaphoreType.DMA],
        input_output_aliases={7: 0},
        compiler_params=pltpu.CompilerParams(vmem_limit_bytes=4 << 20),
        cost_estimate=pl.CostEstimate(flops=10**8, bytes_accessed=1 << 18, transcendentals=0),
        name="end",
    )(vis, dhi, dlo, ehi, elo, other, sides, detection)


def detect_tables():
    dhi, dlo = halves(detect_taps(window_lags(128)))
    idx = np.arange(256, dtype=np.float64)
    bhi, blo = halves(detect_taps(idx[None, :] - idx[:, None]))
    q = np.arange(16, dtype=np.float64)
    edge = np.zeros((32, 32))
    edge[0:16, 0:16] = detect_taps((q[None, :] - 16) - q[:, None])
    edge[16:32, 16:32] = detect_taps((q[None, :] + 16) - q[:, None])
    ehi, elo = halves(edge)
    fhi, flo = halves(edge[:, 0:16] + edge[:, 16:32])
    return dhi, dlo, bhi, blo, ehi, elo, fhi, flo


def shards(pieces, coeffs, weights, routes, offsets):
    count, rows, width = pieces.shape
    pieces2d = pieces.reshape(count * rows, width)
    route1 = routes.reshape(count)
    coeffs_t = jnp.transpose(coeffs, (1, 2, 0))
    whi, wlo = column_weights()
    tables = (jnp.asarray(row_tables()), jnp.asarray(whi), jnp.asarray(wlo))
    dtables = tuple(jnp.asarray(a) for a in detect_tables())
    vis = lax.axis_index("vis").reshape(1)
    nv = lax.axis_size("vis")
    n = lax.axis_size("tile") * nv
    shifts = [[(i, (i + d) % nv) for i in range(nv)] for d in (1, 2, 3)]
    axes = ("tile", "vis")

    first, nt = CHUNKS
    per = 2 * first

    def over_vis(group):
        moved = [group[0]]
        for d in (0, 2, 1):
            moved.append(lax.ppermute(group[d + 1], "vis", shifts[d]))
        return [moved[0], moved[1], moved[3], moved[2]]

    def over_tile(slots):
        return lax.all_to_all(slots, "tile", split_axis=0, concat_axis=0, tiled=True)

    slots = match_slots((route1, offsets, weights, coeffs_t), tables, pieces2d, first)
    recv = over_tile(slots)
    meta = recv[:, 4 * first, 0:2, 0:2]
    landed = land_call(
        functools.partial(land_kernel, first), vis, meta, recv, [SPAN * per + 1] * 3 + [SPAN * first + 1] * 2,
        [
            pltpu.VMEM((66, per, 8, LANES), F32),
            pltpu.VMEM((8, LANES), F32),
            pltpu.SMEM((64,), jnp.int32),
        ],
    )
    blocks = jnp.pad(meta[:, :, 0].T, ((0, 6), (0, LANES - count)))
    told = over_vis([blocks] * nv)
    spot = jnp.stack([x[0:2, 0:count] for x in told]).astype(jnp.int32)
    spot = jnp.transpose(spot, (0, 2, 1))
    own, p1, m1, p2, m2 = landed
    head = p2.shape[0]
    p1 = lax.ppermute(p1, "vis", shifts[0])
    m1 = lax.ppermute(m1, "vis", shifts[2])
    p2 = lax.ppermute(p2 + p1[:head], "vis", shifts[0])
    m2 = lax.ppermute(m2 + m1[:head], "vis", shifts[2])

    facts = jnp.stack([route1.astype(F32), offsets.astype(F32)])
    facts = jnp.pad(facts, ((0, 6), (0, LANES - count)))
    spread = match_call(
        spread_kernel, (vis, weights, coeffs_t), tables, pieces2d, (facts,), first, nt,
        [(2 * count + 1, 8, LANES)] * 4, [],
    )
    traded = over_vis(spread)
    notes = jnp.stack([x[2 * count, 0:2, 0:count] for x in traded])
    slots = pack(notes, traded)
    recv = over_tile(slots)
    landed = land_right(vis, spot, recv)
    bulk = over_vis(landed)

    coadd, mass, top, bottom, *outside = first_coadd((own, p1, m1, p2, m2), first)
    edge = join_edges(vis, mass, bulk, first, top, bottom)
    swaps = [(i - 1, i) for i in range(nv, n, nv)] + [(i, i - 1) for i in range(nv, n, nv)]
    other = lax.ppermute(edge, axes, swaps)
    *before, left = early_detect(first - 1, coadd, dtables)
    coadd, detection, sides = late_detect(
        vis, mass, bulk, first, nt, nt + 1, outside, dtables[:6], left, coadd, before
    )
    detection = end_detect(vis, dtables, other, sides, detection)
    return (coadd, detection)


def solution(mesh):
    placed = (
        P(("tile", "vis"), None, None),
        P(("tile", "vis"), None, None),
        P(("tile", "vis")),
        P(("tile", "vis"), None),
        P(("tile", "vis")),
    )
    return jax.shard_map(
        shards,
        mesh=mesh,
        in_specs=placed,
        out_specs=(P(("tile", "vis"), None), P(("tile", "vis"), None)),
        check_vma=False,
    )
```
